32 devices in a mesh: rows: 8 (over z, y), blk: 4 (over x, core).
Axes of the slice: x: 2, y: 2, z: 4, core: 2. Of those that a mesh axis runs over, the one named last changes fastest.
Arguments:
- tokens: bfloat16 [8, 2048, 768], P('rows', 'blk'), may hold values from -6 to 6
- seg_ids: int32 [8, 2048], P('rows', 'blk'), may hold values from 0 to 3, never falling along the last dimension, each value on 1 to 1024 neighbouring positions
- valid_len: int32 [8], P('rows'), may hold values from 1792 to 2048, as said below
- ln1_gain: float32 [768], replicated, may hold values from 0.5 to 1.5
- ln1_bias: float32 [768], replicated, may hold values from -3 to 3
- w_qkv: bfloat16 [768, 2304], replicated, may hold values from -0.21875 to 0.21875
- b_qkv: float32 [2304], replicated, may hold values from -3 to 3
- w_out: bfloat16 [768, 768], replicated, may hold values from -3.5 to 3.5
- b_out: float32 [768], replicated, may hold values from -2 to 2
- ln2_gain: float32 [768], replicated, may hold values from 0.5 to 1.5
- ln2_bias: float32 [768], replicated, may hold values from -3 to 3
- w_up: bfloat16 [768, 3072], replicated, may hold values from -0.21875 to 0.21875
- b_up: float32 [3072], replicated, may hold values from -3 to 3
- w_down: bfloat16 [3072, 768], replicated, may hold values from -0.109375 to 0.109375
- b_down: float32 [768], replicated, may hold values from -2 to 2
- cotangent: bfloat16 [8, 2048, 768], P('rows', 'blk'), may hold values from -6 to 6
Outputs:
- out: bfloat16 [8, 2048, 768], P('rows', 'blk')
- grad_tokens: bfloat16 [8, 2048, 768], P('rows', 'blk')
- grad_w_qkv: float32 [768, 2304], P('rows', 'blk')
- grad_w_out: float32 [768, 768], P('rows', 'blk')
- grad_w_up: float32 [768, 3072], P('rows', 'blk')
- grad_w_down: float32 [3072, 768], P('rows', 'blk')
- grad_b_qkv: float32 [2304], replicated
- grad_b_out: float32 [768], replicated
- grad_b_up: float32 [3072], replicated
- grad_b_down: float32 [768], replicated
- grad_ln1_gain: float32 [768], replicated
- grad_ln1_bias: float32 [768], replicated
- grad_ln2_gain: float32 [768], replicated
- grad_ln2_bias: float32 [768], replicated
The draws below stay inside these ranges and needn't reach their ends.
Inputs may be any that keep to these rules, and one draw needn't show every extreme that they name: `seg_ids`: segment numbers never fall along a row; a segment holds at most half of the row's 2048 positions, and one holds exactly that many. `valid_len`: some row is full and some row has the fewest valid positions.
All inputs are finite; a program needn't handle non-finite values.
Results may differ from the reference program's by a relative error of at most 0.013.
Values may be sent and summed in bfloat16 or wider, within the bound.
No kernel may reach another device: no remote copies, remote signals or barrier semaphores. Data moves between devices by JAX's collectives and lax.ppermute only.
A program may use at most 128 MiB of HBM per device.

```python
import math
import jax
import jax.numpy as jnp
import numpy as np
from jax import lax

D = 768
HEADS = 12
HDIM = 64
ROT = 16
FF = 3072
SEGS = 4
SEQ_BLK = 512
LENGTH = 2048
ROWS = 8
N_BLK = 4


def draw_valid_len(key, part):
    fewest = LENGTH - SEQ_BLK // 2
    counts = jax.random.randint(jax.random.fold_in(key, 1), (ROWS,), fewest, LENGTH + 1)
    shuffle = jax.random.permutation(jax.random.fold_in(key, 2), ROWS)
    places = jnp.arange(ROWS)
    counts = jnp.where(places == shuffle[0], LENGTH, counts)
    counts = jnp.where(places == shuffle[1], fewest, counts)
    return counts.astype(jnp.int32)


def levels(stream_key, shape, split, least, high):
    level = 1.0
    for axis_at, shards_of in split:
        heights = jax.random.uniform(jax.random.fold_in(jax.random.fold_in(stream_key, 6), axis_at), (shards_of,), jnp.float32, least / len(split), high / len(split))
        level = level * jnp.repeat(jnp.exp(heights), shape[axis_at] // shards_of).reshape((-1,) + (1,) * (len(shape) - 1 - axis_at))
    return level


def split_up(count, total, limit, skew):
    loads = [(1 << 20) // math.isqrt(grade ** skew) + 1 for grade in range(2, count + 1)]
    spare, holding = total - limit - (count - 1), [1] * (count - 1)
    while spare > 0:
        candidates = [i for i in range(count - 1) if holding[i] < limit]
        mass, remaining = sum([loads[i] for i in candidates]), spare
        for i in candidates:
            more = min(limit - holding[i], max(1, remaining * loads[i] // mass), spare)
            holding[i] = holding[i] + more
            spare = spare - more
    return np.array([limit] + holding)


def uneven(key, amount, total, reach, skew):
    if amount == 2:
        one = jax.random.randint(key, (), max(1, total - reach), min(reach, total - 1) + 1)
        return jnp.stack([one, total - one])
    sizes = jnp.asarray(split_up(amount, total, reach, skew), jnp.int32)
    twos = (amount - 1) // 2
    source_of, taker = sizes[1:1 + 2 * twos:2], sizes[2:2 + 2 * twos:2]
    slack = jnp.minimum(source_of - 1, reach - taker)
    shifted = jax.random.randint(jax.random.fold_in(key, 1), (twos,), 0, 1 << 20) % (slack + 1)
    sizes = sizes.at[1:1 + 2 * twos:2].set(source_of - shifted).at[2:2 + 2 * twos:2].set(taker + shifted)
    return sizes[jax.random.permutation(jax.random.fold_in(key, 2), amount)]


def bell_draw(own_key, shape, width, bound, pieces=(), held_as=jnp.bfloat16):
    level = levels(own_key, shape, pieces, -0.22, 0.18) if pieces else 1.0
    values = jax.random.normal(own_key, shape, jnp.float32) * width * level
    return jnp.minimum(jnp.maximum(values, -bound), bound).astype(held_as)


def setup_inputs(seed: int = 0) -> dict:
    arg_keys = jax.random.split(jax.random.key(seed), 17)
    tokens = bell_draw(arg_keys[0], (ROWS, LENGTH, D), 1.0, 6.0, ((0, 8), (1, 4)))
    seg_ids = jax.vmap(lambda own: jnp.searchsorted(jnp.cumsum(uneven(own, SEGS, LENGTH, LENGTH // 2, 0)), jnp.arange(LENGTH), side="right"))(jax.random.split(arg_keys[1], ROWS)).reshape((ROWS, LENGTH)).astype(jnp.int32)
    valid_len = draw_valid_len(jax.random.fold_in(arg_keys[16], 71), 0)
    ln1_gain = jnp.clip(1.0 + 0.1 * jax.random.normal(arg_keys[3], (D,), jnp.float32), 0.5, 1.5)
    ln1_bias = bell_draw(arg_keys[4], (D,), 0.5, 3.0, (), jnp.float32)
    w_qkv = bell_draw(arg_keys[5], (D, 3 * D), D ** -0.5, 0.21875)
    b_qkv = bell_draw(arg_keys[6], (3 * D,), 0.5, 3.0, (), jnp.float32)
    w_out = bell_draw(arg_keys[7], (D, D), (max(D // 256, 1)) ** -0.5, 3.5)
    b_out = bell_draw(arg_keys[8], (D,), 0.3, 2.0, (), jnp.float32)
    ln2_gain = jnp.clip(1.0 + 0.1 * jax.random.normal(arg_keys[9], (D,), jnp.float32), 0.5, 1.5)
    ln2_bias = bell_draw(arg_keys[10], (D,), 0.5, 3.0, (), jnp.float32)
    w_up = bell_draw(arg_keys[11], (D, FF), D ** -0.5, 0.21875)
    b_up = bell_draw(arg_keys[12], (FF,), 0.5, 3.0, (), jnp.float32)
    w_down = bell_draw(arg_keys[13], (FF, D), FF ** -0.5, 0.109375)
    b_down = bell_draw(arg_keys[14], (D,), 0.3, 2.0, (), jnp.float32)
    cotangent = bell_draw(arg_keys[15], (ROWS, LENGTH, D), 1.0, 6.0, ((0, 8), (1, 4)))
    return dict(tokens=tokens, seg_ids=seg_ids, valid_len=valid_len, ln1_gain=ln1_gain, ln1_bias=ln1_bias, w_qkv=w_qkv, b_qkv=b_qkv, w_out=w_out, b_out=b_out, ln2_gain=ln2_gain, ln2_bias=ln2_bias, w_up=w_up, b_up=b_up, w_down=w_down, b_down=b_down, cotangent=cotangent)


@jax.custom_vjp
def low(v):
    return lax.optimization_barrier(v.astype(jnp.bfloat16)).astype(jnp.float32)

@jax.custom_vjp
def low_back(v):
    return v

def low_keep(v):
    return (low(v), None)

def low_pass(kept, grad):
    return (grad,)

def back_keep(v):
    return (v, None)

def back_low(kept, grad):
    return (low(grad),)
low.defvjp(low_keep, low_pass)
low_back.defvjp(back_keep, back_low)
EPS = 1e-05
HIGH = lax.Precision.HIGHEST
MASKED = -1e+30

def layer_norm(value, gain, shift):
    center = value - lax.optimization_barrier(jnp.mean(value, axis=-1, keepdims=True))
    spread = lax.optimization_barrier(jnp.mean(center * center, axis=-1, keepdims=True))
    return center * lax.rsqrt(spread + EPS) * gain + shift

def angle_table(positions):
    inverse = jnp.exp(-jnp.log(10000.0) * (2.0 * jnp.arange(ROT // 2, dtype=jnp.float32) / ROT))
    return positions.astype(jnp.float32)[:, None] * inverse[None, :]

def rotate(tensor, angles):
    half_rot = ROT // 2
    former = tensor[..., :half_rot]
    latter = tensor[..., half_rot:ROT]
    cos_table = jnp.cos(angles)[:, None, :]
    sin_table = jnp.sin(angles)[:, None, :]
    return jnp.concatenate([former * cos_table - latter * sin_table, latter * cos_table + former * sin_table, tensor[..., ROT:]], axis=-1)

def attend_block(query_block, query_tags, query_start, keys, values, key_tags):
    scores = low_back(jnp.einsum('qhd,khd->hqk', query_block, keys, precision=HIGH) * HDIM ** (-0.5))
    query_pos = query_start + jnp.arange(SEQ_BLK, dtype=jnp.int32)
    key_pos = jnp.arange(LENGTH, dtype=jnp.int32)
    earlier = key_pos[None, :] < query_pos[:, None]
    allowed = (key_pos[None, :] == query_pos[:, None]) | earlier & (key_tags[None, :] == query_tags[:, None]) & (query_tags[:, None] >= 0)
    masked = jnp.where(allowed[None], scores, MASKED)
    weights = low(jax.nn.softmax(masked, axis=-1))
    return jnp.einsum('hqk,khd->qhd', weights, values, precision=HIGH)

def forward_row(row_in, tags, params):
    ln1_gain, ln1_bias, w_qkv, b_qkv, w_out, b_out, ln2_gain, ln2_bias, w_up, b_up, w_down, b_down = params
    attn_in = low(layer_norm(row_in, ln1_gain, ln1_bias))
    joined = low_back(jnp.dot(attn_in, w_qkv, precision=HIGH) + b_qkv)
    angles = angle_table(jnp.arange(LENGTH, dtype=jnp.int32))
    query = low(rotate(joined[:, :D].reshape(LENGTH, HEADS, HDIM), angles))
    keys = low(rotate(joined[:, D:2 * D].reshape(LENGTH, HEADS, HDIM), angles))
    values = low(joined[:, 2 * D:].reshape(LENGTH, HEADS, HDIM))

    def attend(items):
        return attend_block(items[0], items[1], items[2], keys, values, tags)
    heads = lax.map(jax.checkpoint(attend), (query.reshape(N_BLK, SEQ_BLK, HEADS, HDIM), tags.reshape(N_BLK, SEQ_BLK), jnp.arange(N_BLK, dtype=jnp.int32) * SEQ_BLK))
    attn_vec = low(low_back(heads.reshape(LENGTH, D)))
    attn = jnp.dot(attn_vec, w_out, precision=HIGH) + b_out
    mlp_in = low(layer_norm(row_in, ln2_gain, ln2_bias))
    hidden = low_back(jnp.dot(mlp_in, w_up, precision=HIGH) + b_up)
    act = low(jax.nn.gelu(hidden, approximate=False))
    mlp = jnp.dot(act, w_down, precision=HIGH) + b_down
    return row_in + attn + mlp

def reference(tokens, seg_ids, valid_len, ln1_gain, ln1_bias, w_qkv, b_qkv, w_out, b_out, ln2_gain, ln2_bias, w_up, b_up, w_down, b_down, cotangent):
    params = tuple((item.astype(jnp.float32) for item in (ln1_gain, ln1_bias, w_qkv, b_qkv, w_out, b_out, ln2_gain, ln2_bias, w_up, b_up, w_down, b_down)))

    def row_step(totals, row_items):
        row_in, row_seg, row_valid, row_cot = row_items
        places = jnp.arange(LENGTH, dtype=jnp.int32)
        tags = jnp.where(places < row_valid, row_seg, -1).astype(jnp.int32)

        def row_forward(inputs, weights):
            return forward_row(inputs, tags, weights)
        result, pullback = jax.vjp(row_forward, row_in.astype(jnp.float32), params)
        grad_in, grad_params = pullback(row_cot.astype(jnp.float32))
        totals = jax.tree.map(jnp.add, totals, grad_params)
        return (totals, (result.astype(jnp.bfloat16), grad_in.astype(jnp.bfloat16)))
    zeros = jax.tree.map(jnp.zeros_like, params)
    totals, (outputs, grad_tokens) = lax.scan(row_step, zeros, (tokens, seg_ids, valid_len, cotangent))
    grad_ln1_gain, grad_ln1_bias, grad_w_qkv, grad_b_qkv, grad_w_out, grad_b_out, grad_ln2_gain, grad_ln2_bias, grad_w_up, grad_b_up, grad_w_down, grad_b_down = totals
    return (outputs, grad_tokens, grad_w_qkv, grad_w_out, grad_w_up, grad_w_down, grad_b_qkv, grad_b_out, grad_b_up, grad_b_down, grad_ln1_gain, grad_ln1_bias, grad_ln2_gain, grad_ln2_bias)
```

```python
import math
from functools import partial

import jax
import jax.numpy as jnp
import numpy as np
from jax import lax
from jax.experimental import pallas as pl
from jax.experimental.pallas import tpu as pltpu
from jax.sharding import PartitionSpec as P

D = 768
HEADS = 12
HDIM = 64
ROT = 16
FF = 3072
EPS = 1e-05
MASKED = -1e30
TILE = 256
LANES = 128
F32 = jnp.float32
BF16 = jnp.bfloat16
NT_DIMS = (((1,), (1,)), ((), ()))
TN_DIMS = (((0,), (0,)), ((), ()))


def dot(left, right):
    return jnp.dot(left, right, preferred_element_type=F32)


def dot_nt(left, right):
    return lax.dot_general(left, right, NT_DIMS, preferred_element_type=F32)


def dot_tn(left, right):
    return lax.dot_general(left, right, TN_DIMS, preferred_element_type=F32)


def normalize(value):
    center = value - jnp.mean(value, axis=-1, keepdims=True)
    spread = jnp.mean(center * center, axis=-1, keepdims=True)
    return center * lax.rsqrt(spread + EPS)


def angle_parts(length):
    dim = np.arange(LANES) % HDIM
    inverse = np.where(dim < ROT, 10000.0 ** (-2.0 * (dim % (ROT // 2)) / ROT), 0.0)
    high = (np.arange(length // LANES) * LANES)[:, None] * inverse
    low = np.arange(LANES)[:, None] * inverse
    parts = np.stack([np.cos(low), np.sin(low)]), np.stack([np.cos(high), np.sin(high)])
    return tuple(jnp.asarray(part, F32) for part in parts)


def rotation(low_ref, high_ref, tile):
    lane = lax.broadcasted_iota(jnp.int32, (1, LANES), 1) % HDIM
    sign = jnp.where(lane < ROT // 2, -1.0, 1.0)
    cos_rows, sin_rows = [], []
    for part in range(TILE // LANES):
        row = tile * (TILE // LANES) + part
        cos_high = high_ref[0, pl.ds(row, 1), :]
        sin_high = high_ref[1, pl.ds(row, 1), :]
        cos_rows.append(low_ref[0] * cos_high - low_ref[1] * sin_high)
        sin_rows.append((low_ref[1] * cos_high + low_ref[0] * sin_high) * sign)
    return jnp.concatenate(cos_rows, axis=0), jnp.concatenate(sin_rows, axis=0)


def swap_halves(value):
    lane = lax.broadcasted_iota(jnp.int32, value.shape, 1) % HDIM
    half = ROT // 2
    return jnp.where(
        lane < half, pltpu.roll(value, LANES - half, 1), pltpu.roll(value, half, 1)
    )


def true_block(meta_ref, slot):
    return jnp.bitwise_xor(meta_ref[0], slot)


def params(*semantics, vmem=None):
    return pltpu.CompilerParams(
        dimension_semantics=semantics or ("arbitrary",), vmem_limit_bytes=vmem or 60 * 2**20
    )


def whole(shape):
    return pl.BlockSpec(shape, lambda *_: (0,) * len(shape))


def qkv_kernel(slot, meta, x_ref, gain, shift, w_ref, b_ref, low, high, *refs):
    q_ref, k_ref, v_ref = refs[-3:]
    per = x_ref.shape[0] // TILE
    for part in range(per):
        rows = pl.ds(part * TILE, TILE)
        normed = normalize(x_ref[rows, :].astype(F32))
        attn_in = (normed * gain[...] + shift[...]).astype(BF16)
        joined = dot(attn_in, w_ref[...]) + b_ref[...]
        cos, sin = rotation(low, high, true_block(meta, slot) * per + part)
        scale = HDIM**-0.5

        def turn(block):
            return block * cos + swap_halves(block) * sin

        query = turn(joined[:, 0:128]) * scale
        keys = turn(joined[:, 128:256])
        mixed = turn(joined[:, 256:384])
        q_ref[rows, 0:128] = query.astype(BF16)
        k_ref[rows, 0:128] = keys.astype(BF16)
        q_ref[rows, 128:192] = (mixed[:, 0:64] * scale).astype(BF16)
        k_ref[rows, 128:192] = mixed[:, 64:128].astype(BF16)
        v_ref[rows, :] = joined[:, 384:576].astype(BF16)


def project(slot, meta, x, gain, shift, w, b, low, high, filled):
    seq = x.shape[0]
    width = w.shape[1] // 3
    total = 4 * seq
    out = jax.ShapeDtypeStruct((total, width), BF16)
    out_spec = pl.BlockSpec((seq, width), lambda i, m: (slot, 0))
    args = [x, gain, shift, w, b, low, high]
    specs = [whole(a.shape) for a in args]
    aliases = {}
    if filled is not None:
        aliases = {1 + len(args) + i: i for i in range(3)}
        args += list(filled)
        specs += [pl.BlockSpec(memory_space=pl.ANY)] * 3
    return pl.pallas_call(
        partial(qkv_kernel, slot),
        out_shape=[out] * 3,
        grid_spec=pltpu.PrefetchScalarGridSpec(
            num_scalar_prefetch=1, grid=(1,), in_specs=specs, out_specs=[out_spec] * 3
        ),
        input_output_aliases=aliases,
        compiler_params=params(),
        cost_estimate=pl.CostEstimate(
            flops=2 * seq * D * 3 * width, bytes_accessed=4 * seq * D, transcendentals=0
        ),
        name=f"qkv_{slot}",
    )(meta, *args)


def mlp_kernel(final, meta, *refs):
    if final:
        (xa, xb, ca, cb, gain, shift, w_up, b_up, w_down, w_out) = refs[:10]
        (up_in, down_in, b_in, g_in, s_in) = refs[10:15]
    else:
        (xa, xb, ca, cb, gain, shift, w_up, b_up, w_down, w_out) = refs[:10]
    (mo_ref, e_ref, gv_ref, gup_ref, gdown_ref, gb_ref, gg_ref, gs_ref) = refs[-12:-4]
    x_s, c_s, up_s, down_s = refs[-4:]
    step = pl.program_id(0)
    half = pl.num_programs(0) // 2

    @pl.when(step < half)
    def _():
        x_s[...] = xa[...]
        c_s[...] = ca[...]

    @pl.when(step >= half)
    def _():
        x_s[...] = xb[...]
        c_s[...] = cb[...]

    @pl.when(step == 0)
    def _():
        if final:
            up_s[...] = up_in[...]
            down_s[...] = down_in[...]
            gb_ref[...] = b_in[...]
            gg_ref[...] = g_in[...]
            gs_ref[...] = s_in[...]
        else:
            up_s[...] = jnp.zeros_like(up_s)
            down_s[...] = jnp.zeros_like(down_s)
            gb_ref[...] = jnp.zeros_like(gb_ref)
            gg_ref[...] = jnp.zeros_like(gg_ref)
            gs_ref[...] = jnp.zeros_like(gs_ref)

    normed = normalize(x_s[...].astype(F32))
    mlp_in = (normed * gain[...] + shift[...]).astype(BF16)
    upstream = c_s[...]
    hidden = dot(mlp_in, w_up[...]) + b_up[...]
    cdf = 0.5 * (1.0 + lax.erf(hidden * (0.5**0.5)))
    act = (hidden * cdf).astype(BF16)
    slope = cdf + hidden * jnp.exp(-0.5 * hidden * hidden) * ((2.0 * math.pi) ** -0.5)
    mo_ref[...] = dot(act, w_down[...]).astype(BF16)
    grad_act = dot_nt(upstream, w_down[...])
    grad_hidden = slope * grad_act
    grad_low = grad_hidden.astype(BF16)
    gb_ref[...] += jnp.sum(grad_low.astype(F32), axis=0, keepdims=True)
    grad_norm = dot_nt(grad_low, w_up[...])
    gg_ref[...] += jnp.sum(grad_norm * normed, axis=0, keepdims=True)
    gs_ref[...] += jnp.sum(grad_norm, axis=0, keepdims=True)
    e_ref[...] = (grad_norm * gain[...]).astype(BF16)
    gv_ref[...] = dot_nt(upstream, w_out[...]).astype(BF16)
    up_s[...] += dot_tn(mlp_in, grad_low)
    down_s[...] += dot_tn(act, upstream)

    @pl.when(step == pl.num_programs(0) - 1)
    def _():
        gup_ref[...] = up_s[...].astype(gup_ref.dtype)
        gdown_ref[...] = down_s[...].astype(gdown_ref.dtype)


def feed_forward(pair, meta, xs, cs, gain, shift, w_up, b_up, w_down, w_out, before):
    seq = xs[0].shape[0]
    per = seq // TILE
    steps = 2 * per
    hid = FF // 4
    width = D // 4
    first = pl.BlockSpec((TILE, D), lambda i, m: (jnp.minimum(i, per - 1), 0))
    second = pl.BlockSpec((TILE, D), lambda i, m: (jnp.maximum(i - per, 0), 0))
    row = whole((1, D))
    specs = [
        first,
        second,
        first,
        second,
        row,
        row,
        pl.BlockSpec((D, hid), lambda i, m: (0, m[0])),
        pl.BlockSpec((1, hid), lambda i, m: (0, m[0])),
        pl.BlockSpec((hid, D), lambda i, m: (m[0], 0)),
        pl.BlockSpec((width, D), lambda i, m: (m[0], 0)),
    ]
    args = [*xs, *cs, gain, shift, w_up, b_up, w_down, w_out]
    aliases = {}
    grad_type = F32
    if before is not None:
        grad_type = BF16
        args += list(before[3:]) + list(before[:3])
        specs += [whole(a.shape) for a in before[3:]]
        specs += [pl.BlockSpec(memory_space=pl.ANY)] * 3
        aliases = {1 + len(args) - 3 + i: i for i in range(3)}
    base = pair * steps

    def rows(cols):
        return pl.BlockSpec((TILE, cols), lambda i, m: (i + base, 0))

    total = 4 * seq
    return pl.pallas_call(
        partial(mlp_kernel, before is not None),
        out_shape=[
            jax.ShapeDtypeStruct((total, D), BF16),
            jax.ShapeDtypeStruct((total, D), BF16),
            jax.ShapeDtypeStruct((total, width), BF16),
            jax.ShapeDtypeStruct((D, hid), grad_type),
            jax.ShapeDtypeStruct((hid, D), grad_type),
            jax.ShapeDtypeStruct((1, hid), F32),
            jax.ShapeDtypeStruct((1, D), F32),
            jax.ShapeDtypeStruct((1, D), F32),
        ],
        grid_spec=pltpu.PrefetchScalarGridSpec(
            num_scalar_prefetch=1,
            grid=(steps,),
            in_specs=specs,
            out_specs=[
                rows(D),
                rows(D),
                rows(width),
                whole((D, hid)),
                whole((hid, D)),
                whole((1, hid)),
                row,
                row,
            ],
            scratch_shapes=[
                pltpu.VMEM((TILE, D), BF16),
                pltpu.VMEM((TILE, D), BF16),
                pltpu.VMEM((D, hid), F32),
                pltpu.VMEM((hid, D), F32),
            ],
        ),
        input_output_aliases=aliases,
        compiler_params=params(),
        cost_estimate=pl.CostEstimate(
            flops=2 * 6 * 2 * seq * D * hid, bytes_accessed=20 * seq * D, transcendentals=0
        ),
        name=f"mlp_{pair}",
    )(meta, *args)


def head_masks():
    lane = lax.broadcasted_iota(jnp.int32, (1, LANES), 1)
    first = jnp.where(lane < HDIM, 1.0, 0.0).astype(BF16)
    second = jnp.where(lane < HDIM, 0.0, 1.0).astype(BF16)
    return first, second


def slot_rows(meta, per, tile):
    slot = jnp.bitwise_xor(tile // per, meta[0])
    return pl.multiple_of((slot * per + tile % per) * TILE, TILE), slot * per + tile % per


def by_head(first, second, block, third):
    return (block * first, block * second, third)


def attend_kernel(per, meta, lo, q_ref, k_ref, v_ref, start_ref, o_ref, lse_ref, vt_ref, acc):
    tiles = q_ref.shape[0] // TILE
    mask0, mask1 = head_masks()

    @pl.loop(0, tiles)
    def _(tile):
        rows = pl.ds(pl.multiple_of(tile * TILE, TILE), TILE)
        vt_ref[:, rows] = v_ref[rows, :].astype(F32).T.astype(BF16)

    key_iota = lax.broadcasted_iota(jnp.int32, (TILE, TILE), 0)
    query_iota = lax.broadcasted_iota(jnp.int32, (TILE, TILE), 1)

    @pl.loop(0, tiles)
    def _(qi):
        q_at, q_slot = slot_rows(meta, per, qi)
        q_rows = pl.ds(q_at, TILE)
        queries = by_head(mask0, mask1, q_ref[q_rows, 0:128], q_ref[q_rows, 128:192])
        starts = start_ref[q_slot]
        acc[...] = jnp.zeros_like(acc)

        def visit(ki, carry):
            k_at, _ = slot_rows(meta, per, ki)
            k_rows = pl.ds(k_at, TILE)
            pair, third = k_ref[k_rows, 0:128], k_ref[k_rows, 128:192]
            key_pos = key_iota + ki * TILE
            allowed = (key_pos >= starts) & (key_pos <= query_iota + qi * TILE)
            after = []
            for head in range(3):
                top, total = carry[head]
                scores = dot_nt(third if head == 2 else pair, queries[head])
                scores = jnp.where(allowed, scores, MASKED)
                new_top = jnp.maximum(top, jnp.max(scores, axis=0, keepdims=True))
                fade = jnp.exp(top - new_top)
                weights = jnp.exp(scores - new_top)
                total = total * fade + jnp.sum(weights, axis=0, keepdims=True)
                cols = pl.ds(head * HDIM, HDIM)
                acc[cols, :] = acc[cols, :] * fade + dot(vt_ref[cols, k_rows], weights.astype(BF16))
                after.append((new_top, total))
            return tuple(after)

        begin = (jnp.full((1, TILE), MASKED, F32), jnp.zeros((1, TILE), F32))
        stats = lax.fori_loop(lo[qi], qi + 1, visit, (begin,) * 3)
        for head, (top, total) in enumerate(stats):
            cols = pl.ds(head * HDIM, HDIM)
            acc[cols, :] = acc[cols, :] / total
            lse_ref[head, q_slot] = top + jnp.log(total)
        o_ref[q_rows, :] = acc[...].T.astype(BF16)


def attend(meta, lo, query, keys, values, starts, per):
    total, width = query.shape
    tiles = total // TILE
    args = [query, keys, values, starts]
    return pl.pallas_call(
        partial(attend_kernel, per),
        out_shape=[
            jax.ShapeDtypeStruct((total, width), BF16),
            jax.ShapeDtypeStruct((3, tiles, 1, TILE), F32),
        ],
        grid_spec=pltpu.PrefetchScalarGridSpec(
            num_scalar_prefetch=2,
            grid=(1,),
            in_specs=[whole(a.shape) for a in args],
            out_specs=[whole((total, width)), whole((3, tiles, 1, TILE))],
            scratch_shapes=[pltpu.VMEM((width, total), BF16), pltpu.VMEM((width, TILE), F32)],
        ),
        compiler_params=params(),
        cost_estimate=pl.CostEstimate(
            flops=60 * 4 * 256 * 256 * 256, bytes_accessed=8 * total * width, transcendentals=0
        ),
        name="attend",
    )(meta, lo, *args)


def attend_back_kernel(
    per, meta, lo, q_ref, k_ref, v_ref, o_ref, gv_ref, start_ref, lse_ref, low, high,
    gj_ref, kt_ref, dk_ref, dv_ref, dqt_ref,
):
    tiles = q_ref.shape[0] // TILE
    mask0, mask1 = head_masks()

    @pl.loop(0, tiles)
    def _(tile):
        rows = pl.ds(pl.multiple_of(tile * TILE, TILE), TILE)
        kt_ref[:, rows] = k_ref[rows, :].astype(F32).T.astype(BF16)

    dk_ref[...] = jnp.zeros_like(dk_ref)
    dv_ref[...] = jnp.zeros_like(dv_ref)
    key_iota = lax.broadcasted_iota(jnp.int32, (TILE, TILE), 0)
    query_iota = lax.broadcasted_iota(jnp.int32, (TILE, TILE), 1)

    @pl.loop(0, tiles)
    def _(turn):
        qi = tiles - 1 - turn
        q_at, q_slot = slot_rows(meta, per, qi)
        q_rows = pl.ds(q_at, TILE)
        queries = by_head(mask0, mask1, q_ref[q_rows, 0:128], q_ref[q_rows, 128:192])
        grads = by_head(mask0, mask1, gv_ref[q_rows, 0:128], gv_ref[q_rows, 128:192])
        starts = start_ref[q_slot]
        lses = [lse_ref[head, q_slot] for head in range(3)]
        product = (gv_ref[q_rows, :].astype(F32) * o_ref[q_rows, :].astype(F32)).T
        deltas = [
            jnp.sum(product[head * HDIM : (head + 1) * HDIM], axis=0, keepdims=True)
            for head in range(3)
        ]
        dqt_ref[...] = jnp.zeros_like(dqt_ref)

        @pl.loop(lo[qi], qi + 1)
        def _(ki):
            k_at, _ = slot_rows(meta, per, ki)
            k_rows = pl.ds(k_at, TILE)
            pair, third = k_ref[k_rows, 0:128], k_ref[k_rows, 128:192]
            v_pair, v_third = v_ref[k_rows, 0:128], v_ref[k_rows, 128:192]
            key_pos = key_iota + ki * TILE
            allowed = (key_pos >= starts) & (key_pos <= query_iota + qi * TILE)
            dk, dv = [], []
            for head in range(3):
                scores = dot_nt(third if head == 2 else pair, queries[head])
                probs = jnp.exp(jnp.where(allowed, scores - lses[head], MASKED))
                grad_probs = dot_nt(v_third if head == 2 else v_pair, grads[head])
                grad_scores = (probs * (grad_probs - deltas[head])).astype(BF16)
                dv.append(dot(probs.astype(BF16), grads[head]))
                dk.append(dot(grad_scores, queries[head]))
                cols = pl.ds(head * HDIM, HDIM)
                dqt_ref[cols, :] += dot(kt_ref[cols, k_rows], grad_scores)
            dk_ref[k_rows, 0:128] += dk[0] + dk[1]
            dk_ref[k_rows, 128:192] += dk[2]
            dv_ref[k_rows, 0:128] += dv[0] + dv[1]
            dv_ref[k_rows, 128:192] += dv[2]

        cos, sin = rotation(low, high, qi)

        def turn_back(block):
            return (block * cos - swap_halves(block) * sin).astype(BF16)

        dq = dqt_ref[...].T * (HDIM**-0.5)
        gj_ref[q_rows, 0:128] = turn_back(dq[:, 0:128])
        mixed = jnp.concatenate([dq[:, 128:192], dk_ref[q_rows, 128:192]], axis=1)
        gj_ref[q_rows, 128:256] = turn_back(dk_ref[q_rows, 0:128])
        gj_ref[q_rows, 256:384] = turn_back(mixed)
        gj_ref[q_rows, 384:576] = dv_ref[q_rows, :].astype(BF16)


def attend_back(meta, lo, query, keys, values, attn, grad_vec, starts, lse, low, high, per):
    total, width = query.shape
    args = [query, keys, values, attn, grad_vec, starts, lse, low, high]
    return pl.pallas_call(
        partial(attend_back_kernel, per),
        out_shape=jax.ShapeDtypeStruct((total, 3 * width), BF16),
        grid_spec=pltpu.PrefetchScalarGridSpec(
            num_scalar_prefetch=2,
            grid=(1,),
            in_specs=[whole(a.shape) for a in args],
            out_specs=whole((total, 3 * width)),
            scratch_shapes=[
                pltpu.VMEM((width, total), BF16),
                pltpu.VMEM((total, width), F32),
                pltpu.VMEM((total, width), F32),
                pltpu.VMEM((width, TILE), F32),
            ],
        ),
        compiler_params=params(),
        cost_estimate=pl.CostEstimate(
            flops=60 * 10 * 256 * 256 * 256, bytes_accessed=16 * total * width, transcendentals=0
        ),
        name="attend_back",
    )(meta, lo, *args)


def pick(refs, into, per):
    step = pl.program_id(0)
    for slot, ref in enumerate(refs):

        @pl.when(step // per == slot)
        def _(ref=ref):
            into[...] = ref[...]


def slot_specs(per, cols):
    def spec(slot):
        return pl.BlockSpec(
            (TILE, cols), lambda i, m: (jnp.clip(i - slot * per, 0, per - 1), 0)
        )

    return [spec(slot) for slot in range(4)]


def output_kernel(per, meta, o_ref, mo_ref, c0, c1, c2, c3, w_ref, out_ref, gw_ref, c_s, gw_s):
    step = pl.program_id(0)
    pick((c0, c1, c2, c3), c_s, per)

    @pl.when(step == 0)
    def _():
        gw_s[...] = jnp.zeros_like(gw_s)

    attn = o_ref[...]
    out_ref[...] = (dot(attn, w_ref[...]) + mo_ref[...].astype(F32)).astype(BF16)
    gw_s[...] += dot_tn(attn, c_s[...])

    @pl.when(step == pl.num_programs(0) - 1)
    def _():
        gw_ref[...] = gw_s[...].astype(BF16)


def output(meta, attn, mlp, cots, w_out):
    total, width = attn.shape
    per = cots[0].shape[0] // TILE
    return pl.pallas_call(
        partial(output_kernel, per),
        out_shape=[
            jax.ShapeDtypeStruct((total, D), BF16),
            jax.ShapeDtypeStruct((width, D), BF16),
        ],
        grid_spec=pltpu.PrefetchScalarGridSpec(
            num_scalar_prefetch=1,
            grid=(4 * per,),
            in_specs=[
                pl.BlockSpec((TILE, width), lambda i, m: (i, 0)),
                pl.BlockSpec((TILE, D), lambda i, m: (i, 0)),
                *slot_specs(per, D),
                pl.BlockSpec((width, D), lambda i, m: (m[0], 0)),
            ],
            out_specs=[pl.BlockSpec((TILE, D), lambda i, m: (i, 0)), whole((width, D))],
            scratch_shapes=[pltpu.VMEM((TILE, D), BF16), pltpu.VMEM((width, D), F32)],
        ),
        compiler_params=params(),
        cost_estimate=pl.CostEstimate(
            flops=4 * total * width * D, bytes_accessed=6 * total * D, transcendentals=0
        ),
        name="output",
    )(meta, attn, mlp, *cots, w_out)


def joined_kernel(
    per, meta, gj_ref, e_in, t0, t1, t2, t3, gain, shift, w_ref,
    e_ref, gw_ref, gb_ref, gg_ref, gs_ref, x_s, gw_s,
):
    step = pl.program_id(0)
    pick((t0, t1, t2, t3), x_s, per)

    @pl.when(step == 0)
    def _():
        gw_s[...] = jnp.zeros_like(gw_s)
        gb_ref[...] = jnp.zeros_like(gb_ref)
        gg_ref[...] = jnp.zeros_like(gg_ref)
        gs_ref[...] = jnp.zeros_like(gs_ref)

    normed = normalize(x_s[...].astype(F32))
    attn_in = (normed * gain[...] + shift[...]).astype(BF16)
    grad = gj_ref[...]
    grad_norm = dot_nt(grad, w_ref[...])
    e_ref[...] = (grad_norm * gain[...] + e_in[...].astype(F32)).astype(BF16)
    gg_ref[...] += jnp.sum(grad_norm * normed, axis=0, keepdims=True)
    gs_ref[...] += jnp.sum(grad_norm, axis=0, keepdims=True)
    gb_ref[...] += jnp.sum(grad.astype(F32), axis=0, keepdims=True)
    gw_s[...] += dot_tn(attn_in, grad)

    @pl.when(step == pl.num_programs(0) - 1)
    def _():
        gw_ref[...] = gw_s[...].astype(BF16)


def joined_back(meta, grad, e_mlp, toks, gain, shift, w):
    total, width = grad.shape
    per = toks[0].shape[0] // TILE
    row = whole((1, D))
    return pl.pallas_call(
        partial(joined_kernel, per),
        out_shape=[
            jax.ShapeDtypeStruct((total, D), BF16),
            jax.ShapeDtypeStruct((D, width), BF16),
            jax.ShapeDtypeStruct((1, width), F32),
            jax.ShapeDtypeStruct((1, D), F32),
            jax.ShapeDtypeStruct((1, D), F32),
        ],
        grid_spec=pltpu.PrefetchScalarGridSpec(
            num_scalar_prefetch=1,
            grid=(4 * per,),
            in_specs=[
                pl.BlockSpec((TILE, width), lambda i, m: (i, 0)),
                pl.BlockSpec((TILE, D), lambda i, m: (i, 0)),
                *slot_specs(per, D),
                row,
                row,
                whole((D, width)),
            ],
            out_specs=[
                pl.BlockSpec((TILE, D), lambda i, m: (i, 0)),
                whole((D, width)),
                whole((1, width)),
                row,
                row,
            ],
            scratch_shapes=[pltpu.VMEM((TILE, D), BF16), pltpu.VMEM((D, width), F32)],
        ),
        compiler_params=params(),
        cost_estimate=pl.CostEstimate(
            flops=4 * total * width * D, bytes_accessed=8 * total * D, transcendentals=0
        ),
        name="joined_back",
    )(meta, grad, e_mlp, *toks, gain, shift, w)


def swap(value, axis, mask):
    size = lax.axis_size(axis)
    return lax.ppermute(value, axis, [(i, i ^ mask) for i in range(size)])


def reduce_rows(value):
    index = lax.axis_index("rows")
    mask = 1
    while value.shape[0] > 1:
        bit = (index // mask) % 2
        value = value.reshape(value.shape[0] // 2, 2, *value.shape[1:])
        mine = lax.dynamic_index_in_dim(value, bit, 1, keepdims=False)
        other = lax.dynamic_index_in_dim(value, 1 - bit, 1, keepdims=False)
        got = swap(other, "rows", mask)
        value = mine.astype(F32) + got.astype(F32)
        mask *= 2
        if value.shape[0] > 1:
            value = value.astype(BF16)
    return value[0]


def spread_rows(chunk, col_width):
    rows, blk = lax.axis_size("rows"), lax.axis_size("blk")
    r, b = lax.axis_index("rows"), lax.axis_index("blk")
    pieces = chunk.reshape(chunk.shape[0], blk, col_width)
    got = []
    for turn in range(blk):
        moves = []
        for rr in range(rows):
            for bb in range(blk):
                moves.append((rr * blk + bb, (rows * bb + rr) // blk * blk + ((rr % blk) ^ turn)))
        piece = lax.dynamic_index_in_dim(pieces, (r % blk) ^ turn, 1, keepdims=False)
        got.append(lax.ppermute(piece, ("rows", "blk"), moves))
    got = jnp.stack(got)
    return [lax.dynamic_index_in_dim(got, b ^ part, 0, keepdims=False) for part in range(blk)]


def spread_columns(chunk):
    blk = lax.axis_size("blk")
    b = lax.axis_index("blk")
    parts = jnp.stack(
        [
            jnp.concatenate([chunk[:, 0:128], chunk[:, 256:320]], axis=1),
            jnp.concatenate([chunk[:, 128:256], chunk[:, 320:384]], axis=1),
            chunk[:, 384:576],
        ]
    )
    got = []
    for turn in range(3):
        moves = [((3 * to + turn) % blk, to) for to in range(blk)]
        to = (3 * (b - turn)) % blk
        piece = lax.dynamic_index_in_dim(parts, (3 * to + turn) // blk, 0, keepdims=False)
        got.append(lax.ppermute(piece, "blk", moves))
    return jnp.concatenate(got, axis=1)


def gather_slots(own, after=None):
    near = swap(own, "blk", 1)
    if after is not None:
        own = lax.optimization_barrier((own, after))[0]
    far = swap(own, "blk", 2)
    return [own, near, far, swap(far, "blk", 1)]


def scatter_slots(parts):
    near = swap(parts[1], "blk", 1)
    far = swap(parts[3], "blk", 1)
    send = (parts[2].astype(F32) + far.astype(F32)).astype(BF16)
    across = swap(send, "blk", 2)
    return parts[0].astype(F32) + near.astype(F32) + across.astype(F32)


def local(
    tokens, seg_ids, valid_len, ln1_gain, ln1_bias, w_qkv, b_qkv, w_out, b_out,
    ln2_gain, ln2_bias, w_up, b_up, w_down, b_down, cotangent,
):
    rows = lax.axis_size("rows")
    blk = lax.axis_index("blk")
    seq = tokens.shape[1]
    per = seq // TILE
    width = D // 4
    meta = blk.astype(jnp.int32).reshape(1)
    low, high = angle_parts(4 * seq)

    tok = gather_slots(tokens[0])
    cot = gather_slots(cotangent[0], tok[2])
    seg = [seg_ids[0]] + [swap(seg_ids[0], "blk", mask) for mask in (1, 2, 3)]

    def own_columns(array, at, size):
        return lax.dynamic_slice_in_dim(array, at + width * blk, size, axis=-1)

    def own_joined(array):
        order = ((0, 128), (D, 128), (128, 64), (D + 128, 64), (2 * D, 192))
        return jnp.concatenate([own_columns(array, at, size) for at, size in order], axis=-1)

    w_own = own_joined(w_qkv)
    b_own = own_joined(b_qkv)[None]
    gain1, shift1, gain2, shift2 = (v[None] for v in (ln1_gain, ln1_bias, ln2_gain, ln2_bias))

    seg_all = jnp.stack(seg)
    pos = (jnp.arange(4, dtype=jnp.int32) ^ blk)[:, None] * seq + jnp.arange(seq, dtype=jnp.int32)
    starts = jnp.zeros_like(seg_all)
    for number in (1, 2, 3):
        starts = jnp.where(seg_all == number, jnp.sum(seg_all < number), starts)
    starts = jnp.where(pos < valid_len[0], starts, pos).astype(jnp.int32)
    starts = starts.reshape(4 * per, 1, TILE)
    tile_at = jnp.arange(4 * per, dtype=jnp.int32)
    tile_slot = (tile_at // per ^ blk) * per + tile_at % per
    lo = starts[:, 0, 0][tile_slot] // TILE

    joined = None
    for slot in range(4):
        joined = project(slot, meta, tok[slot], gain1, shift1, w_own, b_own, low, high, joined)
    query, keys, values = joined

    mlp_args = (gain2, shift2, w_up, b_up[None], w_down, w_out)
    first = feed_forward(0, meta, tok[:2], cot[:2], *mlp_args, None)
    attn, lse = attend(meta, lo, query, keys, values, starts, per)
    second = feed_forward(1, meta, tok[2:], cot[2:], *mlp_args, first)
    mlp_part, e_mlp, grad_vec, gw_up, gw_down, gb_up, g_ln2, s_ln2 = second

    out_part, gw_out = output(meta, attn, mlp_part, cot, w_out)
    grad_joined = attend_back(
        meta, lo, query, keys, values, attn, grad_vec, starts, lse, low, high, per
    )
    e_part, gw_qkv, gb_joined, g_ln1, s_ln1 = joined_back(
        meta, grad_joined, e_mlp, tok, gain1, shift1, w_own
    )

    summed = scatter_slots(out_part.reshape(4, seq, D))
    result = (tokens[0].astype(F32) + (b_out + b_down) + summed).astype(BF16)[None]

    hid = FF // 4
    up = reduce_rows(gw_up.reshape(rows, D // rows, hid))
    lower = jnp.concatenate(
        [gw_down.reshape(rows, hid // rows, D), gw_out.reshape(rows, width // rows, D)], axis=1
    )
    lower = spread_rows(reduce_rows(lower).astype(BF16), width)
    cut = hid // rows
    down = jnp.concatenate([part[:cut] for part in lower]).astype(F32)
    out_w = jnp.concatenate([part[cut:] for part in lower]).astype(F32)
    qkv = spread_columns(reduce_rows(gw_qkv.reshape(rows, D // rows, 3 * width)).astype(BF16))

    e_sum = scatter_slots(e_part.reshape(4, seq, D))
    wide = tokens[0].astype(F32)
    center = wide - jnp.mean(wide, axis=-1, keepdims=True)
    rate = lax.rsqrt(jnp.mean(center * center, axis=-1, keepdims=True) + EPS)
    normed = center * rate
    back = rate * (
        e_sum
        - jnp.mean(e_sum, axis=-1, keepdims=True)
        - normed * jnp.mean(e_sum * normed, axis=-1, keepdims=True)
    )
    up_wide = cotangent[0].astype(F32)
    grad_tokens = (up_wide + back).astype(BF16)[None]

    gb = gb_joined[0]
    own_b = (
        jnp.concatenate([gb[0:128], gb[256:320]]),
        jnp.concatenate([gb[128:256], gb[320:384]]),
        gb[384:576],
    )
    gb_qkv = jnp.zeros((3 * D,), F32)
    for part, piece in enumerate(own_b):
        gb_qkv = lax.dynamic_update_slice(gb_qkv, piece, (part * D + width * blk,))
    gb_up_all = lax.dynamic_update_slice(jnp.zeros((FF,), F32), gb_up[0], (hid * blk,))
    small = lax.psum(
        (
            gb_qkv,
            jnp.sum(up_wide, axis=0),
            gb_up_all,
            g_ln1[0],
            s_ln1[0],
            g_ln2[0],
            s_ln2[0],
        ),
        ("rows", "blk"),
    )
    return (
        result,
        grad_tokens,
        qkv.astype(F32),
        out_w,
        up,
        down,
        small[0],
        small[1],
        small[2],
        small[1],
        small[3],
        small[4],
        small[5],
        small[6],
    )


def solution(mesh):
    split = P("rows", "blk")
    in_specs = (
        P("rows", "blk", None),
        split,
        P("rows"),
        *(P(),) * 12,
        P("rows", "blk", None),
    )
    out_specs = (
        P("rows", "blk", None),
        P("rows", "blk", None),
        *(split,) * 4,
        *(P(),) * 8,
    )
    return jax.shard_map(local, mesh=mesh, in_specs=in_specs, out_specs=out_specs, check_vma=False)
```

```python
import math
from functools import partial

import jax
import jax.numpy as jnp
import numpy as np
from jax import lax
from jax.experimental import pallas as pl
from jax.experimental.pallas import tpu as pltpu
from jax.sharding import PartitionSpec as P

D = 768
HEADS = 12
HDIM = 64
ROT = 16
FF = 3072
EPS = 1e-05
MASKED = -1e30
TILE = 256
LANES = 128
F32 = jnp.float32
BF16 = jnp.bfloat16
NT_DIMS = (((1,), (1,)), ((), ()))
TN_DIMS = (((0,), (0,)), ((), ()))


def dot(left, right):
    return jnp.dot(left, right, preferred_element_type=F32)


def dot_nt(left, right):
    return lax.dot_general(left, right, NT_DIMS, preferred_element_type=F32)


def dot_tn(left, right):
    return lax.dot_general(left, right, TN_DIMS, preferred_element_type=F32)


def normalize(value):
    center = value - jnp.mean(value, axis=-1, keepdims=True)
    spread = jnp.mean(center * center, axis=-1, keepdims=True)
    return center * lax.rsqrt(spread + EPS)


def angle_parts(length):
    dim = np.arange(LANES) % HDIM
    inverse = np.where(dim < ROT, 10000.0 ** (-2.0 * (dim % (ROT // 2)) / ROT), 0.0)
    high = (np.arange(length // LANES) * LANES)[:, None] * inverse
    low = np.arange(LANES)[:, None] * inverse
    parts = np.stack([np.cos(low), np.sin(low)]), np.stack([np.cos(high), np.sin(high)])
    return tuple(jnp.asarray(part, F32) for part in parts)


def rotation(low_ref, high_ref, tile):
    lane = lax.broadcasted_iota(jnp.int32, (1, LANES), 1) % HDIM
    sign = jnp.where(lane < ROT // 2, -1.0, 1.0)
    cos_rows, sin_rows = [], []
    for part in range(TILE // LANES):
        row = tile * (TILE // LANES) + part
        cos_high = high_ref[0, pl.ds(row, 1), :]
        sin_high = high_ref[1, pl.ds(row, 1), :]
        cos_rows.append(low_ref[0] * cos_high - low_ref[1] * sin_high)
        sin_rows.append((low_ref[1] * cos_high + low_ref[0] * sin_high) * sign)
    return jnp.concatenate(cos_rows, axis=0), jnp.concatenate(sin_rows, axis=0)


def swap_halves(value):
    lane = lax.broadcasted_iota(jnp.int32, value.shape, 1) % HDIM
    half = ROT // 2
    return jnp.where(
        lane < half, pltpu.roll(value, LANES - half, 1), pltpu.roll(value, half, 1)
    )


def true_block(meta_ref, slot):
    return jnp.bitwise_xor(meta_ref[0], slot)


def params(*semantics, vmem=None):
    return pltpu.CompilerParams(
        dimension_semantics=semantics or ("arbitrary",), vmem_limit_bytes=vmem or 60 * 2**20
    )


def whole(shape):
    return pl.BlockSpec(shape, lambda *_: (0,) * len(shape))


def own_blocks(refs, odd, into):
    places = ((0, 256), (128, 320), (384, 512))
    for part, (pair_at, third_at) in enumerate(places):
        left, right = refs[2 * part], refs[2 * part + 1]

        @pl.when(odd == 0)
        def _(left=left, right=right, pair_at=pair_at, third_at=third_at):
            into[:, pair_at : pair_at + 128] = left[...]
            into[:, third_at : third_at + 64] = right[:, 0:64]

        @pl.when(odd == 1)
        def _(left=left, right=right, pair_at=pair_at, third_at=third_at):
            into[:, pair_at : pair_at + 128] = jnp.concatenate(
                [left[:, 64:128], right[:, 0:64]], axis=1
            )
            into[:, third_at : third_at + 64] = right[:, 64:128]


def qkv_kernel(slot, meta, x_ref, gain, shift, low, high, *refs):
    if slot == 0:
        odd = meta[0] % 2
        q_ref, k_ref, v_ref, w_ref, b_ref = refs[-5:]
        own_blocks(refs[0:6], odd, w_ref)
        own_blocks(refs[6:12], odd, b_ref)
    else:
        w_ref, b_ref = refs[0:2]
        q_ref, k_ref, v_ref = refs[-3:]
    per = x_ref.shape[0] // TILE
    for part in range(per):
        rows = pl.ds(part * TILE, TILE)
        normed = normalize(x_ref[rows, :].astype(F32))
        attn_in = (normed * gain[...] + shift[...]).astype(BF16)
        joined = dot(attn_in, w_ref[...]) + b_ref[...]
        cos, sin = rotation(low, high, true_block(meta, slot) * per + part)
        scale = HDIM**-0.5

        def turn(block):
            return block * cos + swap_halves(block) * sin

        query = turn(joined[:, 0:128]) * scale
        keys = turn(joined[:, 128:256])
        mixed = turn(joined[:, 256:384])
        q_ref[rows, 0:128] = query.astype(BF16)
        k_ref[rows, 0:128] = keys.astype(BF16)
        q_ref[rows, 128:192] = (mixed[:, 0:64] * scale).astype(BF16)
        k_ref[rows, 128:192] = mixed[:, 64:128].astype(BF16)
        v_ref[rows, :] = joined[:, 384:576].astype(BF16)


def project(slot, meta, x, gain, shift, low, high, w, b, filled):
    seq = x.shape[0]
    width = D // 4
    total = 4 * seq
    out = jax.ShapeDtypeStruct((total, width), BF16)
    out_spec = pl.BlockSpec((seq, width), lambda i, m: (slot, 0))
    outs, out_specs = [out] * 3, [out_spec] * 3
    args = [x, gain, shift, low, high]
    specs = [whole(a.shape) for a in args]
    aliases = {}
    if slot == 0:
        for array in (w, b):
            for part in range(3):
                for side in range(2):
                    specs.append(
                        pl.BlockSpec(
                            (array.shape[0], LANES),
                            lambda i, m, at=part * D // LANES + side: (0, at + 3 * m[0] // 2),
                        )
                    )
                    args.append(array)
        for array in (w, b):
            shape = (array.shape[0], 3 * width)
            outs.append(jax.ShapeDtypeStruct(shape, array.dtype))
            out_specs.append(whole(shape))
    else:
        args += [w, b]
        specs += [whole(w.shape), whole(b.shape)]
        aliases = {1 + len(args) + i: i for i in range(3)}
        args += list(filled)
        specs += [pl.BlockSpec(memory_space=pl.ANY)] * 3
    return pl.pallas_call(
        partial(qkv_kernel, slot),
        out_shape=outs,
        grid_spec=pltpu.PrefetchScalarGridSpec(
            num_scalar_prefetch=1, grid=(1,), in_specs=specs, out_specs=out_specs
        ),
        input_output_aliases=aliases,
        compiler_params=params(),
        cost_estimate=pl.CostEstimate(
            flops=2 * seq * D * 3 * width, bytes_accessed=4 * seq * D, transcendentals=0
        ),
        name=f"qkv_{slot}",
    )(meta, *args)


def store_chunks(grad, keep, send, meta):
    if len(keep.shape) == 2:
        keep[...] = grad[...].astype(keep.dtype)
        return
    size = keep.shape[1]
    for place in range(2 * keep.shape[0]):
        at = pl.multiple_of(jnp.bitwise_xor(meta[1], place) * size, 8)
        into = send if place % 2 else keep
        into[place // 2] = grad[pl.ds(at, size), :].astype(into.dtype)


def chunk_shapes(size, cols, rows):
    if size // rows % 8 == 0 and rows > 1:
        return [(rows // 2, size // rows, cols)] * 2
    return [(size, cols), (8, LANES)]


def chunks_of(keep, send, rows):
    if keep.ndim == 3:
        return keep, send
    places = jnp.arange(rows) ^ lax.axis_index("rows")
    parts = jnp.take(keep.reshape(rows, keep.shape[0] // rows, keep.shape[1]), places, axis=0)
    return parts[0::2], parts[1::2]


def mlp_kernel(final, meta, *refs):
    (xa, xb, ca, cb, gain, shift, w_up, b_up, w_down, w_out) = refs[:10]
    if final:
        (up_in, down_in, b_in, g_in, s_in) = refs[10:15]
        mo_ref, e_ref, gv_ref, gb_ref, gg_ref, gs_ref = refs[-14:-8]
        up_keep, up_send, down_keep, down_send = refs[-8:-4]
        x_s, c_s, up_s, down_s = refs[-4:]
    else:
        mo_ref, e_ref, gv_ref, gb_ref, gg_ref, gs_ref, up_s, down_s = refs[-10:-2]
        x_s, c_s = refs[-2:]
    step = pl.program_id(0)
    half = pl.num_programs(0) // 2

    @pl.when(step < half)
    def _():
        x_s[...] = xa[...]
        c_s[...] = ca[...]

    @pl.when(step >= half)
    def _():
        x_s[...] = xb[...]
        c_s[...] = cb[...]

    @pl.when(step == 0)
    def _():
        if final:
            up_s[...] = up_in[...]
            down_s[...] = down_in[...]
            gb_ref[...] = b_in[...]
            gg_ref[...] = g_in[...]
            gs_ref[...] = s_in[...]
        else:
            up_s[...] = jnp.zeros_like(up_s)
            down_s[...] = jnp.zeros_like(down_s)
            gb_ref[...] = jnp.zeros_like(gb_ref)
            gg_ref[...] = jnp.zeros_like(gg_ref)
            gs_ref[...] = jnp.zeros_like(gs_ref)

    normed = normalize(x_s[...].astype(F32))
    mlp_in = (normed * gain[...] + shift[...]).astype(BF16)
    upstream = c_s[...]
    hidden = dot(mlp_in, w_up[...]) + b_up[...]
    cdf = 0.5 * (1.0 + lax.erf(hidden * (0.5**0.5)))
    act = (hidden * cdf).astype(BF16)
    slope = cdf + hidden * jnp.exp(-0.5 * hidden * hidden) * ((2.0 * math.pi) ** -0.5)
    mo_ref[...] = dot(act, w_down[...]).astype(BF16)
    grad_act = dot_nt(upstream, w_down[...])
    grad_hidden = slope * grad_act
    grad_low = grad_hidden.astype(BF16)
    gb_ref[...] += jnp.sum(grad_low.astype(F32), axis=0, keepdims=True)
    grad_norm = dot_nt(grad_low, w_up[...])
    gg_ref[...] += jnp.sum(grad_norm * normed, axis=0, keepdims=True)
    gs_ref[...] += jnp.sum(grad_norm, axis=0, keepdims=True)
    e_ref[...] = (grad_norm * gain[...]).astype(BF16)
    gv_ref[...] = dot_nt(upstream, w_out[...]).astype(BF16)
    up_s[...] += dot_tn(mlp_in, grad_low)
    down_s[...] += dot_tn(act, upstream)

    if final:

        @pl.when(step == pl.num_programs(0) - 1)
        def _():
            store_chunks(up_s, up_keep, up_send, meta)
            store_chunks(down_s, down_keep, down_send, meta)


def feed_forward(pair, meta, xs, cs, gain, shift, w_up, b_up, w_down, w_out, before, rows):
    seq = xs[0].shape[0]
    per = seq // TILE
    steps = 2 * per
    hid = FF // 4
    width = D // 4
    first = pl.BlockSpec((TILE, D), lambda i, m: (jnp.minimum(i, per - 1), 0))
    second = pl.BlockSpec((TILE, D), lambda i, m: (jnp.maximum(i - per, 0), 0))
    row = whole((1, D))
    specs = [
        first,
        second,
        first,
        second,
        row,
        row,
        pl.BlockSpec((D, hid), lambda i, m: (0, m[0])),
        pl.BlockSpec((1, hid), lambda i, m: (0, m[0])),
        pl.BlockSpec((hid, D), lambda i, m: (m[0], 0)),
        pl.BlockSpec((width, D), lambda i, m: (m[0], 0)),
    ]
    args = [*xs, *cs, gain, shift, w_up, b_up, w_down, w_out]
    aliases = {}
    shapes = [(jnp.float32, (D, hid)), (jnp.float32, (hid, D))]
    scratch = [pltpu.VMEM((TILE, D), BF16), pltpu.VMEM((TILE, D), BF16)]
    if before is not None:
        shapes = [
            (BF16, shape)
            for size, cols in ((D, hid), (hid, D))
            for shape in chunk_shapes(size, cols, rows)
        ]
        scratch += [pltpu.VMEM((D, hid), F32), pltpu.VMEM((hid, D), F32)]
        carried = list(before[6:8]) + list(before[3:6])
        args += carried + list(before[:3])
        specs += [whole(a.shape) for a in carried]
        specs += [pl.BlockSpec(memory_space=pl.ANY)] * 3
        aliases = {1 + len(args) - 3 + i: i for i in range(3)}
    base = pair * steps

    def tiles(cols):
        return pl.BlockSpec((TILE, cols), lambda i, m: (i + base, 0))

    total = 4 * seq
    return pl.pallas_call(
        partial(mlp_kernel, before is not None),
        out_shape=[
            jax.ShapeDtypeStruct((total, D), BF16),
            jax.ShapeDtypeStruct((total, D), BF16),
            jax.ShapeDtypeStruct((total, width), BF16),
            jax.ShapeDtypeStruct((1, hid), F32),
            jax.ShapeDtypeStruct((1, D), F32),
            jax.ShapeDtypeStruct((1, D), F32),
            *(jax.ShapeDtypeStruct(shape, kind) for kind, shape in shapes),
        ],
        grid_spec=pltpu.PrefetchScalarGridSpec(
            num_scalar_prefetch=1,
            grid=(steps,),
            in_specs=specs,
            out_specs=[
                tiles(D),
                tiles(D),
                tiles(width),
                whole((1, hid)),
                row,
                row,
                *(whole(shape) for _, shape in shapes),
            ],
            scratch_shapes=scratch,
        ),
        input_output_aliases=aliases,
        compiler_params=params(),
        cost_estimate=pl.CostEstimate(
            flops=2 * 6 * 2 * seq * D * hid, bytes_accessed=20 * seq * D, transcendentals=0
        ),
        name=f"mlp_{pair}",
    )(meta, *args)


def head_masks():
    lane = lax.broadcasted_iota(jnp.int32, (1, LANES), 1)
    first = jnp.where(lane < HDIM, 1.0, 0.0).astype(BF16)
    second = jnp.where(lane < HDIM, 0.0, 1.0).astype(BF16)
    return first, second


def slot_rows(meta, per, tile):
    slot = jnp.bitwise_xor(tile // per, meta[0])
    return pl.multiple_of((slot * per + tile % per) * TILE, TILE)


def by_head(first, second, block, third):
    return (block * first, block * second, third)


def transpose_all(from_ref, to_ref):
    @pl.loop(0, from_ref.shape[0] // TILE)
    def _(tile):
        rows = pl.ds(pl.multiple_of(tile * TILE, TILE), TILE)
        to_ref[:, rows] = from_ref[rows, :].astype(F32).T.astype(BF16)


def attend_kernel(base, per, meta, lo, q_ref, k_ref, v_ref, start_ref, *refs):
    o_ref, lse_ref, vt_ref, acc = refs[-4:]
    mask0, mask1 = head_masks()

    @pl.when(pl.program_id(0) == 0)
    def _():
        transpose_all(v_ref, vt_ref)

    key_iota = lax.broadcasted_iota(jnp.int32, (TILE, TILE), 0)
    query_iota = lax.broadcasted_iota(jnp.int32, (TILE, TILE), 1)

    @pl.loop(0, per)
    def _(part):
        qi = (base + pl.program_id(0)) * per + part
        q_rows = pl.ds(pl.multiple_of(part * TILE, TILE), TILE)
        queries = by_head(mask0, mask1, q_ref[q_rows, 0:128], q_ref[q_rows, 128:192])
        starts = start_ref[part]
        acc[...] = jnp.zeros_like(acc)

        def visit(ki, carry):
            k_rows = pl.ds(slot_rows(meta, per, ki), TILE)
            pair, third = k_ref[k_rows, 0:128], k_ref[k_rows, 128:192]
            key_pos = key_iota + ki * TILE
            allowed = (key_pos >= starts) & (key_pos <= query_iota + qi * TILE)
            after = []
            for head in range(3):
                top, total = carry[head]
                scores = dot_nt(third if head == 2 else pair, queries[head])
                scores = jnp.where(allowed, scores, MASKED)
                new_top = jnp.maximum(top, jnp.max(scores, axis=0, keepdims=True))
                fade = jnp.exp(top - new_top)
                weights = jnp.exp(scores - new_top)
                total = total * fade + jnp.sum(weights, axis=0, keepdims=True)
                cols = pl.ds(head * HDIM, HDIM)
                acc[cols, :] = acc[cols, :] * fade + dot(vt_ref[cols, k_rows], weights.astype(BF16))
                after.append((new_top, total))
            return tuple(after)

        begin = (jnp.full((1, TILE), MASKED, F32), jnp.zeros((1, TILE), F32))
        stats = lax.fori_loop(lo[qi], qi + 1, visit, (begin,) * 3)
        for head, (top, total) in enumerate(stats):
            cols = pl.ds(head * HDIM, HDIM)
            acc[cols, :] = acc[cols, :] / total
            lse_ref[head, part] = top + jnp.log(total)
        o_ref[q_rows, :] = acc[...].T.astype(BF16)


def block_specs(per, true_of, widths):
    seq = per * TILE
    specs = [
        pl.BlockSpec((seq, w), lambda i, m, lo: (jnp.bitwise_xor(true_of(i), m[0]), 0))
        for w in widths
    ]
    starts = pl.BlockSpec(
        (per, 1, TILE), lambda i, m, lo: (jnp.bitwise_xor(true_of(i), m[0]), 0, 0)
    )
    lse = pl.BlockSpec(
        (3, per, 1, TILE), lambda i, m, lo: (0, jnp.bitwise_xor(true_of(i), m[0]), 0, 0)
    )
    return specs, starts, lse


def attend(base, meta, lo, query, keys, values, starts, per, filled):
    total, width = query.shape
    tiles = total // TILE
    (q_spec,), start_spec, lse_spec = block_specs(per, lambda i: base + i, (width,))
    args = [query, keys, values, starts]
    specs = [q_spec, whole(keys.shape), whole(values.shape), start_spec]
    aliases = {}
    if filled is not None:
        aliases = {2 + len(args) + i: i for i in range(2)}
        args += list(filled)
        specs += [pl.BlockSpec(memory_space=pl.ANY)] * 2
    return pl.pallas_call(
        partial(attend_kernel, base, per),
        out_shape=[
            jax.ShapeDtypeStruct((total, width), BF16),
            jax.ShapeDtypeStruct((3, tiles, 1, TILE), F32),
        ],
        grid_spec=pltpu.PrefetchScalarGridSpec(
            num_scalar_prefetch=2,
            grid=(2,),
            in_specs=specs,
            out_specs=[q_spec, lse_spec],
            scratch_shapes=[pltpu.VMEM((width, total), BF16), pltpu.VMEM((width, TILE), F32)],
        ),
        input_output_aliases=aliases,
        compiler_params=params(),
        cost_estimate=pl.CostEstimate(
            flops=30 * 4 * 256 * 256 * 256, bytes_accessed=8 * total * width, transcendentals=0
        ),
        name=f"attend_{base}",
    )(meta, lo, *args)


def attend_back_kernel(
    top, per, meta, lo, q_ref, k_ref, v_ref, o_ref, gv_ref, start_ref, lse_ref, low, high, *refs
):
    if top == 3:
        gj_ref, dk_ref, dv_ref, kt_ref, dqt_ref = refs
    else:
        dk_in, dv_in = refs[0:2]
        gj_ref, dk_ref, dv_ref, kt_ref, dqt_ref = refs[-5:]
    mask0, mask1 = head_masks()

    @pl.when(pl.program_id(0) == 0)
    def _():
        transpose_all(k_ref, kt_ref)
        if top == 3:
            dk_ref[...] = jnp.zeros_like(dk_ref)
            dv_ref[...] = jnp.zeros_like(dv_ref)
        else:
            dk_ref[...] = dk_in[...]
            dv_ref[...] = dv_in[...]

    key_iota = lax.broadcasted_iota(jnp.int32, (TILE, TILE), 0)
    query_iota = lax.broadcasted_iota(jnp.int32, (TILE, TILE), 1)

    @pl.loop(0, per)
    def _(turn):
        part = per - 1 - turn
        qi = (top - pl.program_id(0)) * per + part
        own_rows = pl.ds(slot_rows(meta, per, qi), TILE)
        q_rows = pl.ds(pl.multiple_of(part * TILE, TILE), TILE)
        queries = by_head(mask0, mask1, q_ref[q_rows, 0:128], q_ref[q_rows, 128:192])
        grads = by_head(mask0, mask1, gv_ref[q_rows, 0:128], gv_ref[q_rows, 128:192])
        starts = start_ref[part]
        lses = [lse_ref[head, part] for head in range(3)]
        product = (gv_ref[q_rows, :].astype(F32) * o_ref[q_rows, :].astype(F32)).T
        deltas = [
            jnp.sum(product[head * HDIM : (head + 1) * HDIM], axis=0, keepdims=True)
            for head in range(3)
        ]
        dqt_ref[...] = jnp.zeros_like(dqt_ref)

        @pl.loop(lo[qi], qi + 1)
        def _(ki):
            k_rows = pl.ds(slot_rows(meta, per, ki), TILE)
            pair, third = k_ref[k_rows, 0:128], k_ref[k_rows, 128:192]
            v_pair, v_third = v_ref[k_rows, 0:128], v_ref[k_rows, 128:192]
            key_pos = key_iota + ki * TILE
            allowed = (key_pos >= starts) & (key_pos <= query_iota + qi * TILE)
            dk, dv = [], []
            for head in range(3):
                scores = dot_nt(third if head == 2 else pair, queries[head])
                probs = jnp.exp(jnp.where(allowed, scores - lses[head], MASKED))
                grad_probs = dot_nt(v_third if head == 2 else v_pair, grads[head])
                grad_scores = (probs * (grad_probs - deltas[head])).astype(BF16)
                dv.append(dot(probs.astype(BF16), grads[head]))
                dk.append(dot(grad_scores, queries[head]))
                cols = pl.ds(head * HDIM, HDIM)
                dqt_ref[cols, :] += dot(kt_ref[cols, k_rows], grad_scores)
            dk_ref[k_rows, 0:128] += dk[0] + dk[1]
            dk_ref[k_rows, 128:192] += dk[2]
            dv_ref[k_rows, 0:128] += dv[0] + dv[1]
            dv_ref[k_rows, 128:192] += dv[2]

        cos, sin = rotation(low, high, qi)

        def turn_back(block):
            return (block * cos - swap_halves(block) * sin).astype(BF16)

        dq = dqt_ref[...].T * (HDIM**-0.5)
        gj_ref[q_rows, 0:128] = turn_back(dq[:, 0:128])
        mixed = jnp.concatenate([dq[:, 128:192], dk_ref[own_rows, 128:192]], axis=1)
        gj_ref[q_rows, 128:256] = turn_back(dk_ref[own_rows, 0:128])
        gj_ref[q_rows, 256:384] = turn_back(mixed)
        gj_ref[q_rows, 384:576] = dv_ref[own_rows, :].astype(BF16)


def attend_back(
    top, meta, lo, query, keys, values, attn, grad_vec, starts, lse, low, high, per, filled
):
    total, width = query.shape
    (q_spec, gj_spec), start_spec, lse_spec = block_specs(
        per, lambda i: top - i, (width, 3 * width)
    )
    args = [query, keys, values, attn, grad_vec, starts, lse, low, high]
    specs = [
        q_spec,
        whole(keys.shape),
        whole(values.shape),
        q_spec,
        q_spec,
        start_spec,
        lse_spec,
        whole(low.shape),
        whole(high.shape),
    ]
    aliases = {}
    if filled is not None:
        args += [filled[1], filled[2], filled[0]]
        specs += [whole(filled[1].shape)] * 2 + [pl.BlockSpec(memory_space=pl.ANY)]
        aliases = {2 + len(args) - 1: 0}
    return pl.pallas_call(
        partial(attend_back_kernel, top, per),
        out_shape=[
            jax.ShapeDtypeStruct((total, 3 * width), BF16),
            jax.ShapeDtypeStruct((total, width), F32),
            jax.ShapeDtypeStruct((total, width), F32),
        ],
        grid_spec=pltpu.PrefetchScalarGridSpec(
            num_scalar_prefetch=2,
            grid=(2,),
            in_specs=specs,
            out_specs=[gj_spec, whole((total, width)), whole((total, width))],
            scratch_shapes=[pltpu.VMEM((width, total), BF16), pltpu.VMEM((width, TILE), F32)],
        ),
        input_output_aliases=aliases,
        compiler_params=params(),
        cost_estimate=pl.CostEstimate(
            flops=30 * 10 * 256 * 256 * 256, bytes_accessed=16 * total * width, transcendentals=0
        ),
        name=f"attend_back_{top}",
    )(meta, lo, *args)


def pick(refs, into, per):
    step = pl.program_id(0)
    for slot, ref in enumerate(refs):

        @pl.when(step // per == slot)
        def _(ref=ref):
            into[...] = ref[...]


def put(refs, value, per):
    step = pl.program_id(0)
    for slot, ref in enumerate(refs):

        @pl.when(step // per == slot)
        def _(ref=ref):
            ref[...] = value


def slot_specs(per, cols, count):
    def spec(slot):
        return pl.BlockSpec(
            (TILE, cols), lambda i, m: (jnp.clip(i - slot * per, 0, per - 1), 0)
        )

    return [spec(slot) for slot in range(count)]


def output_kernel(per, meta, o_ref, mo_ref, c0, c1, c2, c3, w_ref, *refs):
    outs, (keep, send, c_s, gw_s) = refs[:4], refs[4:]
    step = pl.program_id(0)
    pick((c0, c1, c2, c3), c_s, per)

    @pl.when(step == 0)
    def _():
        gw_s[...] = jnp.zeros_like(gw_s)

    attn = o_ref[...]
    put(outs, (dot(attn, w_ref[...]) + mo_ref[...].astype(F32)).astype(BF16), per)
    gw_s[...] += dot_tn(attn, c_s[...])

    @pl.when(step == pl.num_programs(0) - 1)
    def _():
        store_chunks(gw_s, keep, send, meta)


def output(meta, attn, mlp, cots, w_out, rows):
    total, width = attn.shape
    seq = cots[0].shape[0]
    per = seq // TILE
    chunks = chunk_shapes(width, D, rows)
    return pl.pallas_call(
        partial(output_kernel, per),
        out_shape=[jax.ShapeDtypeStruct((seq, D), BF16)] * 4
        + [jax.ShapeDtypeStruct(shape, BF16) for shape in chunks],
        grid_spec=pltpu.PrefetchScalarGridSpec(
            num_scalar_prefetch=1,
            grid=(4 * per,),
            in_specs=[
                pl.BlockSpec((TILE, width), lambda i, m: (i, 0)),
                pl.BlockSpec((TILE, D), lambda i, m: (i, 0)),
                *slot_specs(per, D, 4),
                pl.BlockSpec((width, D), lambda i, m: (m[0], 0)),
            ],
            out_specs=[*slot_specs(per, D, 4), *(whole(shape) for shape in chunks)],
            scratch_shapes=[pltpu.VMEM((TILE, D), BF16), pltpu.VMEM((width, D), F32)],
        ),
        compiler_params=params(),
        cost_estimate=pl.CostEstimate(
            flops=4 * total * width * D, bytes_accessed=6 * total * D, transcendentals=0
        ),
        name="output",
    )(meta, attn, mlp, *cots, w_out)


def norm_grad_kernel(slots, per, meta, *refs):
    count = len(slots)
    gjs, es, toks = refs[0:count], refs[count : 2 * count], refs[2 * count : 3 * count]
    gain, w_ref, gg_in, gs_in = refs[3 * count : 3 * count + 4]
    outs, (gg_ref, gs_ref, gj_s, e_s, x_s) = refs[-5 - count : -5], refs[-5:]
    step = pl.program_id(0)
    pick(gjs, gj_s, per)
    pick(es, e_s, per)
    pick(toks, x_s, per)

    @pl.when(step == 0)
    def _():
        gg_ref[...] = gg_in[...]
        gs_ref[...] = gs_in[...]

    normed = normalize(x_s[...].astype(F32))
    grad_norm = dot_nt(gj_s[...], w_ref[...])
    put(outs, (grad_norm * gain[...] + e_s[...].astype(F32)).astype(BF16), per)
    gg_ref[...] += jnp.sum(grad_norm * normed, axis=0, keepdims=True)
    gs_ref[...] += jnp.sum(grad_norm, axis=0, keepdims=True)


def norm_grad(slots, meta, grad, e_mlp, toks, gain, w, sums):
    width = grad.shape[1]
    seq = toks[0].shape[0]
    per = seq // TILE
    count = len(slots)
    row = whole((1, D))

    def at_slot(place, slot, cols):
        return pl.BlockSpec(
            (TILE, cols), lambda i, m: (slot * per + jnp.clip(i - place * per, 0, per - 1), 0)
        )

    return pl.pallas_call(
        partial(norm_grad_kernel, slots, per),
        out_shape=[jax.ShapeDtypeStruct((seq, D), BF16)] * count
        + [jax.ShapeDtypeStruct((1, D), F32)] * 2,
        grid_spec=pltpu.PrefetchScalarGridSpec(
            num_scalar_prefetch=1,
            grid=(count * per,),
            in_specs=[
                *(at_slot(place, slot, width) for place, slot in enumerate(slots)),
                *(at_slot(place, slot, D) for place, slot in enumerate(slots)),
                *slot_specs(per, D, count),
                row,
                whole((D, width)),
                row,
                row,
            ],
            out_specs=[*slot_specs(per, D, count), row, row],
            scratch_shapes=[
                pltpu.VMEM((TILE, width), BF16),
                pltpu.VMEM((TILE, D), BF16),
                pltpu.VMEM((TILE, D), BF16),
            ],
        ),
        compiler_params=params(),
        cost_estimate=pl.CostEstimate(
            flops=2 * count * seq * width * D, bytes_accessed=8 * count * seq * D, transcendentals=0
        ),
        name=f"norm_grad_{slots[0]}",
    )(
        meta,
        *[grad] * count,
        *[e_mlp] * count,
        *[toks[slot] for slot in slots],
        gain,
        w,
        *sums,
    )


def joined_weight_kernel(per, meta, gj_ref, t0, t1, t2, t3, gain, shift, keep, send, gb_ref, x_s, gw_s):
    step = pl.program_id(0)
    pick((t0, t1, t2, t3), x_s, per)

    @pl.when(step == 0)
    def _():
        gw_s[...] = jnp.zeros_like(gw_s)
        gb_ref[...] = jnp.zeros_like(gb_ref)

    attn_in = (normalize(x_s[...].astype(F32)) * gain[...] + shift[...]).astype(BF16)
    grad = gj_ref[...]
    gb_ref[...] += jnp.sum(grad.astype(F32), axis=0, keepdims=True)
    gw_s[...] += dot_tn(attn_in, grad)

    @pl.when(step == pl.num_programs(0) - 1)
    def _():
        store_chunks(gw_s, keep, send, meta)


def joined_weight(meta, grad, toks, gain, shift, rows):
    total, width = grad.shape
    per = toks[0].shape[0] // TILE
    row = whole((1, D))
    chunks = chunk_shapes(D, width, rows)
    return pl.pallas_call(
        partial(joined_weight_kernel, per),
        out_shape=[
            *(jax.ShapeDtypeStruct(shape, BF16) for shape in chunks),
            jax.ShapeDtypeStruct((1, width), F32),
        ],
        grid_spec=pltpu.PrefetchScalarGridSpec(
            num_scalar_prefetch=1,
            grid=(4 * per,),
            in_specs=[
                pl.BlockSpec((TILE, width), lambda i, m: (i, 0)),
                *slot_specs(per, D, 4),
                row,
                row,
            ],
            out_specs=[*(whole(shape) for shape in chunks), whole((1, width))],
            scratch_shapes=[pltpu.VMEM((TILE, D), BF16), pltpu.VMEM((D, width), F32)],
        ),
        compiler_params=params(),
        cost_estimate=pl.CostEstimate(
            flops=2 * total * width * D, bytes_accessed=4 * total * D, transcendentals=0
        ),
        name="joined_weight",
    )(meta, grad, *toks, gain, shift)


def after(value, *others):
    return lax.optimization_barrier((value, others))[0]


def swap(value, axis, mask):
    size = lax.axis_size(axis)
    return lax.ppermute(value, axis, [(i, i ^ mask) for i in range(size)])


def add_pair(keep, got):
    return [
        (keep[i].astype(F32) + got[i].astype(F32)).astype(BF16) for i in range(keep.shape[0])
    ]


def exchange(parts):
    total = parts[0].astype(F32)
    for place in range(1, len(parts)):
        total += swap(parts[place], "rows", 2 * place).astype(F32)
    return total


def spread_rows(chunk, col_width):
    rows, blk = lax.axis_size("rows"), lax.axis_size("blk")
    r, b = lax.axis_index("rows"), lax.axis_index("blk")
    pieces = chunk.reshape(chunk.shape[0], blk, col_width)
    got = []
    for turn in range(blk):
        moves = []
        for rr in range(rows):
            for bb in range(blk):
                moves.append((rr * blk + bb, (rows * bb + rr) // blk * blk + ((rr % blk) ^ turn)))
        piece = lax.dynamic_index_in_dim(pieces, (r % blk) ^ turn, 1, keepdims=False)
        got.append(lax.ppermute(piece, ("rows", "blk"), moves))
    got = jnp.stack(got)
    return [lax.dynamic_index_in_dim(got, b ^ part, 0, keepdims=False) for part in range(blk)]


def spread_columns(chunk):
    blk = lax.axis_size("blk")
    b = lax.axis_index("blk")
    parts = jnp.stack(
        [
            jnp.concatenate([chunk[:, 0:128], chunk[:, 256:320]], axis=1),
            jnp.concatenate([chunk[:, 128:256], chunk[:, 320:384]], axis=1),
            chunk[:, 384:576],
        ]
    )
    got = []
    for turn in range(3):
        moves = [((3 * to + turn) % blk, to) for to in range(blk)]
        to = (3 * (b - turn)) % blk
        piece = lax.dynamic_index_in_dim(parts, (3 * to + turn) // blk, 0, keepdims=False)
        got.append(lax.ppermute(piece, "blk", moves))
    return jnp.concatenate(got, axis=1)


def add_low(left, right):
    return (left.astype(F32) + right.astype(F32)).astype(BF16)


def local(
    tokens, seg_ids, valid_len, ln1_gain, ln1_bias, w_qkv, b_qkv, w_out, b_out,
    ln2_gain, ln2_bias, w_up, b_up, w_down, b_down, cotangent,
):
    rows = lax.axis_size("rows")
    blk = lax.axis_index("blk")
    seq = tokens.shape[1]
    per = seq // TILE
    width = D // 4
    hid = FF // 4
    meta = jnp.stack([blk, lax.axis_index("rows")]).astype(jnp.int32)
    low, high = angle_parts(4 * seq)
    tok_own, cot_own = tokens[0], cotangent[0]
    gain1, shift1, gain2, shift2 = (v[None] for v in (ln1_gain, ln1_bias, ln2_gain, ln2_bias))

    tok_near = swap(tok_own, "blk", 1)
    tok_far = swap(tok_own, "blk", 2)
    cot_near = swap(cot_own, "blk", 1)
    seg = [seg_ids[0]] + [swap(seg_ids[0], "blk", mask) for mask in (1, 2, 3)]

    *joined, w_own, b_own = project(
        0, meta, tok_own, gain1, shift1, low, high, w_qkv, b_qkv[None], None
    )
    cot_far = swap(after(cot_own, b_own), "blk", 2)

    def more(slot, m, tok, filled):
        return project(slot, m, tok, gain1, shift1, low, high, w_own, b_own, filled)

    joined = more(1, meta, tok_near, joined)
    mlp_args = (gain2, shift2, w_up, b_up[None], w_down, w_out)
    meta = after(meta, joined[0])
    first = feed_forward(
        0, meta, (tok_own, tok_near), (cot_own, cot_near), *mlp_args, None, rows
    )
    meta = after(meta, first[3])
    tok_last = swap(tok_far, "blk", 1)
    joined = more(2, meta, tok_far, joined)

    seg_all = jnp.stack(seg)
    pos = (jnp.arange(4, dtype=jnp.int32) ^ blk)[:, None] * seq + jnp.arange(seq, dtype=jnp.int32)
    starts = jnp.zeros_like(seg_all)
    for number in (1, 2, 3):
        starts = jnp.where(seg_all == number, jnp.sum(seg_all < number), starts)
    starts = jnp.where(pos < valid_len[0], starts, pos).astype(jnp.int32)
    starts = starts.reshape(4 * per, 1, TILE)
    tile_at = jnp.arange(4 * per, dtype=jnp.int32)
    tile_slot = (tile_at // per ^ blk) * per + tile_at % per
    lo = starts[:, 0, 0][tile_slot] // TILE

    query, keys, values = more(3, meta, tok_last, joined)
    toks = (tok_own, tok_near, tok_far, tok_last)

    attended = attend(0, meta, lo, query, keys, values, starts, per, None)
    cot_far = after(cot_far, attended[1])
    cot_last = swap(cot_far, "blk", 1)
    cots = (cot_own, cot_near, cot_far, cot_last)
    meta = after(meta, cot_far)
    attn, lse = attend(2, meta, lo, query, keys, values, starts, per, attended)

    meta = after(meta, lse)
    second = feed_forward(1, meta, toks[2:], cots[2:], *mlp_args, first, rows)
    mlp_part, e_mlp, grad_vec, gb_up, g_ln2, s_ln2 = second[:6]
    up_keep, up_send = chunks_of(*second[6:8], rows)
    down_keep, down_send = chunks_of(*second[8:10], rows)
    up_got = swap(up_send, "rows", 1)
    meta = after(meta, gb_up)
    *out_parts, wo_keep, wo_send = output(meta, attn, mlp_part, cots, w_out, rows)
    wo_keep, wo_send = chunks_of(wo_keep, wo_send, rows)
    down_got = swap(after(down_send, wo_send), "rows", 1)
    wo_got = swap(wo_send, "rows", 1)
    out_near = swap(out_parts[1], "blk", 1)
    out_last = swap(out_parts[3], "blk", 1)

    meta = after(meta, wo_send)
    back_args = (query, keys, values, attn, grad_vec, starts, lse, low, high, per)
    back = attend_back(3, meta, lo, *back_args, None)

    out_send = add_low(out_parts[2], after(out_last, back[1]))
    out_far = swap(out_send, "blk", 2)
    up_parts = add_pair(up_keep, after(up_got, back[1]))
    up = exchange(up_parts)
    meta = after(meta, out_send, up_parts)
    grad_joined = attend_back(1, meta, lo, *back_args, back)[0]

    down_parts = add_pair(down_keep, after(down_got, grad_joined))
    wo_parts = add_pair(wo_keep, after(wo_got, grad_joined))
    down = exchange(down_parts)
    wo = exchange(wo_parts)
    meta = after(meta, down_parts, wo_parts)
    sums = (jnp.zeros((1, D), F32),) * 2
    e_last, e_far, *sums = norm_grad(
        (3, 2), meta, grad_joined, e_mlp, toks, gain1, w_own, sums
    )
    e_got = swap(e_last, "blk", 1)
    meta = after(meta, e_far)
    qkv_keep, qkv_send, gb_joined = joined_weight(meta, grad_joined, toks, gain1, shift1, rows)
    qkv_keep, qkv_send = chunks_of(qkv_keep, qkv_send, rows)
    qkv_got = swap(qkv_send, "rows", 1)
    e_send = add_low(e_far, after(e_got, gb_joined))
    e_across = swap(e_send, "blk", 2)
    meta = after(meta, e_send, qkv_send)
    e_near, e_own, g_ln1, s_ln1 = norm_grad(
        (1, 0), meta, grad_joined, e_mlp, toks, gain1, w_own, sums
    )
    e_got = swap(e_near, "blk", 1)

    up_wide = cot_own.astype(F32)
    own_sums = jnp.concatenate(
        [gb_up, g_ln1, s_ln1, g_ln2, s_ln2, jnp.sum(up_wide, axis=0)[None], gb_joined], axis=1
    )
    own_sums = own_sums + swap(own_sums, "rows", 1)
    qkv_parts = add_pair(qkv_keep, qkv_got)
    qkv = exchange(qkv_parts)
    own_sums = exchange([own_sums] * (rows // 2))
    qkv = spread_columns(qkv.astype(BF16))
    all_sums = jnp.concatenate([own_sums] + [swap(own_sums, "blk", mask) for mask in (1, 2, 3)])
    true = jnp.take(all_sums, jnp.arange(4) ^ blk, axis=0)
    gb_up_all = true[:, :hid].reshape(FF)
    norm_sums = jnp.sum(all_sums[:, hid : hid + 5 * D], axis=0).reshape(5, D)
    gj = true[:, hid + 5 * D :]
    gb_qkv = jnp.concatenate(
        [
            jnp.concatenate([gj[:, 0:128], gj[:, 256:320]], axis=1).reshape(D),
            jnp.concatenate([gj[:, 128:256], gj[:, 320:384]], axis=1).reshape(D),
            gj[:, 384:576].reshape(D),
        ]
    )

    lower = spread_rows(jnp.concatenate([down, wo], axis=0).astype(BF16), width)
    cut = hid // rows
    down = jnp.concatenate([part[:cut] for part in lower]).astype(F32)
    out_w = jnp.concatenate([part[cut:] for part in lower]).astype(F32)

    wide = tok_own.astype(F32)
    summed = out_parts[0].astype(F32) + out_near.astype(F32) + out_far.astype(F32)
    result = (wide + (b_out + b_down) + summed).astype(BF16)[None]

    e_sum = e_own.astype(F32) + e_got.astype(F32) + e_across.astype(F32)
    center = wide - jnp.mean(wide, axis=-1, keepdims=True)
    rate = lax.rsqrt(jnp.mean(center * center, axis=-1, keepdims=True) + EPS)
    normed = center * rate
    grad = rate * (
        e_sum
        - jnp.mean(e_sum, axis=-1, keepdims=True)
        - normed * jnp.mean(e_sum * normed, axis=-1, keepdims=True)
    )
    grad_tokens = (up_wide + grad).astype(BF16)[None]
    return (
        result,
        grad_tokens,
        qkv.astype(F32),
        out_w,
        up,
        down,
        gb_qkv,
        norm_sums[4],
        gb_up_all,
        norm_sums[4],
        norm_sums[0],
        norm_sums[1],
        norm_sums[2],
        norm_sums[3],
    )


def solution(mesh):
    split = P("rows", "blk")
    in_specs = (
        P("rows", "blk", None),
        split,
        P("rows"),
        *(P(),) * 12,
        P("rows", "blk", None),
    )
    out_specs = (
        P("rows", "blk", None),
        P("rows", "blk", None),
        *(split,) * 4,
        *(P(),) * 8,
    )
    return jax.shard_map(local, mesh=mesh, in_specs=in_specs, out_specs=out_specs, check_vma=False)
```

```python
import math
from functools import partial

import jax
import jax.numpy as jnp
import numpy as np
from jax import lax
from jax.experimental import pallas as pl
from jax.experimental.pallas import tpu as pltpu
from jax.sharding import PartitionSpec as P

D = 768
HEADS = 12
HDIM = 64
ROT = 16
FF = 3072
EPS = 1e-05
MASKED = -1e30
TILE = 256
VROWS = 80
LN2 = math.log(2.0)
EXTRA = 16
LANES = 128
F32 = jnp.float32
BF16 = jnp.bfloat16
COST = pl.CostEstimate(flops=1000, bytes_accessed=1000, transcendentals=0)
NT_DIMS = (((1,), (1,)), ((), ()))
TN_DIMS = (((0,), (0,)), ((), ()))


def dot(left, right):
    return jnp.dot(left, right, preferred_element_type=F32)


def dot_nt(left, right):
    return lax.dot_general(left, right, NT_DIMS, preferred_element_type=F32)


def dot_tn(left, right):
    return lax.dot_general(left, right, TN_DIMS, preferred_element_type=F32)


def normalize(value):
    center = value - jnp.mean(value, axis=-1, keepdims=True)
    spread = jnp.mean(center * center, axis=-1, keepdims=True)
    return center * lax.rsqrt(spread + EPS)


def angle_parts(length):
    dim = np.arange(LANES) % HDIM
    inverse = np.where(dim < ROT, 10000.0 ** (-2.0 * (dim % (ROT // 2)) / ROT), 0.0)
    high = (np.arange(length // LANES) * LANES)[:, None] * inverse
    low = np.arange(LANES)[:, None] * inverse
    parts = np.stack([np.cos(low), np.sin(low)]), np.stack([np.cos(high), np.sin(high)])
    return tuple(jnp.asarray(part, F32) for part in parts)


def rotation(low_ref, high_ref, tile):
    lane = lax.broadcasted_iota(jnp.int32, (1, LANES), 1) % HDIM
    sign = jnp.where(lane < ROT // 2, -1.0, 1.0)
    cos_rows, sin_rows = [], []
    for part in range(TILE // LANES):
        row = tile * (TILE // LANES) + part
        cos_high = high_ref[0, pl.ds(row, 1), :]
        sin_high = high_ref[1, pl.ds(row, 1), :]
        cos_rows.append(low_ref[0] * cos_high - low_ref[1] * sin_high)
        sin_rows.append((low_ref[1] * cos_high + low_ref[0] * sin_high) * sign)
    return jnp.concatenate(cos_rows, axis=0), jnp.concatenate(sin_rows, axis=0)


def swap_halves(value):
    lane = lax.broadcasted_iota(jnp.int32, value.shape, 1) % HDIM
    half = ROT // 2
    return jnp.where(
        lane < half, pltpu.roll(value, LANES - half, 1), pltpu.roll(value, half, 1)
    )


def true_block(meta_ref, slot):
    return jnp.bitwise_xor(meta_ref[0], slot)


def params(*semantics, vmem=None):
    return pltpu.CompilerParams(
        dimension_semantics=semantics or ("arbitrary",), vmem_limit_bytes=vmem or 60 * 2**20
    )


def whole(shape):
    return pl.BlockSpec(shape, lambda *_: (0,) * len(shape))


def own_blocks(refs, odd, into):
    places = ((0, 256), (128, 320), (384, 512))
    for part, (pair_at, third_at) in enumerate(places):
        left, right = refs[2 * part], refs[2 * part + 1]

        @pl.when(odd == 0)
        def _(left=left, right=right, pair_at=pair_at, third_at=third_at):
            into[:, pair_at : pair_at + 128] = left[...]
            into[:, third_at : third_at + 64] = right[:, 0:64]

        @pl.when(odd == 1)
        def _(left=left, right=right, pair_at=pair_at, third_at=third_at):
            into[:, pair_at : pair_at + 128] = jnp.concatenate(
                [left[:, 64:128], right[:, 0:64]], axis=1
            )
            into[:, third_at : third_at + 64] = right[:, 64:128]


def row(ref):
    return ref[...].reshape(1, ref.shape[0])


def own_bias(b_ref, odd, blk, into):
    blocks = []
    for part in range(3):
        for side in range(2):
            at = pl.multiple_of((part * (D // LANES) + side + 3 * blk // 2) * LANES, LANES)
            blocks.append(b_ref[pl.ds(at, LANES)].reshape(1, LANES))
    own_blocks(blocks, odd, into)


def project_tile(normed, gain, shift, w_ref, b_ref, low, high, tile, q_ref, k_ref, v_ref):
    attn_in = (normed * row(gain) + row(shift)).astype(BF16)
    joined = dot(attn_in, w_ref[...]) + b_ref[...]
    cos, sin = rotation(low, high, tile)
    scale = HDIM**-0.5 / LN2

    def turn(block):
        return block * cos + swap_halves(block) * sin

    query = turn(joined[:, 0:128]) * scale
    keys = turn(joined[:, 128:256])
    mixed = turn(joined[:, 256:384])
    q_ref[:, 0:128] = query.astype(BF16)
    k_ref[:, 0:128] = keys.astype(BF16)
    q_ref[:, 128:192] = (mixed[:, 0:64] * scale).astype(BF16)
    k_ref[:, 128:192] = mixed[:, 64:128].astype(BF16)
    v_ref[...] = joined[:, 384:576].astype(BF16)


def qkv_kernel(slot, meta, x_ref, gain, shift, low, high, w_ref, b_ref, *refs):
    per = pl.num_programs(0)
    tile = true_block(meta, slot) * per + pl.program_id(0)
    normed = normalize(x_ref[...].astype(F32))
    project_tile(normed, gain, shift, w_ref, b_ref, low, high, tile, *refs[-3:])


def project(slot, meta, x, gain, shift, low, high, w, b, filled, seq):
    width = D // 4
    per = seq // TILE
    out = jax.ShapeDtypeStruct((4 * seq, width), BF16)
    out_spec = pl.BlockSpec((TILE, width), lambda i, m: (slot * per + i, 0))
    args = [x, gain, shift, low, high, w, b, *filled]
    specs = [pl.BlockSpec((TILE, D), lambda i, m: (i, 0))]
    specs += [whole(a.shape) for a in args[1:7]]
    specs += [pl.BlockSpec(memory_space=pl.ANY)] * 3
    return pl.pallas_call(
        partial(qkv_kernel, slot),
        out_shape=[out] * 3,
        grid_spec=pltpu.PrefetchScalarGridSpec(
            num_scalar_prefetch=1, grid=(per,), in_specs=specs, out_specs=[out_spec] * 3
        ),
        input_output_aliases={8 + i: i for i in range(3)},
        compiler_params=params(),
        cost_estimate=COST,
        name=f"qkv_{slot}",
    )(meta, *args)


def starts_kernel(seq, meta, valid, s0, s1, s2, s3, start_ref, lo_ref, hi_ref):
    segs = [ref[0:1, 0:seq].astype(F32) for ref in (s0, s1, s2, s3)]
    below = [
        sum(jnp.sum((seg < number).astype(F32), axis=1, keepdims=True) for seg in segs)
        for number in (1, 2, 3)
    ]
    per = seq // TILE
    iota = lax.broadcasted_iota(jnp.int32, (1, seq), 1)
    for slot, seg in enumerate(segs):
        block = true_block(meta, slot)
        begin = jnp.zeros((1, seq), F32)
        for number in (1, 2, 3):
            begin = jnp.where(seg == number, below[number - 1], begin)
        pos = iota + block * seq
        begin = jnp.where(pos < valid[0], begin.astype(jnp.int32), pos)
        for part in range(per):
            tile = begin[:, part * TILE : (part + 1) * TILE]
            start_ref[slot * per + part] = tile
            lo_ref[block * per + part] = jnp.min(tile) // TILE
            hi_ref[block * per + part] = (jnp.max(tile) + (TILE - 1)) // TILE


def segment_starts(meta, valid_len, toks, seq):
    tiles = 4 * seq // TILE
    smem = pl.BlockSpec(memory_space=pltpu.SMEM)
    return pl.pallas_call(
        partial(starts_kernel, seq),
        out_shape=[
            jax.ShapeDtypeStruct((tiles, 1, TILE), jnp.int32),
            jax.ShapeDtypeStruct((tiles,), jnp.int32),
            jax.ShapeDtypeStruct((tiles,), jnp.int32),
        ],
        grid_spec=pltpu.PrefetchScalarGridSpec(
            num_scalar_prefetch=2,
            grid=(1,),
            in_specs=[pl.BlockSpec((EXTRA, D), lambda i, m, v: (seq // EXTRA, 0))] * 4,
            out_specs=[whole((tiles, 1, TILE)), smem, smem],
        ),
        compiler_params=params(),
        name="segment_starts",
    )(meta, valid_len, *toks)


def places(rows):
    order = [0]
    while len(order) < rows:
        order = [2 * i for i in order] + [2 * i + 1 for i in order]
    return order


def fits(rows):
    return rows == 8 and D // rows % 32 == 0


def store_chunks(grad, keep, send, meta, rows):
    size = grad.shape[0] // rows
    for index, place in enumerate(places(rows)):
        at = pl.multiple_of(jnp.bitwise_xor(meta[1], place) * size, 32)
        into = keep if index < rows // 2 else send
        row = index % (rows // 2) * size
        into[row : row + size, :] = grad[pl.ds(at, size), :].astype(into.dtype)


def chunk_shapes(cols, rows, extra=0):
    if fits(rows):
        return [(D // 2 + extra, cols)] * 2
    return [(D, cols), (8, LANES)]


def chunks_of(keep, send, rows):
    if fits(rows):
        return keep, send
    order = jnp.array(places(rows)) ^ lax.axis_index("rows")
    parts = keep.reshape(rows, D // rows, keep.shape[1])
    parts = jnp.take(parts, order, axis=0).reshape(keep.shape)
    return parts[: D // 2], parts[D // 2 :]


def feed(normed, upstream, gain, shift, w_up, b_up, w_down):
    mlp_in = (normed * row(gain) + row(shift)).astype(BF16)
    hidden = dot(mlp_in, w_up[...]) + b_up
    cdf = 0.5 * (1.0 + lax.erf(hidden * (0.5**0.5)))
    act = (hidden * cdf).astype(BF16)
    slope = cdf + hidden * jnp.exp(-0.5 * hidden * hidden) * ((2.0 * math.pi) ** -0.5)
    grad_low = (slope * dot_nt(upstream, w_down[...])).astype(BF16)
    grad_norm = dot_nt(grad_low, w_up[...])
    return mlp_in, act, grad_low, grad_norm


def add_sums(sums, grad_low, grad_norm, normed):
    sums[0:1, :] += jnp.sum(grad_low.astype(F32), axis=0, keepdims=True)
    sums[1:2, :] += jnp.sum(grad_norm * normed, axis=0, keepdims=True)
    sums[2:3, :] += jnp.sum(grad_norm, axis=0, keepdims=True)


def own_row(ref, blk, size):
    return ref[pl.ds(pl.multiple_of(blk * size, LANES), size)].reshape(1, size)


def mlp_first_kernel(
    half, meta, xa, xb, ca, cb, gain, shift, b_up, w_up, w_down, w_out,
    gain1, shift1, b_qkv, low, high, w0, w1, w2, w3, w4, w5,
    mo_ref, e_ref, gv_ref, sums, gup, gdown, q_ref, k_ref, v_ref, w_own, b_own, x_s, c_s,
):
    step = pl.program_id(0)

    @pl.when(step < half)
    def _():
        x_s[...] = xa[...]
        c_s[...] = ca[...]

    @pl.when(step >= half)
    def _():
        x_s[...] = xb[...]
        c_s[...] = cb[...]

    @pl.when(step == 0)
    def _():
        sums[...] = jnp.zeros_like(sums)
        gup[...] = jnp.zeros_like(gup)
        gdown[...] = jnp.zeros_like(gdown)
        odd = meta[0] % 2
        own_blocks((w0, w1, w2, w3, w4, w5), odd, w_own)
        own_bias(b_qkv, odd, meta[0], b_own)

    upstream = c_s[...]

    @pl.when(step < half)
    def _():
        sums[3:4, :] += jnp.sum(upstream.astype(F32), axis=0, keepdims=True)

    normed = normalize(x_s[...].astype(F32))
    tile = true_block(meta, step // half) * half + step % half
    project_tile(normed, gain1, shift1, w_own, b_own, low, high, tile, q_ref, k_ref, v_ref)
    bias = own_row(b_up, meta[0], gup.shape[1])
    mlp_in, act, grad_low, grad_norm = feed(normed, upstream, gain, shift, w_up, bias, w_down)
    mo_ref[...] = dot(act, w_down[...]).astype(BF16)
    add_sums(sums, grad_low, grad_norm, normed)
    e_ref[...] = (grad_norm * row(gain)).astype(BF16)
    gv_ref[...] = dot_nt(upstream, w_out[...]).astype(BF16)
    gup[...] += dot_tn(mlp_in, grad_low)
    gdown[...] += dot_tn(upstream, act)


def mlp_second_kernel(
    half, rows, meta, xa, xb, ca, cb, gain, shift, b_up, w_up, w_down, w_out,
    c0, c1, mo_in, o_near, o_far, sums_in, gup, gdown, _,
    e_ref, gv_ref, sums, even, odd, keep, send, x_s, c_s, n_s, grad,
):
    step = pl.program_id(0)
    hid = gup.shape[1]

    @pl.when(step < half)
    def _():
        x_s[...] = xa[...]
        c_s[...] = ca[...]
        n_s[...] = c0[...]

    @pl.when(step >= half)
    def _():
        x_s[...] = xb[...]
        c_s[...] = cb[...]
        n_s[...] = c1[...]

    @pl.when(step == 0)
    def _():
        sums[...] = sums_in[...]
        grad[:, 0:hid] = gup[...]
        grad[:, hid : 2 * hid] = gdown[...]
        grad[:, 2 * hid :] = jnp.zeros_like(grad[:, 2 * hid :])

    upstream = c_s[...]
    normed = normalize(x_s[...].astype(F32))
    bias = own_row(b_up, meta[0], hid)
    mlp_in, act, grad_low, grad_norm = feed(normed, upstream, gain, shift, w_up, bias, w_down)
    add_sums(sums, grad_low, grad_norm, normed)
    e_ref[...] = (grad_norm * row(gain)).astype(BF16)
    gv_ref[...] = dot_nt(upstream, w_out[...]).astype(BF16)
    grad[:, 0:hid] += dot_tn(mlp_in, grad_low)
    grad[:, hid : 2 * hid] += dot_tn(upstream, act)
    grad[:, 2 * hid : 2 * hid + D // 4] += dot_tn(upstream, o_far[...]) + dot_tn(
        n_s[...], o_near[...]
    )
    far = (dot(act, w_down[...]) + dot(o_far[...], w_out[...])).astype(BF16)
    near = (mo_in[...].astype(F32) + dot(o_near[...], w_out[...])).astype(BF16)

    @pl.when(step < half)
    def _():
        even[0] = near
        even[1] = far

    @pl.when(step >= half)
    def _():
        odd[0] = near
        odd[1] = far

    @pl.when(step == pl.num_programs(0) - 1)
    def _():
        if fits(rows):
            store_chunks(grad, keep, send, meta, rows)
        else:
            keep[...] = grad[...].astype(BF16)


def feed_forward(
    meta, xs, cs, gain, shift, b_up, w_up, w_down, w_out, rows, seq,
    joined=None, before=None, near=None, attn=None,
):
    per = seq // TILE
    steps = 2 * per
    hid = FF // 4
    width = D // 4
    total = 4 * seq
    first = pl.BlockSpec((TILE, D), lambda i, m: (jnp.minimum(i, per - 1), 0))
    second = pl.BlockSpec((TILE, D), lambda i, m: (jnp.maximum(i - per, 0), 0))
    specs = [
        first,
        second,
        first,
        second,
        whole((D,)),
        whole((D,)),
        whole((FF,)),
        pl.BlockSpec((D, hid), lambda i, m: (0, m[0])),
        pl.BlockSpec((hid, D), lambda i, m: (m[0], 0)),
        pl.BlockSpec((width, D), lambda i, m: (m[0], 0)),
    ]
    args = [*xs, *cs, gain, shift, b_up, w_up, w_down, w_out]
    tile = pl.BlockSpec((TILE, D), lambda i, m: (i, 0))
    narrow = pl.BlockSpec((TILE, width), lambda i, m: (i, 0))
    sums = (8, D)
    scratch = [pltpu.VMEM((TILE, D), BF16), pltpu.VMEM((TILE, D), BF16)]
    pair = jax.ShapeDtypeStruct((steps * TILE, D), BF16)
    vec = jax.ShapeDtypeStruct((total, width), BF16)
    if before is None:
        body = partial(mlp_first_kernel, per)
        gain1, shift1, w_qkv, b_qkv, low, high = joined
        args += [gain1, shift1, b_qkv, low, high]
        specs += [whole(a.shape) for a in args[-5:]]
        for part in range(3):
            for side in range(2):
                specs.append(
                    pl.BlockSpec(
                        (D, LANES),
                        lambda i, m, at=part * D // LANES + side: (0, at + 3 * m[0] // 2),
                    )
                )
                args.append(w_qkv)
        outs = [pair, pair, vec, jax.ShapeDtypeStruct(sums, F32)]
        outs += [jax.ShapeDtypeStruct((D, hid), F32)] * 2 + [vec] * 3
        outs += [
            jax.ShapeDtypeStruct((D, 3 * width), BF16),
            jax.ShapeDtypeStruct((1, 3 * width), F32),
        ]
        out_specs = [tile, tile, narrow, whole(sums)]
        out_specs += [whole((D, hid))] * 2 + [narrow] * 3
        out_specs += [whole((D, 3 * width)), whole((1, 3 * width))]
        aliases = {}
    else:
        body = partial(mlp_second_kernel, per, rows)
        mlp_out, _, grad_vec, sums_in, gup, gdown = before
        chunks = chunk_shapes(2 * hid + 2 * LANES, rows)
        args += [*near, mlp_out, attn, attn, sums_in, gup, gdown, grad_vec]
        specs += [
            first,
            second,
            tile,
            narrow,
            pl.BlockSpec((TILE, width), lambda i, m: (i + steps, 0)),
            whole(sums),
            whole((D, hid)),
            whole((D, hid)),
            pl.BlockSpec(memory_space=pl.ANY),
        ]
        aliases = {len(args): 1}
        both = jax.ShapeDtypeStruct((2, seq, D), BF16)
        outs = [pair, vec, jax.ShapeDtypeStruct(sums, F32), both, both]
        outs += [jax.ShapeDtypeStruct(shape, BF16) for shape in chunks]
        out_specs = [
            tile,
            pl.BlockSpec((TILE, width), lambda i, m: (i + steps, 0)),
            whole(sums),
            pl.BlockSpec((2, TILE, D), lambda i, m: (0, jnp.minimum(i, per - 1), 0)),
            pl.BlockSpec((2, TILE, D), lambda i, m: (0, jnp.maximum(i - per, 0), 0)),
            *(whole(shape) for shape in chunks),
        ]
        scratch += [pltpu.VMEM((TILE, D), BF16), pltpu.VMEM((D, 2 * hid + 2 * LANES), F32)]
    return pl.pallas_call(
        body,
        out_shape=outs,
        grid_spec=pltpu.PrefetchScalarGridSpec(
            num_scalar_prefetch=1,
            grid=(steps,),
            in_specs=specs,
            out_specs=out_specs,
            scratch_shapes=scratch,
        ),
        input_output_aliases=aliases,
        compiler_params=params(),
        cost_estimate=COST,
        name="mlp_first" if before is None else "mlp_second",
    )(meta, *args)


def head_masks():
    lane = lax.broadcasted_iota(jnp.int32, (1, LANES), 1)
    first = jnp.where(lane < HDIM, 1.0, 0.0).astype(BF16)
    second = jnp.where(lane < HDIM, 0.0, 1.0).astype(BF16)
    return first, second


def slot_rows(meta, per, tile):
    slot = jnp.bitwise_xor(tile // per, meta[0])
    return pl.multiple_of((slot * per + tile % per) * TILE, TILE)


def by_head(first, second, block, third):
    return (block * first, block * second, third)


def transpose_all(from_ref, to_ref):
    @pl.loop(0, from_ref.shape[0] // TILE)
    def _(tile):
        rows = pl.ds(pl.multiple_of(tile * TILE, TILE), TILE)
        to_ref[:, rows] = from_ref[rows, :].astype(F32).T.astype(BF16)


def attend_kernel(per, meta, lo, hi, q_ref, k_ref, v_ref, start_ref, o_ref, lse_ref, vt_ref, acc, s_ref):
    mask0, mask1 = head_masks()
    tiles = k_ref.shape[0] // TILE
    qi = pl.program_id(0)

    @pl.when(qi == 0)
    def _():
        ones = jnp.where(lax.broadcasted_iota(jnp.int32, (VROWS - HDIM, TILE), 0) == 0, 1.0, 0.0)

        @pl.loop(0, tiles)
        def _(tile):
            rows = pl.ds(pl.multiple_of(tile * TILE, TILE), TILE)
            block = v_ref[rows, :].astype(F32).T
            for head in range(3):
                at = head * VROWS
                vt_ref[at : at + HDIM, rows] = block[head * HDIM : (head + 1) * HDIM].astype(BF16)
                vt_ref[at + HDIM : at + VROWS, rows] = ones.astype(BF16)

    key_iota = lax.broadcasted_iota(jnp.int32, (TILE, TILE), 0)
    query_iota = lax.broadcasted_iota(jnp.int32, (TILE, TILE), 1)
    queries = by_head(mask0, mask1, q_ref[:, 0:128], q_ref[:, 128:192])
    starts = start_ref[0]
    acc[...] = jnp.zeros_like(acc)

    def key_tile(turn):
        return jnp.where(turn == 0, qi, first + turn - 1)

    def score(masked, ki):
        k_rows = pl.ds(slot_rows(meta, per, ki), TILE)
        pair, third = k_ref[k_rows, 0:128], k_ref[k_rows, 128:192]
        scores = [dot_nt(third if head == 2 else pair, queries[head]) for head in range(3)]
        if masked:
            allowed = (key_iota >= starts - ki * TILE) & (key_iota <= query_iota + (qi - ki) * TILE)
            scores = [jnp.where(allowed, x, MASKED) for x in scores]
        return scores, [jnp.max(x, axis=0, keepdims=True) for x in scores]

    def value(ki, tops, peaks):
        k_rows = pl.ds(slot_rows(meta, per, ki), TILE)
        news = [jnp.maximum(top, peak) for top, peak in zip(tops, peaks)]
        fades = [jnp.exp2(top - new) for top, new in zip(tops, news)]
        weights = [jnp.exp2(s_ref[head] - news[head]).astype(BF16) for head in range(3)]
        terms = [
            dot(vt_ref[head * VROWS : (head + 1) * VROWS, k_rows], weights[head]) for head in range(3)
        ]
        return news, fades, terms

    def put(fades, terms):
        for head in range(3):
            cols = slice(head * VROWS, (head + 1) * VROWS)
            acc[cols, :] = acc[cols, :] * fades[head] + terms[head]

    def visit(masked, turn, carry):
        tops, peaks = carry
        scores, next_peaks = score(masked, key_tile(turn + 1))
        news, fades, terms = value(key_tile(turn), tops, peaks)
        peaks = next_peaks
        for head in range(3):
            s_ref[head] = scores[head]
        put(fades, terms)
        return tuple(news), tuple(peaks)

    first = lo[qi]
    full = jnp.minimum(hi[qi], qi)
    scores, peaks = score(True, qi)
    for head in range(3):
        s_ref[head] = scores[head]
    carry = ((jnp.full((1, TILE), MASKED, F32),) * 3, tuple(peaks))
    carry = lax.fori_loop(0, full - first, partial(visit, True), carry)
    carry = lax.fori_loop(full - first, qi - first, partial(visit, False), carry)
    tops, fades, terms = value(key_tile(qi - first), *carry)
    put(fades, terms)
    heads = []
    for head, top in enumerate(tops):
        at = head * VROWS
        total = acc[at + HDIM : at + HDIM + 1, :]
        heads.append(acc[at : at + HDIM, :] / total)
        lse_ref[head, 0] = top + jnp.log2(total)
    o_ref[...] = jnp.concatenate(heads, axis=0).T.astype(BF16)

def attend(meta, lo, hi, query, keys, values, starts, per):
    total, width = query.shape
    tiles = total // TILE
    def slot(i, m):
        return jnp.bitwise_xor(i // per, m[0]) * per + i % per
    q_spec = pl.BlockSpec((TILE, width), lambda i, m, lo, hi: (slot(i, m), 0))
    start_spec = pl.BlockSpec((1, 1, TILE), lambda i, m, lo, hi: (slot(i, m), 0, 0))
    lse_spec = pl.BlockSpec((3, 1, 1, TILE), lambda i, m, lo, hi: (0, slot(i, m), 0, 0))
    return pl.pallas_call(
        partial(attend_kernel, per),
        out_shape=[
            jax.ShapeDtypeStruct((total, width), BF16),
            jax.ShapeDtypeStruct((3, tiles, 1, TILE), F32),
        ],
        grid_spec=pltpu.PrefetchScalarGridSpec(
            num_scalar_prefetch=3,
            grid=(tiles,),
            in_specs=[q_spec, whole(keys.shape), whole(values.shape), start_spec],
            out_specs=[q_spec, lse_spec],
            scratch_shapes=[pltpu.VMEM((3 * VROWS, total), BF16), pltpu.VMEM((3 * VROWS, TILE), F32), pltpu.VMEM((3, TILE, TILE), F32)],
        ),
        compiler_params=params(),
        cost_estimate=COST,
        name="attend",
    )(meta, lo, hi, query, keys, values, starts)


def attend_back_kernel(
    per, meta, lo, hi, q_ref, k_ref, v_ref, o_ref, gv_ref, start_ref, lse_ref, low, high,
    gj_ref, kt_ref, dk_ref, dv_ref, dqt_ref
):
    mask0, mask1 = head_masks()
    tiles = k_ref.shape[0] // TILE
    qi = tiles - 1 - pl.program_id(0)

    @pl.when(pl.program_id(0) == 0)
    def _():
        transpose_all(k_ref, kt_ref)

    own_rows = pl.ds(slot_rows(meta, per, qi), TILE)
    key_iota = lax.broadcasted_iota(jnp.int32, (TILE, TILE), 0)
    query_iota = lax.broadcasted_iota(jnp.int32, (TILE, TILE), 1)
    queries = by_head(mask0, mask1, q_ref[:, 0:128], q_ref[:, 128:192])
    grads = by_head(mask0, mask1, gv_ref[:, 0:128], gv_ref[:, 128:192])
    starts = start_ref[0]
    lses = [lse_ref[head, 0] for head in range(3)]
    product = (gv_ref[...].astype(F32) * o_ref[...].astype(F32)).T
    deltas = [
        jnp.sum(product[head * HDIM : (head + 1) * HDIM], axis=0, keepdims=True)
        for head in range(3)
    ]
    dqt_ref[...] = jnp.zeros_like(dqt_ref)

    @pl.when(pl.program_id(0) == 0)
    def _():
        dk_ref[...] = jnp.zeros_like(dk_ref)
        dv_ref[...] = jnp.zeros_like(dv_ref)

    def load(ki):
        k_rows = pl.ds(slot_rows(meta, per, ki), TILE)
        return k_rows

    def score(masked, ki):
        k_rows = load(ki)
        pair, third = k_ref[k_rows, 0:128], k_ref[k_rows, 128:192]
        v_pair, v_third = v_ref[k_rows, 0:128], v_ref[k_rows, 128:192]
        scores = [dot_nt(third if head == 2 else pair, queries[head]) for head in range(3)]
        grad_probs = [dot_nt(v_third if head == 2 else v_pair, grads[head]) for head in range(3)]
        if masked:
            allowed = (key_iota >= starts - ki * TILE) & (key_iota <= query_iota + (qi - ki) * TILE)
            scores = [jnp.where(allowed, x, MASKED) for x in scores]
        return scores, grad_probs

    def terms(ki, scores, grad_probs):
        k_rows = load(ki)
        probs = [jnp.exp2(x - lse) for x, lse in zip(scores, lses)]
        grad_scores = [
            (p * (g - delta)).astype(BF16) for p, g, delta in zip(probs, grad_probs, deltas)
        ]
        dv = [dot(p.astype(BF16), g) for p, g in zip(probs, grads)]
        dk = [dot(g, q) for g, q in zip(grad_scores, queries)]
        dq = [
            dot(kt_ref[head * HDIM : (head + 1) * HDIM, k_rows], grad_scores[head])
            for head in range(3)
        ]
        return dk, dv, dq

    def add(ki, dk, dv, dq):
        k_rows = load(ki)
        for into, parts in ((dk_ref, dk), (dv_ref, dv)):
            into[k_rows, 0:128] += parts[0] + parts[1]
            into[k_rows, 128:192] += parts[2]
        for head in range(3):
            dqt_ref[head * HDIM : (head + 1) * HDIM, :] += dq[head]

    first = lo[qi]
    full = jnp.minimum(hi[qi], qi)

    def visit(masked, ki):
        add(ki, *terms(ki, *score(masked, ki)))

    @pl.loop(first, full)
    def _(ki):
        visit(True, ki)

    @pl.loop(full, qi)
    def _(ki):
        visit(False, ki)

    visit(True, qi)

    cos, sin = rotation(low, high, qi)

    def turn_back(block):
        return block * cos - swap_halves(block) * sin

    dq = dqt_ref[...].T * (HDIM**-0.5)
    dk = dk_ref[own_rows, :] * LN2
    gj_ref[:, 0:128] = turn_back(dq[:, 0:128]).astype(BF16)
    gj_ref[:, 128:256] = turn_back(dk[:, 0:128]).astype(BF16)
    mixed = jnp.concatenate([dq[:, 128:192], dk[:, 128:192]], axis=1)
    gj_ref[:, 256:384] = turn_back(mixed).astype(BF16)
    gj_ref[:, 384:576] = dv_ref[own_rows, :].astype(BF16)


def attend_back(
    meta, lo, hi, query, keys, values, attn, grad_vec, starts, lse, low, high, per
):
    total, width = query.shape
    tiles = total // TILE

    def slot(i, m):
        tile = tiles - 1 - i
        return jnp.bitwise_xor(tile // per, m[0]) * per + tile % per

    q_spec = pl.BlockSpec((TILE, width), lambda i, m, lo, hi: (slot(i, m), 0))
    gj_spec = pl.BlockSpec((TILE, 3 * width), lambda i, m, lo, hi: (slot(i, m), 0))
    start_spec = pl.BlockSpec((1, 1, TILE), lambda i, m, lo, hi: (slot(i, m), 0, 0))
    lse_spec = pl.BlockSpec((3, 1, 1, TILE), lambda i, m, lo, hi: (0, slot(i, m), 0, 0))
    return pl.pallas_call(
        partial(attend_back_kernel, per),
        out_shape=jax.ShapeDtypeStruct((total, 3 * width), BF16),
        grid_spec=pltpu.PrefetchScalarGridSpec(
            num_scalar_prefetch=3,
            grid=(tiles,),
            in_specs=[
                q_spec,
                whole(keys.shape),
                whole(values.shape),
                q_spec,
                q_spec,
                start_spec,
                lse_spec,
                whole(low.shape),
                whole(high.shape),
            ],
            out_specs=gj_spec,
            scratch_shapes=[
                pltpu.VMEM((width, total), BF16),
                pltpu.VMEM((total, width), F32),
                pltpu.VMEM((total, width), F32),
                pltpu.VMEM((width, TILE), F32),
            ],
        ),
        compiler_params=params(),
        cost_estimate=COST,
        name="attend_back",
    )(meta, lo, hi, query, keys, values, attn, grad_vec, starts, lse, low, high)


def joined_kernel(final, rows, meta, *refs):
    gj_a, gj_b, e_a, e_b, x_a, x_b, gain_ref, shift_ref, w_ref = refs[:9]
    if final:
        grad_in, bias_in, sums_in, mlp_sums = refs[9:13]
        e_ref, keep, send, grad, bias, sums = refs[13:]
    else:
        e_ref, grad, bias, sums = refs[9:]
    step = pl.program_id(0)

    @pl.when(step == 0)
    def _():
        if final:
            grad[...] = grad_in[...]
            bias[...] = bias_in[...]
            sums[...] = sums_in[...]
        else:
            grad[...] = jnp.zeros_like(grad)
            bias[...] = jnp.zeros_like(bias)
            sums[...] = jnp.zeros_like(sums)

    gain, shift = row(gain_ref), row(shift_ref)
    for index, (gj_ref, e_in, x_ref) in enumerate(((gj_a, e_a, x_a), (gj_b, e_b, x_b))):
        normed = normalize(x_ref[...].astype(F32))
        attn_in = (normed * gain + shift).astype(BF16)
        low = gj_ref[...]
        grad_norm = dot_nt(low, w_ref[...])
        e_ref[index] = (grad_norm * gain + e_in[...].astype(F32)).astype(BF16)
        sums[0:1, :] += jnp.sum(grad_norm * normed, axis=0, keepdims=True)
        sums[1:2, :] += jnp.sum(grad_norm, axis=0, keepdims=True)
        bias[0:1, :] += jnp.sum(low.astype(F32), axis=0, keepdims=True)
        grad[...] += dot_tn(attn_in, low)

    if final:

        @pl.when(step == pl.num_programs(0) - 1)
        def _():
            if fits(rows):
                store_chunks(grad, keep, send, meta, rows)
                small = pack_small(sums[...], mlp_sums[...], bias[...])
                keep[D // 2 :, :] = small
                send[D // 2 :, :] = small
            else:
                keep[...] = grad[...].astype(BF16)
                send[...] = jnp.zeros_like(send)


SMALL = 32


def pack_small(norm_sums, mlp_sums, bias):
    third = 3 * D // 4
    table = jnp.concatenate([norm_sums[0:4], mlp_sums[0:4]], axis=0)
    which = lax.broadcasted_iota(jnp.int32, (8, third), 0)
    head = jnp.where(which == 2, bias[0:1, :], table[:, :third])
    tail = jnp.concatenate([table[:, third:], jnp.zeros((8, 2 * third - D), F32)], axis=1)
    return split_small(jnp.concatenate([head, tail], axis=0))


def add_small(left, right):
    half = SMALL // 2
    total = left.astype(F32) + right.astype(F32)
    return total[:half] + total[half:]


def split_small(rows):
    high = rows.astype(BF16)
    return jnp.concatenate([high, (rows - high.astype(F32)).astype(BF16)], axis=0)


def joined_back(
    meta, slots, grad, e_mlp, toks, gain, shift, w, rows, seq, before=None, mlp_sums=None
):
    width = grad.shape[1]
    per = seq // TILE

    def at(slot, cols):
        return pl.BlockSpec((TILE, cols), lambda i, m: (slot * per + i, 0))

    sums = (8, D)
    args = [grad, grad, *e_mlp, *[toks[slot] for slot in slots], gain, shift, w]
    specs = [
        *(at(slot, width) for slot in slots),
        *(at(slot % 2, D) for slot in slots),
        *(pl.BlockSpec((TILE, D), lambda i, m: (i, 0)),) * 2,
        whole(gain.shape),
        whole(shift.shape),
        whole(w.shape),
    ]
    e_spec = pl.BlockSpec((2, TILE, D), lambda i, m: (0, i, 0))
    outs, out_specs = [jax.ShapeDtypeStruct((2, seq, D), BF16)], [e_spec]
    carried = [(D, width), (8, width), sums]
    scratch = []
    if before is None:
        outs += [jax.ShapeDtypeStruct(shape, F32) for shape in carried]
        out_specs += [whole(shape) for shape in carried]
    else:
        chunks = chunk_shapes(width, rows, SMALL)
        outs += [jax.ShapeDtypeStruct(shape, BF16) for shape in chunks]
        out_specs += [whole(shape) for shape in chunks]
        if not fits(rows):
            outs[-1] = jax.ShapeDtypeStruct((8, LANES), BF16)
        args += [*before, mlp_sums]
        specs += [whole(shape) for shape in carried] + [whole(sums)]
        scratch = [pltpu.VMEM(shape, F32) for shape in carried]
        if not fits(rows):
            outs += [jax.ShapeDtypeStruct(shape, F32) for shape in carried[1:]]
            out_specs += [whole(shape) for shape in carried[1:]]
            scratch = scratch[:1]
    body = partial(joined_kernel, before is not None, rows)
    if before is not None and not fits(rows):

        def body(meta, *refs):
            inputs, (e_ref, keep, send, bias, sums, grad) = refs[:13], refs[13:]
            joined_kernel(True, rows, meta, *inputs, e_ref, keep, send, grad, bias, sums)

    return pl.pallas_call(
        body,
        out_shape=outs,
        grid_spec=pltpu.PrefetchScalarGridSpec(
            num_scalar_prefetch=1,
            grid=(per,),
            in_specs=specs,
            out_specs=out_specs,
            scratch_shapes=scratch,
        ),
        compiler_params=params(),
        cost_estimate=COST,
        name="joined_first" if before is None else "joined_second",
    )(meta, *args)


def fold_kernel(extra, keep, got, *outs):
    size = keep.shape[0] - extra
    for index, out in enumerate(outs):
        rows = slice(index * size // 2, (index + 1) * size // 2)
        total = keep[rows, :].astype(F32) + got[rows, :].astype(F32)
        out[0 : size // 2, :] = total.astype(BF16)
    if extra:
        small = split_small(add_small(keep[size:, :], got[size:, :]))
        for out in outs:
            out[size // 2 :, :] = small


def simple(body, name, shapes, *args):
    return pl.pallas_call(
        body,
        out_shape=[jax.ShapeDtypeStruct(shape, kind) for shape, kind in shapes],
        grid_spec=pltpu.PrefetchScalarGridSpec(
            num_scalar_prefetch=1,
            grid=(1,),
            in_specs=[whole(a.shape) for a in args[1:]],
            out_specs=[whole(shape) for shape, _ in shapes],
        ),
        compiler_params=params(),
        cost_estimate=COST,
        name=name,
    )(*args)


def fold(meta, keep, got, extra):
    size, cols = keep.shape[0] - extra, keep.shape[1]
    shapes = [((size // 2 + extra, cols), BF16)] * 2
    return simple(lambda _, *refs: fold_kernel(extra, *refs), "fold", shapes, meta, keep, got)


def last_packet_kernel(meta, keep, got, up_ref, first, second):
    hid = up_ref.shape[1]
    up_ref[...] = keep[:, :hid].astype(F32) + got[:, :hid].astype(F32)
    low = (keep[:, hid:].astype(F32) + got[:, hid:].astype(F32)).astype(BF16)
    cut, side = hid // 2, D // 8
    even = jnp.concatenate([low[:, :cut], low[:, hid : hid + side]], axis=1)
    odd = jnp.concatenate([low[:, cut:hid], low[:, hid + side : hid + 2 * side]], axis=1)

    @pl.when(meta[1] % 2 == 0)
    def _():
        first[...] = even
        second[...] = odd

    @pl.when(meta[1] % 2 == 1)
    def _():
        first[...] = odd
        second[...] = even


def lower_kernel(meta, first, second, down_ref, out_ref):
    cut = down_ref.shape[0]
    size = first.shape[0]

    def store(ref, at):
        turned = ref[...].astype(F32).T
        down_ref[:, at : at + size] = turned[:cut]
        out_ref[:, at : at + size] = turned[cut:]

    @pl.when(meta[1] % 2 == 0)
    def _():
        store(first, 0)
        store(second, size)

    @pl.when(meta[1] % 2 == 1)
    def _():
        store(second, 0)
        store(first, size)


def last_qkv_kernel(meta, keep, got, kept, near, far, small):
    size = kept.shape[0]
    width = kept.shape[1]
    total = keep[0:size, :].astype(F32) + got[0:size, :].astype(F32)
    rows = add_small(keep[size:, :], got[size:, :])
    for part in range(3):
        small[part * 8 : part * 8 + 8, :] = rows[0:8, part * width : (part + 1) * width]
    small[24:32, :] = rows[8:16, 0:width]
    near[size:, :] = small[...]
    far[size:, :] = small[...]
    query = jnp.concatenate([total[:, 0:128], total[:, 256:320]], axis=1)
    keys = jnp.concatenate([total[:, 128:256], total[:, 320:384]], axis=1)
    values = total[:, 384:576]
    plans = (
        (query, keys, values),
        (keys, query, values),
        (keys, values, query),
        (values, keys, query),
    )
    for blk, plan in enumerate(plans):

        @pl.when(meta[0] == blk)
        def _(plan=plan):
            kept[...] = plan[0]
            near[0:size, :] = plan[1]
            far[0:size, :] = plan[2]


def assemble_kernel(
    meta, kept, small, near, far, diag,
    qkv, b_qkv, b_out, b_up, b_down, gain1, shift1, gain2, shift2, table,
):
    size, width = kept.shape

    @pl.when(meta[0] % 2 == 0)
    def _():
        qkv[:, 0:width] = kept[...]
        qkv[:, 2 * width :] = far[0:size, :]

    @pl.when(meta[0] % 2 == 1)
    def _():
        qkv[:, 0:width] = far[0:size, :]
        qkv[:, 2 * width :] = kept[...]

    qkv[:, width : 2 * width] = near[0:size, :]
    table[0] = small[...]
    table[1] = near[size:, :]
    table[2] = far[size:, :]
    table[3] = diag[...]
    total = table[0] + table[1] + table[2] + table[3]

    def vector(rows, index):
        parts = [rows[part * 8 + index : part * 8 + index + 1, :] for part in range(4)]
        return jnp.concatenate(parts, axis=1)

    for ref, index in ((gain1, 0), (shift1, 1), (gain2, 5), (shift2, 6), (b_out, 7), (b_down, 7)):
        ref[...] = vector(total, index).reshape(D)
    ups, parts = [], ([], [], [])
    for blk in range(4):
        rows = table[jnp.bitwise_xor(meta[0], blk)]
        ups.append(vector(rows, 4))
        joined = vector(rows, 2)
        parts[0].append(jnp.concatenate([joined[:, 0:128], joined[:, 256:320]], axis=1))
        parts[1].append(jnp.concatenate([joined[:, 128:256], joined[:, 320:384]], axis=1))
        parts[2].append(joined[:, 384:576])
    b_up[...] = jnp.concatenate(ups, axis=1).reshape(4 * D)
    b_qkv[...] = jnp.concatenate(parts[0] + parts[1] + parts[2], axis=1).reshape(3 * D)


def assemble(meta, kept, small, near, far, diag):
    size, width = kept.shape
    shapes = [((size, 3 * width), F32), ((3 * D,), F32), ((D,), F32), ((4 * D,), F32)]
    shapes += [((D,), F32)] * 5
    args = (kept, small, near, far, diag)
    return pl.pallas_call(
        assemble_kernel,
        out_shape=[jax.ShapeDtypeStruct(shape, kind) for shape, kind in shapes],
        grid_spec=pltpu.PrefetchScalarGridSpec(
            num_scalar_prefetch=1,
            grid=(1,),
            in_specs=[whole(a.shape) for a in args],
            out_specs=[whole(shape) for shape, _ in shapes],
            scratch_shapes=[pltpu.VMEM((4, 32, width), F32)],
        ),
        compiler_params=params(),
        cost_estimate=COST,
        name="assemble",
    )(meta, *args)


def fold_plain(keep, got, last):
    total = keep.astype(F32) + got.astype(F32)
    if last:
        return [total]
    half = total.shape[0] // 2
    return [total[:half].astype(BF16), total[half:].astype(BF16)]


def reduce_plain(keep, got, rows):
    mask = 2
    while mask < rows:
        keep, send = fold_plain(keep, got, False)
        got = swap(send, "rows", mask)
        mask *= 2
    return fold_plain(keep, got, True)[0]


def after(value, *others):
    return lax.optimization_barrier((value, others))[0]


def swap(value, axis, mask):
    size = lax.axis_size(axis)
    return lax.ppermute(value, axis, [(i, i ^ mask) for i in range(size)])


def add_low(left, right):
    return (left.astype(F32) + right.astype(F32)).astype(BF16)


def spread_rows(lower):
    rows, blk = lax.axis_size("rows"), lax.axis_size("blk")
    r = lax.axis_index("rows")
    count = rows // blk
    hid, width = FF // 4, D // 4
    chunk = lower.shape[0]
    down = lower[:, :hid].reshape(chunk, count, hid // count)
    out = lower[:, hid:].reshape(chunk, count, width // count)
    pieces = jnp.concatenate([down, out], axis=2).astype(BF16)
    got = []
    for turn in range(count):
        moves = spread_moves(rows, blk, turn)
        piece = lax.dynamic_index_in_dim(pieces, (r % count) ^ turn, 1, keepdims=False)
        got.append(lax.ppermute(piece, ("rows", "blk"), moves))
    got = jnp.stack(got)
    parts = [
        lax.dynamic_index_in_dim(got, (r % count) ^ part, 0, keepdims=False)
        for part in range(count)
    ]
    whole_cols = jnp.concatenate(parts, axis=0).astype(F32).T
    cut = hid // count
    return whole_cols[:cut], whole_cols[cut:]


def spread_moves(rows, blk, turn):
    count = rows // blk
    moves = []
    for r in range(rows):
        for b in range(blk):
            to = count * b + ((r % count) ^ turn)
            moves.append((r * blk + b, to * blk + r // count))
    return moves


def split_columns(chunk):
    b = lax.axis_index("blk")
    q = jnp.concatenate([chunk[:, 0:128], chunk[:, 256:320]], axis=1)
    k = jnp.concatenate([chunk[:, 128:256], chunk[:, 320:384]], axis=1)
    v = chunk[:, 384:576]

    def choose(zero, one, two, three):
        return jnp.where(b < 2, jnp.where(b == 0, zero, one), jnp.where(b == 2, two, three))

    return choose(q, k, k, v), choose(k, q, v, k), choose(v, v, q, q)


def result_kernel(x_ref, even, near, far, b_out, b_down, out_ref):
    bias = row(b_out) + row(b_down)
    total = even[0].astype(F32) + near[0].astype(F32) + far[...].astype(F32)
    out_ref[...] = (x_ref[...].astype(F32) + bias + total).astype(BF16)


def token_kernel(x_ref, even, near, far, c_ref, out_ref):
    wide = x_ref[...].astype(F32)
    center = wide - jnp.mean(wide, axis=-1, keepdims=True)
    rate = lax.rsqrt(jnp.mean(center * center, axis=-1, keepdims=True) + EPS)
    normed = center * rate
    grad = even[0].astype(F32) + near[0].astype(F32) + far[...].astype(F32)
    mean = jnp.mean(grad, axis=-1, keepdims=True)
    along = jnp.mean(grad * normed, axis=-1, keepdims=True)
    back = rate * (grad - mean - normed * along)
    out_ref[...] = (c_ref[...].astype(F32) + back).astype(BF16)


def finish(body, name, seq, x, even, near, far, *more):
    flat = pl.BlockSpec((TILE, D), lambda i: (i, 0))
    own = pl.BlockSpec((1, TILE, D), lambda i: (0, i, 0))
    return pl.pallas_call(
        body,
        out_shape=jax.ShapeDtypeStruct((seq, D), BF16),
        grid=(seq // TILE,),
        in_specs=[flat, own, own, flat, *(flat if a.ndim == 2 else whole(a.shape) for a in more)],
        out_specs=flat,
        compiler_params=params(),
        cost_estimate=COST,
        name=name,
    )(x, even, near, far, *more)


def local(
    tokens, seg_ids, valid_len, ln1_gain, ln1_bias, w_qkv, b_qkv, w_out, b_out,
    ln2_gain, ln2_bias, w_up, b_up, w_down, b_down, cotangent,
):
    rows = lax.axis_size("rows")
    blk = lax.axis_index("blk")
    seq = tokens.shape[1]
    per = seq // TILE
    width = D // 4
    hid = FF // 4
    low, high = angle_parts(4 * seq)
    seg_row = jnp.pad(seg_ids.astype(BF16), ((0, EXTRA - 1), (0, D - seq)))
    tok_own = jnp.concatenate([tokens[0], seg_row], axis=0)
    cot_own = cotangent[0]

    cot_near = swap(cot_own, "blk", 1)
    tok_far = swap(tok_own, "blk", 2)
    tok_near = swap(tok_own, "blk", 1)
    cot_far = swap(after(cot_own, tok_near), "blk", 2)

    meta = jnp.stack([blk, lax.axis_index("rows")]).astype(jnp.int32)
    mlp_args = (ln2_gain, ln2_bias, b_up, w_up, w_down, w_out, rows, seq)
    joined = (ln1_gain, ln1_bias, w_qkv, b_qkv, low, high)
    *first, query, keys, values, w_own, b_own = feed_forward(
        meta, (tok_own, tok_near), (cot_own, cot_near), *mlp_args, joined
    )
    meta = after(meta, b_own)

    def more(slot, m, tok, filled):
        return project(slot, m, tok, ln1_gain, ln1_bias, low, high, w_own, b_own, filled, seq)

    tok_last = swap(after(tok_far, b_own), "blk", 1)
    joined = more(2, meta, tok_far, (query, keys, values))
    toks = (tok_own, tok_near, tok_far, tok_last)
    query, keys, values = more(3, after(meta, joined[0]), tok_last, joined)
    starts, lo, hi = segment_starts(after(meta, query), valid_len, toks, seq)
    cot_last = swap(after(cot_far, lo), "blk", 1)
    cots = (cot_own, cot_near, cot_far, cot_last)
    attn, lse = attend(meta, lo, hi, query, keys, values, starts, per)

    meta = after(meta, lse)
    e_far, grad_vec, mlp_sums, out_even, out_odd, keep, send = feed_forward(
        meta, toks[2:], cots[2:], *mlp_args, before=first, near=cots[:2], attn=attn
    )
    e_mlp = (first[1], e_far)
    keep, send = chunks_of(keep, send, rows)
    out_got = swap(out_odd, "blk", 1)
    got = swap(send, "rows", 1)

    meta = after(meta, mlp_sums)
    grad_joined = attend_back(
        meta, lo, hi, query, keys, values, attn, grad_vec, starts, lse, low, high, per
    )

    out_send = add_low(after(out_even, grad_joined)[1], out_got[1])
    out_far = swap(out_send, "blk", 2)
    joined_args = (grad_joined, e_mlp, toks, ln1_gain, ln1_bias, w_own, rows, seq)
    meta = after(meta, out_send)
    e_odd, *carried = joined_back(meta, (1, 3), *joined_args)
    e_got = swap(e_odd, "blk", 1)
    meta = after(meta, carried[1])
    if fits(rows):
        keep, send = fold(meta, keep, got, 0)
        got = swap(send, "rows", 2)
        meta = after(meta, send)
    e_even, qkv_keep, qkv_send, *rest = joined_back(
        meta, (0, 2), *joined_args, carried, mlp_sums
    )
    qkv_keep, qkv_send = chunks_of(qkv_keep, qkv_send, rows)
    qkv_got = swap(qkv_send, "rows", 1)
    e_send = add_low(e_even[1], e_got[1])
    e_far = swap(e_send, "blk", 2)

    out_args = (after(tok_own, e_send), out_even, out_got, out_far, b_out, b_down)
    result = finish(result_kernel, "result", seq, *out_args)
    if fits(rows):
        meta = after(meta, result)
        keep, send = fold(meta, keep, got, 0)
        got = swap(send, "rows", 4)
        meta = after(meta, send)
        qkv_keep, qkv_send = fold(meta, qkv_keep, qkv_got, SMALL)
        qkv_got = swap(qkv_send, "rows", 2)
        tok_args = (after(tok_own, qkv_send), e_even, e_got, e_far, cot_own)
        grad_tokens = finish(token_kernel, "token_grad", seq, *tok_args)
        meta = after(meta, grad_tokens)
        qkv_keep, qkv_send = fold(meta, qkv_keep, qkv_got, SMALL)
        qkv_got = swap(qkv_send, "rows", 4)
        meta = after(meta, qkv_send)
        chunk = D // rows
        part = ((chunk, hid // 2 + width // 2), BF16)
        up, *pieces = simple(
            last_packet_kernel, "last_packet", [((chunk, hid), F32), part, part], meta, keep, got
        )
        pieces = [
            lax.ppermute(piece, ("rows", "blk"), spread_moves(rows, 4, turn))
            for turn, piece in enumerate(pieces)
        ]
        meta = after(meta, up)
        packet = ((chunk + 32, width), F32)
        kept, near, far, small = simple(
            last_qkv_kernel,
            "last_qkv",
            [((chunk, width), F32), packet, packet, ((32, width), F32)],
            meta,
            qkv_keep,
            qkv_got,
        )
        near, far, diag = swap(near, "blk", 1), swap(far, "blk", 2), swap(small, "blk", 3)
        lower = [((hid // 2, width), F32), ((width // 2, width), F32)]
        down, out_w = simple(lower_kernel, "lower", lower, meta, *pieces)
        meta = after(meta, down)
        qkv, gb_qkv, gb_out, gb_up, gb_down, *norms = assemble(
            meta, kept, small, near, far, diag
        )
    else:
        weights = reduce_plain(keep, got, rows)
        qkv = reduce_plain(qkv_keep, qkv_got, rows)
        up = weights[:, :hid]
        down, out_w = spread_rows(weights[:, hid : 2 * hid + width])
        kept, near, far = split_columns(qkv)
        near, far = swap(near, "blk", 1), swap(far, "blk", 2)
        ends = [jnp.where(blk % 2 == 0, a, b) for a, b in ((kept, far), (far, kept))]
        qkv = jnp.concatenate([ends[0], near, ends[1]], axis=1)
        tok_args = (tok_own, e_even, e_got, e_far, cot_own)
        grad_tokens = finish(token_kernel, "token_grad", seq, *tok_args)
        bias, sums = rest
        mine = (jnp.arange(4) == blk)[:, None]
        joined = lax.psum(jnp.where(mine, bias[0:1], 0.0), ("rows", "blk"))
        gb_up = lax.psum(jnp.where(mine, mlp_sums[0:1], 0.0), ("rows", "blk")).reshape(FF)
        gb_qkv = jnp.concatenate(
            [
                jnp.concatenate([joined[:, 0:128], joined[:, 256:320]], axis=1).reshape(D),
                jnp.concatenate([joined[:, 128:256], joined[:, 320:384]], axis=1).reshape(D),
                joined[:, 384:576].reshape(D),
            ]
        )
        sums = jnp.concatenate([sums[0:2], mlp_sums[1:4]])
        *norms, gb_out = lax.psum(sums, ("rows", "blk"))
        gb_down = gb_out
    return (
        result[None],
        grad_tokens[None],
        qkv,
        out_w,
        up,
        down,
        gb_qkv,
        gb_out,
        gb_up,
        gb_down,
        *norms,
    )


def solution(mesh):
    split = P("rows", "blk")
    in_specs = (
        P("rows", "blk", None),
        split,
        P("rows"),
        *(P(),) * 12,
        P("rows", "blk", None),
    )
    out_specs = (
        P("rows", "blk", None),
        P("rows", "blk", None),
        *(split,) * 4,
        *(P(),) * 8,
    )
    return jax.shard_map(local, mesh=mesh, in_specs=in_specs, out_specs=out_specs, check_vma=False)
```

```python
import math
from functools import partial

import jax
import jax.numpy as jnp
import numpy as np
from jax import lax
from jax.experimental import pallas as pl
from jax.experimental.pallas import tpu as pltpu
from jax.sharding import PartitionSpec as P

D = 768
HEADS = 12
HDIM = 64
ROT = 16
FF = 3072
EPS = 1e-05
MASKED = -1e30
TILE = 256
VROWS = 80
LN2 = math.log(2.0)
EXTRA = 16
LANES = 128
F32 = jnp.float32
BF16 = jnp.bfloat16
COST = pl.CostEstimate(flops=0, bytes_accessed=0, transcendentals=0)
NT_DIMS = (((1,), (1,)), ((), ()))
TN_DIMS = (((0,), (0,)), ((), ()))


def dot(left, right):
    return jnp.dot(left, right, preferred_element_type=F32)


def dot_nt(left, right):
    return lax.dot_general(left, right, NT_DIMS, preferred_element_type=F32)


def dot_tn(left, right):
    return lax.dot_general(left, right, TN_DIMS, preferred_element_type=F32)


def normalize(value):
    center = value - jnp.mean(value, axis=-1, keepdims=True)
    spread = jnp.mean(center * center, axis=-1, keepdims=True)
    return center * lax.rsqrt(spread + EPS)


def angle_parts(length):
    dim = np.arange(LANES) % HDIM
    inverse = np.where(dim < ROT, 10000.0 ** (-2.0 * (dim % (ROT // 2)) / ROT), 0.0)
    high = (np.arange(length // LANES) * LANES)[:, None] * inverse
    low = np.arange(LANES)[:, None] * inverse
    parts = np.stack([np.cos(low), np.sin(low)]), np.stack([np.cos(high), np.sin(high)])
    return tuple(jnp.asarray(part, F32) for part in parts)


def rotation(low_ref, high_ref, tile):
    lane = lax.broadcasted_iota(jnp.int32, (1, LANES), 1) % HDIM
    sign = jnp.where(lane < ROT // 2, -1.0, 1.0)
    cos_rows, sin_rows = [], []
    for part in range(TILE // LANES):
        row = tile * (TILE // LANES) + part
        cos_high = high_ref[0, pl.ds(row, 1), :]
        sin_high = high_ref[1, pl.ds(row, 1), :]
        cos_rows.append(low_ref[0] * cos_high - low_ref[1] * sin_high)
        sin_rows.append((low_ref[1] * cos_high + low_ref[0] * sin_high) * sign)
    return jnp.concatenate(cos_rows, axis=0), jnp.concatenate(sin_rows, axis=0)


def swap_halves(value):
    lane = lax.broadcasted_iota(jnp.int32, value.shape, 1) % HDIM
    half = ROT // 2
    return jnp.where(
        lane < half, pltpu.roll(value, LANES - half, 1), pltpu.roll(value, half, 1)
    )


def true_block(meta_ref, slot):
    return jnp.bitwise_xor(meta_ref[0], slot)


def params(*semantics, vmem=None):
    return pltpu.CompilerParams(
        dimension_semantics=semantics or ("arbitrary",), vmem_limit_bytes=vmem or 60 * 2**20
    )


def whole(shape):
    return pl.BlockSpec(shape, lambda *_: (0,) * len(shape))


def own_blocks(refs, odd, into):
    places = ((0, 256), (128, 320), (384, 512))
    for part, (pair_at, third_at) in enumerate(places):
        left, right = refs[2 * part], refs[2 * part + 1]

        @pl.when(odd == 0)
        def _(left=left, right=right, pair_at=pair_at, third_at=third_at):
            into[:, pair_at : pair_at + 128] = left[...]
            into[:, third_at : third_at + 64] = right[:, 0:64]

        @pl.when(odd == 1)
        def _(left=left, right=right, pair_at=pair_at, third_at=third_at):
            into[:, pair_at : pair_at + 128] = jnp.concatenate(
                [left[:, 64:128], right[:, 0:64]], axis=1
            )
            into[:, third_at : third_at + 64] = right[:, 64:128]


def row(ref):
    return ref[...].reshape(1, ref.shape[0])


def own_bias(b_ref, odd, blk, into):
    blocks = []
    for part in range(3):
        for side in range(2):
            at = pl.multiple_of((part * (D // LANES) + side + 3 * blk // 2) * LANES, LANES)
            blocks.append(b_ref[pl.ds(at, LANES)].reshape(1, LANES))
    own_blocks(blocks, odd, into)


def project_tile(normed, gain, shift, w_ref, b_ref, low, high, tile, q_ref, k_ref, v_ref):
    attn_in = (normed * row(gain) + row(shift)).astype(BF16)
    joined = dot(attn_in, w_ref[...]) + b_ref[...]
    cos, sin = rotation(low, high, tile)
    scale = HDIM**-0.5 / LN2

    def turn(block):
        return block * cos + swap_halves(block) * sin

    query = turn(joined[:, 0:128]) * scale
    keys = turn(joined[:, 128:256])
    mixed = turn(joined[:, 256:384])
    q_ref[:, 0:128] = query.astype(BF16)
    k_ref[:, 0:128] = keys.astype(BF16)
    q_ref[:, 128:192] = (mixed[:, 0:64] * scale).astype(BF16)
    k_ref[:, 128:192] = mixed[:, 64:128].astype(BF16)
    v_ref[...] = joined[:, 384:576].astype(BF16)


def qkv_kernel(slot, meta, x_ref, gain, shift, low, high, w_ref, b_ref, *refs):
    per = pl.num_programs(0)
    tile = true_block(meta, slot) * per + pl.program_id(0)
    normed = normalize(x_ref[...].astype(F32))
    project_tile(normed, gain, shift, w_ref, b_ref, low, high, tile, *refs[-3:])


def project(slot, meta, x, gain, shift, low, high, w, b, filled, seq):
    width = D // 4
    per = seq // TILE
    out = jax.ShapeDtypeStruct((4 * seq, width), BF16)
    out_spec = pl.BlockSpec((TILE, width), lambda i, m: (slot * per + i, 0))
    args = [x, gain, shift, low, high, w, b, *filled]
    specs = [pl.BlockSpec((TILE, D), lambda i, m: (i, 0))]
    specs += [whole(a.shape) for a in args[1:7]]
    specs += [pl.BlockSpec(memory_space=pl.ANY)] * 3
    return pl.pallas_call(
        partial(qkv_kernel, slot),
        out_shape=[out] * 3,
        grid_spec=pltpu.PrefetchScalarGridSpec(
            num_scalar_prefetch=1, grid=(per,), in_specs=specs, out_specs=[out_spec] * 3
        ),
        input_output_aliases={8 + i: i for i in range(3)},
        compiler_params=params(),
        cost_estimate=COST,
        name=f"qkv_{slot}",
    )(meta, *args)


def starts_kernel(seq, meta, valid, s0, s1, s2, s3, start_ref, lo_ref, hi_ref):
    segs = [ref[0:1, 0:seq].astype(F32) for ref in (s0, s1, s2, s3)]
    below = [
        sum(jnp.sum((seg < number).astype(F32), axis=1, keepdims=True) for seg in segs)
        for number in (1, 2, 3)
    ]
    per = seq // TILE
    iota = lax.broadcasted_iota(jnp.int32, (1, seq), 1)
    for slot, seg in enumerate(segs):
        block = true_block(meta, slot)
        begin = jnp.zeros((1, seq), F32)
        for number in (1, 2, 3):
            begin = jnp.where(seg == number, below[number - 1], begin)
        pos = iota + block * seq
        begin = jnp.where(pos < valid[0], begin.astype(jnp.int32), pos)
        for part in range(per):
            tile = begin[:, part * TILE : (part + 1) * TILE]
            start_ref[slot * per + part] = tile
            lo_ref[block * per + part] = jnp.min(tile) // TILE
            hi_ref[block * per + part] = (jnp.max(tile) + (TILE - 1)) // TILE


def segment_starts(meta, valid_len, toks, seq):
    tiles = 4 * seq // TILE
    smem = pl.BlockSpec(memory_space=pltpu.SMEM)
    return pl.pallas_call(
        partial(starts_kernel, seq),
        out_shape=[
            jax.ShapeDtypeStruct((tiles, 1, TILE), jnp.int32),
            jax.ShapeDtypeStruct((tiles,), jnp.int32),
            jax.ShapeDtypeStruct((tiles,), jnp.int32),
        ],
        grid_spec=pltpu.PrefetchScalarGridSpec(
            num_scalar_prefetch=2,
            grid=(1,),
            in_specs=[pl.BlockSpec((EXTRA, D), lambda i, m, v: (seq // EXTRA, 0))] * 4,
            out_specs=[whole((tiles, 1, TILE)), smem, smem],
        ),
        compiler_params=params(),
        cost_estimate=COST,
        name="segment_starts",
    )(meta, valid_len, *toks)


def places(rows):
    order = [0]
    while len(order) < rows:
        order = [2 * i for i in order] + [2 * i + 1 for i in order]
    return order


def fits(rows):
    return rows == 8 and D // rows % 32 == 0


def store_chunks(grad, keep, send, meta, rows):
    size = grad.shape[0] // rows
    for index, place in enumerate(places(rows)):
        at = pl.multiple_of(jnp.bitwise_xor(meta[1], place) * size, 32)
        into = keep if index < rows // 2 else send
        row = index % (rows // 2) * size
        into[row : row + size, :] = grad[pl.ds(at, size), :].astype(into.dtype)


def chunk_shapes(cols, rows, extra=0):
    if fits(rows):
        return [(D // 2 + extra, cols)] * 2
    return [(D, cols), (8, LANES)]


def chunks_of(keep, send, rows):
    if fits(rows):
        return keep, send
    order = jnp.array(places(rows)) ^ lax.axis_index("rows")
    parts = keep.reshape(rows, D // rows, keep.shape[1])
    parts = jnp.take(parts, order, axis=0).reshape(keep.shape)
    return parts[: D // 2], parts[D // 2 :]


def feed(normed, upstream, gain, shift, w_up, b_up, w_down):
    mlp_in = (normed * row(gain) + row(shift)).astype(BF16)
    hidden = dot(mlp_in, w_up[...]) + b_up
    cdf = 0.5 * (1.0 + lax.erf(hidden * (0.5**0.5)))
    act = (hidden * cdf).astype(BF16)
    slope = cdf + hidden * jnp.exp(-0.5 * hidden * hidden) * ((2.0 * math.pi) ** -0.5)
    grad_low = (slope * dot_nt(upstream, w_down[...])).astype(BF16)
    grad_norm = dot_nt(grad_low, w_up[...])
    return mlp_in, act, grad_low, grad_norm


def add_sums(sums, grad_low, grad_norm, normed):
    sums[0:1, :] += jnp.sum(grad_low.astype(F32), axis=0, keepdims=True)
    sums[1:2, :] += jnp.sum(grad_norm * normed, axis=0, keepdims=True)
    sums[2:3, :] += jnp.sum(grad_norm, axis=0, keepdims=True)


def own_row(ref, blk, size):
    return ref[pl.ds(pl.multiple_of(blk * size, LANES), size)].reshape(1, size)


def mlp_first_kernel(
    half, meta, xa, xb, ca, cb, gain, shift, b_up, w_up, w_down, w_out,
    gain1, shift1, b_qkv, low, high, w0, w1, w2, w3, w4, w5,
    mo_ref, e_ref, gv_ref, sums, gup, gdown, q_ref, k_ref, v_ref, w_own, b_own, x_s, c_s,
):
    step = pl.program_id(0)

    @pl.when(step < half)
    def _():
        x_s[...] = xa[...]
        c_s[...] = ca[...]

    @pl.when(step >= half)
    def _():
        x_s[...] = xb[...]
        c_s[...] = cb[...]

    @pl.when(step == 0)
    def _():
        sums[...] = jnp.zeros_like(sums)
        gup[...] = jnp.zeros_like(gup)
        gdown[...] = jnp.zeros_like(gdown)
        odd = meta[0] % 2
        own_blocks((w0, w1, w2, w3, w4, w5), odd, w_own)
        own_bias(b_qkv, odd, meta[0], b_own)

    upstream = c_s[...]

    @pl.when(step < half)
    def _():
        sums[3:4, :] += jnp.sum(upstream.astype(F32), axis=0, keepdims=True)

    normed = normalize(x_s[...].astype(F32))
    tile = true_block(meta, step // half) * half + step % half
    project_tile(normed, gain1, shift1, w_own, b_own, low, high, tile, q_ref, k_ref, v_ref)
    bias = own_row(b_up, meta[0], gup.shape[1])
    mlp_in, act, grad_low, grad_norm = feed(normed, upstream, gain, shift, w_up, bias, w_down)
    mo_ref[...] = dot(act, w_down[...]).astype(BF16)
    add_sums(sums, grad_low, grad_norm, normed)
    e_ref[...] = (grad_norm * row(gain)).astype(BF16)
    gv_ref[...] = dot_nt(upstream, w_out[...]).astype(BF16)
    gup[...] += dot_tn(mlp_in, grad_low)
    gdown[...] += dot_tn(upstream, act)


def mlp_second_kernel(
    half, rows, meta, xa, xb, ca, cb, gain, shift, b_up, w_up, w_down, w_out,
    c0, c1, mo_in, o_near, o_far, sums_in, gup, gdown, _,
    e_ref, gv_ref, sums, even, odd, keep, send, x_s, c_s, n_s, grad,
):
    step = pl.program_id(0)
    hid = gup.shape[1]

    @pl.when(step < half)
    def _():
        x_s[...] = xa[...]
        c_s[...] = ca[...]
        n_s[...] = c0[...]

    @pl.when(step >= half)
    def _():
        x_s[...] = xb[...]
        c_s[...] = cb[...]
        n_s[...] = c1[...]

    @pl.when(step == 0)
    def _():
        sums[...] = sums_in[...]
        grad[:, 0:hid] = gup[...]
        grad[:, hid : 2 * hid] = gdown[...]
        grad[:, 2 * hid :] = jnp.zeros_like(grad[:, 2 * hid :])

    upstream = c_s[...]
    normed = normalize(x_s[...].astype(F32))
    bias = own_row(b_up, meta[0], hid)
    mlp_in, act, grad_low, grad_norm = feed(normed, upstream, gain, shift, w_up, bias, w_down)
    add_sums(sums, grad_low, grad_norm, normed)
    e_ref[...] = (grad_norm * row(gain)).astype(BF16)
    gv_ref[...] = dot_nt(upstream, w_out[...]).astype(BF16)
    grad[:, 0:hid] += dot_tn(mlp_in, grad_low)
    grad[:, hid : 2 * hid] += dot_tn(upstream, act)
    grad[:, 2 * hid : 2 * hid + D // 4] += dot_tn(upstream, o_far[...]) + dot_tn(
        n_s[...], o_near[...]
    )
    far = (dot(act, w_down[...]) + dot(o_far[...], w_out[...])).astype(BF16)
    near = (mo_in[...].astype(F32) + dot(o_near[...], w_out[...])).astype(BF16)

    @pl.when(step < half)
    def _():
        even[0] = near
        even[1] = far

    @pl.when(step >= half)
    def _():
        odd[0] = near
        odd[1] = far

    @pl.when(step == pl.num_programs(0) - 1)
    def _():
        if fits(rows):
            store_chunks(grad, keep, send, meta, rows)
        else:
            keep[...] = grad[...].astype(BF16)


def feed_forward(
    meta, xs, cs, gain, shift, b_up, w_up, w_down, w_out, rows, seq,
    joined=None, before=None, near=None, attn=None,
):
    per = seq // TILE
    steps = 2 * per
    hid = FF // 4
    width = D // 4
    total = 4 * seq
    first = pl.BlockSpec((TILE, D), lambda i, m: (jnp.minimum(i, per - 1), 0))
    second = pl.BlockSpec((TILE, D), lambda i, m: (jnp.maximum(i - per, 0), 0))
    specs = [
        first,
        second,
        first,
        second,
        whole((D,)),
        whole((D,)),
        whole((FF,)),
        pl.BlockSpec((D, hid), lambda i, m: (0, m[0])),
        pl.BlockSpec((hid, D), lambda i, m: (m[0], 0)),
        pl.BlockSpec((width, D), lambda i, m: (m[0], 0)),
    ]
    args = [*xs, *cs, gain, shift, b_up, w_up, w_down, w_out]
    tile = pl.BlockSpec((TILE, D), lambda i, m: (i, 0))
    narrow = pl.BlockSpec((TILE, width), lambda i, m: (i, 0))
    sums = (8, D)
    scratch = [pltpu.VMEM((TILE, D), BF16), pltpu.VMEM((TILE, D), BF16)]
    pair = jax.ShapeDtypeStruct((steps * TILE, D), BF16)
    vec = jax.ShapeDtypeStruct((total, width), BF16)
    if before is None:
        body = partial(mlp_first_kernel, per)
        gain1, shift1, w_qkv, b_qkv, low, high = joined
        args += [gain1, shift1, b_qkv, low, high]
        specs += [whole(a.shape) for a in args[-5:]]
        for part in range(3):
            for side in range(2):
                specs.append(
                    pl.BlockSpec(
                        (D, LANES),
                        lambda i, m, at=part * D // LANES + side: (0, at + 3 * m[0] // 2),
                    )
                )
                args.append(w_qkv)
        outs = [pair, pair, vec, jax.ShapeDtypeStruct(sums, F32)]
        outs += [jax.ShapeDtypeStruct((D, hid), F32)] * 2 + [vec] * 3
        outs += [
            jax.ShapeDtypeStruct((D, 3 * width), BF16),
            jax.ShapeDtypeStruct((1, 3 * width), F32),
        ]
        out_specs = [tile, tile, narrow, whole(sums)]
        out_specs += [whole((D, hid))] * 2 + [narrow] * 3
        out_specs += [whole((D, 3 * width)), whole((1, 3 * width))]
        aliases = {}
    else:
        body = partial(mlp_second_kernel, per, rows)
        mlp_out, _, grad_vec, sums_in, gup, gdown = before
        chunks = chunk_shapes(2 * hid + 2 * LANES, rows)
        args += [*near, mlp_out, attn, attn, sums_in, gup, gdown, grad_vec]
        specs += [
            first,
            second,
            tile,
            narrow,
            pl.BlockSpec((TILE, width), lambda i, m: (i + steps, 0)),
            whole(sums),
            whole((D, hid)),
            whole((D, hid)),
            pl.BlockSpec(memory_space=pl.ANY),
        ]
        aliases = {len(args): 1}
        both = jax.ShapeDtypeStruct((2, seq, D), BF16)
        outs = [pair, vec, jax.ShapeDtypeStruct(sums, F32), both, both]
        outs += [jax.ShapeDtypeStruct(shape, BF16) for shape in chunks]
        out_specs = [
            tile,
            pl.BlockSpec((TILE, width), lambda i, m: (i + steps, 0)),
            whole(sums),
            pl.BlockSpec((2, TILE, D), lambda i, m: (0, jnp.minimum(i, per - 1), 0)),
            pl.BlockSpec((2, TILE, D), lambda i, m: (0, jnp.maximum(i - per, 0), 0)),
            *(whole(shape) for shape in chunks),
        ]
        scratch += [pltpu.VMEM((TILE, D), BF16), pltpu.VMEM((D, 2 * hid + 2 * LANES), F32)]
    return pl.pallas_call(
        body,
        out_shape=outs,
        grid_spec=pltpu.PrefetchScalarGridSpec(
            num_scalar_prefetch=1,
            grid=(steps,),
            in_specs=specs,
            out_specs=out_specs,
            scratch_shapes=scratch,
        ),
        input_output_aliases=aliases,
        compiler_params=params(),
        cost_estimate=COST,
        name="mlp_first" if before is None else "mlp_second",
    )(meta, *args)


def head_masks():
    lane = lax.broadcasted_iota(jnp.int32, (1, LANES), 1)
    first = jnp.where(lane < HDIM, 1.0, 0.0).astype(BF16)
    second = jnp.where(lane < HDIM, 0.0, 1.0).astype(BF16)
    return first, second


def slot_rows(meta, per, tile):
    slot = jnp.bitwise_xor(tile // per, meta[0])
    return pl.multiple_of((slot * per + tile % per) * TILE, TILE)


def by_head(first, second, block, third):
    return (block * first, block * second, third)


def transpose_all(from_ref, to_ref):
    @pl.loop(0, from_ref.shape[0] // TILE)
    def _(tile):
        rows = pl.ds(pl.multiple_of(tile * TILE, TILE), TILE)
        to_ref[:, rows] = from_ref[rows, :].astype(F32).T.astype(BF16)


def attend_kernel(per, meta, lo, hi, q_ref, k_ref, v_ref, start_ref, o_ref, lse_ref, vt_ref, acc, s_ref):
    mask0, mask1 = head_masks()
    tiles = k_ref.shape[0] // TILE
    qi = pl.program_id(0)

    @pl.when(qi == 0)
    def _():
        ones = jnp.where(lax.broadcasted_iota(jnp.int32, (VROWS - HDIM, TILE), 0) == 0, 1.0, 0.0)

        @pl.loop(0, tiles)
        def _(tile):
            rows = pl.ds(pl.multiple_of(tile * TILE, TILE), TILE)
            block = v_ref[rows, :].astype(F32).T
            for head in range(3):
                at = head * VROWS
                vt_ref[at : at + HDIM, rows] = block[head * HDIM : (head + 1) * HDIM].astype(BF16)
                vt_ref[at + HDIM : at + VROWS, rows] = ones.astype(BF16)

    key_iota = lax.broadcasted_iota(jnp.int32, (TILE, TILE), 0)
    query_iota = lax.broadcasted_iota(jnp.int32, (TILE, TILE), 1)
    queries = by_head(mask0, mask1, q_ref[:, 0:128], q_ref[:, 128:192])
    starts = start_ref[0]
    acc[...] = jnp.zeros_like(acc)

    def key_tile(turn):
        return jnp.where(turn == 0, qi, first + turn - 1)

    def score(masked, ki):
        k_rows = pl.ds(slot_rows(meta, per, ki), TILE)
        pair, third = k_ref[k_rows, 0:128], k_ref[k_rows, 128:192]
        scores = [dot_nt(third if head == 2 else pair, queries[head]) for head in range(3)]
        if masked:
            allowed = (key_iota >= starts - ki * TILE) & (key_iota <= query_iota + (qi - ki) * TILE)
            scores = [jnp.where(allowed, x, MASKED) for x in scores]
        return scores, [jnp.max(x, axis=0, keepdims=True) for x in scores]

    def value(ki, tops, peaks):
        k_rows = pl.ds(slot_rows(meta, per, ki), TILE)
        news = [jnp.maximum(top, peak) for top, peak in zip(tops, peaks)]
        fades = [jnp.exp2(top - new) for top, new in zip(tops, news)]
        weights = [jnp.exp2(s_ref[head] - news[head]).astype(BF16) for head in range(3)]
        terms = [
            dot(vt_ref[head * VROWS : (head + 1) * VROWS, k_rows], weights[head]) for head in range(3)
        ]
        return news, fades, terms

    def put(fades, terms):
        for head in range(3):
            cols = slice(head * VROWS, (head + 1) * VROWS)
            acc[cols, :] = acc[cols, :] * fades[head] + terms[head]

    def visit(masked, turn, carry):
        tops, peaks = carry
        scores, next_peaks = score(masked, key_tile(turn + 1))
        news, fades, terms = value(key_tile(turn), tops, peaks)
        peaks = next_peaks
        for head in range(3):
            s_ref[head] = scores[head]
        put(fades, terms)
        return tuple(news), tuple(peaks)

    first = lo[qi]
    full = jnp.minimum(hi[qi], qi)
    scores, peaks = score(True, qi)
    for head in range(3):
        s_ref[head] = scores[head]
    carry = ((jnp.full((1, TILE), MASKED, F32),) * 3, tuple(peaks))
    carry = lax.fori_loop(0, full - first, partial(visit, True), carry)
    carry = lax.fori_loop(full - first, qi - first, partial(visit, False), carry)
    tops, fades, terms = value(key_tile(qi - first), *carry)
    put(fades, terms)
    heads = []
    for head, top in enumerate(tops):
        at = head * VROWS
        total = acc[at + HDIM : at + HDIM + 1, :]
        heads.append(acc[at : at + HDIM, :] / total)
        lse_ref[head, 0] = top + jnp.log2(total)
    o_ref[...] = jnp.concatenate(heads, axis=0).T.astype(BF16)

def attend(meta, lo, hi, query, keys, values, starts, per):
    total, width = query.shape
    tiles = total // TILE
    def slot(i, m):
        return jnp.bitwise_xor(i // per, m[0]) * per + i % per
    q_spec = pl.BlockSpec((TILE, width), lambda i, m, lo, hi: (slot(i, m), 0))
    start_spec = pl.BlockSpec((1, 1, TILE), lambda i, m, lo, hi: (slot(i, m), 0, 0))
    lse_spec = pl.BlockSpec((3, 1, 1, TILE), lambda i, m, lo, hi: (0, slot(i, m), 0, 0))
    return pl.pallas_call(
        partial(attend_kernel, per),
        out_shape=[
            jax.ShapeDtypeStruct((total, width), BF16),
            jax.ShapeDtypeStruct((3, tiles, 1, TILE), F32),
        ],
        grid_spec=pltpu.PrefetchScalarGridSpec(
            num_scalar_prefetch=3,
            grid=(tiles,),
            in_specs=[q_spec, whole(keys.shape), whole(values.shape), start_spec],
            out_specs=[q_spec, lse_spec],
            scratch_shapes=[pltpu.VMEM((3 * VROWS, total), BF16), pltpu.VMEM((3 * VROWS, TILE), F32), pltpu.VMEM((3, TILE, TILE), F32)],
        ),
        compiler_params=params(),
        cost_estimate=COST,
        name="attend",
    )(meta, lo, hi, query, keys, values, starts)


def attend_back_kernel(
    per, meta, lo, hi, q_ref, k_ref, v_ref, o_ref, gv_ref, start_ref, lse_ref, low, high,
    gj_ref, kt_ref, dk_ref, dv_ref, dqt_ref
):
    mask0, mask1 = head_masks()
    tiles = k_ref.shape[0] // TILE
    qi = tiles - 1 - pl.program_id(0)

    @pl.when(pl.program_id(0) == 0)
    def _():
        transpose_all(k_ref, kt_ref)

    own_rows = pl.ds(slot_rows(meta, per, qi), TILE)
    key_iota = lax.broadcasted_iota(jnp.int32, (TILE, TILE), 0)
    query_iota = lax.broadcasted_iota(jnp.int32, (TILE, TILE), 1)
    queries = by_head(mask0, mask1, q_ref[:, 0:128], q_ref[:, 128:192])
    grads = by_head(mask0, mask1, gv_ref[:, 0:128], gv_ref[:, 128:192])
    starts = start_ref[0]
    lses = [lse_ref[head, 0] for head in range(3)]
    product = (gv_ref[...].astype(F32) * o_ref[...].astype(F32)).T
    deltas = [
        jnp.sum(product[head * HDIM : (head + 1) * HDIM], axis=0, keepdims=True)
        for head in range(3)
    ]
    dqt_ref[...] = jnp.zeros_like(dqt_ref)

    @pl.when(pl.program_id(0) == 0)
    def _():
        dk_ref[...] = jnp.zeros_like(dk_ref)
        dv_ref[...] = jnp.zeros_like(dv_ref)

    def load(ki):
        k_rows = pl.ds(slot_rows(meta, per, ki), TILE)
        return k_rows

    def score(masked, ki):
        k_rows = load(ki)
        pair, third = k_ref[k_rows, 0:128], k_ref[k_rows, 128:192]
        v_pair, v_third = v_ref[k_rows, 0:128], v_ref[k_rows, 128:192]
        scores = [dot_nt(third if head == 2 else pair, queries[head]) for head in range(3)]
        grad_probs = [dot_nt(v_third if head == 2 else v_pair, grads[head]) for head in range(3)]
        if masked:
            allowed = (key_iota >= starts - ki * TILE) & (key_iota <= query_iota + (qi - ki) * TILE)
            scores = [jnp.where(allowed, x, MASKED) for x in scores]
        return scores, grad_probs

    def terms(ki, scores, grad_probs):
        k_rows = load(ki)
        probs = [jnp.exp2(x - lse) for x, lse in zip(scores, lses)]
        grad_scores = [
            (p * (g - delta)).astype(BF16) for p, g, delta in zip(probs, grad_probs, deltas)
        ]
        dv = [dot(p.astype(BF16), g) for p, g in zip(probs, grads)]
        dk = [dot(g, q) for g, q in zip(grad_scores, queries)]
        dq = [
            dot(kt_ref[head * HDIM : (head + 1) * HDIM, k_rows], grad_scores[head])
            for head in range(3)
        ]
        return dk, dv, dq

    def add(ki, dk, dv, dq):
        k_rows = load(ki)
        for into, parts in ((dk_ref, dk), (dv_ref, dv)):
            into[k_rows, 0:128] += parts[0] + parts[1]
            into[k_rows, 128:192] += parts[2]
        for head in range(3):
            dqt_ref[head * HDIM : (head + 1) * HDIM, :] += dq[head]

    first = lo[qi]
    full = jnp.minimum(hi[qi], qi)

    def visit(masked, ki):
        add(ki, *terms(ki, *score(masked, ki)))

    @pl.loop(first, full)
    def _(ki):
        visit(True, ki)

    @pl.loop(full, qi)
    def _(ki):
        visit(False, ki)

    visit(True, qi)

    cos, sin = rotation(low, high, qi)

    def turn_back(block):
        return block * cos - swap_halves(block) * sin

    dq = dqt_ref[...].T * (HDIM**-0.5)
    dk = dk_ref[own_rows, :] * LN2
    gj_ref[:, 0:128] = turn_back(dq[:, 0:128]).astype(BF16)
    gj_ref[:, 128:256] = turn_back(dk[:, 0:128]).astype(BF16)
    mixed = jnp.concatenate([dq[:, 128:192], dk[:, 128:192]], axis=1)
    gj_ref[:, 256:384] = turn_back(mixed).astype(BF16)
    gj_ref[:, 384:576] = dv_ref[own_rows, :].astype(BF16)


def attend_back(
    meta, lo, hi, query, keys, values, attn, grad_vec, starts, lse, low, high, per
):
    total, width = query.shape
    tiles = total // TILE

    def slot(i, m):
        tile = tiles - 1 - i
        return jnp.bitwise_xor(tile // per, m[0]) * per + tile % per

    q_spec = pl.BlockSpec((TILE, width), lambda i, m, lo, hi: (slot(i, m), 0))
    gj_spec = pl.BlockSpec((TILE, 3 * width), lambda i, m, lo, hi: (slot(i, m), 0))
    start_spec = pl.BlockSpec((1, 1, TILE), lambda i, m, lo, hi: (slot(i, m), 0, 0))
    lse_spec = pl.BlockSpec((3, 1, 1, TILE), lambda i, m, lo, hi: (0, slot(i, m), 0, 0))
    return pl.pallas_call(
        partial(attend_back_kernel, per),
        out_shape=jax.ShapeDtypeStruct((total, 3 * width), BF16),
        grid_spec=pltpu.PrefetchScalarGridSpec(
            num_scalar_prefetch=3,
            grid=(tiles,),
            in_specs=[
                q_spec,
                whole(keys.shape),
                whole(values.shape),
                q_spec,
                q_spec,
                start_spec,
                lse_spec,
                whole(low.shape),
                whole(high.shape),
            ],
            out_specs=gj_spec,
            scratch_shapes=[
                pltpu.VMEM((width, total), BF16),
                pltpu.VMEM((total, width), F32),
                pltpu.VMEM((total, width), F32),
                pltpu.VMEM((width, TILE), F32),
            ],
        ),
        compiler_params=params(),
        cost_estimate=COST,
        name="attend_back",
    )(meta, lo, hi, query, keys, values, attn, grad_vec, starts, lse, low, high)


def joined_kernel(final, rows, meta, *refs):
    gj_a, gj_b, e_a, e_b, x_a, x_b, gain_ref, shift_ref, w_ref = refs[:9]
    if final:
        grad_in, bias_in, sums_in, mlp_sums = refs[9:13]
        *e_refs, keep, send, grad, bias, sums = refs[13:]
    else:
        *e_refs, grad, bias, sums = refs[9:]
    step = pl.program_id(0)

    @pl.when(step == 0)
    def _():
        if final:
            grad[...] = grad_in[...]
            bias[...] = bias_in[...]
            sums[...] = sums_in[...]
        else:
            grad[...] = jnp.zeros_like(grad)
            bias[...] = jnp.zeros_like(bias)
            sums[...] = jnp.zeros_like(sums)

    gain, shift = row(gain_ref), row(shift_ref)
    for index, (gj_ref, e_in, x_ref) in enumerate(((gj_a, e_a, x_a), (gj_b, e_b, x_b))):
        normed = normalize(x_ref[...].astype(F32))
        attn_in = (normed * gain + shift).astype(BF16)
        low = gj_ref[...]
        grad_norm = dot_nt(low, w_ref[...])
        e_refs[index][...] = (grad_norm * gain + e_in[...].astype(F32)).astype(BF16)
        sums[0:1, :] += jnp.sum(grad_norm * normed, axis=0, keepdims=True)
        sums[1:2, :] += jnp.sum(grad_norm, axis=0, keepdims=True)
        bias[0:1, :] += jnp.sum(low.astype(F32), axis=0, keepdims=True)
        grad[...] += dot_tn(attn_in, low)

    if final:

        @pl.when(step == pl.num_programs(0) - 1)
        def _():
            if fits(rows):
                store_chunks(grad, keep, send, meta, rows)
                small = pack_small(sums[...], mlp_sums[...], bias[...])
                keep[D // 2 :, :] = small
                send[D // 2 :, :] = small
            else:
                keep[...] = grad[...].astype(BF16)
                send[...] = jnp.zeros_like(send)


SMALL = 32


def pack_small(norm_sums, mlp_sums, bias):
    third = 3 * D // 4
    table = jnp.concatenate([norm_sums[0:4], mlp_sums[0:4]], axis=0)
    which = lax.broadcasted_iota(jnp.int32, (8, third), 0)
    head = jnp.where(which == 2, bias[0:1, :], table[:, :third])
    tail = jnp.concatenate([table[:, third:], jnp.zeros((8, 2 * third - D), F32)], axis=1)
    return split_small(jnp.concatenate([head, tail], axis=0))


def add_small(left, right):
    half = SMALL // 2
    total = left.astype(F32) + right.astype(F32)
    return total[:half] + total[half:]


def split_small(rows):
    high = rows.astype(BF16)
    return jnp.concatenate([high, (rows - high.astype(F32)).astype(BF16)], axis=0)


def joined_back(
    meta, slots, grad, e_mlp, toks, gain, shift, w, rows, seq, before=None, mlp_sums=None
):
    width = grad.shape[1]
    per = seq // TILE

    def at(slot, cols):
        return pl.BlockSpec((TILE, cols), lambda i, m: (slot * per + i, 0))

    sums = (8, D)
    args = [grad, grad, *e_mlp, *[toks[slot] for slot in slots], gain, shift, w]
    specs = [
        *(at(slot, width) for slot in slots),
        *(at(slot % 2, D) for slot in slots),
        *(pl.BlockSpec((TILE, D), lambda i, m: (i, 0)),) * 2,
        whole(gain.shape),
        whole(shift.shape),
        whole(w.shape),
    ]
    e_spec = pl.BlockSpec((TILE, D), lambda i, m: (i, 0))
    outs, out_specs = [jax.ShapeDtypeStruct((seq, D), BF16)] * 2, [e_spec] * 2
    carried = [(D, width), (8, width), sums]
    scratch = []
    if before is None:
        outs += [jax.ShapeDtypeStruct(shape, F32) for shape in carried]
        out_specs += [whole(shape) for shape in carried]
    else:
        chunks = chunk_shapes(width, rows, SMALL)
        outs += [jax.ShapeDtypeStruct(shape, BF16) for shape in chunks]
        out_specs += [whole(shape) for shape in chunks]
        if not fits(rows):
            outs[-1] = jax.ShapeDtypeStruct((8, LANES), BF16)
        args += [*before, mlp_sums]
        specs += [whole(shape) for shape in carried] + [whole(sums)]
        scratch = [pltpu.VMEM(shape, F32) for shape in carried]
        if not fits(rows):
            outs += [jax.ShapeDtypeStruct(shape, F32) for shape in carried[1:]]
            out_specs += [whole(shape) for shape in carried[1:]]
            scratch = scratch[:1]
    body = partial(joined_kernel, before is not None, rows)
    if before is not None and not fits(rows):

        def body(meta, *refs):
            inputs, (e_a, e_b, keep, send, bias, sums, grad) = refs[:13], refs[13:]
            joined_kernel(True, rows, meta, *inputs, e_a, e_b, keep, send, grad, bias, sums)

    return pl.pallas_call(
        body,
        out_shape=outs,
        grid_spec=pltpu.PrefetchScalarGridSpec(
            num_scalar_prefetch=1,
            grid=(per,),
            in_specs=specs,
            out_specs=out_specs,
            scratch_shapes=scratch,
        ),
        compiler_params=params(),
        cost_estimate=COST,
        name="joined_first" if before is None else "joined_second",
    )(meta, *args)


def fold_kernel(extra, keep, got, *outs):
    size = keep.shape[0] - extra
    for index, out in enumerate(outs):
        rows = slice(index * size // 2, (index + 1) * size // 2)
        total = keep[rows, :].astype(F32) + got[rows, :].astype(F32)
        out[0 : size // 2, :] = total.astype(BF16)
    if extra:
        small = split_small(add_small(keep[size:, :], got[size:, :]))
        for out in outs:
            out[size // 2 :, :] = small


def simple(body, name, shapes, *args):
    return pl.pallas_call(
        body,
        out_shape=[jax.ShapeDtypeStruct(shape, kind) for shape, kind in shapes],
        grid_spec=pltpu.PrefetchScalarGridSpec(
            num_scalar_prefetch=1,
            grid=(1,),
            in_specs=[whole(a.shape) for a in args[1:]],
            out_specs=[whole(shape) for shape, _ in shapes],
        ),
        compiler_params=params(),
        cost_estimate=COST,
        name=name,
    )(*args)


def fold(meta, keep, got, extra):
    size, cols = keep.shape[0] - extra, keep.shape[1]
    shapes = [((size // 2 + extra, cols), BF16)] * 2
    return simple(lambda _, *refs: fold_kernel(extra, *refs), "fold", shapes, meta, keep, got)


def last_packet_kernel(meta, keep, got, up_ref, first, second):
    hid = up_ref.shape[1]
    up_ref[...] = keep[:, :hid].astype(F32) + got[:, :hid].astype(F32)
    low = (keep[:, hid:].astype(F32) + got[:, hid:].astype(F32)).astype(BF16)
    cut, side = hid // 2, D // 8
    even = jnp.concatenate([low[:, :cut], low[:, hid : hid + side]], axis=1)
    odd = jnp.concatenate([low[:, cut:hid], low[:, hid + side : hid + 2 * side]], axis=1)

    @pl.when(meta[1] % 2 == 0)
    def _():
        first[...] = even
        second[...] = odd

    @pl.when(meta[1] % 2 == 1)
    def _():
        first[...] = odd
        second[...] = even


def lower_kernel(meta, first, second, down_ref, out_ref):
    cut = down_ref.shape[0]
    size = first.shape[0]

    def store(ref, at):
        turned = ref[...].astype(F32).T
        down_ref[:, at : at + size] = turned[:cut]
        out_ref[:, at : at + size] = turned[cut:]

    @pl.when(meta[1] % 2 == 0)
    def _():
        store(first, 0)
        store(second, size)

    @pl.when(meta[1] % 2 == 1)
    def _():
        store(second, 0)
        store(first, size)


def last_qkv_kernel(meta, keep, got, kept, near, far, small):
    size = kept.shape[0]
    width = kept.shape[1]
    total = keep[0:size, :].astype(F32) + got[0:size, :].astype(F32)
    rows = add_small(keep[size:, :], got[size:, :])
    for part in range(3):
        small[part * 8 : part * 8 + 8, :] = rows[0:8, part * width : (part + 1) * width]
    small[24:32, :] = rows[8:16, 0:width]
    near[size:, :] = small[...]
    far[size:, :] = small[...]
    query = jnp.concatenate([total[:, 0:128], total[:, 256:320]], axis=1)
    keys = jnp.concatenate([total[:, 128:256], total[:, 320:384]], axis=1)
    values = total[:, 384:576]
    plans = (
        (query, keys, values),
        (keys, query, values),
        (keys, values, query),
        (values, keys, query),
    )
    for blk, plan in enumerate(plans):

        @pl.when(meta[0] == blk)
        def _(plan=plan):
            kept[...] = plan[0]
            near[0:size, :] = plan[1]
            far[0:size, :] = plan[2]


def assemble_kernel(
    meta, kept, small, near, far, diag,
    qkv, b_qkv, b_out, b_up, b_down, gain1, shift1, gain2, shift2, table,
):
    size, width = kept.shape

    @pl.when(meta[0] % 2 == 0)
    def _():
        qkv[:, 0:width] = kept[...]
        qkv[:, 2 * width :] = far[0:size, :]

    @pl.when(meta[0] % 2 == 1)
    def _():
        qkv[:, 0:width] = far[0:size, :]
        qkv[:, 2 * width :] = kept[...]

    qkv[:, width : 2 * width] = near[0:size, :]
    table[0] = small[...]
    table[1] = near[size:, :]
    table[2] = far[size:, :]
    table[3] = diag[...]
    total = table[0] + table[1] + table[2] + table[3]

    def vector(rows, index):
        parts = [rows[part * 8 + index : part * 8 + index + 1, :] for part in range(4)]
        return jnp.concatenate(parts, axis=1)

    for ref, index in ((gain1, 0), (shift1, 1), (gain2, 5), (shift2, 6), (b_out, 7), (b_down, 7)):
        ref[...] = vector(total, index).reshape(D)
    ups, parts = [], ([], [], [])
    for blk in range(4):
        rows = table[jnp.bitwise_xor(meta[0], blk)]
        ups.append(vector(rows, 4))
        joined = vector(rows, 2)
        parts[0].append(jnp.concatenate([joined[:, 0:128], joined[:, 256:320]], axis=1))
        parts[1].append(jnp.concatenate([joined[:, 128:256], joined[:, 320:384]], axis=1))
        parts[2].append(joined[:, 384:576])
    b_up[...] = jnp.concatenate(ups, axis=1).reshape(4 * D)
    b_qkv[...] = jnp.concatenate(parts[0] + parts[1] + parts[2], axis=1).reshape(3 * D)


def assemble(meta, kept, small, near, far, diag):
    size, width = kept.shape
    shapes = [((size, 3 * width), F32), ((3 * D,), F32), ((D,), F32), ((4 * D,), F32)]
    shapes += [((D,), F32)] * 5
    args = (kept, small, near, far, diag)
    return pl.pallas_call(
        assemble_kernel,
        out_shape=[jax.ShapeDtypeStruct(shape, kind) for shape, kind in shapes],
        grid_spec=pltpu.PrefetchScalarGridSpec(
            num_scalar_prefetch=1,
            grid=(1,),
            in_specs=[whole(a.shape) for a in args],
            out_specs=[whole(shape) for shape, _ in shapes],
            scratch_shapes=[pltpu.VMEM((4, 32, width), F32)],
        ),
        compiler_params=params(),
        cost_estimate=COST,
        name="assemble",
    )(meta, *args)


def fold_plain(keep, got, last):
    total = keep.astype(F32) + got.astype(F32)
    if last:
        return [total]
    half = total.shape[0] // 2
    return [total[:half].astype(BF16), total[half:].astype(BF16)]


def reduce_plain(keep, got, rows):
    mask = 2
    while mask < rows:
        keep, send = fold_plain(keep, got, False)
        got = swap(send, "rows", mask)
        mask *= 2
    return fold_plain(keep, got, True)[0]


def after(value, *others):
    return lax.optimization_barrier((value, others))[0]


def swap(value, axis, mask):
    size = lax.axis_size(axis)
    return lax.ppermute(value, axis, [(i, i ^ mask) for i in range(size)])


def add_low(left, right):
    return (left.astype(F32) + right.astype(F32)).astype(BF16)


def spread_rows(lower):
    rows, blk = lax.axis_size("rows"), lax.axis_size("blk")
    r = lax.axis_index("rows")
    count = rows // blk
    hid, width = FF // 4, D // 4
    chunk = lower.shape[0]
    down = lower[:, :hid].reshape(chunk, count, hid // count)
    out = lower[:, hid:].reshape(chunk, count, width // count)
    pieces = jnp.concatenate([down, out], axis=2).astype(BF16)
    got = []
    for turn in range(count):
        moves = spread_moves(rows, blk, turn)
        piece = lax.dynamic_index_in_dim(pieces, (r % count) ^ turn, 1, keepdims=False)
        got.append(lax.ppermute(piece, ("rows", "blk"), moves))
    got = jnp.stack(got)
    parts = [
        lax.dynamic_index_in_dim(got, (r % count) ^ part, 0, keepdims=False)
        for part in range(count)
    ]
    whole_cols = jnp.concatenate(parts, axis=0).astype(F32).T
    cut = hid // count
    return whole_cols[:cut], whole_cols[cut:]


def spread_moves(rows, blk, turn):
    count = rows // blk
    moves = []
    for r in range(rows):
        for b in range(blk):
            to = count * b + ((r % count) ^ turn)
            moves.append((r * blk + b, to * blk + r // count))
    return moves


def split_columns(chunk):
    b = lax.axis_index("blk")
    q = jnp.concatenate([chunk[:, 0:128], chunk[:, 256:320]], axis=1)
    k = jnp.concatenate([chunk[:, 128:256], chunk[:, 320:384]], axis=1)
    v = chunk[:, 384:576]

    def choose(zero, one, two, three):
        return jnp.where(b < 2, jnp.where(b == 0, zero, one), jnp.where(b == 2, two, three))

    return choose(q, k, k, v), choose(k, q, v, k), choose(v, v, q, q)


def result_kernel(x_ref, even, near, far, b_out, b_down, out_ref):
    bias = row(b_out) + row(b_down)
    total = even[0].astype(F32) + near[0].astype(F32) + far[...].astype(F32)
    out_ref[...] = (x_ref[...].astype(F32) + bias + total).astype(BF16)


def token_kernel(x_ref, even, near, far, c_ref, out_ref):
    wide = x_ref[...].astype(F32)
    center = wide - jnp.mean(wide, axis=-1, keepdims=True)
    rate = lax.rsqrt(jnp.mean(center * center, axis=-1, keepdims=True) + EPS)
    normed = center * rate
    grad = even[...].astype(F32) + near[...].astype(F32) + far[...].astype(F32)
    mean = jnp.mean(grad, axis=-1, keepdims=True)
    along = jnp.mean(grad * normed, axis=-1, keepdims=True)
    back = rate * (grad - mean - normed * along)
    out_ref[...] = (c_ref[...].astype(F32) + back).astype(BF16)


def finish(body, name, seq, x, even, near, far, *more):
    flat = pl.BlockSpec((TILE, D), lambda i: (i, 0))
    own = pl.BlockSpec((1, TILE, D), lambda i: (0, i, 0))
    return pl.pallas_call(
        body,
        out_shape=jax.ShapeDtypeStruct((seq, D), BF16),
        grid=(seq // TILE,),
        in_specs=[
            *(own if a.ndim == 3 else flat for a in (x, even, near, far)),
            *(flat if a.ndim == 2 else whole(a.shape) for a in more),
        ],
        out_specs=flat,
        compiler_params=params(),
        cost_estimate=COST,
        name=name,
    )(x, even, near, far, *more)


def local(
    tokens, seg_ids, valid_len, ln1_gain, ln1_bias, w_qkv, b_qkv, w_out, b_out,
    ln2_gain, ln2_bias, w_up, b_up, w_down, b_down, cotangent,
):
    rows = lax.axis_size("rows")
    blk = lax.axis_index("blk")
    seq = tokens.shape[1]
    per = seq // TILE
    width = D // 4
    hid = FF // 4
    low, high = angle_parts(4 * seq)
    seg_row = jnp.pad(seg_ids.astype(BF16), ((0, EXTRA - 1), (0, D - seq)))
    tok_own = jnp.concatenate([tokens[0], seg_row], axis=0)
    cot_own = cotangent[0]

    cot_near = swap(cot_own, "blk", 1)
    tok_far = swap(tok_own, "blk", 2)
    tok_near = swap(tok_own, "blk", 1)
    cot_long = jnp.pad(cot_own, ((0, 2 * EXTRA), (0, 0)))
    cot_far = swap(cot_long, "blk", 2)

    meta = jnp.stack([blk, lax.axis_index("rows")]).astype(jnp.int32)
    mlp_args = (ln2_gain, ln2_bias, b_up, w_up, w_down, w_out, rows, seq)
    joined = (ln1_gain, ln1_bias, w_qkv, b_qkv, low, high)
    *first, query, keys, values, w_own, b_own = feed_forward(
        meta, (tok_own, tok_near), (cot_own, cot_near), *mlp_args, joined
    )
    meta = after(meta, b_own)

    def more(slot, m, tok, filled):
        return project(slot, m, tok, ln1_gain, ln1_bias, low, high, w_own, b_own, filled, seq)

    tok_last = swap(after(tok_far, b_own), "blk", 1)
    joined = more(2, meta, tok_far, (query, keys, values))
    toks = (tok_own, tok_near, tok_far, tok_last)
    query, keys, values = more(3, after(meta, joined[0]), tok_last, joined)
    starts, lo, hi = segment_starts(after(meta, query), valid_len, toks, seq)
    cot_last = swap(after(cot_far, lo), "blk", 1)
    cots = (cot_own, cot_near, cot_far, cot_last)
    attn, lse = attend(meta, lo, hi, query, keys, values, starts, per)

    meta = after(meta, lse)
    e_far, grad_vec, mlp_sums, out_even, out_odd, keep, send = feed_forward(
        meta, toks[2:], cots[2:], *mlp_args, before=first, near=cots[:2], attn=attn
    )
    e_mlp = (first[1], e_far)
    keep, send = chunks_of(keep, send, rows)
    out_got = swap(out_odd, "blk", 1)
    got = swap(send, "rows", 1)

    meta = after(meta, mlp_sums)
    grad_joined = attend_back(
        meta, lo, hi, query, keys, values, attn, grad_vec, starts, lse, low, high, per
    )

    out_send = add_low(after(out_even, grad_joined)[1], out_got[1])
    out_far = swap(out_send, "blk", 2)
    joined_args = (grad_joined, e_mlp, toks, ln1_gain, ln1_bias, w_own, rows, seq)
    meta = after(meta, out_send)
    e_near, e_last, *carried = joined_back(meta, (1, 3), *joined_args)
    e_last = swap(e_last, "blk", 1)
    e_near = swap(e_near, "blk", 1)
    meta = after(meta, carried[1])
    if fits(rows):
        keep, send = fold(meta, keep, got, 0)
        got = swap(send, "rows", 2)
        meta = after(meta, send)
    e_own, e_send, qkv_keep, qkv_send, *rest = joined_back(
        meta, (0, 2), *joined_args, carried, mlp_sums
    )
    qkv_keep, qkv_send = chunks_of(qkv_keep, qkv_send, rows)
    qkv_got = swap(qkv_send, "rows", 1)
    e_send = add_low(e_send, e_last)
    e_far = swap(e_send, "blk", 2)

    out_args = (after(tok_own, e_send), out_even, out_got, out_far, b_out, b_down)
    result = finish(result_kernel, "result", seq, *out_args)
    if fits(rows):
        meta = after(meta, result)
        keep, send = fold(meta, keep, got, 0)
        got = swap(send, "rows", 4)
        meta = after(meta, send)
        qkv_keep, qkv_send = fold(meta, qkv_keep, qkv_got, SMALL)
        qkv_got = swap(qkv_send, "rows", 2)
        tok_args = (after(tok_own, qkv_send), e_own, e_near, e_far, cot_own)
        grad_tokens = finish(token_kernel, "token_grad", seq, *tok_args)
        meta = after(meta, grad_tokens)
        qkv_keep, qkv_send = fold(meta, qkv_keep, qkv_got, SMALL)
        qkv_got = swap(qkv_send, "rows", 4)
        meta = after(meta, qkv_send)
        chunk = D // rows
        part = ((chunk, hid // 2 + width // 2), BF16)
        up, *pieces = simple(
            last_packet_kernel, "last_packet", [((chunk, hid), F32), part, part], meta, keep, got
        )
        pieces = [
            lax.ppermute(piece, ("rows", "blk"), spread_moves(rows, 4, turn))
            for turn, piece in enumerate(pieces)
        ]
        meta = after(meta, up)
        packet = ((chunk + 32, width), F32)
        kept, near, far, small = simple(
            last_qkv_kernel,
            "last_qkv",
            [((chunk, width), F32), packet, packet, ((32, width), F32)],
            meta,
            qkv_keep,
            qkv_got,
        )
        near, far, diag = swap(near, "blk", 1), swap(far, "blk", 2), swap(small, "blk", 3)
        lower = [((hid // 2, width), F32), ((width // 2, width), F32)]
        down, out_w = simple(lower_kernel, "lower", lower, meta, *pieces)
        meta = after(meta, down)
        qkv, gb_qkv, gb_out, gb_up, gb_down, *norms = assemble(
            meta, kept, small, near, far, diag
        )
    else:
        weights = reduce_plain(keep, got, rows)
        qkv = reduce_plain(qkv_keep, qkv_got, rows)
        up = weights[:, :hid]
        down, out_w = spread_rows(weights[:, hid : 2 * hid + width])
        kept, near, far = split_columns(qkv)
        near, far = swap(near, "blk", 1), swap(far, "blk", 2)
        ends = [jnp.where(blk % 2 == 0, a, b) for a, b in ((kept, far), (far, kept))]
        qkv = jnp.concatenate([ends[0], near, ends[1]], axis=1)
        tok_args = (tok_own, e_own, e_near, e_far, cot_own)
        grad_tokens = finish(token_kernel, "token_grad", seq, *tok_args)
        bias, sums = rest
        mine = (jnp.arange(4) == blk)[:, None]
        joined = lax.psum(jnp.where(mine, bias[0:1], 0.0), ("rows", "blk"))
        gb_up = lax.psum(jnp.where(mine, mlp_sums[0:1], 0.0), ("rows", "blk")).reshape(FF)
        gb_qkv = jnp.concatenate(
            [
                jnp.concatenate([joined[:, 0:128], joined[:, 256:320]], axis=1).reshape(D),
                jnp.concatenate([joined[:, 128:256], joined[:, 320:384]], axis=1).reshape(D),
                joined[:, 384:576].reshape(D),
            ]
        )
        sums = jnp.concatenate([sums[0:2], mlp_sums[1:4]])
        *norms, gb_out = lax.psum(sums, ("rows", "blk"))
        gb_down = gb_out
    return (
        result[None],
        grad_tokens[None],
        qkv,
        out_w,
        up,
        down,
        gb_qkv,
        gb_out,
        gb_up,
        gb_down,
        *norms,
    )


def solution(mesh):
    split = P("rows", "blk")
    in_specs = (
        P("rows", "blk", None),
        split,
        P("rows"),
        *(P(),) * 12,
        P("rows", "blk", None),
    )
    out_specs = (
        P("rows", "blk", None),
        P("rows", "blk", None),
        *(split,) * 4,
        *(P(),) * 8,
    )
    return jax.shard_map(local, mesh=mesh, in_specs=in_specs, out_specs=out_specs, check_vma=False)
```

```python
import math
from functools import partial

import jax
import jax.numpy as jnp
import numpy as np
from jax import lax
from jax.experimental import pallas as pl
from jax.experimental.pallas import tpu as pltpu
from jax.sharding import PartitionSpec as P

D = 768
HEADS = 12
HDIM = 64
ROT = 16
FF = 3072
EPS = 1e-05
MASKED = -1e30
TILE = 256
VROWS = 80
LN2 = math.log(2.0)
EXTRA = 16
LANES = 128
F32 = jnp.float32
BF16 = jnp.bfloat16
COST = pl.CostEstimate(flops=0, bytes_accessed=0, transcendentals=0)
NT_DIMS = (((1,), (1,)), ((), ()))
TN_DIMS = (((0,), (0,)), ((), ()))


def dot(left, right):
    return jnp.dot(left, right, preferred_element_type=F32)


def dot_nt(left, right):
    return lax.dot_general(left, right, NT_DIMS, preferred_element_type=F32)


def dot_tn(left, right):
    return lax.dot_general(left, right, TN_DIMS, preferred_element_type=F32)


def normalize(value):
    center = value - jnp.mean(value, axis=-1, keepdims=True)
    spread = jnp.mean(center * center, axis=-1, keepdims=True)
    return center * lax.rsqrt(spread + EPS)


def angle_parts(length):
    dim = np.arange(LANES) % HDIM
    inverse = np.where(dim < ROT, 10000.0 ** (-2.0 * (dim % (ROT // 2)) / ROT), 0.0)
    high = (np.arange(length // LANES) * LANES)[:, None] * inverse
    low = np.arange(LANES)[:, None] * inverse
    parts = np.stack([np.cos(low), np.sin(low)]), np.stack([np.cos(high), np.sin(high)])
    return tuple(jnp.asarray(part, F32) for part in parts)


def rotation(low_ref, high_ref, tile):
    lane = lax.broadcasted_iota(jnp.int32, (1, LANES), 1) % HDIM
    sign = jnp.where(lane < ROT // 2, -1.0, 1.0)
    cos_rows, sin_rows = [], []
    for part in range(TILE // LANES):
        row = tile * (TILE // LANES) + part
        cos_high = high_ref[0, pl.ds(row, 1), :]
        sin_high = high_ref[1, pl.ds(row, 1), :]
        cos_rows.append(low_ref[0] * cos_high - low_ref[1] * sin_high)
        sin_rows.append((low_ref[1] * cos_high + low_ref[0] * sin_high) * sign)
    return jnp.concatenate(cos_rows, axis=0), jnp.concatenate(sin_rows, axis=0)


def swap_halves(value):
    lane = lax.broadcasted_iota(jnp.int32, value.shape, 1) % HDIM
    half = ROT // 2
    return jnp.where(
        lane < half, pltpu.roll(value, LANES - half, 1), pltpu.roll(value, half, 1)
    )


def true_block(meta_ref, slot):
    return jnp.bitwise_xor(meta_ref[0], slot)


def params(*semantics, vmem=None):
    return pltpu.CompilerParams(
        dimension_semantics=semantics or ("arbitrary",), vmem_limit_bytes=vmem or 60 * 2**20
    )


def whole(shape):
    return pl.BlockSpec(shape, lambda *_: (0,) * len(shape))


def own_blocks(refs, odd, into):
    places = ((0, 256), (128, 320), (384, 512))
    for part, (pair_at, third_at) in enumerate(places):
        left, right = refs[2 * part], refs[2 * part + 1]

        @pl.when(odd == 0)
        def _(left=left, right=right, pair_at=pair_at, third_at=third_at):
            into[:, pair_at : pair_at + 128] = left[...]
            into[:, third_at : third_at + 64] = right[:, 0:64]

        @pl.when(odd == 1)
        def _(left=left, right=right, pair_at=pair_at, third_at=third_at):
            into[:, pair_at : pair_at + 128] = jnp.concatenate(
                [left[:, 64:128], right[:, 0:64]], axis=1
            )
            into[:, third_at : third_at + 64] = right[:, 64:128]


def row(ref):
    return ref[...].reshape(1, ref.shape[0])


def own_bias(b_ref, odd, blk, into):
    blocks = []
    for part in range(3):
        for side in range(2):
            at = pl.multiple_of((part * (D // LANES) + side + 3 * blk // 2) * LANES, LANES)
            blocks.append(b_ref[pl.ds(at, LANES)].reshape(1, LANES))
    own_blocks(blocks, odd, into)


def project_tile(normed, gain, shift, w_ref, b_ref, low, high, tile, q_ref, k_ref, v_ref):
    attn_in = (normed * row(gain) + row(shift)).astype(BF16)
    joined = dot(attn_in, w_ref[...]) + b_ref[...]
    cos, sin = rotation(low, high, tile)
    scale = HDIM**-0.5 / LN2

    def turn(block):
        return block * cos + swap_halves(block) * sin

    query = turn(joined[:, 0:128]) * scale
    keys = turn(joined[:, 128:256])
    mixed = turn(joined[:, 256:384])
    q_ref[:, 0:128] = query.astype(BF16)
    k_ref[:, 0:128] = keys.astype(BF16)
    q_ref[:, 128:192] = (mixed[:, 0:64] * scale).astype(BF16)
    k_ref[:, 128:192] = mixed[:, 64:128].astype(BF16)
    v_ref[...] = joined[:, 384:576].astype(BF16)


def qkv_kernel(slot, meta, x_ref, gain, shift, low, high, w_ref, b_ref, *refs):
    per = pl.num_programs(0)
    tile = true_block(meta, slot) * per + pl.program_id(0)
    normed = normalize(x_ref[...].astype(F32))
    project_tile(normed, gain, shift, w_ref, b_ref, low, high, tile, *refs[-3:])


def project(slot, meta, x, gain, shift, low, high, w, b, filled, seq):
    width = D // 4
    per = seq // TILE
    out = jax.ShapeDtypeStruct((4 * seq, width), BF16)
    out_spec = pl.BlockSpec((TILE, width), lambda i, m: (slot * per + i, 0))
    args = [x, gain, shift, low, high, w, b, *filled]
    specs = [pl.BlockSpec((TILE, D), lambda i, m: (i, 0))]
    specs += [whole(a.shape) for a in args[1:7]]
    specs += [pl.BlockSpec(memory_space=pl.ANY)] * 3
    return pl.pallas_call(
        partial(qkv_kernel, slot),
        out_shape=[out] * 3,
        grid_spec=pltpu.PrefetchScalarGridSpec(
            num_scalar_prefetch=1, grid=(per,), in_specs=specs, out_specs=[out_spec] * 3
        ),
        input_output_aliases={8 + i: i for i in range(3)},
        compiler_params=params(),
        cost_estimate=COST,
        name=f"qkv_{slot}",
    )(meta, *args)


def starts_kernel(seq, meta, valid, s0, s1, s2, s3, start_ref, lo_ref, hi_ref):
    segs = [ref[0:1, 0:seq].astype(F32) for ref in (s0, s1, s2, s3)]
    below = [
        sum(jnp.sum((seg < number).astype(F32), axis=1, keepdims=True) for seg in segs)
        for number in (1, 2, 3)
    ]
    per = seq // TILE
    iota = lax.broadcasted_iota(jnp.int32, (1, seq), 1)
    for slot, seg in enumerate(segs):
        block = true_block(meta, slot)
        begin = jnp.zeros((1, seq), F32)
        for number in (1, 2, 3):
            begin = jnp.where(seg == number, below[number - 1], begin)
        pos = iota + block * seq
        begin = jnp.where(pos < valid[0], begin.astype(jnp.int32), pos)
        for part in range(per):
            tile = begin[:, part * TILE : (part + 1) * TILE]
            start_ref[slot * per + part] = tile
            lo_ref[block * per + part] = jnp.min(tile) // TILE
            hi_ref[block * per + part] = (jnp.max(tile) + (TILE - 1)) // TILE


def segment_starts(meta, valid_len, toks, seq):
    tiles = 4 * seq // TILE
    smem = pl.BlockSpec(memory_space=pltpu.SMEM)
    return pl.pallas_call(
        partial(starts_kernel, seq),
        out_shape=[
            jax.ShapeDtypeStruct((tiles, 1, TILE), jnp.int32),
            jax.ShapeDtypeStruct((tiles,), jnp.int32),
            jax.ShapeDtypeStruct((tiles,), jnp.int32),
        ],
        grid_spec=pltpu.PrefetchScalarGridSpec(
            num_scalar_prefetch=2,
            grid=(1,),
            in_specs=[pl.BlockSpec((EXTRA, D), lambda i, m, v: (seq // EXTRA, 0))] * 4,
            out_specs=[whole((tiles, 1, TILE)), smem, smem],
        ),
        compiler_params=params(),
        cost_estimate=COST,
        name="segment_starts",
    )(meta, valid_len, *toks)


def mask_order(rows, first):
    masks = [1 << bit for bit in range(rows.bit_length() - 1)]
    return [m for m in masks if m >= first] + [m for m in masks if m < first]


def places(masks):
    order = [0]
    for mask in reversed(masks):
        order = order + [mask + i for i in order]
    return order


def fits(rows):
    return rows == 8 and D // rows % 32 == 0


def store_chunks(load, keep, send, meta, rows, first):
    size = D // rows
    for index, place in enumerate(places(mask_order(rows, first))):
        at = pl.multiple_of(jnp.bitwise_xor(meta[1], place) * size, 32)
        into = keep if index < rows // 2 else send
        row_at = index % (rows // 2) * size
        into[row_at : row_at + size, :] = load(pl.ds(at, size)).astype(into.dtype)


def chunk_shapes(cols, rows, extra=0):
    if fits(rows):
        return [(D // 2 + extra, cols)] * 2
    return [(D, cols), (8, LANES)]


def chunks_of(keep, send, rows, first):
    if fits(rows):
        return keep, send
    order = jnp.array(places(mask_order(rows, first))) ^ lax.axis_index("rows")
    parts = keep.reshape(rows, D // rows, keep.shape[1])
    parts = jnp.take(parts, order, axis=0).reshape(keep.shape)
    return parts[: D // 2], parts[D // 2 :]


def feed(normed, upstream, gain, shift, w_up, b_up, w_down):
    mlp_in = (normed * row(gain) + row(shift)).astype(BF16)
    hidden = dot(mlp_in, w_up[...]) + b_up
    cdf = 0.5 * (1.0 + lax.erf(hidden * (0.5**0.5)))
    act = (hidden * cdf).astype(BF16)
    slope = cdf + hidden * jnp.exp(-0.5 * hidden * hidden) * ((2.0 * math.pi) ** -0.5)
    grad_low = (slope * dot_nt(upstream, w_down[...])).astype(BF16)
    grad_norm = dot_nt(grad_low, w_up[...])
    return mlp_in, act, grad_low, grad_norm


def add_sums(sums, grad_low, grad_norm, normed):
    sums[0:1, :] += jnp.sum(grad_low.astype(F32), axis=0, keepdims=True)
    sums[1:2, :] += jnp.sum(grad_norm * normed, axis=0, keepdims=True)
    sums[2:3, :] += jnp.sum(grad_norm, axis=0, keepdims=True)


def own_row(ref, blk, size):
    return ref[pl.ds(pl.multiple_of(blk * size, LANES), size)].reshape(1, size)


def mlp_first_kernel(
    half, meta, xa, xb, ca, cb, gain, shift, b_up, w_up, w_down, w_out,
    gain1, shift1, b_qkv, low, high, w0, w1, w2, w3, w4, w5,
    mo_ref, e_ref, gv_ref, sums, gup, gdown, q_ref, k_ref, v_ref, w_own, b_own, x_s, c_s,
):
    step = pl.program_id(0)

    @pl.when(step < half)
    def _():
        x_s[...] = xa[...]
        c_s[...] = ca[...]

    @pl.when(step >= half)
    def _():
        x_s[...] = xb[...]
        c_s[...] = cb[...]

    @pl.when(step == 0)
    def _():
        sums[...] = jnp.zeros_like(sums)
        gup[...] = jnp.zeros_like(gup)
        gdown[...] = jnp.zeros_like(gdown)
        odd = meta[0] % 2
        own_blocks((w0, w1, w2, w3, w4, w5), odd, w_own)
        own_bias(b_qkv, odd, meta[0], b_own)

    upstream = c_s[...]

    @pl.when(step < half)
    def _():
        sums[3:4, :] += jnp.sum(upstream.astype(F32), axis=0, keepdims=True)

    normed = normalize(x_s[...].astype(F32))
    tile = true_block(meta, step // half) * half + step % half
    project_tile(normed, gain1, shift1, w_own, b_own, low, high, tile, q_ref, k_ref, v_ref)
    bias = own_row(b_up, meta[0], gup.shape[1])
    mlp_in, act, grad_low, grad_norm = feed(normed, upstream, gain, shift, w_up, bias, w_down)
    mo_ref[...] = dot(act, w_down[...]).astype(BF16)
    add_sums(sums, grad_low, grad_norm, normed)
    e_ref[...] = (grad_norm * row(gain)).astype(BF16)
    gv_ref[...] = dot_nt(upstream, w_out[...]).astype(BF16)
    gup[...] += dot_tn(mlp_in, grad_low)
    gdown[...] += dot_tn(upstream, act)


def mlp_second_kernel(
    half, rows, meta, xa, xb, ca, cb, gain, shift, b_up, w_up, w_down, w_out,
    c0, c1, mo_in, o_near, o_far, sums_in, gup, gdown, _,
    e_ref, gv_ref, sums, even, odd, up_keep, up_send, low_keep, low_send, x_s, c_s, n_s, grad,
):
    step = pl.program_id(0)
    hid = gup.shape[1]

    @pl.when(step < half)
    def _():
        x_s[...] = xa[...]
        c_s[...] = ca[...]
        n_s[...] = c0[...]

    @pl.when(step >= half)
    def _():
        x_s[...] = xb[...]
        c_s[...] = cb[...]
        n_s[...] = c1[...]

    @pl.when(step == 0)
    def _():
        sums[...] = sums_in[...]
        grad[:, 0:hid] = gup[...]
        grad[:, hid : 2 * hid] = gdown[...]
        grad[:, 2 * hid :] = jnp.zeros_like(grad[:, 2 * hid :])

    upstream = c_s[...]
    normed = normalize(x_s[...].astype(F32))
    bias = own_row(b_up, meta[0], hid)
    mlp_in, act, grad_low, grad_norm = feed(normed, upstream, gain, shift, w_up, bias, w_down)
    add_sums(sums, grad_low, grad_norm, normed)
    e_ref[...] = (grad_norm * row(gain)).astype(BF16)
    gv_ref[...] = dot_nt(upstream, w_out[...]).astype(BF16)
    grad[:, 0:hid] += dot_tn(mlp_in, grad_low)
    grad[:, hid : 2 * hid] += dot_tn(upstream, act)
    grad[:, 2 * hid : 2 * hid + D // 4] += dot_tn(upstream, o_far[...]) + dot_tn(
        n_s[...], o_near[...]
    )
    far = (dot(act, w_down[...]) + dot(o_far[...], w_out[...])).astype(BF16)
    near = (mo_in[...].astype(F32) + dot(o_near[...], w_out[...])).astype(BF16)

    @pl.when(step < half)
    def _():
        even[0] = near
        even[1] = far

    @pl.when(step >= half)
    def _():
        odd[0] = near
        odd[1] = far

    @pl.when(step == pl.num_programs(0) - 1)
    def _():
        if fits(rows):
            store_chunks(lambda at: grad[at, 0:hid], up_keep, up_send, meta, rows, 1)
            store_chunks(lambda at: grad[at, hid:], low_keep, low_send, meta, rows, 2)
        else:
            up_keep[...] = grad[:, 0:hid].astype(BF16)
            low_keep[...] = grad[:, hid:].astype(BF16)


def feed_forward(
    meta, xs, cs, gain, shift, b_up, w_up, w_down, w_out, rows, seq,
    joined=None, before=None, near=None, attn=None,
):
    per = seq // TILE
    steps = 2 * per
    hid = FF // 4
    width = D // 4
    total = 4 * seq
    first = pl.BlockSpec((TILE, D), lambda i, m: (jnp.minimum(i, per - 1), 0))
    second = pl.BlockSpec((TILE, D), lambda i, m: (jnp.maximum(i - per, 0), 0))
    specs = [
        first,
        second,
        first,
        second,
        whole((D,)),
        whole((D,)),
        whole((FF,)),
        pl.BlockSpec((D, hid), lambda i, m: (0, m[0])),
        pl.BlockSpec((hid, D), lambda i, m: (m[0], 0)),
        pl.BlockSpec((width, D), lambda i, m: (m[0], 0)),
    ]
    args = [*xs, *cs, gain, shift, b_up, w_up, w_down, w_out]
    tile = pl.BlockSpec((TILE, D), lambda i, m: (i, 0))
    narrow = pl.BlockSpec((TILE, width), lambda i, m: (i, 0))
    sums = (8, D)
    scratch = [pltpu.VMEM((TILE, D), BF16), pltpu.VMEM((TILE, D), BF16)]
    pair = jax.ShapeDtypeStruct((steps * TILE, D), BF16)
    vec = jax.ShapeDtypeStruct((total, width), BF16)
    if before is None:
        body = partial(mlp_first_kernel, per)
        gain1, shift1, w_qkv, b_qkv, low, high = joined
        args += [gain1, shift1, b_qkv, low, high]
        specs += [whole(a.shape) for a in args[-5:]]
        for part in range(3):
            for side in range(2):
                specs.append(
                    pl.BlockSpec(
                        (D, LANES),
                        lambda i, m, at=part * D // LANES + side: (0, at + 3 * m[0] // 2),
                    )
                )
                args.append(w_qkv)
        outs = [pair, pair, vec, jax.ShapeDtypeStruct(sums, F32)]
        outs += [jax.ShapeDtypeStruct((D, hid), F32)] * 2 + [vec] * 3
        outs += [
            jax.ShapeDtypeStruct((D, 3 * width), BF16),
            jax.ShapeDtypeStruct((1, 3 * width), F32),
        ]
        out_specs = [tile, tile, narrow, whole(sums)]
        out_specs += [whole((D, hid))] * 2 + [narrow] * 3
        out_specs += [whole((D, 3 * width)), whole((1, 3 * width))]
        aliases = {}
    else:
        body = partial(mlp_second_kernel, per, rows)
        mlp_out, _, grad_vec, sums_in, gup, gdown = before
        chunks = chunk_shapes(hid, rows) + chunk_shapes(hid + 2 * LANES, rows)
        args += [*near, mlp_out, attn, attn, sums_in, gup, gdown, grad_vec]
        specs += [
            first,
            second,
            tile,
            narrow,
            pl.BlockSpec((TILE, width), lambda i, m: (i + steps, 0)),
            whole(sums),
            whole((D, hid)),
            whole((D, hid)),
            pl.BlockSpec(memory_space=pl.ANY),
        ]
        aliases = {len(args): 1}
        both = jax.ShapeDtypeStruct((2, seq, D), BF16)
        outs = [pair, vec, jax.ShapeDtypeStruct(sums, F32), both, both]
        outs += [jax.ShapeDtypeStruct(shape, BF16) for shape in chunks]
        out_specs = [
            tile,
            pl.BlockSpec((TILE, width), lambda i, m: (i + steps, 0)),
            whole(sums),
            pl.BlockSpec((2, TILE, D), lambda i, m: (0, jnp.minimum(i, per - 1), 0)),
            pl.BlockSpec((2, TILE, D), lambda i, m: (0, jnp.maximum(i - per, 0), 0)),
            *(whole(shape) for shape in chunks),
        ]
        scratch += [pltpu.VMEM((TILE, D), BF16), pltpu.VMEM((D, 2 * hid + 2 * LANES), F32)]
    return pl.pallas_call(
        body,
        out_shape=outs,
        grid_spec=pltpu.PrefetchScalarGridSpec(
            num_scalar_prefetch=1,
            grid=(steps,),
            in_specs=specs,
            out_specs=out_specs,
            scratch_shapes=scratch,
        ),
        input_output_aliases=aliases,
        compiler_params=params(),
        cost_estimate=COST,
        name="mlp_first" if before is None else "mlp_second",
    )(meta, *args)


def head_masks():
    lane = lax.broadcasted_iota(jnp.int32, (1, LANES), 1)
    first = jnp.where(lane < HDIM, 1.0, 0.0).astype(BF16)
    second = jnp.where(lane < HDIM, 0.0, 1.0).astype(BF16)
    return first, second


def slot_rows(meta, per, tile):
    slot = jnp.bitwise_xor(tile // per, meta[0])
    return pl.multiple_of((slot * per + tile % per) * TILE, TILE)


def by_head(first, second, block, third):
    return (block * first, block * second, third)


def transpose_all(from_ref, to_ref):
    @pl.loop(0, from_ref.shape[0] // TILE)
    def _(tile):
        rows = pl.ds(pl.multiple_of(tile * TILE, TILE), TILE)
        to_ref[:, rows] = from_ref[rows, :].astype(F32).T.astype(BF16)


def attend_kernel(per, meta, lo, hi, q_ref, k_ref, v_ref, start_ref, o_ref, lse_ref, vt_ref, acc, s_ref):
    mask0, mask1 = head_masks()
    tiles = k_ref.shape[0] // TILE
    qi = pl.program_id(0)

    @pl.when(qi == 0)
    def _():
        ones = jnp.where(lax.broadcasted_iota(jnp.int32, (VROWS - HDIM, TILE), 0) == 0, 1.0, 0.0)

        @pl.loop(0, tiles)
        def _(tile):
            rows = pl.ds(pl.multiple_of(tile * TILE, TILE), TILE)
            block = v_ref[rows, :].astype(F32).T
            for head in range(3):
                at = head * VROWS
                vt_ref[at : at + HDIM, rows] = block[head * HDIM : (head + 1) * HDIM].astype(BF16)
                vt_ref[at + HDIM : at + VROWS, rows] = ones.astype(BF16)

    key_iota = lax.broadcasted_iota(jnp.int32, (TILE, TILE), 0)
    query_iota = lax.broadcasted_iota(jnp.int32, (TILE, TILE), 1)
    queries = by_head(mask0, mask1, q_ref[:, 0:128], q_ref[:, 128:192])
    starts = start_ref[0]
    acc[...] = jnp.zeros_like(acc)

    def key_tile(turn):
        return jnp.where(turn == 0, qi, first + turn - 1)

    def score(masked, ki):
        k_rows = pl.ds(slot_rows(meta, per, ki), TILE)
        pair, third = k_ref[k_rows, 0:128], k_ref[k_rows, 128:192]
        scores = [dot_nt(third if head == 2 else pair, queries[head]) for head in range(3)]
        if masked:
            allowed = (key_iota >= starts - ki * TILE) & (key_iota <= query_iota + (qi - ki) * TILE)
            scores = [jnp.where(allowed, x, MASKED) for x in scores]
        return scores, [jnp.max(x, axis=0, keepdims=True) for x in scores]

    def value(ki, tops, peaks):
        k_rows = pl.ds(slot_rows(meta, per, ki), TILE)
        news = [jnp.maximum(top, peak) for top, peak in zip(tops, peaks)]
        fades = [jnp.exp2(top - new) for top, new in zip(tops, news)]
        weights = [jnp.exp2(s_ref[head] - news[head]).astype(BF16) for head in range(3)]
        terms = [
            dot(vt_ref[head * VROWS : (head + 1) * VROWS, k_rows], weights[head]) for head in range(3)
        ]
        return news, fades, terms

    def put(fades, terms):
        for head in range(3):
            cols = slice(head * VROWS, (head + 1) * VROWS)
            acc[cols, :] = acc[cols, :] * fades[head] + terms[head]

    def visit(masked, turn, carry):
        tops, peaks = carry
        scores, next_peaks = score(masked, key_tile(turn + 1))
        news, fades, terms = value(key_tile(turn), tops, peaks)
        peaks = next_peaks
        for head in range(3):
            s_ref[head] = scores[head]
        put(fades, terms)
        return tuple(news), tuple(peaks)

    first = lo[qi]
    full = jnp.minimum(hi[qi], qi)
    scores, peaks = score(True, qi)
    for head in range(3):
        s_ref[head] = scores[head]
    carry = ((jnp.full((1, TILE), MASKED, F32),) * 3, tuple(peaks))
    carry = lax.fori_loop(0, full - first, partial(visit, True), carry)
    carry = lax.fori_loop(full - first, qi - first, partial(visit, False), carry)
    tops, fades, terms = value(key_tile(qi - first), *carry)
    put(fades, terms)
    heads = []
    for head, top in enumerate(tops):
        at = head * VROWS
        total = acc[at + HDIM : at + HDIM + 1, :]
        heads.append(acc[at : at + HDIM, :] / total)
        lse_ref[head, 0] = top + jnp.log2(total)
    o_ref[...] = jnp.concatenate(heads, axis=0).T.astype(BF16)

def attend(meta, lo, hi, query, keys, values, starts, per):
    total, width = query.shape
    tiles = total // TILE
    def slot(i, m):
        return jnp.bitwise_xor(i // per, m[0]) * per + i % per
    q_spec = pl.BlockSpec((TILE, width), lambda i, m, lo, hi: (slot(i, m), 0))
    start_spec = pl.BlockSpec((1, 1, TILE), lambda i, m, lo, hi: (slot(i, m), 0, 0))
    lse_spec = pl.BlockSpec((3, 1, 1, TILE), lambda i, m, lo, hi: (0, slot(i, m), 0, 0))
    return pl.pallas_call(
        partial(attend_kernel, per),
        out_shape=[
            jax.ShapeDtypeStruct((total, width), BF16),
            jax.ShapeDtypeStruct((3, tiles, 1, TILE), F32),
        ],
        grid_spec=pltpu.PrefetchScalarGridSpec(
            num_scalar_prefetch=3,
            grid=(tiles,),
            in_specs=[q_spec, whole(keys.shape), whole(values.shape), start_spec],
            out_specs=[q_spec, lse_spec],
            scratch_shapes=[pltpu.VMEM((3 * VROWS, total), BF16), pltpu.VMEM((3 * VROWS, TILE), F32), pltpu.VMEM((3, TILE, TILE), F32)],
        ),
        compiler_params=params(),
        cost_estimate=COST,
        name="attend",
    )(meta, lo, hi, query, keys, values, starts)


def attend_back_kernel(
    per, meta, lo, hi, q_ref, k_ref, v_ref, o_ref, gv_ref, start_ref, lse_ref, low, high,
    gj_ref, kt_ref, dk_ref, dv_ref, dqt_ref
):
    mask0, mask1 = head_masks()
    tiles = k_ref.shape[0] // TILE
    qi = tiles - 1 - pl.program_id(0)

    @pl.when(pl.program_id(0) == 0)
    def _():
        transpose_all(k_ref, kt_ref)

    own_rows = pl.ds(slot_rows(meta, per, qi), TILE)
    key_iota = lax.broadcasted_iota(jnp.int32, (TILE, TILE), 0)
    query_iota = lax.broadcasted_iota(jnp.int32, (TILE, TILE), 1)
    queries = by_head(mask0, mask1, q_ref[:, 0:128], q_ref[:, 128:192])
    grads = by_head(mask0, mask1, gv_ref[:, 0:128], gv_ref[:, 128:192])
    starts = start_ref[0]
    lses = [lse_ref[head, 0] for head in range(3)]
    product = (gv_ref[...].astype(F32) * o_ref[...].astype(F32)).T
    deltas = [
        jnp.sum(product[head * HDIM : (head + 1) * HDIM], axis=0, keepdims=True)
        for head in range(3)
    ]
    dqt_ref[...] = jnp.zeros_like(dqt_ref)

    @pl.when(pl.program_id(0) == 0)
    def _():
        dk_ref[...] = jnp.zeros_like(dk_ref)
        dv_ref[...] = jnp.zeros_like(dv_ref)

    def load(ki):
        k_rows = pl.ds(slot_rows(meta, per, ki), TILE)
        return k_rows

    def score(masked, ki):
        k_rows = load(ki)
        pair, third = k_ref[k_rows, 0:128], k_ref[k_rows, 128:192]
        v_pair, v_third = v_ref[k_rows, 0:128], v_ref[k_rows, 128:192]
        scores = [dot_nt(third if head == 2 else pair, queries[head]) for head in range(3)]
        grad_probs = [dot_nt(v_third if head == 2 else v_pair, grads[head]) for head in range(3)]
        if masked:
            allowed = (key_iota >= starts - ki * TILE) & (key_iota <= query_iota + (qi - ki) * TILE)
            scores = [jnp.where(allowed, x, MASKED) for x in scores]
        return scores, grad_probs

    def terms(ki, scores, grad_probs):
        k_rows = load(ki)
        probs = [jnp.exp2(x - lse) for x, lse in zip(scores, lses)]
        grad_scores = [
            (p * (g - delta)).astype(BF16) for p, g, delta in zip(probs, grad_probs, deltas)
        ]
        dv = [dot(p.astype(BF16), g) for p, g in zip(probs, grads)]
        dk = [dot(g, q) for g, q in zip(grad_scores, queries)]
        dq = [
            dot(kt_ref[head * HDIM : (head + 1) * HDIM, k_rows], grad_scores[head])
            for head in range(3)
        ]
        return dk, dv, dq

    def add(ki, dk, dv, dq):
        k_rows = load(ki)
        for into, parts in ((dk_ref, dk), (dv_ref, dv)):
            into[k_rows, 0:128] += parts[0] + parts[1]
            into[k_rows, 128:192] += parts[2]
        for head in range(3):
            dqt_ref[head * HDIM : (head + 1) * HDIM, :] += dq[head]

    first = lo[qi]
    full = jnp.minimum(hi[qi], qi)

    def visit(masked, ki):
        add(ki, *terms(ki, *score(masked, ki)))

    @pl.loop(first, full)
    def _(ki):
        visit(True, ki)

    @pl.loop(full, qi)
    def _(ki):
        visit(False, ki)

    visit(True, qi)

    cos, sin = rotation(low, high, qi)

    def turn_back(block):
        return block * cos - swap_halves(block) * sin

    dq = dqt_ref[...].T * (HDIM**-0.5)
    dk = dk_ref[own_rows, :] * LN2
    gj_ref[:, 0:128] = turn_back(dq[:, 0:128]).astype(BF16)
    gj_ref[:, 128:256] = turn_back(dk[:, 0:128]).astype(BF16)
    mixed = jnp.concatenate([dq[:, 128:192], dk[:, 128:192]], axis=1)
    gj_ref[:, 256:384] = turn_back(mixed).astype(BF16)
    gj_ref[:, 384:576] = dv_ref[own_rows, :].astype(BF16)


def attend_back(
    meta, lo, hi, query, keys, values, attn, grad_vec, starts, lse, low, high, per
):
    total, width = query.shape
    tiles = total // TILE

    def slot(i, m):
        tile = tiles - 1 - i
        return jnp.bitwise_xor(tile // per, m[0]) * per + tile % per

    q_spec = pl.BlockSpec((TILE, width), lambda i, m, lo, hi: (slot(i, m), 0))
    gj_spec = pl.BlockSpec((TILE, 3 * width), lambda i, m, lo, hi: (slot(i, m), 0))
    start_spec = pl.BlockSpec((1, 1, TILE), lambda i, m, lo, hi: (slot(i, m), 0, 0))
    lse_spec = pl.BlockSpec((3, 1, 1, TILE), lambda i, m, lo, hi: (0, slot(i, m), 0, 0))
    return pl.pallas_call(
        partial(attend_back_kernel, per),
        out_shape=jax.ShapeDtypeStruct((total, 3 * width), BF16),
        grid_spec=pltpu.PrefetchScalarGridSpec(
            num_scalar_prefetch=3,
            grid=(tiles,),
            in_specs=[
                q_spec,
                whole(keys.shape),
                whole(values.shape),
                q_spec,
                q_spec,
                start_spec,
                lse_spec,
                whole(low.shape),
                whole(high.shape),
            ],
            out_specs=gj_spec,
            scratch_shapes=[
                pltpu.VMEM((width, total), BF16),
                pltpu.VMEM((total, width), F32),
                pltpu.VMEM((total, width), F32),
                pltpu.VMEM((width, TILE), F32),
            ],
        ),
        compiler_params=params(),
        cost_estimate=COST,
        name="attend_back",
    )(meta, lo, hi, query, keys, values, attn, grad_vec, starts, lse, low, high)


SMALL = 16


def pack_small(gain_sum, shift_sum, bias, mlp_sums):
    third = 3 * D // 4
    which = lax.broadcasted_iota(jnp.int32, (8, D), 0)
    table = jnp.concatenate([jnp.zeros((4, D), F32), mlp_sums[0:4]], axis=0)
    table = jnp.where(which == 0, gain_sum, jnp.where(which == 1, shift_sum, table))
    head = jnp.where(which[:, :third] == 2, bias, table[:, :third])
    tail = jnp.concatenate([table[:, third:], jnp.zeros((8, 2 * third - D), F32)], axis=1)
    return jnp.concatenate([head, tail], axis=0)


def high_low(value):
    high = value.astype(BF16)
    return high, (value - high.astype(F32)).astype(BF16)


def weight_kernel(rows, meta, *refs):
    gjs, xs = refs[0:4], refs[4:8]
    gain, shift, w_ref, mlp_sums, keep, send, small, n_s, gj_s, grad, bias = refs[8:]
    step = pl.program_id(0)

    @pl.when(step == 0)
    def _():
        grad[...] = jnp.zeros_like(grad)
        bias[...] = jnp.zeros_like(bias)

    for index, (gj_ref, x_ref) in enumerate(zip(gjs, xs)):
        at = slice(index * TILE, (index + 1) * TILE)
        n_s[at, :] = normalize(x_ref[...].astype(F32)).astype(BF16)
        gj_s[at, :] = gj_ref[...]
    bias[0:1, :] += jnp.sum(gj_s[...].astype(F32), axis=0, keepdims=True)
    grad[...] += dot_tn(n_s[...], gj_s[...])

    @pl.when(step == pl.num_programs(0) - 1)
    def _():
        total = bias[0:1, :]
        width = total.shape[1]
        parts = jnp.concatenate(
            [*high_low(jnp.broadcast_to(total, (8, width)))], axis=0
        )
        shift_sum = dot_nt(parts, w_ref[...])
        shift_sum = shift_sum[0:1] + shift_sum[8:9]
        ones = jnp.ones((16, width), BF16)
        high, low = high_low(grad[...] * w_ref[...].astype(F32))
        gain_sum = (dot_nt(ones, high) + dot_nt(ones, low))[0:1]
        columns = jnp.concatenate(
            [jnp.broadcast_to(row(gain), (8, D)), jnp.broadcast_to(row(shift), (8, D))], axis=0
        ).T
        grad[...] = grad[...] * columns[:, 0:1] + columns[:, 8:9] * total
        rest = pack_small(gain_sum, shift_sum, total, mlp_sums[...])
        small[...] = rest
        if fits(rows):
            store_chunks(lambda at: grad[at, :], keep, send, meta, rows, 1)
            keep[D // 2 :, :] = rest.astype(BF16)
            send[D // 2 :, :] = rest.astype(BF16)
        else:
            keep[...] = grad[...].astype(BF16)


def slot_tiles(slot, cols, per):
    return pl.BlockSpec((TILE, cols), lambda i, m: (slot * per + i, 0))


def joined_weight(meta, grad, toks, gain, shift, w, mlp_sums, rows, seq):
    width = grad.shape[1]
    per = seq // TILE
    chunks = chunk_shapes(width, rows, SMALL)
    return pl.pallas_call(
        partial(weight_kernel, rows),
        out_shape=[jax.ShapeDtypeStruct(shape, BF16) for shape in chunks]
        + [jax.ShapeDtypeStruct((SMALL, width), F32)],
        grid_spec=pltpu.PrefetchScalarGridSpec(
            num_scalar_prefetch=1,
            grid=(per,),
            in_specs=[
                *(slot_tiles(slot, width, per) for slot in range(4)),
                *(slot_tiles(0, D, per) for _ in range(4)),
                whole(gain.shape),
                whole(shift.shape),
                whole(w.shape),
                whole(mlp_sums.shape),
            ],
            out_specs=[*(whole(shape) for shape in chunks), whole((SMALL, width))],
            scratch_shapes=[
                pltpu.VMEM((4 * TILE, D), BF16),
                pltpu.VMEM((4 * TILE, width), BF16),
                pltpu.VMEM((D, width), F32),
                pltpu.VMEM((8, width), F32),
            ],
        ),
        compiler_params=params(),
        cost_estimate=COST,
        name="joined_weight",
    )(meta, *[grad] * 4, *toks, gain, shift, w, mlp_sums)


def norm_kernel(meta, *refs):
    gjs, es, (gain, w_ref), outs = refs[0:4], refs[4:8], refs[8:10], refs[10:]
    for gj_ref, e_in, out in zip(gjs, es, outs):
        grad_norm = dot_nt(gj_ref[...], w_ref[...])
        out[...] = (grad_norm * row(gain) + e_in[...].astype(F32)).astype(BF16)


def norm_grad(meta, grad, e_mlp, gain, w, seq):
    width = grad.shape[1]
    per = seq // TILE
    return pl.pallas_call(
        norm_kernel,
        out_shape=[jax.ShapeDtypeStruct((seq, D), BF16)] * 4,
        grid_spec=pltpu.PrefetchScalarGridSpec(
            num_scalar_prefetch=1,
            grid=(per,),
            in_specs=[
                *(slot_tiles(slot, width, per) for slot in range(4)),
                *(slot_tiles(slot % 2, D, per) for slot in range(4)),
                whole(gain.shape),
                whole(w.shape),
            ],
            out_specs=[slot_tiles(0, D, per)] * 4,
        ),
        compiler_params=params(),
        cost_estimate=COST,
        name="norm_grad",
    )(meta, *[grad] * 4, e_mlp[0], e_mlp[0], e_mlp[1], e_mlp[1], gain, w)


def simple(body, name, shapes, *args):
    return pl.pallas_call(
        body,
        out_shape=[jax.ShapeDtypeStruct(shape, kind) for shape, kind in shapes],
        grid_spec=pltpu.PrefetchScalarGridSpec(
            num_scalar_prefetch=1,
            grid=(1,),
            in_specs=[whole(a.shape) for a in args[1:]],
            out_specs=[whole(shape) for shape, _ in shapes],
        ),
        compiler_params=params(),
        cost_estimate=COST,
        name=name,
    )(*args)


def last_low_kernel(meta, keep, got, first, second):
    low = (keep[...].astype(F32) + got[...].astype(F32)).astype(BF16)
    hid, side = FF // 4, D // 8
    cut = hid // 2
    even = jnp.concatenate([low[:, :cut], low[:, hid : hid + side]], axis=1)
    odd = jnp.concatenate([low[:, cut:hid], low[:, hid + side : hid + 2 * side]], axis=1)

    @pl.when(meta[1] % 2 == 0)
    def _():
        first[...] = even
        second[...] = odd

    @pl.when(meta[1] % 2 == 1)
    def _():
        first[...] = odd
        second[...] = even


def lower_kernel(meta, first, second, down_ref, out_ref):
    cut = down_ref.shape[0]
    size = first.shape[0]

    def store(ref, at):
        turned = ref[...].astype(F32).T
        down_ref[:, at : at + size] = turned[:cut]
        out_ref[:, at : at + size] = turned[cut:]

    @pl.when(meta[1] % 2 == 0)
    def _():
        store(first, 0)
        store(second, size)

    @pl.when(meta[1] % 2 == 1)
    def _():
        store(second, 0)
        store(first, size)


def last_qkv_kernel(meta, keep, got, kept, near, far, small):
    size = kept.shape[0]
    width = kept.shape[1]
    both = keep[...].astype(F32) + got[...].astype(F32)
    total, rows = both[0:size], both[size:]
    for part in range(3):
        small[part * 8 : part * 8 + 8, :] = rows[0:8, part * width : (part + 1) * width]
    small[24:32, :] = rows[8:16, 0:width]
    near[size:, :] = small[...]
    far[size:, :] = small[...]
    query = jnp.concatenate([total[:, 0:128], total[:, 256:320]], axis=1)
    keys = jnp.concatenate([total[:, 128:256], total[:, 320:384]], axis=1)
    values = total[:, 384:576]
    plans = (
        (query, keys, values),
        (keys, query, values),
        (keys, values, query),
        (values, keys, query),
    )
    for blk, plan in enumerate(plans):

        @pl.when(meta[0] == blk)
        def _(plan=plan):
            kept[...] = plan[0]
            near[0:size, :] = plan[1]
            far[0:size, :] = plan[2]


def assemble_kernel(
    meta, kept, small, near, far, diag,
    qkv, b_qkv, b_out, b_up, b_down, gain1, shift1, gain2, shift2, table,
):
    size, width = kept.shape

    @pl.when(meta[0] % 2 == 0)
    def _():
        qkv[:, 0:width] = kept[...]
        qkv[:, 2 * width :] = far[0:size, :]

    @pl.when(meta[0] % 2 == 1)
    def _():
        qkv[:, 0:width] = far[0:size, :]
        qkv[:, 2 * width :] = kept[...]

    qkv[:, width : 2 * width] = near[0:size, :]
    table[0] = small[...]
    table[1] = near[size:, :]
    table[2] = far[size:, :]
    table[3] = diag[...]
    blocks = [table[jnp.bitwise_xor(meta[0], blk)] for blk in range(4)]
    total = blocks[0] + blocks[1] + blocks[2] + blocks[3]

    def vector(rows, index):
        parts = [rows[part * 8 + index : part * 8 + index + 1, :] for part in range(4)]
        return jnp.concatenate(parts, axis=1)

    for ref, index in ((gain1, 0), (shift1, 1), (gain2, 5), (shift2, 6), (b_out, 7), (b_down, 7)):
        ref[...] = vector(total, index).reshape(D)
    ups, parts = [], ([], [], [])
    for rows in blocks:
        ups.append(vector(rows, 4))
        joined = vector(rows, 2)
        parts[0].append(jnp.concatenate([joined[:, 0:128], joined[:, 256:320]], axis=1))
        parts[1].append(jnp.concatenate([joined[:, 128:256], joined[:, 320:384]], axis=1))
        parts[2].append(joined[:, 384:576])
    b_up[...] = jnp.concatenate(ups, axis=1).reshape(4 * D)
    b_qkv[...] = jnp.concatenate(parts[0] + parts[1] + parts[2], axis=1).reshape(3 * D)


def assemble(meta, kept, small, near, far, diag):
    size, width = kept.shape
    shapes = [((size, 3 * width), F32), ((3 * D,), F32), ((D,), F32), ((4 * D,), F32)]
    shapes += [((D,), F32)] * 5
    args = (kept, small, near, far, diag)
    return pl.pallas_call(
        assemble_kernel,
        out_shape=[jax.ShapeDtypeStruct(shape, kind) for shape, kind in shapes],
        grid_spec=pltpu.PrefetchScalarGridSpec(
            num_scalar_prefetch=1,
            grid=(1,),
            in_specs=[whole(a.shape) for a in args],
            out_specs=[whole(shape) for shape, _ in shapes],
            scratch_shapes=[pltpu.VMEM((4, 32, width), F32)],
        ),
        compiler_params=params(),
        cost_estimate=COST,
        name="assemble",
    )(meta, *args)


def halve(keep, got):
    half = keep.shape[0] // 2
    send = add_low(keep[half:], got[half:])
    return add_low(after(keep, send)[:half], got[:half]), send


def halve_packet(keep, got, extra):
    size = keep.shape[0] - extra
    half = size // 2
    tail = add_low(keep[size:], got[size:])
    send = jnp.concatenate([add_low(keep[half:size], got[half:size]), tail])
    first = add_low(after(keep, send)[:half], got[:half])
    return jnp.concatenate([first, tail]), send


def reduce_plain(keep, got, masks):
    for mask in masks:
        keep, send = halve(keep, got)
        got = swap(send, "rows", mask)
    return keep.astype(F32) + got.astype(F32)


def after(value, *others):
    return lax.optimization_barrier((value, others))[0]


def swap(value, axis, mask):
    size = lax.axis_size(axis)
    return lax.ppermute(value, axis, [(i, i ^ mask) for i in range(size)])


def add_low(left, right):
    return (left.astype(F32) + right.astype(F32)).astype(BF16)


def spread_rows(lower):
    rows, blk = lax.axis_size("rows"), lax.axis_size("blk")
    r = lax.axis_index("rows")
    count = rows // blk
    hid, width = FF // 4, D // 4
    chunk = lower.shape[0]
    down = lower[:, :hid].reshape(chunk, count, hid // count)
    out = lower[:, hid:].reshape(chunk, count, width // count)
    pieces = jnp.concatenate([down, out], axis=2).astype(BF16)
    got = []
    for turn in range(count):
        moves = spread_moves(rows, blk, turn)
        piece = lax.dynamic_index_in_dim(pieces, (r % count) ^ turn, 1, keepdims=False)
        got.append(lax.ppermute(piece, ("rows", "blk"), moves))
    got = jnp.stack(got)
    parts = [
        lax.dynamic_index_in_dim(got, (r % count) ^ part, 0, keepdims=False)
        for part in range(count)
    ]
    whole_cols = jnp.concatenate(parts, axis=0).astype(F32).T
    cut = hid // count
    return whole_cols[:cut], whole_cols[cut:]


def spread_moves(rows, blk, turn):
    count = rows // blk
    moves = []
    for r in range(rows):
        for b in range(blk):
            to = count * b + ((r % count) ^ turn)
            moves.append((r * blk + b, to * blk + r // count))
    return moves


def split_columns(chunk):
    b = lax.axis_index("blk")
    q = jnp.concatenate([chunk[:, 0:128], chunk[:, 256:320]], axis=1)
    k = jnp.concatenate([chunk[:, 128:256], chunk[:, 320:384]], axis=1)
    v = chunk[:, 384:576]

    def choose(zero, one, two, three):
        return jnp.where(b < 2, jnp.where(b == 0, zero, one), jnp.where(b == 2, two, three))

    return choose(q, k, k, v), choose(k, q, v, k), choose(v, v, q, q)


def result_kernel(x_ref, even, near, far, b_out, b_down, out_ref):
    bias = row(b_out) + row(b_down)
    total = even[0].astype(F32) + near[0].astype(F32) + far[...].astype(F32)
    out_ref[...] = (x_ref[...].astype(F32) + bias + total).astype(BF16)


def token_kernel(x_ref, even, near, far, c_ref, out_ref):
    wide = x_ref[...].astype(F32)
    center = wide - jnp.mean(wide, axis=-1, keepdims=True)
    rate = lax.rsqrt(jnp.mean(center * center, axis=-1, keepdims=True) + EPS)
    normed = center * rate
    grad = even[...].astype(F32) + near[...].astype(F32) + far[...].astype(F32)
    mean = jnp.mean(grad, axis=-1, keepdims=True)
    along = jnp.mean(grad * normed, axis=-1, keepdims=True)
    back = rate * (grad - mean - normed * along)
    out_ref[...] = (c_ref[...].astype(F32) + back).astype(BF16)


def finish(body, name, seq, x, even, near, far, *more):
    flat = pl.BlockSpec((TILE, D), lambda i: (i, 0))
    own = pl.BlockSpec((1, TILE, D), lambda i: (0, i, 0))
    return pl.pallas_call(
        body,
        out_shape=jax.ShapeDtypeStruct((seq, D), BF16),
        grid=(seq // TILE,),
        in_specs=[
            *(own if a.ndim == 3 else flat for a in (x, even, near, far)),
            *(flat if a.ndim == 2 else whole(a.shape) for a in more),
        ],
        out_specs=flat,
        compiler_params=params(),
        cost_estimate=COST,
        name=name,
    )(x, even, near, far, *more)


def local(
    tokens, seg_ids, valid_len, ln1_gain, ln1_bias, w_qkv, b_qkv, w_out, b_out,
    ln2_gain, ln2_bias, w_up, b_up, w_down, b_down, cotangent,
):
    rows = lax.axis_size("rows")
    blk = lax.axis_index("blk")
    seq = tokens.shape[1]
    per = seq // TILE
    width = D // 4
    hid = FF // 4
    low, high = angle_parts(4 * seq)
    seg_row = jnp.pad(seg_ids.astype(BF16), ((0, EXTRA - 1), (0, D - seq)))
    tok_own = jnp.concatenate([tokens[0], seg_row], axis=0)
    cot_own = cotangent[0]

    cot_near = swap(cot_own, "blk", 1)
    tok_far = swap(tok_own, "blk", 2)
    tok_near = swap(tok_own, "blk", 1)
    cot_long = jnp.pad(cot_own, ((0, 2 * EXTRA), (0, 0)))
    cot_far = swap(cot_long, "blk", 2)

    meta = jnp.stack([blk, lax.axis_index("rows")]).astype(jnp.int32)
    mlp_args = (ln2_gain, ln2_bias, b_up, w_up, w_down, w_out, rows, seq)
    joined = (ln1_gain, ln1_bias, w_qkv, b_qkv, low, high)
    *first, query, keys, values, w_own, b_own = feed_forward(
        meta, (tok_own, tok_near), (cot_own, cot_near), *mlp_args, joined
    )
    meta = after(meta, b_own)

    def more(slot, m, tok, filled):
        return project(slot, m, tok, ln1_gain, ln1_bias, low, high, w_own, b_own, filled, seq)

    tok_last = swap(after(tok_far, b_own), "blk", 1)
    joined = more(2, meta, tok_far, (query, keys, values))
    toks = (tok_own, tok_near, tok_far, tok_last)
    query, keys, values = more(3, after(meta, joined[0]), tok_last, joined)
    starts, lo, hi = segment_starts(after(meta, query), valid_len, toks, seq)
    cot_last = swap(after(cot_far, lo), "blk", 1)
    cots = (cot_own, cot_near, cot_far, cot_last)
    attn, lse = attend(meta, lo, hi, query, keys, values, starts, per)

    meta = after(meta, lse)
    e_far, grad_vec, mlp_sums, out_even, out_odd, *packets = feed_forward(
        meta, toks[2:], cots[2:], *mlp_args, before=first, near=cots[:2], attn=attn
    )
    e_mlp = (first[1], e_far)
    up_keep, up_send = chunks_of(*packets[:2], rows, 1)
    low_keep, low_send = chunks_of(*packets[2:], rows, 2)
    up_masks, low_masks = mask_order(rows, 1), mask_order(rows, 2)
    out_got = swap(out_odd, "blk", 1)
    up_got = swap(up_send, "rows", up_masks[0])
    low_got = swap(low_send, "rows", low_masks[0])

    meta = after(meta, mlp_sums)
    grad_joined = attend_back(
        meta, lo, hi, query, keys, values, attn, grad_vec, starts, lse, low, high, per
    )
    meta = after(meta, grad_joined)
    qkv_keep, qkv_send, small = joined_weight(
        meta, grad_joined, toks, ln1_gain, ln1_bias, w_own, mlp_sums, rows, seq
    )
    qkv_keep, qkv_send = chunks_of(qkv_keep, qkv_send, rows, 1)
    qkv_got = swap(qkv_send, "rows", 1)

    meta = after(meta, small)
    out_send = add_low(after(out_even, small)[1], out_got[1])
    out_far = swap(out_send, "blk", 2)
    if fits(rows):
        up_keep, up_send = halve(after(up_keep, small), up_got)
        up_got = swap(up_send, "rows", up_masks[1])
        low_keep, low_send = halve(after(low_keep, small), low_got)
        low_got = swap(low_send, "rows", low_masks[1])
        meta = after(meta, up_send, low_send)
    meta = after(meta, out_send)
    e_own, e_near, e_send, e_last = norm_grad(meta, grad_joined, e_mlp, ln1_gain, w_own, seq)
    e_last = swap(e_last, "blk", 1)
    e_near = swap(e_near, "blk", 1)
    if fits(rows):
        chunk = D // rows
        qkv_keep, qkv_send = halve_packet(after(qkv_keep, e_own), qkv_got, SMALL)
        qkv_got = swap(qkv_send, "rows", 2)
        e_send = after(e_send, qkv_send)
    e_send = add_low(e_send, e_last)
    e_far = swap(e_send, "blk", 2)
    if fits(rows):
        out_args = (after(tok_own, e_send), out_even, out_got, out_far, b_out, b_down)
        result = finish(result_kernel, "result", seq, *out_args)
        low_keep, low_send = halve(after(low_keep, result), low_got)
        low_got = swap(low_send, "rows", low_masks[2])
        up_keep, up_send = halve(after(up_keep, low_send), up_got)
        up_got = swap(up_send, "rows", up_masks[2])
        qkv_keep, qkv_send = halve_packet(after(qkv_keep, up_send), qkv_got, SMALL)
        qkv_got = swap(qkv_send, "rows", 4)
        tok_args = (after(tok_own, qkv_send), e_own, e_near, e_far, cot_own)
        grad_tokens = finish(token_kernel, "token_grad", seq, *tok_args)
        meta = after(meta, grad_tokens)
        part = ((chunk, hid // 2 + width // 2), BF16)
        pieces = simple(last_low_kernel, "last_low", [part, part], meta, low_keep, low_got)
        meta = after(meta, pieces[0])
        pieces = [
            lax.ppermute(piece, ("rows", "blk"), spread_moves(rows, 4, turn))
            for turn, piece in enumerate(pieces)
        ]
        packet = ((chunk + 32, width), F32)
        kept, near, far, small = simple(
            last_qkv_kernel,
            "last_qkv",
            [((chunk, width), F32), packet, packet, ((32, width), F32)],
            meta,
            qkv_keep,
            qkv_got,
        )
        near, far, diag = swap(near, "blk", 1), swap(far, "blk", 2), swap(small, "blk", 3)
        up = after(up_keep, small).astype(F32) + up_got.astype(F32)
        lower = [((hid // 2, width), F32), ((width // 2, width), F32)]
        meta = after(meta, up)
        down, out_w = simple(lower_kernel, "lower", lower, meta, *pieces)
        meta = after(meta, down)
        qkv, gb_qkv, gb_out, gb_up, gb_down, *norms = assemble(
            meta, kept, small, near, far, diag
        )
    else:
        up = reduce_plain(up_keep, up_got, up_masks[1:])
        weights = reduce_plain(low_keep, low_got, low_masks[1:])
        qkv = reduce_plain(qkv_keep, qkv_got, up_masks[1:])
        down, out_w = spread_rows(weights[:, : hid + width])
        kept, near, far = split_columns(qkv)
        near, far = swap(near, "blk", 1), swap(far, "blk", 2)
        ends = [jnp.where(blk % 2 == 0, a, b) for a, b in ((kept, far), (far, kept))]
        qkv = jnp.concatenate([ends[0], near, ends[1]], axis=1)
        out_args = (tok_own, out_even, out_got, out_far, b_out, b_down)
        result = finish(result_kernel, "result", seq, *out_args)
        tok_args = (tok_own, e_own, e_near, e_far, cot_own)
        grad_tokens = finish(token_kernel, "token_grad", seq, *tok_args)
        third = 3 * width
        table = jnp.concatenate([small[0:8], small[8:16, : D - third]], axis=1)
        mine = (jnp.arange(4) == blk)[:, None]
        joined = lax.psum(jnp.where(mine, small[2:3], 0.0), ("rows", "blk"))
        gb_up = lax.psum(jnp.where(mine, table[4:5], 0.0), ("rows", "blk")).reshape(FF)
        gb_qkv = jnp.concatenate(
            [
                jnp.concatenate([joined[:, 0:128], joined[:, 256:320]], axis=1).reshape(D),
                jnp.concatenate([joined[:, 128:256], joined[:, 320:384]], axis=1).reshape(D),
                joined[:, 384:576].reshape(D),
            ]
        )
        gain_1, shift_1, _, _, _, gain_2, shift_2, gb_out = lax.psum(table, ("rows", "blk"))
        norms, gb_down = (gain_1, shift_1, gain_2, shift_2), gb_out
    return (
        result[None],
        grad_tokens[None],
        qkv,
        out_w,
        up,
        down,
        gb_qkv,
        gb_out,
        gb_up,
        gb_down,
        *norms,
    )


def solution(mesh):
    split = P("rows", "blk")
    in_specs = (
        P("rows", "blk", None),
        split,
        P("rows"),
        *(P(),) * 12,
        P("rows", "blk", None),
    )
    out_specs = (
        P("rows", "blk", None),
        P("rows", "blk", None),
        *(split,) * 4,
        *(P(),) * 8,
    )
    return jax.shard_map(local, mesh=mesh, in_specs=in_specs, out_specs=out_specs, check_vma=False)
```

```python
import math
from functools import partial

import jax
import jax.numpy as jnp
import numpy as np
from jax import lax
from jax.experimental import pallas as pl
from jax.experimental.pallas import tpu as pltpu
from jax.sharding import PartitionSpec as P

D = 768
HEADS = 12
HDIM = 64
ROT = 16
FF = 3072
EPS = 1e-05
MASKED = -1e30
TILE = 256
VROWS = 80
LN2 = math.log(2.0)
EXTRA = 16
LANES = 128
F32 = jnp.float32
BF16 = jnp.bfloat16
COST = pl.CostEstimate(flops=0, bytes_accessed=0, transcendentals=0)
NT_DIMS = (((1,), (1,)), ((), ()))
TN_DIMS = (((0,), (0,)), ((), ()))


def dot(left, right):
    return jnp.dot(left, right, preferred_element_type=F32)


def dot_nt(left, right):
    return lax.dot_general(left, right, NT_DIMS, preferred_element_type=F32)


def dot_tn(left, right):
    return lax.dot_general(left, right, TN_DIMS, preferred_element_type=F32)


def normalize(value):
    center = value - jnp.mean(value, axis=-1, keepdims=True)
    spread = jnp.mean(center * center, axis=-1, keepdims=True)
    return center * lax.rsqrt(spread + EPS)


def angle_parts(length):
    dim = np.arange(LANES) % HDIM
    inverse = np.where(dim < ROT, 10000.0 ** (-2.0 * (dim % (ROT // 2)) / ROT), 0.0)
    high = (np.arange(length // LANES) * LANES)[:, None] * inverse
    low = np.arange(LANES)[:, None] * inverse
    parts = np.stack([np.cos(low), np.sin(low)]), np.stack([np.cos(high), np.sin(high)])
    return tuple(jnp.asarray(part, F32) for part in parts)


def rotation(low_ref, high_ref, tile):
    lane = lax.broadcasted_iota(jnp.int32, (1, LANES), 1) % HDIM
    sign = jnp.where(lane < ROT // 2, -1.0, 1.0)
    cos_rows, sin_rows = [], []
    for part in range(TILE // LANES):
        row = tile * (TILE // LANES) + part
        cos_high = high_ref[0, pl.ds(row, 1), :]
        sin_high = high_ref[1, pl.ds(row, 1), :]
        cos_rows.append(low_ref[0] * cos_high - low_ref[1] * sin_high)
        sin_rows.append((low_ref[1] * cos_high + low_ref[0] * sin_high) * sign)
    return jnp.concatenate(cos_rows, axis=0), jnp.concatenate(sin_rows, axis=0)


def swap_halves(value):
    lane = lax.broadcasted_iota(jnp.int32, value.shape, 1) % HDIM
    half = ROT // 2
    return jnp.where(
        lane < half, pltpu.roll(value, LANES - half, 1), pltpu.roll(value, half, 1)
    )


def true_block(meta_ref, slot):
    return jnp.bitwise_xor(meta_ref[0], slot)


def params(*semantics, vmem=None):
    return pltpu.CompilerParams(
        dimension_semantics=semantics or ("arbitrary",), vmem_limit_bytes=vmem or 60 * 2**20
    )


def whole(shape):
    return pl.BlockSpec(shape, lambda *_: (0,) * len(shape))


def own_blocks(refs, odd, into):
    places = ((0, 256), (128, 320), (384, 512))
    for part, (pair_at, third_at) in enumerate(places):
        left, right = refs[2 * part], refs[2 * part + 1]

        @pl.when(odd == 0)
        def _(left=left, right=right, pair_at=pair_at, third_at=third_at):
            into[:, pair_at : pair_at + 128] = left[...]
            into[:, third_at : third_at + 64] = right[:, 0:64]

        @pl.when(odd == 1)
        def _(left=left, right=right, pair_at=pair_at, third_at=third_at):
            into[:, pair_at : pair_at + 128] = jnp.concatenate(
                [left[:, 64:128], right[:, 0:64]], axis=1
            )
            into[:, third_at : third_at + 64] = right[:, 64:128]


def row(ref):
    return ref[...].reshape(1, ref.shape[0])


def own_bias(b_ref, odd, blk, into):
    blocks = []
    for part in range(3):
        for side in range(2):
            at = pl.multiple_of((part * (D // LANES) + side + 3 * blk // 2) * LANES, LANES)
            blocks.append(b_ref[pl.ds(at, LANES)].reshape(1, LANES))
    own_blocks(blocks, odd, into)


def project_tile(normed, gain, shift, w_ref, b_ref, low, high, tile, q_ref, k_ref, v_ref):
    attn_in = (normed * row(gain) + row(shift)).astype(BF16)
    joined = dot(attn_in, w_ref[...]) + b_ref[...]
    cos, sin = rotation(low, high, tile)
    scale = HDIM**-0.5 / LN2

    def turn(block):
        return block * cos + swap_halves(block) * sin

    query = turn(joined[:, 0:128]) * scale
    keys = turn(joined[:, 128:256])
    mixed = turn(joined[:, 256:384])
    q_ref[:, 0:128] = query.astype(BF16)
    k_ref[:, 0:128] = keys.astype(BF16)
    q_ref[:, 128:192] = (mixed[:, 0:64] * scale).astype(BF16)
    k_ref[:, 128:192] = mixed[:, 64:128].astype(BF16)
    v_ref[...] = joined[:, 384:576].astype(BF16)


def find_starts(seq, meta, valid, rows, start_ref, lo_ref, hi_ref):
    segs = [ref[0:1, 0:seq].astype(F32) for ref in rows]
    below = [
        sum(jnp.sum((seg < number).astype(F32), axis=1, keepdims=True) for seg in segs)
        for number in (1, 2, 3)
    ]
    per = seq // TILE
    iota = lax.broadcasted_iota(jnp.int32, (1, seq), 1)
    for slot, seg in enumerate(segs):
        block = true_block(meta, slot)
        begin = jnp.zeros((1, seq), F32)
        for number in (1, 2, 3):
            begin = jnp.where(seg == number, below[number - 1], begin)
        pos = iota + block * seq
        begin = jnp.where(pos < valid[0], begin.astype(jnp.int32), pos)
        for part in range(per):
            tile = begin[:, part * TILE : (part + 1) * TILE]
            start_ref[slot * per + part] = tile
            lo_ref[block * per + part] = jnp.min(tile) // TILE
            hi_ref[block * per + part] = (jnp.max(tile) + (TILE - 1)) // TILE


def qkv_kernel(slot, meta, valid, x_ref, gain, shift, low, high, w_ref, b_ref, *refs):
    per = pl.num_programs(0)
    tile = true_block(meta, slot) * per + pl.program_id(0)
    normed = normalize(x_ref[...].astype(F32))
    if slot == 3:
        segs, (*outs, start_ref, lo_ref, hi_ref) = refs[3:7], refs[7:]

        @pl.when(pl.program_id(0) == 0)
        def _():
            find_starts(per * TILE, meta, valid, segs, start_ref, lo_ref, hi_ref)
    else:
        outs = refs[3:]
    project_tile(normed, gain, shift, w_ref, b_ref, low, high, tile, *outs)


def project(slot, meta, valid, x, gain, shift, low, high, w, b, filled, seq, toks=()):
    width = D // 4
    per = seq // TILE
    tiles = 4 * per
    outs = [jax.ShapeDtypeStruct((4 * seq, width), BF16)] * 3
    out_specs = [pl.BlockSpec((TILE, width), lambda i, m, v: (slot * per + i, 0))] * 3
    args = [x, gain, shift, low, high, w, b, *filled, *toks]
    specs = [pl.BlockSpec((TILE, D), lambda i, m, v: (i, 0))]
    specs += [whole(a.shape) for a in args[1:7]]
    specs += [pl.BlockSpec(memory_space=pl.ANY)] * 3
    specs += [pl.BlockSpec((EXTRA, D), lambda i, m, v: (seq // EXTRA, 0)) for _ in toks]
    if toks:
        smem = pl.BlockSpec(memory_space=pltpu.SMEM)
        outs.append(jax.ShapeDtypeStruct((tiles, 1, TILE), jnp.int32))
        outs += [jax.ShapeDtypeStruct((tiles,), jnp.int32)] * 2
        out_specs += [whole((tiles, 1, TILE)), smem, smem]
    return pl.pallas_call(
        partial(qkv_kernel, slot),
        out_shape=outs,
        grid_spec=pltpu.PrefetchScalarGridSpec(
            num_scalar_prefetch=2, grid=(per,), in_specs=specs, out_specs=out_specs
        ),
        input_output_aliases={9 + i: i for i in range(3)},
        compiler_params=params(),
        cost_estimate=COST,
        name=f"qkv_{slot}",
    )(meta, valid, *args)


def mask_order(rows, first):
    masks = [1 << bit for bit in range(rows.bit_length() - 1)]
    return [m for m in masks if m >= first] + [m for m in masks if m < first]


def places(masks):
    order = [0]
    for mask in reversed(masks):
        order = order + [mask + i for i in order]
    return order


def fits(rows):
    return rows == 8 and D // rows % 32 == 0


def store_chunks(load, keep, send, meta, rows, first):
    size = D // rows
    for index, place in enumerate(places(mask_order(rows, first))):
        at = pl.multiple_of(jnp.bitwise_xor(meta[1], place) * size, 32)
        into = keep if index < rows // 2 else send
        row_at = index % (rows // 2) * size
        into[row_at : row_at + size, :] = load(pl.ds(at, size)).astype(into.dtype)


def store_low(grad, keep, send, meta, rows):
    size, hid = D // 4, FF // 4
    for index, place in enumerate(places(mask_order(rows, 2))):
        chunk = jnp.bitwise_xor(meta[1], place)
        at = pl.ds(pl.multiple_of(chunk % 4 * size, 64), size)
        down = pl.multiple_of(hid + chunk // 4 * (hid // 2), LANES)
        out = pl.multiple_of(2 * hid + chunk // 4 * LANES, LANES)
        into = keep if index < rows // 2 else send
        row_at = slice(index % (rows // 2) * size, (index % (rows // 2) + 1) * size)
        into[row_at, : hid // 2] = grad[at, pl.ds(down, hid // 2)].astype(BF16)
        into[row_at, hid // 2 :] = grad[at, pl.ds(out, LANES)].astype(BF16)


def low_shapes(rows):
    if fits(rows):
        return [(D, FF // 8 + LANES)] * 2
    return [(D, FF // 4 + 2 * LANES), (8, LANES)]


def low_chunks(keep, send, rows):
    if fits(rows):
        return keep, send
    hid, width, count = FF // 4, D // 4, rows // 4
    parts = [
        part.reshape(4, width, count, part.shape[1] // count).transpose(2, 0, 1, 3)
        for part in (keep[:, :hid], keep[:, hid : hid + width])
    ]
    chunks = jnp.concatenate(parts, axis=3).reshape(rows, width, -1)
    order = jnp.array(places(mask_order(rows, 2))) ^ lax.axis_index("rows")
    chunks = jnp.take(chunks, order, axis=0).reshape(rows * width, -1)
    return chunks[: rows * width // 2], chunks[rows * width // 2 :]


def chunk_shapes(cols, rows, extra=0):
    if fits(rows):
        return [(D // 2 + extra, cols)] * 2
    return [(D, cols), (8, LANES)]


def chunks_of(keep, send, rows, first):
    if fits(rows):
        return keep, send
    order = jnp.array(places(mask_order(rows, first))) ^ lax.axis_index("rows")
    parts = keep.reshape(rows, D // rows, keep.shape[1])
    parts = jnp.take(parts, order, axis=0).reshape(keep.shape)
    return parts[: D // 2], parts[D // 2 :]


def feed(normed, upstream, gain, shift, w_up, b_up, w_down):
    mlp_in = (normed * row(gain) + row(shift)).astype(BF16)
    hidden = dot(mlp_in, w_up[...]) + b_up
    cdf = 0.5 * (1.0 + lax.erf(hidden * (0.5**0.5)))
    act = (hidden * cdf).astype(BF16)
    slope = cdf + hidden * jnp.exp(-0.5 * hidden * hidden) * ((2.0 * math.pi) ** -0.5)
    grad_low = (slope * dot_nt(upstream, w_down[...])).astype(BF16)
    grad_norm = dot_nt(grad_low, w_up[...])
    return mlp_in, act, grad_low, grad_norm


def add_sums(sums, grad_low, grad_norm, normed):
    sums[0:1, :] += jnp.sum(grad_low.astype(F32), axis=0, keepdims=True)
    sums[1:2, :] += jnp.sum(grad_norm * normed, axis=0, keepdims=True)
    sums[2:3, :] += jnp.sum(grad_norm, axis=0, keepdims=True)


def own_row(ref, blk, size):
    return ref[pl.ds(pl.multiple_of(blk * size, LANES), size)].reshape(1, size)


def mlp_first_kernel(
    half, meta, xa, xb, ca, cb, gain, shift, b_up, w_up, w_down, w_out,
    gain1, shift1, b_qkv, low, high, w0, w1, w2, w3, w4, w5,
    mo_ref, e_ref, n_ref, gv_ref, sums, gup, gdown, q_ref, k_ref, v_ref, w_own, b_own, x_s, c_s,
):
    step = pl.program_id(0)

    @pl.when(step < half)
    def _():
        x_s[...] = xa[...]
        c_s[...] = ca[...]

    @pl.when(step >= half)
    def _():
        x_s[...] = xb[...]
        c_s[...] = cb[...]

    @pl.when(step == 0)
    def _():
        sums[...] = jnp.zeros_like(sums)
        gup[...] = jnp.zeros_like(gup)
        gdown[...] = jnp.zeros_like(gdown)
        odd = meta[0] % 2
        own_blocks((w0, w1, w2, w3, w4, w5), odd, w_own)
        own_bias(b_qkv, odd, meta[0], b_own)

    upstream = c_s[...]

    @pl.when(step < half)
    def _():
        sums[3:4, :] += jnp.sum(upstream.astype(F32), axis=0, keepdims=True)

    normed = normalize(x_s[...].astype(F32))
    n_ref[...] = normed.astype(BF16)
    tile = true_block(meta, step // half) * half + step % half
    project_tile(normed, gain1, shift1, w_own, b_own, low, high, tile, q_ref, k_ref, v_ref)
    bias = own_row(b_up, meta[0], gup.shape[1])
    mlp_in, act, grad_low, grad_norm = feed(normed, upstream, gain, shift, w_up, bias, w_down)
    mo_ref[...] = dot(act, w_down[...]).astype(BF16)
    add_sums(sums, grad_low, grad_norm, normed)
    e_ref[...] = (grad_norm * row(gain)).astype(BF16)
    gv_ref[...] = dot_nt(upstream, w_out[...]).astype(BF16)
    gup[...] += dot_tn(mlp_in, grad_low)
    gdown[...] += dot_tn(upstream, act)


def mlp_second_kernel(
    half, rows, meta, xa, xb, ca, cb, gain, shift, b_up, w_up, w_down, w_out,
    c0, c1, mo_in, o_near, o_far, sums_in, gup, gdown, *refs
):
    e_ref, n_ref, gv_ref, sums, even, odd, up_keep, up_send, low_keep, low_send = refs[3:13]
    x_s, c_s, n_s, grad = refs[13:]
    step = pl.program_id(0)
    hid = gup.shape[1]

    @pl.when(step < half)
    def _():
        x_s[...] = xa[...]
        c_s[...] = ca[...]
        n_s[...] = c0[...]

    @pl.when(step >= half)
    def _():
        x_s[...] = xb[...]
        c_s[...] = cb[...]
        n_s[...] = c1[...]

    @pl.when(step == 0)
    def _():
        sums[...] = sums_in[...]
        grad[:, 0:hid] = gup[...]
        grad[:, hid : 2 * hid] = gdown[...]
        grad[:, 2 * hid :] = jnp.zeros_like(grad[:, 2 * hid :])

    upstream = c_s[...]
    normed = normalize(x_s[...].astype(F32))
    n_ref[...] = normed.astype(BF16)
    bias = own_row(b_up, meta[0], hid)
    mlp_in, act, grad_low, grad_norm = feed(normed, upstream, gain, shift, w_up, bias, w_down)
    add_sums(sums, grad_low, grad_norm, normed)
    e_ref[...] = (grad_norm * row(gain)).astype(BF16)
    gv_ref[...] = dot_nt(upstream, w_out[...]).astype(BF16)
    grad[:, 0:hid] += dot_tn(mlp_in, grad_low)
    grad[:, hid : 2 * hid] += dot_tn(upstream, act)
    out_grad = dot_tn(upstream, o_far[...]) + dot_tn(n_s[...], o_near[...])
    side = out_grad.shape[1] // 2
    if fits(rows):
        grad[:, 2 * hid : 2 * hid + side] += out_grad[:, :side]
        grad[:, 2 * hid + LANES : 2 * hid + LANES + side] += out_grad[:, side:]
    else:
        grad[:, 2 * hid : 2 * hid + 2 * side] += out_grad
    far = (dot(act, w_down[...]) + dot(o_far[...], w_out[...])).astype(BF16)
    near = (mo_in[...].astype(F32) + dot(o_near[...], w_out[...])).astype(BF16)

    @pl.when(step < half)
    def _():
        even[0] = near
        even[1] = far

    @pl.when(step >= half)
    def _():
        odd[0] = near
        odd[1] = far

    @pl.when(step == pl.num_programs(0) - 1)
    def _():
        if fits(rows):
            store_chunks(lambda at: grad[at, 0:hid], up_keep, up_send, meta, rows, 1)
            store_low(grad, low_keep, low_send, meta, rows)
        else:
            up_keep[...] = grad[:, 0:hid].astype(BF16)
            low_keep[...] = grad[:, hid:].astype(BF16)


def feed_forward(
    meta, xs, cs, gain, shift, b_up, w_up, w_down, w_out, rows, seq,
    joined=None, before=None, near=None, attn=None,
):
    per = seq // TILE
    steps = 2 * per
    hid = FF // 4
    width = D // 4
    total = 4 * seq
    first = pl.BlockSpec((TILE, D), lambda i, m: (jnp.minimum(i, per - 1), 0))
    second = pl.BlockSpec((TILE, D), lambda i, m: (jnp.maximum(i - per, 0), 0))
    specs = [
        first,
        second,
        first,
        second,
        whole((D,)),
        whole((D,)),
        whole((FF,)),
        pl.BlockSpec((D, hid), lambda i, m: (0, m[0])),
        pl.BlockSpec((hid, D), lambda i, m: (m[0], 0)),
        pl.BlockSpec((width, D), lambda i, m: (m[0], 0)),
    ]
    args = [*xs, *cs, gain, shift, b_up, w_up, w_down, w_out]
    tile = pl.BlockSpec((TILE, D), lambda i, m: (i, 0))
    narrow = pl.BlockSpec((TILE, width), lambda i, m: (i, 0))
    sums = (8, D)
    scratch = [pltpu.VMEM((TILE, D), BF16), pltpu.VMEM((TILE, D), BF16)]
    pair = jax.ShapeDtypeStruct((steps * TILE, D), BF16)
    full = jax.ShapeDtypeStruct((total, D), BF16)
    vec = jax.ShapeDtypeStruct((total, width), BF16)
    if before is None:
        body = partial(mlp_first_kernel, per)
        gain1, shift1, w_qkv, b_qkv, low, high = joined
        args += [gain1, shift1, b_qkv, low, high]
        specs += [whole(a.shape) for a in args[-5:]]
        for part in range(3):
            for side in range(2):
                specs.append(
                    pl.BlockSpec(
                        (D, LANES),
                        lambda i, m, at=part * D // LANES + side: (0, at + 3 * m[0] // 2),
                    )
                )
                args.append(w_qkv)
        outs = [pair, full, full, vec, jax.ShapeDtypeStruct(sums, F32)]
        outs += [jax.ShapeDtypeStruct((D, hid), F32)] * 2 + [vec] * 3
        outs += [
            jax.ShapeDtypeStruct((D, 3 * width), BF16),
            jax.ShapeDtypeStruct((1, 3 * width), F32),
        ]
        out_specs = [tile, tile, tile, narrow, whole(sums)]
        out_specs += [whole((D, hid))] * 2 + [narrow] * 3
        out_specs += [whole((D, 3 * width)), whole((1, 3 * width))]
        aliases = {}
    else:
        body = partial(mlp_second_kernel, per, rows)
        mlp_out, norm_part, normed, grad_vec, sums_in, gup, gdown = before
        chunks = chunk_shapes(hid, rows) + low_shapes(rows)
        args += [*near, mlp_out, attn, attn, sums_in, gup, gdown, norm_part, normed, grad_vec]
        specs += [
            first,
            second,
            tile,
            narrow,
            pl.BlockSpec((TILE, width), lambda i, m: (i + steps, 0)),
            whole(sums),
            whole((D, hid)),
            whole((D, hid)),
            *(pl.BlockSpec(memory_space=pl.ANY),) * 3,
        ]
        aliases = {len(args) - 2 + i: i for i in range(3)}
        both = jax.ShapeDtypeStruct((2, seq, D), BF16)
        outs = [full, full, vec, jax.ShapeDtypeStruct(sums, F32), both, both]
        late = pl.BlockSpec((TILE, D), lambda i, m: (i + steps, 0))
        outs += [jax.ShapeDtypeStruct(shape, BF16) for shape in chunks]
        out_specs = [
            late,
            late,
            pl.BlockSpec((TILE, width), lambda i, m: (i + steps, 0)),
            whole(sums),
            pl.BlockSpec((2, TILE, D), lambda i, m: (0, jnp.minimum(i, per - 1), 0)),
            pl.BlockSpec((2, TILE, D), lambda i, m: (0, jnp.maximum(i - per, 0), 0)),
            *(whole(shape) for shape in chunks),
        ]
        scratch += [pltpu.VMEM((TILE, D), BF16), pltpu.VMEM((D, 2 * hid + 2 * LANES), F32)]
    return pl.pallas_call(
        body,
        out_shape=outs,
        grid_spec=pltpu.PrefetchScalarGridSpec(
            num_scalar_prefetch=1,
            grid=(steps,),
            in_specs=specs,
            out_specs=out_specs,
            scratch_shapes=scratch,
        ),
        input_output_aliases=aliases,
        compiler_params=params(),
        cost_estimate=COST,
        name="mlp_first" if before is None else "mlp_second",
    )(meta, *args)


def head_masks():
    lane = lax.broadcasted_iota(jnp.int32, (1, LANES), 1)
    first = jnp.where(lane < HDIM, 1.0, 0.0).astype(BF16)
    second = jnp.where(lane < HDIM, 0.0, 1.0).astype(BF16)
    return first, second


def slot_rows(meta, per, tile):
    slot = jnp.bitwise_xor(tile // per, meta[0])
    return pl.multiple_of((slot * per + tile % per) * TILE, TILE)


def by_head(first, second, block, third):
    return (block * first, block * second, third)


def transpose_all(from_ref, to_ref):
    @pl.loop(0, from_ref.shape[0] // TILE)
    def _(tile):
        rows = pl.ds(pl.multiple_of(tile * TILE, TILE), TILE)
        to_ref[:, rows] = from_ref[rows, :].astype(F32).T.astype(BF16)


def attend_kernel(per, meta, lo, hi, q_ref, k_ref, v_ref, start_ref, o_ref, lse_ref, vt_ref, acc, s_ref):
    mask0, mask1 = head_masks()
    tiles = k_ref.shape[0] // TILE
    qi = pl.program_id(0)

    @pl.when(qi == 0)
    def _():
        ones = jnp.where(lax.broadcasted_iota(jnp.int32, (VROWS - HDIM, TILE), 0) == 0, 1.0, 0.0)

        @pl.loop(0, tiles)
        def _(tile):
            rows = pl.ds(pl.multiple_of(tile * TILE, TILE), TILE)
            block = v_ref[rows, :].astype(F32).T
            for head in range(3):
                at = head * VROWS
                vt_ref[at : at + HDIM, rows] = block[head * HDIM : (head + 1) * HDIM].astype(BF16)
                vt_ref[at + HDIM : at + VROWS, rows] = ones.astype(BF16)

    key_iota = lax.broadcasted_iota(jnp.int32, (TILE, TILE), 0)
    query_iota = lax.broadcasted_iota(jnp.int32, (TILE, TILE), 1)
    queries = by_head(mask0, mask1, q_ref[:, 0:128], q_ref[:, 128:192])
    starts = start_ref[0]
    acc[...] = jnp.zeros_like(acc)

    def key_tile(turn):
        return jnp.where(turn == 0, qi, first + turn - 1)

    def score(masked, ki):
        k_rows = pl.ds(slot_rows(meta, per, ki), TILE)
        pair, third = k_ref[k_rows, 0:128], k_ref[k_rows, 128:192]
        scores = [dot_nt(third if head == 2 else pair, queries[head]) for head in range(3)]
        if masked:
            allowed = (key_iota >= starts - ki * TILE) & (key_iota <= query_iota + (qi - ki) * TILE)
            scores = [jnp.where(allowed, x, MASKED) for x in scores]
        return scores, [jnp.max(x, axis=0, keepdims=True) for x in scores]

    def value(ki, tops, peaks):
        k_rows = pl.ds(slot_rows(meta, per, ki), TILE)
        news = [jnp.maximum(top, peak) for top, peak in zip(tops, peaks)]
        fades = [jnp.exp2(top - new) for top, new in zip(tops, news)]
        weights = [jnp.exp2(s_ref[head] - news[head]).astype(BF16) for head in range(3)]
        terms = [
            dot(vt_ref[head * VROWS : (head + 1) * VROWS, k_rows], weights[head]) for head in range(3)
        ]
        return news, fades, terms

    def put(fades, terms):
        for head in range(3):
            cols = slice(head * VROWS, (head + 1) * VROWS)
            acc[cols, :] = acc[cols, :] * fades[head] + terms[head]

    def visit(masked, turn, carry):
        tops, peaks = carry
        scores, next_peaks = score(masked, key_tile(turn + 1))
        news, fades, terms = value(key_tile(turn), tops, peaks)
        peaks = next_peaks
        for head in range(3):
            s_ref[head] = scores[head]
        put(fades, terms)
        return tuple(news), tuple(peaks)

    first = lo[qi]
    full = jnp.minimum(hi[qi], qi)
    scores, peaks = score(True, qi)
    for head in range(3):
        s_ref[head] = scores[head]
    carry = ((jnp.full((1, TILE), MASKED, F32),) * 3, tuple(peaks))
    carry = lax.fori_loop(0, full - first, partial(visit, True), carry)
    carry = lax.fori_loop(full - first, qi - first, partial(visit, False), carry)
    tops, fades, terms = value(key_tile(qi - first), *carry)
    put(fades, terms)
    heads = []
    for head, top in enumerate(tops):
        at = head * VROWS
        total = acc[at + HDIM : at + HDIM + 1, :]
        heads.append(acc[at : at + HDIM, :] / total)
        lse_ref[head, 0] = top + jnp.log2(total)
    o_ref[...] = jnp.concatenate(heads, axis=0).T.astype(BF16)

def attend(meta, lo, hi, query, keys, values, starts, per):
    total, width = query.shape
    tiles = total // TILE
    def slot(i, m):
        return jnp.bitwise_xor(i // per, m[0]) * per + i % per
    q_spec = pl.BlockSpec((TILE, width), lambda i, m, lo, hi: (slot(i, m), 0))
    start_spec = pl.BlockSpec((1, 1, TILE), lambda i, m, lo, hi: (slot(i, m), 0, 0))
    lse_spec = pl.BlockSpec((3, 1, 1, TILE), lambda i, m, lo, hi: (0, slot(i, m), 0, 0))
    return pl.pallas_call(
        partial(attend_kernel, per),
        out_shape=[
            jax.ShapeDtypeStruct((total, width), BF16),
            jax.ShapeDtypeStruct((3, tiles, 1, TILE), F32),
        ],
        grid_spec=pltpu.PrefetchScalarGridSpec(
            num_scalar_prefetch=3,
            grid=(tiles,),
            in_specs=[q_spec, whole(keys.shape), whole(values.shape), start_spec],
            out_specs=[q_spec, lse_spec],
            scratch_shapes=[pltpu.VMEM((3 * VROWS, total), BF16), pltpu.VMEM((3 * VROWS, TILE), F32), pltpu.VMEM((3, TILE, TILE), F32)],
        ),
        compiler_params=params(),
        cost_estimate=COST,
        name="attend",
    )(meta, lo, hi, query, keys, values, starts)


def attend_back_kernel(
    per, meta, lo, hi, q_ref, k_ref, v_ref, o_ref, gv_ref, start_ref, lse_ref, low, high,
    gj_ref, kt_ref, dk_ref, dv_ref, dqt_ref
):
    mask0, mask1 = head_masks()
    tiles = k_ref.shape[0] // TILE
    qi = tiles - 1 - pl.program_id(0)

    @pl.when(pl.program_id(0) == 0)
    def _():
        transpose_all(k_ref, kt_ref)

    own_rows = pl.ds(slot_rows(meta, per, qi), TILE)
    key_iota = lax.broadcasted_iota(jnp.int32, (TILE, TILE), 0)
    query_iota = lax.broadcasted_iota(jnp.int32, (TILE, TILE), 1)
    queries = by_head(mask0, mask1, q_ref[:, 0:128], q_ref[:, 128:192])
    grads = by_head(mask0, mask1, gv_ref[:, 0:128], gv_ref[:, 128:192])
    starts = start_ref[0]
    lses = [lse_ref[head, 0] for head in range(3)]
    product = (gv_ref[...].astype(F32) * o_ref[...].astype(F32)).T
    deltas = [
        jnp.sum(product[head * HDIM : (head + 1) * HDIM], axis=0, keepdims=True)
        for head in range(3)
    ]
    dqt_ref[...] = jnp.zeros_like(dqt_ref)

    @pl.when(pl.program_id(0) == 0)
    def _():
        dk_ref[...] = jnp.zeros_like(dk_ref)
        dv_ref[...] = jnp.zeros_like(dv_ref)

    def load(ki):
        k_rows = pl.ds(slot_rows(meta, per, ki), TILE)
        return k_rows

    def score(masked, ki):
        k_rows = load(ki)
        pair, third = k_ref[k_rows, 0:128], k_ref[k_rows, 128:192]
        v_pair, v_third = v_ref[k_rows, 0:128], v_ref[k_rows, 128:192]
        scores = [dot_nt(third if head == 2 else pair, queries[head]) for head in range(3)]
        grad_probs = [dot_nt(v_third if head == 2 else v_pair, grads[head]) for head in range(3)]
        if masked:
            allowed = (key_iota >= starts - ki * TILE) & (key_iota <= query_iota + (qi - ki) * TILE)
            scores = [jnp.where(allowed, x, MASKED) for x in scores]
        return scores, grad_probs

    def terms(ki, scores, grad_probs):
        k_rows = load(ki)
        probs = [jnp.exp2(x - lse) for x, lse in zip(scores, lses)]
        grad_scores = [
            (p * (g - delta)).astype(BF16) for p, g, delta in zip(probs, grad_probs, deltas)
        ]
        dv = [dot(p.astype(BF16), g) for p, g in zip(probs, grads)]
        dk = [dot(g, q) for g, q in zip(grad_scores, queries)]
        dq = [
            dot(kt_ref[head * HDIM : (head + 1) * HDIM, k_rows], grad_scores[head])
            for head in range(3)
        ]
        return dk, dv, dq

    def add(ki, dk, dv, dq):
        k_rows = load(ki)
        for into, parts in ((dk_ref, dk), (dv_ref, dv)):
            into[k_rows, 0:128] += parts[0] + parts[1]
            into[k_rows, 128:192] += parts[2]
        for head in range(3):
            dqt_ref[head * HDIM : (head + 1) * HDIM, :] += dq[head]

    first = lo[qi]
    full = jnp.minimum(hi[qi], qi)

    def visit(masked, ki):
        add(ki, *terms(ki, *score(masked, ki)))

    @pl.loop(first, full)
    def _(ki):
        visit(True, ki)

    @pl.loop(full, qi)
    def _(ki):
        visit(False, ki)

    visit(True, qi)

    cos, sin = rotation(low, high, qi)

    def turn_back(block):
        return block * cos - swap_halves(block) * sin

    dq = dqt_ref[...].T * (HDIM**-0.5)
    dk = dk_ref[own_rows, :] * LN2
    gj_ref[:, 0:128] = turn_back(dq[:, 0:128]).astype(BF16)
    gj_ref[:, 128:256] = turn_back(dk[:, 0:128]).astype(BF16)
    mixed = jnp.concatenate([dq[:, 128:192], dk[:, 128:192]], axis=1)
    gj_ref[:, 256:384] = turn_back(mixed).astype(BF16)
    gj_ref[:, 384:576] = dv_ref[own_rows, :].astype(BF16)


def attend_back(
    meta, lo, hi, query, keys, values, attn, grad_vec, starts, lse, low, high, per
):
    total, width = query.shape
    tiles = total // TILE

    def slot(i, m):
        tile = tiles - 1 - i
        return jnp.bitwise_xor(tile // per, m[0]) * per + tile % per

    q_spec = pl.BlockSpec((TILE, width), lambda i, m, lo, hi: (slot(i, m), 0))
    gj_spec = pl.BlockSpec((TILE, 3 * width), lambda i, m, lo, hi: (slot(i, m), 0))
    start_spec = pl.BlockSpec((1, 1, TILE), lambda i, m, lo, hi: (slot(i, m), 0, 0))
    lse_spec = pl.BlockSpec((3, 1, 1, TILE), lambda i, m, lo, hi: (0, slot(i, m), 0, 0))
    return pl.pallas_call(
        partial(attend_back_kernel, per),
        out_shape=jax.ShapeDtypeStruct((total, 3 * width), BF16),
        grid_spec=pltpu.PrefetchScalarGridSpec(
            num_scalar_prefetch=3,
            grid=(tiles,),
            in_specs=[
                q_spec,
                whole(keys.shape),
                whole(values.shape),
                q_spec,
                q_spec,
                start_spec,
                lse_spec,
                whole(low.shape),
                whole(high.shape),
            ],
            out_specs=gj_spec,
            scratch_shapes=[
                pltpu.VMEM((width, total), BF16),
                pltpu.VMEM((total, width), F32),
                pltpu.VMEM((total, width), F32),
                pltpu.VMEM((width, TILE), F32),
            ],
        ),
        compiler_params=params(),
        cost_estimate=COST,
        name="attend_back",
    )(meta, lo, hi, query, keys, values, attn, grad_vec, starts, lse, low, high)


SMALL = 16


def pack_small(gain_sum, shift_sum, bias, mlp_sums):
    third = 3 * D // 4
    which = lax.broadcasted_iota(jnp.int32, (8, D), 0)
    table = jnp.concatenate([jnp.zeros((4, D), F32), mlp_sums[0:4]], axis=0)
    table = jnp.where(which == 0, gain_sum, jnp.where(which == 1, shift_sum, table))
    head = jnp.where(which[:, :third] == 2, bias, table[:, :third])
    tail = jnp.concatenate([table[:, third:], jnp.zeros((8, 2 * third - D), F32)], axis=1)
    return jnp.concatenate([head, tail], axis=0)


def high_low(value):
    high = value.astype(BF16)
    return high, (value - high.astype(F32)).astype(BF16)


def weight_kernel(rows, meta, *refs):
    gj_ref, n_ref, gain, shift, w_ref, mlp_sums, keep, send, small, grad, bias = refs
    step = pl.program_id(0)

    @pl.when(step == 0)
    def _():
        grad[...] = jnp.zeros_like(grad)
        bias[...] = jnp.zeros_like(bias)

    joined = gj_ref[...]
    bias[0:1, :] += jnp.sum(joined.astype(F32), axis=0, keepdims=True)
    grad[...] += dot_tn(n_ref[...], joined)

    @pl.when(step == pl.num_programs(0) - 1)
    def _():
        total = bias[0:1, :]
        width = total.shape[1]
        parts = jnp.concatenate(
            [*high_low(jnp.broadcast_to(total, (8, width)))], axis=0
        )
        shift_sum = dot_nt(parts, w_ref[...])
        shift_sum = shift_sum[0:1] + shift_sum[8:9]
        ones = jnp.ones((16, width), BF16)
        high, low = high_low(grad[...] * w_ref[...].astype(F32))
        gain_sum = (dot_nt(ones, high) + dot_nt(ones, low))[0:1]
        columns = jnp.concatenate(
            [jnp.broadcast_to(row(gain), (8, D)), jnp.broadcast_to(row(shift), (8, D))], axis=0
        ).T
        grad[...] = grad[...] * columns[:, 0:1] + columns[:, 8:9] * total
        rest = pack_small(gain_sum, shift_sum, total, mlp_sums[...])
        small[...] = rest
        if fits(rows):
            store_chunks(lambda at: grad[at, :], keep, send, meta, rows, 1)
            keep[D // 2 :, :] = rest.astype(BF16)
            send[D // 2 :, :] = rest.astype(BF16)
        else:
            keep[...] = grad[...].astype(BF16)


def row_tiles(cols, tile=TILE):
    return pl.BlockSpec((tile, cols), lambda i, m: (i, 0))


def joined_weight(meta, grad, normed, gain, shift, w, mlp_sums, rows):
    total, width = grad.shape
    tile = 2 * TILE
    chunks = chunk_shapes(width, rows, SMALL)
    args = [gain, shift, w, mlp_sums]
    return pl.pallas_call(
        partial(weight_kernel, rows),
        out_shape=[jax.ShapeDtypeStruct(shape, BF16) for shape in chunks]
        + [jax.ShapeDtypeStruct((SMALL, width), F32)],
        grid_spec=pltpu.PrefetchScalarGridSpec(
            num_scalar_prefetch=1,
            grid=(total // tile,),
            in_specs=[row_tiles(width, tile), row_tiles(D, tile), *(whole(a.shape) for a in args)],
            out_specs=[*(whole(shape) for shape in chunks), whole((SMALL, width))],
            scratch_shapes=[pltpu.VMEM((D, width), F32), pltpu.VMEM((8, width), F32)],
        ),
        compiler_params=params(),
        cost_estimate=COST,
        name="joined_weight",
    )(meta, grad, normed, *args)


def norm_kernel(per, meta, gj_ref, e_in, gain, w_ref, *outs):
    grad_norm = dot_nt(gj_ref[...], w_ref[...])
    value = (grad_norm * row(gain) + e_in[...].astype(F32)).astype(BF16)
    for slot, out in enumerate(outs):

        @pl.when(pl.program_id(0) // per == slot)
        def _(out=out):
            out[...] = value


def norm_grad(meta, grad, e_mlp, gain, w, seq):
    per = seq // TILE

    def slot_out(slot):
        return pl.BlockSpec((TILE, D), lambda i, m: (jnp.clip(i - slot * per, 0, per - 1), 0))

    return pl.pallas_call(
        partial(norm_kernel, per),
        out_shape=[jax.ShapeDtypeStruct((seq, D), BF16)] * 4,
        grid_spec=pltpu.PrefetchScalarGridSpec(
            num_scalar_prefetch=1,
            grid=(4 * per,),
            in_specs=[
                row_tiles(grad.shape[1]),
                row_tiles(D),
                whole(gain.shape),
                whole(w.shape),
            ],
            out_specs=[slot_out(slot) for slot in range(4)],
        ),
        compiler_params=params(),
        cost_estimate=COST,
        name="norm_grad",
    )(meta, grad, e_mlp, gain, w)


def simple(body, name, shapes, *args, specs=None):
    return pl.pallas_call(
        body,
        out_shape=[jax.ShapeDtypeStruct(shape, kind) for shape, kind in shapes],
        grid_spec=pltpu.PrefetchScalarGridSpec(
            num_scalar_prefetch=1,
            grid=(1,),
            in_specs=specs or [whole(a.shape) for a in args[1:]],
            out_specs=[whole(shape) for shape, _ in shapes],
        ),
        compiler_params=params(),
        cost_estimate=COST,
        name=name,
    )(*args)


def add_up(refs):
    total = refs[0][...].astype(F32)
    for ref in refs[1:]:
        total += ref[...].astype(F32)
    return total


def lower_kernel(meta, piece, down_ref, out_ref):
    cut = down_ref.shape[1]
    down_ref[...] = piece[:, :cut].astype(F32)
    out_ref[...] = piece[:, cut:].astype(F32).T[: out_ref.shape[0]]


def last_qkv_kernel(meta, *refs):
    *terms, sums, got_sums, kept, near, far, small = refs
    size = kept.shape[0]
    width = kept.shape[1]
    total = add_up(terms)
    rows = sums[...].astype(F32) + got_sums[...].astype(F32)
    for part in range(3):
        small[part * 8 : part * 8 + 8, :] = rows[0:8, part * width : (part + 1) * width]
    small[24:32, :] = rows[8:16, 0:width]
    near[size:, :] = small[...]
    far[size:, :] = small[...]
    query = jnp.concatenate([total[:, 0:128], total[:, 256:320]], axis=1)
    keys = jnp.concatenate([total[:, 128:256], total[:, 320:384]], axis=1)
    values = total[:, 384:576]
    plans = (
        (query, keys, values),
        (keys, query, values),
        (keys, values, query),
        (values, keys, query),
    )
    for blk, plan in enumerate(plans):

        @pl.when(meta[0] == blk)
        def _(plan=plan):
            kept[...] = plan[0]
            near[0:size, :] = plan[1]
            far[0:size, :] = plan[2]


def assemble_kernel(
    meta, kept, small, near, far, diag,
    qkv, b_qkv, b_out, b_up, b_down, gain1, shift1, gain2, shift2, table,
):
    size, width = kept.shape

    @pl.when(meta[0] % 2 == 0)
    def _():
        qkv[:, 0:width] = kept[...]
        qkv[:, 2 * width :] = far[0:size, :]

    @pl.when(meta[0] % 2 == 1)
    def _():
        qkv[:, 0:width] = far[0:size, :]
        qkv[:, 2 * width :] = kept[...]

    qkv[:, width : 2 * width] = near[0:size, :]
    table[0] = small[...]
    table[1] = near[size:, :]
    table[2] = far[size:, :]
    table[3] = diag[...]
    blocks = [table[jnp.bitwise_xor(meta[0], blk)] for blk in range(4)]
    total = blocks[0] + blocks[1] + blocks[2] + blocks[3]

    def vector(rows, index):
        parts = [rows[part * 8 + index : part * 8 + index + 1, :] for part in range(4)]
        return jnp.concatenate(parts, axis=1)

    for ref, index in ((gain1, 0), (shift1, 1), (gain2, 5), (shift2, 6), (b_out, 7), (b_down, 7)):
        ref[...] = vector(total, index).reshape(D)
    ups, parts = [], ([], [], [])
    for rows in blocks:
        ups.append(vector(rows, 4))
        joined = vector(rows, 2)
        parts[0].append(jnp.concatenate([joined[:, 0:128], joined[:, 256:320]], axis=1))
        parts[1].append(jnp.concatenate([joined[:, 128:256], joined[:, 320:384]], axis=1))
        parts[2].append(joined[:, 384:576])
    b_up[...] = jnp.concatenate(ups, axis=1).reshape(4 * D)
    b_qkv[...] = jnp.concatenate(parts[0] + parts[1] + parts[2], axis=1).reshape(3 * D)


def assemble(meta, kept, small, near, far, diag):
    size, width = kept.shape
    shapes = [((size, 3 * width), F32), ((3 * D,), F32), ((D,), F32), ((4 * D,), F32)]
    shapes += [((D,), F32)] * 5
    args = (kept, small, near, far, diag)
    return pl.pallas_call(
        assemble_kernel,
        out_shape=[jax.ShapeDtypeStruct(shape, kind) for shape, kind in shapes],
        grid_spec=pltpu.PrefetchScalarGridSpec(
            num_scalar_prefetch=1,
            grid=(1,),
            in_specs=[whole(a.shape) for a in args],
            out_specs=[whole(shape) for shape, _ in shapes],
            scratch_shapes=[pltpu.VMEM((4, 32, width), F32)],
        ),
        compiler_params=params(),
        cost_estimate=COST,
        name="assemble",
    )(meta, *args)


def next_send(terms, size):
    return sum(term[size // 2 : size].astype(F32) for term in terms).astype(BF16)


def reduce_plain(keep, got, masks):
    terms, size = [keep, got], keep.shape[0]
    for mask in masks:
        terms.append(swap(next_send(terms, size), "rows", mask))
        size //= 2
    return sum(term[:size].astype(F32) for term in terms)


def after(value, *others):
    return lax.optimization_barrier((value, others))[0]


def swap(value, axis, mask):
    size = lax.axis_size(axis)
    return lax.ppermute(value, axis, [(i, i ^ mask) for i in range(size)])


def add_low(left, right):
    return (left.astype(F32) + right.astype(F32)).astype(BF16)


def spread_rows(chunk):
    rows = lax.axis_size("rows")
    moves = [
        (r * 4 + b, (rows // 4 * b + r // 4) * 4 + r % 4) for r in range(rows) for b in range(4)
    ]
    return lax.ppermute(chunk, ("rows", "blk"), moves)


def split_columns(chunk):
    b = lax.axis_index("blk")
    q = jnp.concatenate([chunk[:, 0:128], chunk[:, 256:320]], axis=1)
    k = jnp.concatenate([chunk[:, 128:256], chunk[:, 320:384]], axis=1)
    v = chunk[:, 384:576]

    def choose(zero, one, two, three):
        return jnp.where(b < 2, jnp.where(b == 0, zero, one), jnp.where(b == 2, two, three))

    return choose(q, k, k, v), choose(k, q, v, k), choose(v, v, q, q)


def result_kernel(x_ref, even, near, far, b_out, b_down, out_ref):
    bias = row(b_out) + row(b_down)
    total = even[0].astype(F32) + near[0].astype(F32) + far[...].astype(F32)
    out_ref[...] = (x_ref[...].astype(F32) + bias + total).astype(BF16)


def token_kernel(x_ref, even, near, far, c_ref, out_ref):
    wide = x_ref[...].astype(F32)
    center = wide - jnp.mean(wide, axis=-1, keepdims=True)
    rate = lax.rsqrt(jnp.mean(center * center, axis=-1, keepdims=True) + EPS)
    normed = center * rate
    grad = even[...].astype(F32) + near[...].astype(F32) + far[...].astype(F32)
    mean = jnp.mean(grad, axis=-1, keepdims=True)
    along = jnp.mean(grad * normed, axis=-1, keepdims=True)
    back = rate * (grad - mean - normed * along)
    out_ref[...] = (c_ref[...].astype(F32) + back).astype(BF16)


def finish(body, name, seq, x, even, near, far, *more):
    flat = pl.BlockSpec((TILE, D), lambda i: (i, 0))
    own = pl.BlockSpec((1, TILE, D), lambda i: (0, i, 0))
    return pl.pallas_call(
        body,
        out_shape=jax.ShapeDtypeStruct((seq, D), BF16),
        grid=(seq // TILE,),
        in_specs=[
            *(own if a.ndim == 3 else flat for a in (x, even, near, far)),
            *(flat if a.ndim == 2 else whole(a.shape) for a in more),
        ],
        out_specs=flat,
        compiler_params=params(),
        cost_estimate=COST,
        name=name,
    )(x, even, near, far, *more)


def local(
    tokens, seg_ids, valid_len, ln1_gain, ln1_bias, w_qkv, b_qkv, w_out, b_out,
    ln2_gain, ln2_bias, w_up, b_up, w_down, b_down, cotangent,
):
    rows = lax.axis_size("rows")
    blk = lax.axis_index("blk")
    seq = tokens.shape[1]
    per = seq // TILE
    width = D // 4
    hid = FF // 4
    low, high = angle_parts(4 * seq)
    seg_row = jnp.pad(seg_ids.astype(BF16), ((0, EXTRA - 1), (0, D - seq)))
    tok_own = jnp.concatenate([tokens[0], seg_row], axis=0)
    cot_own = cotangent[0]

    cot_near = swap(cot_own, "blk", 1)
    tok_far = swap(tok_own, "blk", 2)
    tok_near = swap(tok_own, "blk", 1)
    cot_long = jnp.pad(cot_own, ((0, 2 * EXTRA), (0, 0)))
    cot_far = swap(cot_long, "blk", 2)

    meta = jnp.stack([blk, lax.axis_index("rows")]).astype(jnp.int32)
    mlp_args = (ln2_gain, ln2_bias, b_up, w_up, w_down, w_out, rows, seq)
    joined = (ln1_gain, ln1_bias, w_qkv, b_qkv, low, high)
    *first, query, keys, values, w_own, b_own = feed_forward(
        meta, (tok_own, tok_near), (cot_own, cot_near), *mlp_args, joined
    )
    meta = after(meta, b_own)

    def more(slot, m, tok, filled, slots=()):
        args = (ln1_gain, ln1_bias, low, high, w_own, b_own, filled, seq, slots)
        return project(slot, m, valid_len, tok, *args)

    tok_last = swap(after(tok_far, b_own), "blk", 1)
    joined = more(2, meta, tok_far, (query, keys, values))
    toks = (tok_own, tok_near, tok_far, tok_last)
    query, keys, values, starts, lo, hi = more(
        3, after(meta, joined[0]), tok_last, joined, toks
    )
    cot_last = swap(after(cot_far, lo), "blk", 1)
    cots = (cot_own, cot_near, cot_far, cot_last)
    attn, lse = attend(meta, lo, hi, query, keys, values, starts, per)

    meta = after(meta, lse)
    e_mlp, normed, grad_vec, mlp_sums, out_even, out_odd, *packets = feed_forward(
        meta, toks[2:], cots[2:], *mlp_args, before=first, near=cots[:2], attn=attn
    )
    up_keep, up_send = chunks_of(*packets[:2], rows, 1)
    low_keep, low_send = low_chunks(*packets[2:], rows)
    up_masks, low_masks = mask_order(rows, 1), mask_order(rows, 2)
    out_got = swap(out_odd, "blk", 1)
    up_got = swap(up_send, "rows", up_masks[0])
    low_got = swap(low_send, "rows", low_masks[0])

    meta = after(meta, mlp_sums)
    grad_joined = attend_back(
        meta, lo, hi, query, keys, values, attn, grad_vec, starts, lse, low, high, per
    )
    meta = after(meta, grad_joined)
    qkv_keep, qkv_send, small = joined_weight(
        meta, grad_joined, normed, ln1_gain, ln1_bias, w_own, mlp_sums, rows
    )
    qkv_keep, qkv_send = chunks_of(qkv_keep, qkv_send, rows, 1)
    qkv_got = swap(qkv_send, "rows", 1)

    meta = after(meta, qkv_keep)
    out_send = add_low(after(out_even, qkv_keep)[1], out_got[1])
    out_far = swap(out_send, "blk", 2)
    half = D // 2
    if fits(rows):
        up = [after(up_keep, qkv_keep), up_got]
        up_send = next_send(up, half)
        up.append(swap(up_send, "rows", up_masks[1]))
        lower = [after(low_keep, qkv_keep), low_got]
        low_send = next_send(lower, D)
        lower.append(swap(low_send, "rows", low_masks[1]))
        meta = after(meta, up_send, low_send)
    meta = after(meta, out_send)
    e_own, e_near, e_send, e_last = norm_grad(meta, grad_joined, e_mlp, ln1_gain, w_own, seq)
    e_last = swap(e_last, "blk", 1)
    e_near = swap(e_near, "blk", 1)
    if fits(rows):
        chunk = D // rows
        joined = [after(qkv_keep, e_own), qkv_got]
        tail = add_low(joined[0][half:], qkv_got[half:])
        qkv_send = jnp.concatenate([next_send(joined, half), tail])
        joined.append(swap(qkv_send, "rows", 2))
        e_send = after(e_send, qkv_send)
    e_send = add_low(e_send, e_last)
    e_far = swap(e_send, "blk", 2)
    if fits(rows):
        lower[0] = after(lower[0], e_send)
        low_send = next_send(lower, half)
        lower.append(swap(low_send, "rows", low_masks[2]))
        up[0] = after(up[0], low_send)
        up_send = next_send(up, half // 2)
        up.append(swap(up_send, "rows", up_masks[2]))
        joined[0] = after(joined[0], up_send)
        tail = add_low(after(qkv_send, up_send)[half // 2 :], joined[2][half // 2 :])
        qkv_send = jnp.concatenate([next_send(joined, half // 2), tail])
        joined.append(swap(qkv_send, "rows", 4))
        out_args = (after(tok_own, qkv_send), out_even, out_got, out_far, b_out, b_down)
        result = finish(result_kernel, "result", seq, *out_args)
        meta = after(meta, result)
        lower[0] = after(lower[0], result)
        piece = sum(term[:width].astype(F32) for term in lower).astype(BF16)
        meta = after(meta, piece)
        piece = spread_rows(piece)
        packet = ((chunk + 32, width), F32)
        last = pl.BlockSpec((SMALL, 3 * width), lambda i, m: (chunk // SMALL, 0))
        kept, near, far, small = simple(
            last_qkv_kernel,
            "last_qkv",
            [((chunk, width), F32), packet, packet, ((32, width), F32)],
            meta,
            *joined,
            qkv_send,
            joined[3],
            specs=[pl.BlockSpec((chunk, 3 * width), lambda i, m: (0, 0))] * 4 + [last] * 2,
        )
        near, far, diag = swap(near, "blk", 1), swap(far, "blk", 2), swap(small, "blk", 3)
        tok_args = (after(tok_own, small), e_own, e_near, e_far, cot_own)
        grad_tokens = finish(token_kernel, "token_grad", seq, *tok_args)
        up[0] = after(up[0], grad_tokens)
        up = sum(term[:chunk].astype(F32) for term in up)
        ends = [((width, hid // 2), F32), ((width // 2, width), F32)]
        meta = after(meta, up)
        down, out_w = simple(lower_kernel, "lower", ends, meta, piece)
        meta = after(meta, down)
        down = down.T
        qkv, gb_qkv, gb_out, gb_up, gb_down, *norms = assemble(
            meta, kept, small, near, far, diag
        )
    else:
        up = reduce_plain(up_keep, up_got, up_masks[1:])
        weights = reduce_plain(low_keep, low_got, low_masks[1:])
        qkv = reduce_plain(qkv_keep, qkv_got, up_masks[1:])
        piece = spread_rows(weights).T
        cut = 4 * hid // rows
        down, out_w = piece[:cut], piece[cut:]
        kept, near, far = split_columns(qkv)
        near, far = swap(near, "blk", 1), swap(far, "blk", 2)
        ends = [jnp.where(blk % 2 == 0, a, b) for a, b in ((kept, far), (far, kept))]
        qkv = jnp.concatenate([ends[0], near, ends[1]], axis=1)
        out_args = (tok_own, out_even, out_got, out_far, b_out, b_down)
        result = finish(result_kernel, "result", seq, *out_args)
        tok_args = (tok_own, e_own, e_near, e_far, cot_own)
        grad_tokens = finish(token_kernel, "token_grad", seq, *tok_args)
        third = 3 * width
        table = jnp.concatenate([small[0:8], small[8:16, : D - third]], axis=1)
        mine = (jnp.arange(4) == blk)[:, None]
        joined = lax.psum(jnp.where(mine, small[2:3], 0.0), ("rows", "blk"))
        gb_up = lax.psum(jnp.where(mine, table[4:5], 0.0), ("rows", "blk")).reshape(FF)
        gb_qkv = jnp.concatenate(
            [
                jnp.concatenate([joined[:, 0:128], joined[:, 256:320]], axis=1).reshape(D),
                jnp.concatenate([joined[:, 128:256], joined[:, 320:384]], axis=1).reshape(D),
                joined[:, 384:576].reshape(D),
            ]
        )
        gain_1, shift_1, _, _, _, gain_2, shift_2, gb_out = lax.psum(table, ("rows", "blk"))
        norms, gb_down = (gain_1, shift_1, gain_2, shift_2), gb_out
    return (
        result[None],
        grad_tokens[None],
        qkv,
        out_w,
        up,
        down,
        gb_qkv,
        gb_out,
        gb_up,
        gb_down,
        *norms,
    )


def solution(mesh):
    split = P("rows", "blk")
    in_specs = (
        P("rows", "blk", None),
        split,
        P("rows"),
        *(P(),) * 12,
        P("rows", "blk", None),
    )
    out_specs = (
        P("rows", "blk", None),
        P("rows", "blk", None),
        *(split,) * 4,
        *(P(),) * 8,
    )
    return jax.shard_map(local, mesh=mesh, in_specs=in_specs, out_specs=out_specs, check_vma=False)
```

```python
import math
from functools import partial

import jax
import jax.numpy as jnp
import numpy as np
from jax import lax
from jax.experimental import pallas as pl
from jax.experimental.pallas import tpu as pltpu
from jax.sharding import PartitionSpec as P

D = 768
HEADS = 12
HDIM = 64
ROT = 16
FF = 3072
EPS = 1e-05
MASKED = -1e30
TILE = 256
VROWS = 80
LN2 = math.log(2.0)
EXTRA = 16
LANES = 128
F32 = jnp.float32
BF16 = jnp.bfloat16
COST = pl.CostEstimate(flops=0, bytes_accessed=0, transcendentals=0)
NT_DIMS = (((1,), (1,)), ((), ()))
TN_DIMS = (((0,), (0,)), ((), ()))


def dot(left, right):
    return jnp.dot(left, right, preferred_element_type=F32)


def dot_nt(left, right):
    return lax.dot_general(left, right, NT_DIMS, preferred_element_type=F32)


def dot_tn(left, right):
    return lax.dot_general(left, right, TN_DIMS, preferred_element_type=F32)


def normalize(value):
    center = value - jnp.mean(value, axis=-1, keepdims=True)
    spread = jnp.mean(center * center, axis=-1, keepdims=True)
    return center * lax.rsqrt(spread + EPS)


def angle_parts(length):
    dim = np.arange(LANES) % HDIM
    inverse = np.where(dim < ROT, 10000.0 ** (-2.0 * (dim % (ROT // 2)) / ROT), 0.0)
    high = (np.arange(length // LANES) * LANES)[:, None] * inverse
    low = np.arange(LANES)[:, None] * inverse
    parts = np.stack([np.cos(low), np.sin(low)]), np.stack([np.cos(high), np.sin(high)])
    return tuple(jnp.asarray(part, F32) for part in parts)


def rotation(low_ref, high_ref, tile):
    lane = lax.broadcasted_iota(jnp.int32, (1, LANES), 1) % HDIM
    sign = jnp.where(lane < ROT // 2, -1.0, 1.0)
    cos_rows, sin_rows = [], []
    for part in range(TILE // LANES):
        row = tile * (TILE // LANES) + part
        cos_high = high_ref[0, pl.ds(row, 1), :]
        sin_high = high_ref[1, pl.ds(row, 1), :]
        cos_rows.append(low_ref[0] * cos_high - low_ref[1] * sin_high)
        sin_rows.append((low_ref[1] * cos_high + low_ref[0] * sin_high) * sign)
    return jnp.concatenate(cos_rows, axis=0), jnp.concatenate(sin_rows, axis=0)


def swap_halves(value):
    lane = lax.broadcasted_iota(jnp.int32, value.shape, 1) % HDIM
    half = ROT // 2
    return jnp.where(
        lane < half, pltpu.roll(value, LANES - half, 1), pltpu.roll(value, half, 1)
    )


def true_block(meta_ref, slot):
    return jnp.bitwise_xor(meta_ref[0], slot)


def params(*semantics, vmem=None):
    return pltpu.CompilerParams(
        dimension_semantics=semantics or ("arbitrary",), vmem_limit_bytes=vmem or 67_043_328
    )


def whole(shape):
    return pl.BlockSpec(shape, lambda *_: (0,) * len(shape))


def own_blocks(refs, odd, into):
    places = ((0, 256), (128, 320), (384, 512))
    for part, (pair_at, third_at) in enumerate(places):
        left, right = refs[2 * part], refs[2 * part + 1]

        @pl.when(odd == 0)
        def _(left=left, right=right, pair_at=pair_at, third_at=third_at):
            into[:, pair_at : pair_at + 128] = left[...]
            into[:, third_at : third_at + 64] = right[:, 0:64]

        @pl.when(odd == 1)
        def _(left=left, right=right, pair_at=pair_at, third_at=third_at):
            into[:, pair_at : pair_at + 128] = jnp.concatenate(
                [left[:, 64:128], right[:, 0:64]], axis=1
            )
            into[:, third_at : third_at + 64] = right[:, 64:128]


def row(ref):
    return ref[...].reshape(1, ref.shape[0])


def own_bias(b_ref, odd, blk, into):
    blocks = []
    for part in range(3):
        for side in range(2):
            at = pl.multiple_of((part * (D // LANES) + side + 3 * blk // 2) * LANES, LANES)
            blocks.append(b_ref[pl.ds(at, LANES)].reshape(1, LANES))
    own_blocks(blocks, odd, into)


def project_tile(normed, gain, shift, w_ref, b_ref, low, high, tile, q_ref, k_ref, v_ref):
    attn_in = (normed * row(gain) + row(shift)).astype(BF16)
    joined = dot(attn_in, w_ref[...]) + b_ref[...]
    cos, sin = rotation(low, high, tile)
    scale = HDIM**-0.5 / LN2

    def turn(block):
        return block * cos + swap_halves(block) * sin

    query = turn(joined[:, 0:128]) * scale
    keys = turn(joined[:, 128:256])
    mixed = turn(joined[:, 256:384])
    q_ref[:, 0:128] = query.astype(BF16)
    k_ref[:, 0:128] = keys.astype(BF16)
    q_ref[:, 128:192] = (mixed[:, 0:64] * scale).astype(BF16)
    k_ref[:, 128:192] = mixed[:, 64:128].astype(BF16)
    v_ref[...] = joined[:, 384:576].astype(BF16)


def find_starts(seq, meta, valid, rows, start_ref, lo_ref, hi_ref):
    segs = [ref[0:1, 0:seq].astype(F32) for ref in rows]
    below = [
        sum(jnp.sum((seg < number).astype(F32), axis=1, keepdims=True) for seg in segs)
        for number in (1, 2, 3)
    ]
    per = seq // TILE
    iota = lax.broadcasted_iota(jnp.int32, (1, seq), 1)
    for slot, seg in enumerate(segs):
        block = true_block(meta, slot)
        begin = jnp.zeros((1, seq), F32)
        for number in (1, 2, 3):
            begin = jnp.where(seg == number, below[number - 1], begin)
        pos = iota + block * seq
        begin = jnp.where(pos < valid[0], begin.astype(jnp.int32), pos)
        for part in range(per):
            tile = begin[:, part * TILE : (part + 1) * TILE]
            start_ref[slot * per + part] = tile
            lo_ref[block * per + part] = jnp.min(tile) // TILE
            hi_ref[block * per + part] = (jnp.max(tile) + (TILE - 1)) // TILE


def qkv_kernel(slot, meta, valid, x_ref, gain, shift, low, high, w_ref, b_ref, *refs):
    per = pl.num_programs(0)
    tile = true_block(meta, slot) * per + pl.program_id(0)
    normed = normalize(x_ref[...].astype(F32))
    if slot == 3:
        segs, (*outs, start_ref, lo_ref, hi_ref) = refs[3:7], refs[7:]

        @pl.when(pl.program_id(0) == 0)
        def _():
            find_starts(per * TILE, meta, valid, segs, start_ref, lo_ref, hi_ref)
    else:
        outs = refs[3:]
    project_tile(normed, gain, shift, w_ref, b_ref, low, high, tile, *outs)


def project(slot, meta, valid, x, gain, shift, low, high, w, b, filled, seq, toks=()):
    width = D // 4
    per = seq // TILE
    tiles = 4 * per
    outs = [jax.ShapeDtypeStruct((4 * seq, width), BF16)] * 3
    out_specs = [pl.BlockSpec((TILE, width), lambda i, m, v: (slot * per + i, 0))] * 3
    args = [x, gain, shift, low, high, w, b, *filled, *toks]
    specs = [pl.BlockSpec((TILE, D), lambda i, m, v: (i, 0))]
    specs += [whole(a.shape) for a in args[1:7]]
    specs += [pl.BlockSpec(memory_space=pl.ANY)] * 3
    specs += [pl.BlockSpec((EXTRA, D), lambda i, m, v: (seq // EXTRA, 0)) for _ in toks]
    if toks:
        smem = pl.BlockSpec(memory_space=pltpu.SMEM)
        outs.append(jax.ShapeDtypeStruct((tiles, 1, TILE), jnp.int32))
        outs += [jax.ShapeDtypeStruct((tiles,), jnp.int32)] * 2
        out_specs += [whole((tiles, 1, TILE)), smem, smem]
    return pl.pallas_call(
        partial(qkv_kernel, slot),
        out_shape=outs,
        grid_spec=pltpu.PrefetchScalarGridSpec(
            num_scalar_prefetch=2, grid=(per,), in_specs=specs, out_specs=out_specs
        ),
        input_output_aliases={9 + i: i for i in range(3)},
        compiler_params=params(),
        cost_estimate=COST,
        name=f"qkv_{slot}",
    )(meta, valid, *args)


def mask_order(rows, first):
    masks = [1 << bit for bit in range(rows.bit_length() - 1)]
    return masks if first == 1 else masks[1::-1] + masks[2:]


def places(masks):
    order = [0]
    for mask in reversed(masks):
        order = order + [mask + i for i in order]
    return order


def fits(rows):
    return rows == 8 and D // rows % 32 == 0


def store_chunks(load, keep, send, meta, rows, first):
    size = D // rows
    for index, place in enumerate(places(mask_order(rows, first))):
        at = pl.multiple_of(jnp.bitwise_xor(meta[1], place) * size, 32)
        into = keep if index < rows // 2 else send
        row_at = index % (rows // 2) * size
        into[row_at : row_at + size, :] = load(pl.ds(at, size)).astype(into.dtype)


def store_low(grad, keep, send, meta, rows):
    size, hid = D // 4, FF // 4
    for index, place in enumerate(places(mask_order(rows, 2))):
        chunk = jnp.bitwise_xor(meta[1], place)
        at = pl.ds(pl.multiple_of(chunk % 4 * size, 64), size)
        down = pl.multiple_of(hid + chunk // 4 * (hid // 2), LANES)
        out = pl.multiple_of(2 * hid + chunk // 4 * LANES, LANES)
        into = keep if index < rows // 2 else send
        row_at = slice(index % (rows // 2) * size, (index % (rows // 2) + 1) * size)
        into[row_at, : hid // 2] = grad[at, pl.ds(down, hid // 2)].astype(BF16)
        into[row_at, hid // 2 :] = grad[at, pl.ds(out, LANES)].astype(BF16)


def low_shapes(rows):
    if fits(rows):
        return [(D, FF // 8 + LANES)] * 2
    return [(D, FF // 4 + 2 * LANES), (8, LANES)]


def low_chunks(keep, send, rows):
    if fits(rows):
        return keep, send
    hid, width, count = FF // 4, D // 4, rows // 4
    parts = [
        part.reshape(4, width, count, part.shape[1] // count).transpose(2, 0, 1, 3)
        for part in (keep[:, :hid], keep[:, hid : hid + width])
    ]
    chunks = jnp.concatenate(parts, axis=3).reshape(rows, width, -1)
    order = jnp.array(places(mask_order(rows, 2))) ^ lax.axis_index("rows")
    chunks = jnp.take(chunks, order, axis=0).reshape(rows * width, -1)
    return chunks[: rows * width // 2], chunks[rows * width // 2 :]


def chunk_shapes(cols, rows, extra=0):
    if fits(rows):
        return [(D // 2 + extra, cols)] * 2
    return [(D, cols), (8, LANES)]


def chunks_of(keep, send, rows, first):
    if fits(rows):
        return keep, send
    order = jnp.array(places(mask_order(rows, first))) ^ lax.axis_index("rows")
    parts = keep.reshape(rows, D // rows, keep.shape[1])
    parts = jnp.take(parts, order, axis=0).reshape(keep.shape)
    return parts[: D // 2], parts[D // 2 :]


def feed(normed, upstream, gain, shift, w_up, b_up, w_down):
    mlp_in = (normed * row(gain) + row(shift)).astype(BF16)
    hidden = dot(mlp_in, w_up[...]) + b_up
    cdf = 0.5 * (1.0 + lax.erf(hidden * (0.5**0.5)))
    act = (hidden * cdf).astype(BF16)
    slope = cdf + hidden * jnp.exp(-0.5 * hidden * hidden) * ((2.0 * math.pi) ** -0.5)
    grad_low = (slope * dot_nt(upstream, w_down[...])).astype(BF16)
    grad_norm = dot_nt(grad_low, w_up[...])
    return mlp_in, act, grad_low, grad_norm


def add_sums(sums, grad_low, grad_norm, normed):
    sums[0:1, :] += jnp.sum(grad_low.astype(F32), axis=0, keepdims=True)
    sums[1:2, :] += jnp.sum(grad_norm * normed, axis=0, keepdims=True)
    sums[2:3, :] += jnp.sum(grad_norm, axis=0, keepdims=True)


def own_row(ref, blk, size):
    return ref[pl.ds(pl.multiple_of(blk * size, LANES), size)].reshape(1, size)


def mlp_first_kernel(
    half, meta, xa, xb, ca, cb, gain, shift, b_up, w_up, w_down, w_out,
    gain1, shift1, b_qkv, low, high, w0, w1, w2, w3, w4, w5,
    mo_ref, e_ref, n_ref, gv_ref, sums, gup, gdown, q_ref, k_ref, v_ref, w_own, b_own, x_s, c_s,
):
    step = pl.program_id(0)

    @pl.when(step < half)
    def _():
        x_s[...] = xa[...]
        c_s[...] = ca[...]

    @pl.when(step >= half)
    def _():
        x_s[...] = xb[...]
        c_s[...] = cb[...]

    @pl.when(step == 0)
    def _():
        sums[...] = jnp.zeros_like(sums)
        gup[...] = jnp.zeros_like(gup)
        gdown[...] = jnp.zeros_like(gdown)
        odd = meta[0] % 2
        own_blocks((w0, w1, w2, w3, w4, w5), odd, w_own)
        own_bias(b_qkv, odd, meta[0], b_own)

    upstream = c_s[...]

    @pl.when(step < half)
    def _():
        sums[3:4, :] += jnp.sum(upstream.astype(F32), axis=0, keepdims=True)

    normed = normalize(x_s[...].astype(F32))
    n_ref[...] = normed.astype(BF16)
    tile = true_block(meta, step // half) * half + step % half
    project_tile(normed, gain1, shift1, w_own, b_own, low, high, tile, q_ref, k_ref, v_ref)
    bias = own_row(b_up, meta[0], gup.shape[1])
    mlp_in, act, grad_low, grad_norm = feed(normed, upstream, gain, shift, w_up, bias, w_down)
    mo_ref[...] = dot(act, w_down[...]).astype(BF16)
    add_sums(sums, grad_low, grad_norm, normed)
    e_ref[...] = (grad_norm * row(gain)).astype(BF16)
    gv_ref[...] = dot_nt(upstream, w_out[...]).astype(BF16)
    gup[...] += dot_tn(mlp_in, grad_low)
    gdown[...] += dot_tn(upstream, act)


def mlp_second_kernel(
    half, rows, meta, xa, xb, ca, cb, gain, shift, b_up, w_up, w_down, w_out,
    c0, c1, mo_in, o_near, o_far, sums_in, gup, gdown, *refs
):
    e_ref, n_ref, gv_ref, sums, even, odd, up_keep, up_send, low_keep, low_send = refs[3:13]
    x_s, c_s, n_s, grad = refs[13:]
    step = pl.program_id(0)
    hid = gup.shape[1]

    @pl.when(step < half)
    def _():
        x_s[...] = xa[...]
        c_s[...] = ca[...]
        n_s[...] = c0[...]

    @pl.when(step >= half)
    def _():
        x_s[...] = xb[...]
        c_s[...] = cb[...]
        n_s[...] = c1[...]

    @pl.when(step == 0)
    def _():
        sums[...] = sums_in[...]
        grad[:, 0:hid] = gup[...]
        grad[:, hid : 2 * hid] = gdown[...]
        grad[:, 2 * hid :] = jnp.zeros_like(grad[:, 2 * hid :])

    upstream = c_s[...]
    normed = normalize(x_s[...].astype(F32))
    n_ref[...] = normed.astype(BF16)
    bias = own_row(b_up, meta[0], hid)
    mlp_in, act, grad_low, grad_norm = feed(normed, upstream, gain, shift, w_up, bias, w_down)
    add_sums(sums, grad_low, grad_norm, normed)
    e_ref[...] = (grad_norm * row(gain)).astype(BF16)
    gv_ref[...] = dot_nt(upstream, w_out[...]).astype(BF16)
    grad[:, 0:hid] += dot_tn(mlp_in, grad_low)
    grad[:, hid : 2 * hid] += dot_tn(upstream, act)
    out_grad = dot_tn(upstream, o_far[...]) + dot_tn(n_s[...], o_near[...])
    side = out_grad.shape[1] // 2
    if fits(rows):
        grad[:, 2 * hid : 2 * hid + side] += out_grad[:, :side]
        grad[:, 2 * hid + LANES : 2 * hid + LANES + side] += out_grad[:, side:]
    else:
        grad[:, 2 * hid : 2 * hid + 2 * side] += out_grad
    far = (dot(act, w_down[...]) + dot(o_far[...], w_out[...])).astype(BF16)
    near = (mo_in[...].astype(F32) + dot(o_near[...], w_out[...])).astype(BF16)

    @pl.when(step < half)
    def _():
        even[0] = near
        even[1] = far

    @pl.when(step >= half)
    def _():
        odd[0] = near
        odd[1] = far

    @pl.when(step == pl.num_programs(0) - 1)
    def _():
        if fits(rows):
            store_chunks(lambda at: grad[at, 0:hid], up_keep, up_send, meta, rows, 1)
            store_low(grad, low_keep, low_send, meta, rows)
        else:
            up_keep[...] = grad[:, 0:hid].astype(BF16)
            low_keep[...] = grad[:, hid:].astype(BF16)


def feed_forward(
    meta, xs, cs, gain, shift, b_up, w_up, w_down, w_out, rows, seq,
    joined=None, before=None, near=None, attn=None,
):
    per = seq // TILE
    steps = 2 * per
    hid = FF // 4
    width = D // 4
    total = 4 * seq
    first = pl.BlockSpec((TILE, D), lambda i, m: (jnp.minimum(i, per - 1), 0))
    second = pl.BlockSpec((TILE, D), lambda i, m: (jnp.maximum(i - per, 0), 0))
    specs = [
        first,
        second,
        first,
        second,
        whole((D,)),
        whole((D,)),
        whole((FF,)),
        pl.BlockSpec((D, hid), lambda i, m: (0, m[0])),
        pl.BlockSpec((hid, D), lambda i, m: (m[0], 0)),
        pl.BlockSpec((width, D), lambda i, m: (m[0], 0)),
    ]
    args = [*xs, *cs, gain, shift, b_up, w_up, w_down, w_out]
    tile = pl.BlockSpec((TILE, D), lambda i, m: (i, 0))
    narrow = pl.BlockSpec((TILE, width), lambda i, m: (i, 0))
    sums = (8, D)
    scratch = [pltpu.VMEM((TILE, D), BF16), pltpu.VMEM((TILE, D), BF16)]
    pair = jax.ShapeDtypeStruct((steps * TILE, D), BF16)
    full = jax.ShapeDtypeStruct((total, D), BF16)
    vec = jax.ShapeDtypeStruct((total, width), BF16)
    if before is None:
        body = partial(mlp_first_kernel, per)
        gain1, shift1, w_qkv, b_qkv, low, high = joined
        args += [gain1, shift1, b_qkv, low, high]
        specs += [whole(a.shape) for a in args[-5:]]
        for part in range(3):
            for side in range(2):
                specs.append(
                    pl.BlockSpec(
                        (D, LANES),
                        lambda i, m, at=part * D // LANES + side: (0, at + 3 * m[0] // 2),
                    )
                )
                args.append(w_qkv)
        outs = [pair, full, full, vec, jax.ShapeDtypeStruct(sums, F32)]
        outs += [jax.ShapeDtypeStruct((D, hid), F32)] * 2 + [vec] * 3
        outs += [
            jax.ShapeDtypeStruct((D, 3 * width), BF16),
            jax.ShapeDtypeStruct((1, 3 * width), F32),
        ]
        out_specs = [tile, tile, tile, narrow, whole(sums)]
        out_specs += [whole((D, hid))] * 2 + [narrow] * 3
        out_specs += [whole((D, 3 * width)), whole((1, 3 * width))]
        aliases = {}
    else:
        body = partial(mlp_second_kernel, per, rows)
        mlp_out, norm_part, normed, grad_vec, sums_in, gup, gdown = before
        chunks = chunk_shapes(hid, rows) + low_shapes(rows)
        args += [*near, mlp_out, attn, attn, sums_in, gup, gdown, norm_part, normed, grad_vec]
        specs += [
            first,
            second,
            tile,
            narrow,
            pl.BlockSpec((TILE, width), lambda i, m: (i + steps, 0)),
            whole(sums),
            whole((D, hid)),
            whole((D, hid)),
            *(pl.BlockSpec(memory_space=pl.ANY),) * 3,
        ]
        aliases = {len(args) - 2 + i: i for i in range(3)}
        both = jax.ShapeDtypeStruct((2, seq, D), BF16)
        outs = [full, full, vec, jax.ShapeDtypeStruct(sums, F32), both, both]
        late = pl.BlockSpec((TILE, D), lambda i, m: (i + steps, 0))
        outs += [jax.ShapeDtypeStruct(shape, BF16) for shape in chunks]
        out_specs = [
            late,
            late,
            pl.BlockSpec((TILE, width), lambda i, m: (i + steps, 0)),
            whole(sums),
            pl.BlockSpec((2, TILE, D), lambda i, m: (0, jnp.minimum(i, per - 1), 0)),
            pl.BlockSpec((2, TILE, D), lambda i, m: (0, jnp.maximum(i - per, 0), 0)),
            *(whole(shape) for shape in chunks),
        ]
        scratch += [pltpu.VMEM((TILE, D), BF16), pltpu.VMEM((D, 2 * hid + 2 * LANES), F32)]
    return pl.pallas_call(
        body,
        out_shape=outs,
        grid_spec=pltpu.PrefetchScalarGridSpec(
            num_scalar_prefetch=1,
            grid=(steps,),
            in_specs=specs,
            out_specs=out_specs,
            scratch_shapes=scratch,
        ),
        input_output_aliases=aliases,
        compiler_params=params(),
        cost_estimate=COST,
        name="mlp_first" if before is None else "mlp_second",
    )(meta, *args)


def head_masks():
    lane = lax.broadcasted_iota(jnp.int32, (1, LANES), 1)
    first = jnp.where(lane < HDIM, 1.0, 0.0).astype(BF16)
    second = jnp.where(lane < HDIM, 0.0, 1.0).astype(BF16)
    return first, second


def slot_rows(meta, per, tile):
    slot = jnp.bitwise_xor(tile // per, meta[0])
    return pl.multiple_of((slot * per + tile % per) * TILE, TILE)


def by_head(first, second, block, third):
    return (block * first, block * second, third)


def transpose_all(from_ref, to_ref):
    @pl.loop(0, from_ref.shape[0] // TILE)
    def _(tile):
        rows = pl.ds(pl.multiple_of(tile * TILE, TILE), TILE)
        to_ref[:, rows] = from_ref[rows, :].astype(F32).T.astype(BF16)


def attend_kernel(per, meta, lo, hi, q_ref, k_ref, v_ref, start_ref, o_ref, lse_ref, vt_ref, acc, s_ref):
    mask0, mask1 = head_masks()
    tiles = k_ref.shape[0] // TILE
    qi = pl.program_id(0)

    @pl.when(qi == 0)
    def _():
        ones = jnp.where(lax.broadcasted_iota(jnp.int32, (VROWS - HDIM, TILE), 0) == 0, 1.0, 0.0)

        @pl.loop(0, tiles)
        def _(tile):
            rows = pl.ds(pl.multiple_of(tile * TILE, TILE), TILE)
            block = v_ref[rows, :].astype(F32).T
            for head in range(3):
                at = head * VROWS
                vt_ref[at : at + HDIM, rows] = block[head * HDIM : (head + 1) * HDIM].astype(BF16)
                vt_ref[at + HDIM : at + VROWS, rows] = ones.astype(BF16)

    key_iota = lax.broadcasted_iota(jnp.int32, (TILE, TILE), 0)
    query_iota = lax.broadcasted_iota(jnp.int32, (TILE, TILE), 1)
    queries = by_head(mask0, mask1, q_ref[:, 0:128], q_ref[:, 128:192])
    starts = start_ref[0]
    acc[...] = jnp.zeros_like(acc)

    def key_tile(turn):
        return jnp.where(turn == 0, qi, first + turn - 1)

    def score(masked, ki):
        k_rows = pl.ds(slot_rows(meta, per, ki), TILE)
        pair, third = k_ref[k_rows, 0:128], k_ref[k_rows, 128:192]
        scores = [dot_nt(third if head == 2 else pair, queries[head]) for head in range(3)]
        if masked:
            allowed = (key_iota >= starts - ki * TILE) & (key_iota <= query_iota + (qi - ki) * TILE)
            scores = [jnp.where(allowed, x, MASKED) for x in scores]
        return scores, [jnp.max(x, axis=0, keepdims=True) for x in scores]

    def value(ki, tops, peaks):
        k_rows = pl.ds(slot_rows(meta, per, ki), TILE)
        news = [jnp.maximum(top, peak) for top, peak in zip(tops, peaks)]
        fades = [jnp.exp2(top - new) for top, new in zip(tops, news)]
        weights = [jnp.exp2(s_ref[head] - news[head]).astype(BF16) for head in range(3)]
        terms = [
            dot(vt_ref[head * VROWS : (head + 1) * VROWS, k_rows], weights[head]) for head in range(3)
        ]
        return news, fades, terms

    def put(fades, terms):
        for head in range(3):
            cols = slice(head * VROWS, (head + 1) * VROWS)
            acc[cols, :] = acc[cols, :] * fades[head] + terms[head]

    def visit(masked, turn, carry):
        tops, peaks = carry
        scores, next_peaks = score(masked, key_tile(turn + 1))
        news, fades, terms = value(key_tile(turn), tops, peaks)
        peaks = next_peaks
        for head in range(3):
            s_ref[head] = scores[head]
        put(fades, terms)
        return tuple(news), tuple(peaks)

    first = lo[qi]
    full = jnp.minimum(hi[qi], qi)
    scores, peaks = score(True, qi)
    for head in range(3):
        s_ref[head] = scores[head]
    carry = ((jnp.full((1, TILE), MASKED, F32),) * 3, tuple(peaks))
    carry = lax.fori_loop(0, full - first, partial(visit, True), carry)
    carry = lax.fori_loop(full - first, qi - first, partial(visit, False), carry)
    tops, fades, terms = value(key_tile(qi - first), *carry)
    put(fades, terms)
    heads = []
    for head, top in enumerate(tops):
        at = head * VROWS
        total = acc[at + HDIM : at + HDIM + 1, :]
        heads.append(acc[at : at + HDIM, :] / total)
        lse_ref[head, 0] = top + jnp.log2(total)
    o_ref[...] = jnp.concatenate(heads, axis=0).T.astype(BF16)

def attend(meta, lo, hi, query, keys, values, starts, per):
    total, width = query.shape
    tiles = total // TILE
    def slot(i, m):
        return jnp.bitwise_xor(i // per, m[0]) * per + i % per
    q_spec = pl.BlockSpec((TILE, width), lambda i, m, lo, hi: (slot(i, m), 0))
    start_spec = pl.BlockSpec((1, 1, TILE), lambda i, m, lo, hi: (slot(i, m), 0, 0))
    lse_spec = pl.BlockSpec((3, 1, 1, TILE), lambda i, m, lo, hi: (0, slot(i, m), 0, 0))
    return pl.pallas_call(
        partial(attend_kernel, per),
        out_shape=[
            jax.ShapeDtypeStruct((total, width), BF16),
            jax.ShapeDtypeStruct((3, tiles, 1, TILE), F32),
        ],
        grid_spec=pltpu.PrefetchScalarGridSpec(
            num_scalar_prefetch=3,
            grid=(tiles,),
            in_specs=[q_spec, whole(keys.shape), whole(values.shape), start_spec],
            out_specs=[q_spec, lse_spec],
            scratch_shapes=[pltpu.VMEM((3 * VROWS, total), BF16), pltpu.VMEM((3 * VROWS, TILE), F32), pltpu.VMEM((3, TILE, TILE), F32)],
        ),
        compiler_params=params(),
        cost_estimate=COST,
        name="attend",
    )(meta, lo, hi, query, keys, values, starts)


def attend_back_kernel(
    per, meta, lo, hi, q_ref, k_ref, v_ref, o_ref, gv_ref, start_ref, lse_ref, low, high,
    gj_ref, kt_ref, dk_ref, dv_ref, dqt_ref
):
    mask0, mask1 = head_masks()
    tiles = k_ref.shape[0] // TILE
    qi = tiles - 1 - pl.program_id(0)

    @pl.when(pl.program_id(0) == 0)
    def _():
        transpose_all(k_ref, kt_ref)

    own_rows = pl.ds(slot_rows(meta, per, qi), TILE)
    key_iota = lax.broadcasted_iota(jnp.int32, (TILE, TILE), 0)
    query_iota = lax.broadcasted_iota(jnp.int32, (TILE, TILE), 1)
    queries = by_head(mask0, mask1, q_ref[:, 0:128], q_ref[:, 128:192])
    grads = by_head(mask0, mask1, gv_ref[:, 0:128], gv_ref[:, 128:192])
    starts = start_ref[0]
    lses = [lse_ref[head, 0] for head in range(3)]
    product = (gv_ref[...].astype(F32) * o_ref[...].astype(F32)).T
    deltas = [
        jnp.sum(product[head * HDIM : (head + 1) * HDIM], axis=0, keepdims=True)
        for head in range(3)
    ]
    dqt_ref[...] = jnp.zeros_like(dqt_ref)

    @pl.when(pl.program_id(0) == 0)
    def _():
        dk_ref[...] = jnp.zeros_like(dk_ref)
        dv_ref[...] = jnp.zeros_like(dv_ref)

    def load(ki):
        k_rows = pl.ds(slot_rows(meta, per, ki), TILE)
        return k_rows

    def score(masked, ki):
        k_rows = load(ki)
        pair, third = k_ref[k_rows, 0:128], k_ref[k_rows, 128:192]
        v_pair, v_third = v_ref[k_rows, 0:128], v_ref[k_rows, 128:192]
        scores = [dot_nt(third if head == 2 else pair, queries[head]) for head in range(3)]
        grad_probs = [dot_nt(v_third if head == 2 else v_pair, grads[head]) for head in range(3)]
        if masked:
            allowed = (key_iota >= starts - ki * TILE) & (key_iota <= query_iota + (qi - ki) * TILE)
            scores = [jnp.where(allowed, x, MASKED) for x in scores]
        return scores, grad_probs

    def terms(ki, scores, grad_probs):
        k_rows = load(ki)
        probs = [jnp.exp2(x - lse) for x, lse in zip(scores, lses)]
        grad_scores = [
            (p * (g - delta)).astype(BF16) for p, g, delta in zip(probs, grad_probs, deltas)
        ]
        dv = [dot(p.astype(BF16), g) for p, g in zip(probs, grads)]
        dk = [dot(g, q) for g, q in zip(grad_scores, queries)]
        dq = [
            dot(kt_ref[head * HDIM : (head + 1) * HDIM, k_rows], grad_scores[head])
            for head in range(3)
        ]
        return dk, dv, dq

    def add(ki, dk, dv, dq):
        k_rows = load(ki)
        for into, parts in ((dk_ref, dk), (dv_ref, dv)):
            into[k_rows, 0:128] += parts[0] + parts[1]
            into[k_rows, 128:192] += parts[2]
        for head in range(3):
            dqt_ref[head * HDIM : (head + 1) * HDIM, :] += dq[head]

    first = lo[qi]
    full = jnp.minimum(hi[qi], qi)

    def visit(masked, ki):
        add(ki, *terms(ki, *score(masked, ki)))

    @pl.loop(first, full)
    def _(ki):
        visit(True, ki)

    @pl.loop(full, qi)
    def _(ki):
        visit(False, ki)

    visit(True, qi)

    cos, sin = rotation(low, high, qi)

    def turn_back(block):
        return block * cos - swap_halves(block) * sin

    dq = dqt_ref[...].T * (HDIM**-0.5)
    dk = dk_ref[own_rows, :] * LN2
    gj_ref[:, 0:128] = turn_back(dq[:, 0:128]).astype(BF16)
    gj_ref[:, 128:256] = turn_back(dk[:, 0:128]).astype(BF16)
    mixed = jnp.concatenate([dq[:, 128:192], dk[:, 128:192]], axis=1)
    gj_ref[:, 256:384] = turn_back(mixed).astype(BF16)
    gj_ref[:, 384:576] = dv_ref[own_rows, :].astype(BF16)


def attend_back(
    meta, lo, hi, query, keys, values, attn, grad_vec, starts, lse, low, high, per
):
    total, width = query.shape
    tiles = total // TILE

    def slot(i, m):
        tile = tiles - 1 - i
        return jnp.bitwise_xor(tile // per, m[0]) * per + tile % per

    q_spec = pl.BlockSpec((TILE, width), lambda i, m, lo, hi: (slot(i, m), 0))
    gj_spec = pl.BlockSpec((TILE, 3 * width), lambda i, m, lo, hi: (slot(i, m), 0))
    start_spec = pl.BlockSpec((1, 1, TILE), lambda i, m, lo, hi: (slot(i, m), 0, 0))
    lse_spec = pl.BlockSpec((3, 1, 1, TILE), lambda i, m, lo, hi: (0, slot(i, m), 0, 0))
    return pl.pallas_call(
        partial(attend_back_kernel, per),
        out_shape=jax.ShapeDtypeStruct((total, 3 * width), BF16),
        grid_spec=pltpu.PrefetchScalarGridSpec(
            num_scalar_prefetch=3,
            grid=(tiles,),
            in_specs=[
                q_spec,
                whole(keys.shape),
                whole(values.shape),
                q_spec,
                q_spec,
                start_spec,
                lse_spec,
                whole(low.shape),
                whole(high.shape),
            ],
            out_specs=gj_spec,
            scratch_shapes=[
                pltpu.VMEM((width, total), BF16),
                pltpu.VMEM((total, width), F32),
                pltpu.VMEM((total, width), F32),
                pltpu.VMEM((width, TILE), F32),
            ],
        ),
        compiler_params=params(),
        cost_estimate=COST,
        name="attend_back",
    )(meta, lo, hi, query, keys, values, attn, grad_vec, starts, lse, low, high)


SMALL = 16


def pack_small(gain_sum, shift_sum, bias, mlp_sums):
    third = 3 * D // 4
    which = lax.broadcasted_iota(jnp.int32, (8, D), 0)
    table = jnp.concatenate([jnp.zeros((4, D), F32), mlp_sums[0:4]], axis=0)
    table = jnp.where(which == 0, gain_sum, jnp.where(which == 1, shift_sum, table))
    head = jnp.where(which[:, :third] == 2, bias, table[:, :third])
    tail = jnp.concatenate([table[:, third:], jnp.zeros((8, 2 * third - D), F32)], axis=1)
    return jnp.concatenate([head, tail], axis=0)


def high_low(value):
    high = value.astype(BF16)
    return high, (value - high.astype(F32)).astype(BF16)


def weight_kernel(rows, meta, *refs):
    gj_ref, n_ref, gain, shift, w_ref, mlp_sums, keep, send, small, grad, bias = refs
    step = pl.program_id(0)

    @pl.when(step == 0)
    def _():
        grad[...] = jnp.zeros_like(grad)
        bias[...] = jnp.zeros_like(bias)

    joined = gj_ref[...]
    bias[0:1, :] += jnp.sum(joined.astype(F32), axis=0, keepdims=True)
    grad[...] += dot_tn(n_ref[...], joined)

    @pl.when(step == pl.num_programs(0) - 1)
    def _():
        total = bias[0:1, :]
        width = total.shape[1]
        parts = jnp.concatenate(
            [*high_low(jnp.broadcast_to(total, (8, width)))], axis=0
        )
        shift_sum = dot_nt(parts, w_ref[...])
        shift_sum = shift_sum[0:1] + shift_sum[8:9]
        ones = jnp.ones((16, width), BF16)
        high, low = high_low(grad[...] * w_ref[...].astype(F32))
        gain_sum = (dot_nt(ones, high) + dot_nt(ones, low))[0:1]
        columns = jnp.concatenate(
            [jnp.broadcast_to(row(gain), (8, D)), jnp.broadcast_to(row(shift), (8, D))], axis=0
        ).T
        grad[...] = grad[...] * columns[:, 0:1] + columns[:, 8:9] * total
        rest = pack_small(gain_sum, shift_sum, total, mlp_sums[...])
        small[...] = rest
        if fits(rows):
            store_chunks(lambda at: grad[at, :], keep, send, meta, rows, 1)
            keep[D // 2 :, :] = rest.astype(BF16)
            send[D // 2 :, :] = rest.astype(BF16)
        else:
            keep[...] = grad[...].astype(BF16)


def row_tiles(cols, tile=TILE):
    return pl.BlockSpec((tile, cols), lambda i, m: (i, 0))


def joined_weight(meta, grad, normed, gain, shift, w, mlp_sums, rows):
    total, width = grad.shape
    tile = 2 * TILE
    chunks = chunk_shapes(width, rows, SMALL)
    args = [gain, shift, w, mlp_sums]
    return pl.pallas_call(
        partial(weight_kernel, rows),
        out_shape=[jax.ShapeDtypeStruct(shape, BF16) for shape in chunks]
        + [jax.ShapeDtypeStruct((SMALL, width), F32)],
        grid_spec=pltpu.PrefetchScalarGridSpec(
            num_scalar_prefetch=1,
            grid=(total // tile,),
            in_specs=[row_tiles(width, tile), row_tiles(D, tile), *(whole(a.shape) for a in args)],
            out_specs=[*(whole(shape) for shape in chunks), whole((SMALL, width))],
            scratch_shapes=[pltpu.VMEM((D, width), F32), pltpu.VMEM((8, width), F32)],
        ),
        compiler_params=params(),
        cost_estimate=COST,
        name="joined_weight",
    )(meta, grad, normed, *args)


def norm_kernel(meta, *refs):
    gjs, es, (gain, w_ref), outs = refs[0:4], refs[4:8], refs[8:10], refs[10:]
    for gj_ref, e_in, out in zip(gjs, es, outs):
        grad_norm = dot_nt(gj_ref[...], w_ref[...])
        out[...] = (grad_norm * row(gain) + e_in[...].astype(F32)).astype(BF16)


def norm_grad(meta, grad, e_mlp, gain, w, seq):
    tile = TILE // 2
    per = seq // tile

    def slot_tiles(slot, cols):
        return pl.BlockSpec((tile, cols), lambda i, m: (slot * per + i, 0))

    return pl.pallas_call(
        norm_kernel,
        out_shape=[jax.ShapeDtypeStruct((seq, D), BF16)] * 4,
        grid_spec=pltpu.PrefetchScalarGridSpec(
            num_scalar_prefetch=1,
            grid=(per,),
            in_specs=[
                *(slot_tiles(slot, grad.shape[1]) for slot in range(4)),
                *(slot_tiles(slot, D) for slot in range(4)),
                whole(gain.shape),
                whole(w.shape),
            ],
            out_specs=[slot_tiles(0, D)] * 4,
        ),
        compiler_params=params(),
        cost_estimate=COST,
        name="norm_grad",
    )(meta, *[grad] * 4, *[e_mlp] * 4, gain, w)


def simple(body, name, shapes, *args, specs=None):
    return pl.pallas_call(
        body,
        out_shape=[jax.ShapeDtypeStruct(shape, kind) for shape, kind in shapes],
        grid_spec=pltpu.PrefetchScalarGridSpec(
            num_scalar_prefetch=1,
            grid=(1,),
            in_specs=specs or [whole(a.shape) for a in args[1:]],
            out_specs=[whole(shape) for shape, _ in shapes],
        ),
        compiler_params=params(),
        cost_estimate=COST,
        name=name,
    )(*args)


def add_up(refs):
    total = refs[0][...].astype(F32)
    for ref in refs[1:]:
        total += ref[...].astype(F32)
    return total


def lower_kernel(meta, piece, down_ref, out_ref):
    cut = down_ref.shape[1]
    down_ref[...] = piece[:, :cut].astype(F32)
    out_ref[...] = piece[:, cut:].astype(F32).T[: out_ref.shape[0]]


def last_qkv_kernel(meta, *refs):
    *terms, sums, got_sums, kept, near, far, small = refs
    size = kept.shape[0]
    width = kept.shape[1]
    total = add_up(terms)
    rows = sums[...].astype(F32) + got_sums[...].astype(F32)
    for part in range(3):
        small[part * 8 : part * 8 + 8, :] = rows[0:8, part * width : (part + 1) * width]
    small[24:32, :] = rows[8:16, 0:width]
    near[size:, :] = small[...]
    far[size:, :] = small[...]
    query = jnp.concatenate([total[:, 0:128], total[:, 256:320]], axis=1)
    keys = jnp.concatenate([total[:, 128:256], total[:, 320:384]], axis=1)
    values = total[:, 384:576]
    plans = (
        (query, keys, values),
        (keys, query, values),
        (keys, values, query),
        (values, keys, query),
    )
    for blk, plan in enumerate(plans):

        @pl.when(meta[0] == blk)
        def _(plan=plan):
            kept[...] = plan[0]
            near[0:size, :] = plan[1]
            far[0:size, :] = plan[2]


def assemble_kernel(
    meta, kept, small, near, far, diag,
    qkv, b_qkv, b_out, b_up, b_down, gain1, shift1, gain2, shift2, table,
):
    size, width = kept.shape

    @pl.when(meta[0] % 2 == 0)
    def _():
        qkv[:, 0:width] = kept[...]
        qkv[:, 2 * width :] = far[0:size, :]

    @pl.when(meta[0] % 2 == 1)
    def _():
        qkv[:, 0:width] = far[0:size, :]
        qkv[:, 2 * width :] = kept[...]

    qkv[:, width : 2 * width] = near[0:size, :]
    table[0] = small[...]
    table[1] = near[size:, :]
    table[2] = far[size:, :]
    table[3] = diag[...]
    blocks = [table[jnp.bitwise_xor(meta[0], blk)] for blk in range(4)]
    total = blocks[0] + blocks[1] + blocks[2] + blocks[3]

    def vector(rows, index):
        parts = [rows[part * 8 + index : part * 8 + index + 1, :] for part in range(4)]
        return jnp.concatenate(parts, axis=1)

    for ref, index in ((gain1, 0), (shift1, 1), (gain2, 5), (shift2, 6), (b_out, 7), (b_down, 7)):
        ref[...] = vector(total, index).reshape(D)
    ups, parts = [], ([], [], [])
    for rows in blocks:
        ups.append(vector(rows, 4))
        joined = vector(rows, 2)
        parts[0].append(jnp.concatenate([joined[:, 0:128], joined[:, 256:320]], axis=1))
        parts[1].append(jnp.concatenate([joined[:, 128:256], joined[:, 320:384]], axis=1))
        parts[2].append(joined[:, 384:576])
    b_up[...] = jnp.concatenate(ups, axis=1).reshape(4 * D)
    b_qkv[...] = jnp.concatenate(parts[0] + parts[1] + parts[2], axis=1).reshape(3 * D)


def assemble(meta, kept, small, near, far, diag):
    size, width = kept.shape
    shapes = [((size, 3 * width), F32), ((3 * D,), F32), ((D,), F32), ((4 * D,), F32)]
    shapes += [((D,), F32)] * 5
    args = (kept, small, near, far, diag)
    return pl.pallas_call(
        assemble_kernel,
        out_shape=[jax.ShapeDtypeStruct(shape, kind) for shape, kind in shapes],
        grid_spec=pltpu.PrefetchScalarGridSpec(
            num_scalar_prefetch=1,
            grid=(1,),
            in_specs=[whole(a.shape) for a in args],
            out_specs=[whole(shape) for shape, _ in shapes],
            scratch_shapes=[pltpu.VMEM((4, 32, width), F32)],
        ),
        compiler_params=params(),
        cost_estimate=COST,
        name="assemble",
    )(meta, *args)


def next_send(terms, size):
    return sum(term[size // 2 : size].astype(F32) for term in terms).astype(BF16)


def reduce_plain(keep, got, masks):
    terms, size = [keep, got], keep.shape[0]
    for mask in masks:
        terms.append(swap(next_send(terms, size), "rows", mask))
        size //= 2
    return sum(term[:size].astype(F32) for term in terms)


def after(value, *others):
    return lax.optimization_barrier((value, others))[0]


def swap(value, axis, mask):
    size = lax.axis_size(axis)
    return lax.ppermute(value, axis, [(i, i ^ mask) for i in range(size)])


def add_low(left, right):
    return (left.astype(F32) + right.astype(F32)).astype(BF16)


def spread_rows(chunk):
    rows = lax.axis_size("rows")
    moves = [
        (r * 4 + b, (rows // 4 * b + r // 4) * 4 + r % 4) for r in range(rows) for b in range(4)
    ]
    return lax.ppermute(chunk, ("rows", "blk"), moves)


def split_columns(chunk):
    b = lax.axis_index("blk")
    q = jnp.concatenate([chunk[:, 0:128], chunk[:, 256:320]], axis=1)
    k = jnp.concatenate([chunk[:, 128:256], chunk[:, 320:384]], axis=1)
    v = chunk[:, 384:576]

    def choose(zero, one, two, three):
        return jnp.where(b < 2, jnp.where(b == 0, zero, one), jnp.where(b == 2, two, three))

    return choose(q, k, k, v), choose(k, q, v, k), choose(v, v, q, q)


def result_kernel(x_ref, even, near, far, b_out, b_down, out_ref):
    bias = row(b_out) + row(b_down)
    total = even[0].astype(F32) + near[0].astype(F32) + far[...].astype(F32)
    out_ref[...] = (x_ref[...].astype(F32) + bias + total).astype(BF16)


def token_kernel(x_ref, even, near, far, c_ref, out_ref):
    wide = x_ref[...].astype(F32)
    center = wide - jnp.mean(wide, axis=-1, keepdims=True)
    rate = lax.rsqrt(jnp.mean(center * center, axis=-1, keepdims=True) + EPS)
    normed = center * rate
    grad = even[...].astype(F32) + near[...].astype(F32) + far[...].astype(F32)
    mean = jnp.mean(grad, axis=-1, keepdims=True)
    along = jnp.mean(grad * normed, axis=-1, keepdims=True)
    back = rate * (grad - mean - normed * along)
    out_ref[...] = (c_ref[...].astype(F32) + back).astype(BF16)


def finish(body, name, seq, x, even, near, far, *more):
    flat = pl.BlockSpec((TILE, D), lambda i: (i, 0))
    own = pl.BlockSpec((1, TILE, D), lambda i: (0, i, 0))
    return pl.pallas_call(
        body,
        out_shape=jax.ShapeDtypeStruct((seq, D), BF16),
        grid=(seq // TILE,),
        in_specs=[
            *(own if a.ndim == 3 else flat for a in (x, even, near, far)),
            *(flat if a.ndim == 2 else whole(a.shape) for a in more),
        ],
        out_specs=flat,
        compiler_params=params(),
        cost_estimate=COST,
        name=name,
    )(x, even, near, far, *more)


def local(
    tokens, seg_ids, valid_len, ln1_gain, ln1_bias, w_qkv, b_qkv, w_out, b_out,
    ln2_gain, ln2_bias, w_up, b_up, w_down, b_down, cotangent,
):
    rows = lax.axis_size("rows")
    blk = lax.axis_index("blk")
    seq = tokens.shape[1]
    per = seq // TILE
    width = D // 4
    hid = FF // 4
    low, high = angle_parts(4 * seq)
    seg_row = jnp.pad(seg_ids.astype(BF16), ((0, EXTRA - 1), (0, D - seq)))
    tok_own = jnp.concatenate([tokens[0], seg_row], axis=0)
    cot_own = cotangent[0]

    cot_near = swap(cot_own, "blk", 1)
    tok_far = swap(tok_own, "blk", 2)
    tok_near = swap(tok_own, "blk", 1)
    cot_long = jnp.pad(cot_own, ((0, 2 * EXTRA), (0, 0)))
    cot_far = swap(cot_long, "blk", 2)

    meta = jnp.stack([blk, lax.axis_index("rows")]).astype(jnp.int32)
    mlp_args = (ln2_gain, ln2_bias, b_up, w_up, w_down, w_out, rows, seq)
    joined = (ln1_gain, ln1_bias, w_qkv, b_qkv, low, high)
    *first, query, keys, values, w_own, b_own = feed_forward(
        meta, (tok_own, tok_near), (cot_own, cot_near), *mlp_args, joined
    )
    meta = after(meta, b_own)

    def more(slot, m, tok, filled, slots=()):
        args = (ln1_gain, ln1_bias, low, high, w_own, b_own, filled, seq, slots)
        return project(slot, m, valid_len, tok, *args)

    tok_last = swap(after(tok_far, b_own), "blk", 1)
    joined = more(2, meta, tok_far, (query, keys, values))
    toks = (tok_own, tok_near, tok_far, tok_last)
    query, keys, values, starts, lo, hi = more(
        3, after(meta, joined[0]), tok_last, joined, toks
    )
    cot_last = swap(after(cot_far, lo), "blk", 1)
    cots = (cot_own, cot_near, cot_far, cot_last)
    attn, lse = attend(meta, lo, hi, query, keys, values, starts, per)

    meta = after(meta, lse)
    e_mlp, normed, grad_vec, mlp_sums, out_even, out_odd, *packets = feed_forward(
        meta, toks[2:], cots[2:], *mlp_args, before=first, near=cots[:2], attn=attn
    )
    up_keep, up_send = chunks_of(*packets[:2], rows, 1)
    low_keep, low_send = low_chunks(*packets[2:], rows)
    up_masks, low_masks = mask_order(rows, 1), mask_order(rows, 2)
    out_got = swap(out_odd, "blk", 1)
    up_got = swap(up_send, "rows", up_masks[0])
    low_got = swap(low_send, "rows", low_masks[0])

    meta = after(meta, mlp_sums)
    grad_joined = attend_back(
        meta, lo, hi, query, keys, values, attn, grad_vec, starts, lse, low, high, per
    )
    meta = after(meta, grad_joined)
    qkv_keep, qkv_send, small = joined_weight(
        meta, grad_joined, normed, ln1_gain, ln1_bias, w_own, mlp_sums, rows
    )
    qkv_keep, qkv_send = chunks_of(qkv_keep, qkv_send, rows, 1)
    qkv_got = swap(qkv_send, "rows", 1)

    out_send = add_low(after(out_even, qkv_keep)[1], out_got[1])
    out_far = swap(out_send, "blk", 2)
    half = D // 2
    if fits(rows):
        up = [up_keep, up_got]
        up_send = next_send(up, half)
        up.append(swap(up_send, "rows", up_masks[1]))
        lower = [after(low_keep, qkv_keep), low_got]
        low_send = next_send(lower, D)
        lower.append(swap(low_send, "rows", low_masks[1]))
        meta = after(meta, up_send, low_send)
    meta = after(meta, out_send)
    e_own, e_near, e_send, e_last = norm_grad(meta, grad_joined, e_mlp, ln1_gain, w_own, seq)
    e_last = swap(e_last, "blk", 1)
    e_near = swap(e_near, "blk", 1)
    if fits(rows):
        chunk = D // rows
        joined = [after(qkv_keep, e_own), qkv_got]
        tail = add_low(joined[0][half:], qkv_got[half:])
        qkv_send = jnp.concatenate([next_send(joined, half), tail])
        joined.append(swap(qkv_send, "rows", 2))
        e_send = after(e_send, qkv_send)
    e_send = add_low(e_send, e_last)
    e_far = swap(e_send, "blk", 2)
    if fits(rows):
        lower[0] = after(lower[0], e_send)
        low_send = next_send(lower, half)
        lower.append(swap(low_send, "rows", low_masks[2]))
        up[0] = after(up[0], low_send)
        up_send = next_send(up, half // 2)
        up.append(swap(up_send, "rows", up_masks[2]))
        joined[0] = after(joined[0], up_send)
        tail = add_low(after(qkv_send, up_send)[half // 2 :], joined[2][half // 2 :])
        qkv_send = jnp.concatenate([next_send(joined, half // 2), tail])
        joined.append(swap(qkv_send, "rows", 4))
        out_args = (after(tok_own, qkv_send), out_even, out_got, out_far, b_out, b_down)
        result = finish(result_kernel, "result", seq, *out_args)
        meta = after(meta, result)
        piece = sum(term[:width].astype(F32) for term in lower).astype(BF16)
        meta = after(meta, piece)
        piece = spread_rows(piece)
        packet = ((chunk + 32, width), F32)
        last = pl.BlockSpec((SMALL, 3 * width), lambda i, m: (chunk // SMALL, 0))
        kept, near, far, small = simple(
            last_qkv_kernel,
            "last_qkv",
            [((chunk, width), F32), packet, packet, ((32, width), F32)],
            meta,
            *joined,
            qkv_send,
            joined[3],
            specs=[pl.BlockSpec((chunk, 3 * width), lambda i, m: (0, 0))] * 4 + [last] * 2,
        )
        near, far, diag = swap(near, "blk", 1), swap(far, "blk", 2), swap(small, "blk", 3)
        tok_args = (after(tok_own, small), e_own, e_near, e_far, cot_own)
        grad_tokens = finish(token_kernel, "token_grad", seq, *tok_args)
        up[0] = after(up[0], grad_tokens)
        up = sum(term[:chunk].astype(F32) for term in up)
        ends = [((width, hid // 2), F32), ((width // 2, width), F32)]
        meta = after(meta, up)
        down, out_w = simple(lower_kernel, "lower", ends, meta, piece)
        down = down.T
        qkv, gb_qkv, gb_out, gb_up, gb_down, *norms = assemble(
            meta, kept, small, near, far, diag
        )
    else:
        up = reduce_plain(up_keep, up_got, up_masks[1:])
        weights = reduce_plain(low_keep, low_got, low_masks[1:])
        qkv = reduce_plain(qkv_keep, qkv_got, up_masks[1:])
        piece = spread_rows(weights).T
        cut = 4 * hid // rows
        down, out_w = piece[:cut], piece[cut:]
        kept, near, far = split_columns(qkv)
        near, far = swap(near, "blk", 1), swap(far, "blk", 2)
        ends = [jnp.where(blk % 2 == 0, a, b) for a, b in ((kept, far), (far, kept))]
        qkv = jnp.concatenate([ends[0], near, ends[1]], axis=1)
        out_args = (tok_own, out_even, out_got, out_far, b_out, b_down)
        result = finish(result_kernel, "result", seq, *out_args)
        tok_args = (tok_own, e_own, e_near, e_far, cot_own)
        grad_tokens = finish(token_kernel, "token_grad", seq, *tok_args)
        third = 3 * width
        table = jnp.concatenate([small[0:8], small[8:16, : D - third]], axis=1)
        mine = (jnp.arange(4) == blk)[:, None]
        joined = lax.psum(jnp.where(mine, small[2:3], 0.0), ("rows", "blk"))
        gb_up = lax.psum(jnp.where(mine, table[4:5], 0.0), ("rows", "blk")).reshape(FF)
        gb_qkv = jnp.concatenate(
            [
                jnp.concatenate([joined[:, 0:128], joined[:, 256:320]], axis=1).reshape(D),
                jnp.concatenate([joined[:, 128:256], joined[:, 320:384]], axis=1).reshape(D),
                joined[:, 384:576].reshape(D),
            ]
        )
        gain_1, shift_1, _, _, _, gain_2, shift_2, gb_out = lax.psum(table, ("rows", "blk"))
        norms, gb_down = (gain_1, shift_1, gain_2, shift_2), gb_out
    return (
        result[None],
        grad_tokens[None],
        qkv,
        out_w,
        up,
        down,
        gb_qkv,
        gb_out,
        gb_up,
        gb_down,
        *norms,
    )


def solution(mesh):
    split = P("rows", "blk")
    in_specs = (
        P("rows", "blk", None),
        split,
        P("rows"),
        *(P(),) * 12,
        P("rows", "blk", None),
    )
    out_specs = (
        P("rows", "blk", None),
        P("rows", "blk", None),
        *(split,) * 4,
        *(P(),) * 8,
    )
    return jax.shard_map(local, mesh=mesh, in_specs=in_specs, out_specs=out_specs, check_vma=False)
```

```python
import math
from functools import partial

import jax
import jax.numpy as jnp
import numpy as np
from jax import lax
from jax.experimental import pallas as pl
from jax.experimental.pallas import tpu as pltpu
from jax.sharding import PartitionSpec as P

D = 768
HEADS = 12
HDIM = 64
ROT = 16
FF = 3072
EPS = 1e-05
MASKED = -1e30
TILE = 256
VROWS = 80
LN2 = math.log(2.0)
EXTRA = 16
LANES = 128
F32 = jnp.float32
BF16 = jnp.bfloat16
COST = pl.CostEstimate(flops=0, bytes_accessed=0, transcendentals=0)
NT_DIMS = (((1,), (1,)), ((), ()))
TN_DIMS = (((0,), (0,)), ((), ()))


def dot(left, right):
    return jnp.dot(left, right, preferred_element_type=F32)


def dot_nt(left, right):
    return lax.dot_general(left, right, NT_DIMS, preferred_element_type=F32)


def dot_tn(left, right):
    return lax.dot_general(left, right, TN_DIMS, preferred_element_type=F32)


def normalize(value):
    center = value - jnp.mean(value, axis=-1, keepdims=True)
    spread = jnp.mean(center * center, axis=-1, keepdims=True)
    return center * lax.rsqrt(spread + EPS)


def angle_parts(length):
    dim = np.arange(LANES) % HDIM
    inverse = np.where(dim < ROT, 10000.0 ** (-2.0 * (dim % (ROT // 2)) / ROT), 0.0)
    high = (np.arange(length // LANES) * LANES)[:, None] * inverse
    low = np.arange(LANES)[:, None] * inverse
    parts = np.stack([np.cos(low), np.sin(low)]), np.stack([np.cos(high), np.sin(high)])
    return tuple(jnp.asarray(part, F32) for part in parts)


def rotation(low_ref, high_ref, tile):
    lane = lax.broadcasted_iota(jnp.int32, (1, LANES), 1) % HDIM
    sign = jnp.where(lane < ROT // 2, -1.0, 1.0)
    cos_rows, sin_rows = [], []
    for part in range(TILE // LANES):
        row = tile * (TILE // LANES) + part
        cos_high = high_ref[0, pl.ds(row, 1), :]
        sin_high = high_ref[1, pl.ds(row, 1), :]
        cos_rows.append(low_ref[0] * cos_high - low_ref[1] * sin_high)
        sin_rows.append((low_ref[1] * cos_high + low_ref[0] * sin_high) * sign)
    return jnp.concatenate(cos_rows, axis=0), jnp.concatenate(sin_rows, axis=0)


def swap_halves(value):
    lane = lax.broadcasted_iota(jnp.int32, value.shape, 1) % HDIM
    half = ROT // 2
    return jnp.where(
        lane < half, pltpu.roll(value, LANES - half, 1), pltpu.roll(value, half, 1)
    )


def true_block(meta_ref, slot):
    return jnp.bitwise_xor(meta_ref[0], slot)


def params(*semantics, vmem=None):
    return pltpu.CompilerParams(
        dimension_semantics=semantics or ("arbitrary",), vmem_limit_bytes=vmem or 67_043_328
    )


def whole(shape):
    return pl.BlockSpec(shape, lambda *_: (0,) * len(shape))


def own_blocks(refs, odd, into):
    places = ((0, 256), (128, 320), (384, 512))
    for part, (pair_at, third_at) in enumerate(places):
        left, right = refs[2 * part], refs[2 * part + 1]

        @pl.when(odd == 0)
        def _(left=left, right=right, pair_at=pair_at, third_at=third_at):
            into[:, pair_at : pair_at + 128] = left[...]
            into[:, third_at : third_at + 64] = right[:, 0:64]

        @pl.when(odd == 1)
        def _(left=left, right=right, pair_at=pair_at, third_at=third_at):
            into[:, pair_at : pair_at + 128] = jnp.concatenate(
                [left[:, 64:128], right[:, 0:64]], axis=1
            )
            into[:, third_at : third_at + 64] = right[:, 64:128]


def row(ref):
    return ref[...].reshape(1, ref.shape[0])


def own_bias(b_ref, odd, blk, into):
    blocks = []
    for part in range(3):
        for side in range(2):
            at = pl.multiple_of((part * (D // LANES) + side + 3 * blk // 2) * LANES, LANES)
            blocks.append(b_ref[pl.ds(at, LANES)].reshape(1, LANES))
    own_blocks(blocks, odd, into)


def project_tile(normed, gain, shift, w_ref, b_ref, low, high, tile, q_ref, k_ref, v_ref):
    attn_in = (normed * row(gain) + row(shift)).astype(BF16)
    joined = dot(attn_in, w_ref[...]) + b_ref[...]
    cos, sin = rotation(low, high, tile)
    scale = HDIM**-0.5 / LN2

    def turn(block):
        return block * cos + swap_halves(block) * sin

    query = turn(joined[:, 0:128]) * scale
    keys = turn(joined[:, 128:256])
    mixed = turn(joined[:, 256:384])
    q_ref[:, 0:128] = query.astype(BF16)
    k_ref[:, 0:128] = keys.astype(BF16)
    q_ref[:, 128:192] = (mixed[:, 0:64] * scale).astype(BF16)
    k_ref[:, 128:192] = mixed[:, 64:128].astype(BF16)
    v_ref[...] = joined[:, 384:576].astype(BF16)


def find_starts(seq, meta, valid, rows, start_ref, lo_ref, hi_ref):
    segs = [ref[0:1, 0:seq].astype(F32) for ref in rows]
    below = [
        sum(jnp.sum((seg < number).astype(F32), axis=1, keepdims=True) for seg in segs)
        for number in (1, 2, 3)
    ]
    per = seq // TILE
    iota = lax.broadcasted_iota(jnp.int32, (1, seq), 1)
    for slot, seg in enumerate(segs):
        block = true_block(meta, slot)
        begin = jnp.zeros((1, seq), F32)
        for number in (1, 2, 3):
            begin = jnp.where(seg == number, below[number - 1], begin)
        pos = iota + block * seq
        begin = jnp.where(pos < valid[0], begin.astype(jnp.int32), pos)
        for part in range(per):
            tile = begin[:, part * TILE : (part + 1) * TILE]
            start_ref[slot * per + part] = tile
            lo_ref[block * per + part] = jnp.min(tile) // TILE
            hi_ref[block * per + part] = (jnp.max(tile) + (TILE - 1)) // TILE


def qkv_kernel(slot, meta, valid, x_ref, gain, shift, low, high, w_ref, b_ref, *refs):
    per = pl.num_programs(0)
    tile = true_block(meta, slot) * per + pl.program_id(0)
    normed = normalize(x_ref[...].astype(F32))
    if slot == 3:
        segs, (*outs, start_ref, lo_ref, hi_ref) = refs[3:7], refs[7:]

        @pl.when(pl.program_id(0) == 0)
        def _():
            find_starts(per * TILE, meta, valid, segs, start_ref, lo_ref, hi_ref)
    else:
        outs = refs[3:]
    project_tile(normed, gain, shift, w_ref, b_ref, low, high, tile, *outs)


def project(slot, meta, valid, x, gain, shift, low, high, w, b, filled, seq, toks=()):
    width = D // 4
    per = seq // TILE
    tiles = 4 * per
    outs = [jax.ShapeDtypeStruct((4 * seq, width), BF16)] * 3
    out_specs = [pl.BlockSpec((TILE, width), lambda i, m, v: (slot * per + i, 0))] * 3
    args = [x, gain, shift, low, high, w, b, *filled, *toks]
    specs = [pl.BlockSpec((TILE, D), lambda i, m, v: (i, 0))]
    specs += [whole(a.shape) for a in args[1:7]]
    specs += [pl.BlockSpec(memory_space=pl.ANY)] * 3
    specs += [pl.BlockSpec((EXTRA, D), lambda i, m, v: (seq // EXTRA, 0)) for _ in toks]
    if toks:
        smem = pl.BlockSpec(memory_space=pltpu.SMEM)
        outs.append(jax.ShapeDtypeStruct((tiles, 1, TILE), jnp.int32))
        outs += [jax.ShapeDtypeStruct((tiles,), jnp.int32)] * 2
        out_specs += [whole((tiles, 1, TILE)), smem, smem]
    return pl.pallas_call(
        partial(qkv_kernel, slot),
        out_shape=outs,
        grid_spec=pltpu.PrefetchScalarGridSpec(
            num_scalar_prefetch=2, grid=(per,), in_specs=specs, out_specs=out_specs
        ),
        input_output_aliases={9 + i: i for i in range(3)},
        compiler_params=params(),
        cost_estimate=COST,
        name=f"qkv_{slot}",
    )(meta, valid, *args)


def mask_order(rows, first):
    masks = [1 << bit for bit in range(rows.bit_length() - 1)]
    return masks if first == 1 else masks[1::-1] + masks[2:]


def places(masks):
    order = [0]
    for mask in reversed(masks):
        order = order + [mask + i for i in order]
    return order


def fits(rows):
    return rows == 8 and D // rows % 32 == 0


def store_chunks(load, keep, send, meta, rows, first):
    size = D // rows
    for index, place in enumerate(places(mask_order(rows, first))):
        at = pl.multiple_of(jnp.bitwise_xor(meta[1], place) * size, 32)
        into = keep if index < rows // 2 else send
        row_at = index % (rows // 2) * size
        into[row_at : row_at + size, :] = load(pl.ds(at, size)).astype(into.dtype)


def store_low(grad, keep, send, meta, rows):
    size, hid = D // 4, FF // 4
    for index, place in enumerate(places(mask_order(rows, 2))):
        chunk = jnp.bitwise_xor(meta[1], place)
        at = pl.ds(pl.multiple_of(chunk % 4 * size, 64), size)
        down = pl.multiple_of(hid + chunk // 4 * (hid // 2), LANES)
        out = pl.multiple_of(2 * hid + chunk // 4 * LANES, LANES)
        into = keep if index < rows // 2 else send
        row_at = slice(index % (rows // 2) * size, (index % (rows // 2) + 1) * size)
        into[row_at, : hid // 2] = grad[at, pl.ds(down, hid // 2)].astype(BF16)
        into[row_at, hid // 2 :] = grad[at, pl.ds(out, LANES)].astype(BF16)


def low_shapes(rows):
    if fits(rows):
        return [(D, FF // 8 + LANES)] * 2
    return [(D, FF // 4 + 2 * LANES), (8, LANES)]


def low_chunks(keep, send, rows):
    if fits(rows):
        return keep, send
    hid, width, count = FF // 4, D // 4, rows // 4
    parts = [
        part.reshape(4, width, count, part.shape[1] // count).transpose(2, 0, 1, 3)
        for part in (keep[:, :hid], keep[:, hid : hid + width])
    ]
    chunks = jnp.concatenate(parts, axis=3).reshape(rows, width, -1)
    order = jnp.array(places(mask_order(rows, 2))) ^ lax.axis_index("rows")
    chunks = jnp.take(chunks, order, axis=0).reshape(rows * width, -1)
    return chunks[: rows * width // 2], chunks[rows * width // 2 :]


def chunk_shapes(cols, rows, extra=0):
    if fits(rows):
        return [(D // 2 + extra, cols)] * 2
    return [(D, cols), (8, LANES)]


def chunks_of(keep, send, rows, first):
    if fits(rows):
        return keep, send
    order = jnp.array(places(mask_order(rows, first))) ^ lax.axis_index("rows")
    parts = keep.reshape(rows, D // rows, keep.shape[1])
    parts = jnp.take(parts, order, axis=0).reshape(keep.shape)
    return parts[: D // 2], parts[D // 2 :]


def feed(normed, upstream, gain, shift, w_up, b_up, w_down):
    mlp_in = (normed * row(gain) + row(shift)).astype(BF16)
    hidden = dot(mlp_in, w_up[...]) + b_up
    cdf = 0.5 * (1.0 + lax.erf(hidden * (0.5**0.5)))
    act = (hidden * cdf).astype(BF16)
    slope = cdf + hidden * jnp.exp(-0.5 * hidden * hidden) * ((2.0 * math.pi) ** -0.5)
    grad_low = (slope * dot_nt(upstream, w_down[...])).astype(BF16)
    grad_norm = dot_nt(grad_low, w_up[...])
    return mlp_in, act, grad_low, grad_norm


def add_sums(sums, grad_low, grad_norm, normed):
    sums[0:1, :] += jnp.sum(grad_low.astype(F32), axis=0, keepdims=True)
    sums[1:2, :] += jnp.sum(grad_norm * normed, axis=0, keepdims=True)
    sums[2:3, :] += jnp.sum(grad_norm, axis=0, keepdims=True)


def own_row(ref, blk, size):
    return ref[pl.ds(pl.multiple_of(blk * size, LANES), size)].reshape(1, size)


def mlp_first_kernel(
    half, meta, xa, xb, ca, cb, gain, shift, b_up, w_up, w_down, w_out,
    gain1, shift1, b_qkv, low, high, w0, w1, w2, w3, w4, w5,
    mo_ref, e_ref, n_ref, gv_ref, sums, gup, gdown, q_ref, k_ref, v_ref, w_own, b_own, x_s, c_s,
):
    step = pl.program_id(0)

    @pl.when(step < half)
    def _():
        x_s[...] = xa[...]
        c_s[...] = ca[...]

    @pl.when(step >= half)
    def _():
        x_s[...] = xb[...]
        c_s[...] = cb[...]

    @pl.when(step == 0)
    def _():
        sums[...] = jnp.zeros_like(sums)
        gup[...] = jnp.zeros_like(gup)
        gdown[...] = jnp.zeros_like(gdown)
        odd = meta[0] % 2
        own_blocks((w0, w1, w2, w3, w4, w5), odd, w_own)
        own_bias(b_qkv, odd, meta[0], b_own)

    upstream = c_s[...]

    @pl.when(step < half)
    def _():
        sums[3:4, :] += jnp.sum(upstream.astype(F32), axis=0, keepdims=True)

    normed = normalize(x_s[...].astype(F32))
    n_ref[...] = normed.astype(BF16)
    tile = true_block(meta, step // half) * half + step % half
    project_tile(normed, gain1, shift1, w_own, b_own, low, high, tile, q_ref, k_ref, v_ref)
    bias = own_row(b_up, meta[0], gup.shape[1])
    mlp_in, act, grad_low, grad_norm = feed(normed, upstream, gain, shift, w_up, bias, w_down)
    mo_ref[...] = dot(act, w_down[...]).astype(BF16)
    add_sums(sums, grad_low, grad_norm, normed)
    e_ref[...] = (grad_norm * row(gain)).astype(BF16)
    gv_ref[...] = dot_nt(upstream, w_out[...]).astype(BF16)
    gup[...] += dot_tn(mlp_in, grad_low)
    gdown[...] += dot_tn(upstream, act)


def mlp_second_kernel(
    half, rows, meta, xa, xb, ca, cb, gain, shift, b_up, w_up, w_down, w_out,
    c0, c1, mo_in, o_near, o_far, sums_in, gup, gdown, *refs
):
    e_ref, n_ref, gv_ref, sums, even, odd, up_keep, up_send, low_keep, low_send = refs[3:13]
    x_s, c_s, n_s, grad = refs[13:]
    step = pl.program_id(0)
    hid = gup.shape[1]

    @pl.when(step < half)
    def _():
        x_s[...] = xa[...]
        c_s[...] = ca[...]
        n_s[...] = c0[...]

    @pl.when(step >= half)
    def _():
        x_s[...] = xb[...]
        c_s[...] = cb[...]
        n_s[...] = c1[...]

    @pl.when(step == 0)
    def _():
        sums[...] = sums_in[...]
        grad[:, 0:hid] = gup[...]
        grad[:, hid : 2 * hid] = gdown[...]
        grad[:, 2 * hid :] = jnp.zeros_like(grad[:, 2 * hid :])

    upstream = c_s[...]
    normed = normalize(x_s[...].astype(F32))
    n_ref[...] = normed.astype(BF16)
    bias = own_row(b_up, meta[0], hid)
    mlp_in, act, grad_low, grad_norm = feed(normed, upstream, gain, shift, w_up, bias, w_down)
    add_sums(sums, grad_low, grad_norm, normed)
    e_ref[...] = (grad_norm * row(gain)).astype(BF16)
    gv_ref[...] = dot_nt(upstream, w_out[...]).astype(BF16)
    grad[:, 0:hid] += dot_tn(mlp_in, grad_low)
    grad[:, hid : 2 * hid] += dot_tn(upstream, act)
    out_grad = dot_tn(upstream, o_far[...]) + dot_tn(n_s[...], o_near[...])
    side = out_grad.shape[1] // 2
    if fits(rows):
        grad[:, 2 * hid : 2 * hid + side] += out_grad[:, :side]
        grad[:, 2 * hid + LANES : 2 * hid + LANES + side] += out_grad[:, side:]
    else:
        grad[:, 2 * hid : 2 * hid + 2 * side] += out_grad
    far = (dot(act, w_down[...]) + dot(o_far[...], w_out[...])).astype(BF16)
    near = (mo_in[...].astype(F32) + dot(o_near[...], w_out[...])).astype(BF16)

    @pl.when(step < half)
    def _():
        even[0] = near
        even[1] = far

    @pl.when(step >= half)
    def _():
        odd[0] = near
        odd[1] = far

    @pl.when(step == pl.num_programs(0) - 1)
    def _():
        if fits(rows):
            store_chunks(lambda at: grad[at, 0:hid], up_keep, up_send, meta, rows, 1)
            store_low(grad, low_keep, low_send, meta, rows)
        else:
            up_keep[...] = grad[:, 0:hid].astype(BF16)
            low_keep[...] = grad[:, hid:].astype(BF16)


def feed_forward(
    meta, xs, cs, gain, shift, b_up, w_up, w_down, w_out, rows, seq,
    joined=None, before=None, near=None, attn=None,
):
    per = seq // TILE
    steps = 2 * per
    hid = FF // 4
    width = D // 4
    total = 4 * seq
    first = pl.BlockSpec((TILE, D), lambda i, m: (jnp.minimum(i, per - 1), 0))
    second = pl.BlockSpec((TILE, D), lambda i, m: (jnp.maximum(i - per, 0), 0))
    specs = [
        first,
        second,
        first,
        second,
        whole((D,)),
        whole((D,)),
        whole((FF,)),
        pl.BlockSpec((D, hid), lambda i, m: (0, m[0])),
        pl.BlockSpec((hid, D), lambda i, m: (m[0], 0)),
        pl.BlockSpec((width, D), lambda i, m: (m[0], 0)),
    ]
    args = [*xs, *cs, gain, shift, b_up, w_up, w_down, w_out]
    tile = pl.BlockSpec((TILE, D), lambda i, m: (i, 0))
    narrow = pl.BlockSpec((TILE, width), lambda i, m: (i, 0))
    sums = (8, D)
    scratch = [pltpu.VMEM((TILE, D), BF16), pltpu.VMEM((TILE, D), BF16)]
    pair = jax.ShapeDtypeStruct((steps * TILE, D), BF16)
    full = jax.ShapeDtypeStruct((total, D), BF16)
    vec = jax.ShapeDtypeStruct((total, width), BF16)
    if before is None:
        body = partial(mlp_first_kernel, per)
        gain1, shift1, w_qkv, b_qkv, low, high = joined
        args += [gain1, shift1, b_qkv, low, high]
        specs += [whole(a.shape) for a in args[-5:]]
        for part in range(3):
            for side in range(2):
                specs.append(
                    pl.BlockSpec(
                        (D, LANES),
                        lambda i, m, at=part * D // LANES + side: (0, at + 3 * m[0] // 2),
                    )
                )
                args.append(w_qkv)
        outs = [pair, full, full, vec, jax.ShapeDtypeStruct(sums, F32)]
        outs += [jax.ShapeDtypeStruct((D, hid), F32)] * 2 + [vec] * 3
        outs += [
            jax.ShapeDtypeStruct((D, 3 * width), BF16),
            jax.ShapeDtypeStruct((1, 3 * width), F32),
        ]
        out_specs = [tile, tile, tile, narrow, whole(sums)]
        out_specs += [whole((D, hid))] * 2 + [narrow] * 3
        out_specs += [whole((D, 3 * width)), whole((1, 3 * width))]
        aliases = {}
    else:
        body = partial(mlp_second_kernel, per, rows)
        mlp_out, norm_part, normed, grad_vec, sums_in, gup, gdown = before
        chunks = chunk_shapes(hid, rows) + low_shapes(rows)
        args += [*near, mlp_out, attn, attn, sums_in, gup, gdown, norm_part, normed, grad_vec]
        specs += [
            first,
            second,
            tile,
            narrow,
            pl.BlockSpec((TILE, width), lambda i, m: (i + steps, 0)),
            whole(sums),
            whole((D, hid)),
            whole((D, hid)),
            *(pl.BlockSpec(memory_space=pl.ANY),) * 3,
        ]
        aliases = {len(args) - 2 + i: i for i in range(3)}
        both = jax.ShapeDtypeStruct((2, seq, D), BF16)
        outs = [full, full, vec, jax.ShapeDtypeStruct(sums, F32), both, both]
        late = pl.BlockSpec((TILE, D), lambda i, m: (i + steps, 0))
        outs += [jax.ShapeDtypeStruct(shape, BF16) for shape in chunks]
        out_specs = [
            late,
            late,
            pl.BlockSpec((TILE, width), lambda i, m: (i + steps, 0)),
            whole(sums),
            pl.BlockSpec((2, TILE, D), lambda i, m: (0, jnp.minimum(i, per - 1), 0)),
            pl.BlockSpec((2, TILE, D), lambda i, m: (0, jnp.maximum(i - per, 0), 0)),
            *(whole(shape) for shape in chunks),
        ]
        scratch += [pltpu.VMEM((TILE, D), BF16), pltpu.VMEM((D, 2 * hid + 2 * LANES), F32)]
    return pl.pallas_call(
        body,
        out_shape=outs,
        grid_spec=pltpu.PrefetchScalarGridSpec(
            num_scalar_prefetch=1,
            grid=(steps,),
            in_specs=specs,
            out_specs=out_specs,
            scratch_shapes=scratch,
        ),
        input_output_aliases=aliases,
        compiler_params=params(),
        cost_estimate=COST,
        name="mlp_first" if before is None else "mlp_second",
    )(meta, *args)


def head_masks():
    lane = lax.broadcasted_iota(jnp.int32, (1, LANES), 1)
    first = jnp.where(lane < HDIM, 1.0, 0.0).astype(BF16)
    second = jnp.where(lane < HDIM, 0.0, 1.0).astype(BF16)
    return first, second


def slot_rows(meta, per, tile):
    slot = jnp.bitwise_xor(tile // per, meta[0])
    return pl.multiple_of((slot * per + tile % per) * TILE, TILE)


def by_head(first, second, block, third):
    return (block * first, block * second, third)


def transpose_all(from_ref, to_ref):
    @pl.loop(0, from_ref.shape[0] // TILE)
    def _(tile):
        rows = pl.ds(pl.multiple_of(tile * TILE, TILE), TILE)
        to_ref[:, rows] = from_ref[rows, :].astype(F32).T.astype(BF16)


def attend_kernel(per, meta, lo, hi, q_ref, k_ref, v_ref, start_ref, o_ref, lse_ref, vt_ref, acc, s_ref):
    mask0, mask1 = head_masks()
    tiles = k_ref.shape[0] // TILE
    qi = pl.program_id(0)

    @pl.when(qi == 0)
    def _():
        ones = jnp.where(lax.broadcasted_iota(jnp.int32, (VROWS - HDIM, TILE), 0) == 0, 1.0, 0.0)

        @pl.loop(0, tiles)
        def _(tile):
            rows = pl.ds(pl.multiple_of(tile * TILE, TILE), TILE)
            block = v_ref[rows, :].astype(F32).T
            for head in range(3):
                at = head * VROWS
                vt_ref[at : at + HDIM, rows] = block[head * HDIM : (head + 1) * HDIM].astype(BF16)
                vt_ref[at + HDIM : at + VROWS, rows] = ones.astype(BF16)

    key_iota = lax.broadcasted_iota(jnp.int32, (TILE, TILE), 0)
    query_iota = lax.broadcasted_iota(jnp.int32, (TILE, TILE), 1)
    queries = by_head(mask0, mask1, q_ref[:, 0:128], q_ref[:, 128:192])
    starts = start_ref[0]
    acc[...] = jnp.zeros_like(acc)

    def key_tile(turn):
        return jnp.where(turn == 0, qi, first + turn - 1)

    def score(masked, ki):
        k_rows = pl.ds(slot_rows(meta, per, ki), TILE)
        pair, third = k_ref[k_rows, 0:128], k_ref[k_rows, 128:192]
        scores = [dot_nt(third if head == 2 else pair, queries[head]) for head in range(3)]
        if masked:
            allowed = (key_iota >= starts - ki * TILE) & (key_iota <= query_iota + (qi - ki) * TILE)
            scores = [jnp.where(allowed, x, MASKED) for x in scores]
        return scores, [jnp.max(x, axis=0, keepdims=True) for x in scores]

    def value(ki, tops, peaks):
        k_rows = pl.ds(slot_rows(meta, per, ki), TILE)
        news = [jnp.maximum(top, peak) for top, peak in zip(tops, peaks)]
        fades = [jnp.exp2(top - new) for top, new in zip(tops, news)]
        weights = [jnp.exp2(s_ref[head] - news[head]).astype(BF16) for head in range(3)]
        terms = [
            dot(vt_ref[head * VROWS : (head + 1) * VROWS, k_rows], weights[head]) for head in range(3)
        ]
        return news, fades, terms

    def put(fades, terms):
        for head in range(3):
            cols = slice(head * VROWS, (head + 1) * VROWS)
            acc[cols, :] = acc[cols, :] * fades[head] + terms[head]

    def visit(masked, turn, carry):
        tops, peaks = carry
        scores, next_peaks = score(masked, key_tile(turn + 1))
        news, fades, terms = value(key_tile(turn), tops, peaks)
        peaks = next_peaks
        for head in range(3):
            s_ref[head] = scores[head]
        put(fades, terms)
        return tuple(news), tuple(peaks)

    first = lo[qi]
    full = jnp.minimum(hi[qi], qi)
    scores, peaks = score(True, qi)
    for head in range(3):
        s_ref[head] = scores[head]
    carry = ((jnp.full((1, TILE), MASKED, F32),) * 3, tuple(peaks))
    carry = lax.fori_loop(0, full - first, partial(visit, True), carry)
    carry = lax.fori_loop(full - first, qi - first, partial(visit, False), carry)
    tops, fades, terms = value(key_tile(qi - first), *carry)
    put(fades, terms)
    heads = []
    for head, top in enumerate(tops):
        at = head * VROWS
        total = acc[at + HDIM : at + HDIM + 1, :]
        heads.append(acc[at : at + HDIM, :] / total)
        lse_ref[head, 0] = top + jnp.log2(total)
    o_ref[...] = jnp.concatenate(heads, axis=0).T.astype(BF16)

def attend(meta, lo, hi, query, keys, values, starts, per):
    total, width = query.shape
    tiles = total // TILE
    def slot(i, m):
        return jnp.bitwise_xor(i // per, m[0]) * per + i % per
    q_spec = pl.BlockSpec((TILE, width), lambda i, m, lo, hi: (slot(i, m), 0))
    start_spec = pl.BlockSpec((1, 1, TILE), lambda i, m, lo, hi: (slot(i, m), 0, 0))
    lse_spec = pl.BlockSpec((3, 1, 1, TILE), lambda i, m, lo, hi: (0, slot(i, m), 0, 0))
    return pl.pallas_call(
        partial(attend_kernel, per),
        out_shape=[
            jax.ShapeDtypeStruct((total, width), BF16),
            jax.ShapeDtypeStruct((3, tiles, 1, TILE), F32),
        ],
        grid_spec=pltpu.PrefetchScalarGridSpec(
            num_scalar_prefetch=3,
            grid=(tiles,),
            in_specs=[q_spec, whole(keys.shape), whole(values.shape), start_spec],
            out_specs=[q_spec, lse_spec],
            scratch_shapes=[pltpu.VMEM((3 * VROWS, total), BF16), pltpu.VMEM((3 * VROWS, TILE), F32), pltpu.VMEM((3, TILE, TILE), F32)],
        ),
        compiler_params=params(),
        cost_estimate=COST,
        name="attend",
    )(meta, lo, hi, query, keys, values, starts)


def attend_back_kernel(
    per, meta, lo, hi, q_ref, k_ref, v_ref, o_ref, gv_ref, start_ref, lse_ref, low, high,
    gj_ref, kt_ref, dk_ref, dv_ref, dqt_ref
):
    mask0, mask1 = head_masks()
    tiles = k_ref.shape[0] // TILE
    qi = tiles - 1 - pl.program_id(0)

    @pl.when(pl.program_id(0) == 0)
    def _():
        transpose_all(k_ref, kt_ref)

    own_rows = pl.ds(slot_rows(meta, per, qi), TILE)
    key_iota = lax.broadcasted_iota(jnp.int32, (TILE, TILE), 0)
    query_iota = lax.broadcasted_iota(jnp.int32, (TILE, TILE), 1)
    queries = by_head(mask0, mask1, q_ref[:, 0:128], q_ref[:, 128:192])
    grads = by_head(mask0, mask1, gv_ref[:, 0:128], gv_ref[:, 128:192])
    starts = start_ref[0]
    lses = [lse_ref[head, 0] for head in range(3)]
    product = (gv_ref[...].astype(F32) * o_ref[...].astype(F32)).T
    deltas = [
        jnp.sum(product[head * HDIM : (head + 1) * HDIM], axis=0, keepdims=True)
        for head in range(3)
    ]
    dqt_ref[...] = jnp.zeros_like(dqt_ref)

    @pl.when(pl.program_id(0) == 0)
    def _():
        dk_ref[...] = jnp.zeros_like(dk_ref)
        dv_ref[...] = jnp.zeros_like(dv_ref)

    def load(ki):
        k_rows = pl.ds(slot_rows(meta, per, ki), TILE)
        return k_rows

    def score(masked, ki):
        k_rows = load(ki)
        pair, third = k_ref[k_rows, 0:128], k_ref[k_rows, 128:192]
        v_pair, v_third = v_ref[k_rows, 0:128], v_ref[k_rows, 128:192]
        scores = [dot_nt(third if head == 2 else pair, queries[head]) for head in range(3)]
        grad_probs = [dot_nt(v_third if head == 2 else v_pair, grads[head]) for head in range(3)]
        if masked:
            allowed = (key_iota >= starts - ki * TILE) & (key_iota <= query_iota + (qi - ki) * TILE)
            scores = [jnp.where(allowed, x, MASKED) for x in scores]
        return scores, grad_probs

    def terms(ki, scores, grad_probs):
        k_rows = load(ki)
        probs = [jnp.exp2(x - lse) for x, lse in zip(scores, lses)]
        grad_scores = [
            (p * (g - delta)).astype(BF16) for p, g, delta in zip(probs, grad_probs, deltas)
        ]
        dv = [dot(p.astype(BF16), g) for p, g in zip(probs, grads)]
        dk = [dot(g, q) for g, q in zip(grad_scores, queries)]
        dq = [
            dot(kt_ref[head * HDIM : (head + 1) * HDIM, k_rows], grad_scores[head])
            for head in range(3)
        ]
        return dk, dv, dq

    def add(ki, dk, dv, dq):
        k_rows = load(ki)
        for into, parts in ((dk_ref, dk), (dv_ref, dv)):
            into[k_rows, 0:128] += parts[0] + parts[1]
            into[k_rows, 128:192] += parts[2]
        for head in range(3):
            dqt_ref[head * HDIM : (head + 1) * HDIM, :] += dq[head]

    first = lo[qi]
    full = jnp.minimum(hi[qi], qi)

    def visit(masked, ki):
        add(ki, *terms(ki, *score(masked, ki)))

    @pl.loop(first, full)
    def _(ki):
        visit(True, ki)

    @pl.loop(full, qi)
    def _(ki):
        visit(False, ki)

    visit(True, qi)

    cos, sin = rotation(low, high, qi)

    def turn_back(block):
        return block * cos - swap_halves(block) * sin

    dq = dqt_ref[...].T * (HDIM**-0.5)
    dk = dk_ref[own_rows, :] * LN2
    gj_ref[:, 0:128] = turn_back(dq[:, 0:128]).astype(BF16)
    gj_ref[:, 128:256] = turn_back(dk[:, 0:128]).astype(BF16)
    mixed = jnp.concatenate([dq[:, 128:192], dk[:, 128:192]], axis=1)
    gj_ref[:, 256:384] = turn_back(mixed).astype(BF16)
    gj_ref[:, 384:576] = dv_ref[own_rows, :].astype(BF16)


def attend_back(
    meta, lo, hi, query, keys, values, attn, grad_vec, starts, lse, low, high, per
):
    total, width = query.shape
    tiles = total // TILE

    def slot(i, m):
        tile = tiles - 1 - i
        return jnp.bitwise_xor(tile // per, m[0]) * per + tile % per

    q_spec = pl.BlockSpec((TILE, width), lambda i, m, lo, hi: (slot(i, m), 0))
    gj_spec = pl.BlockSpec((TILE, 3 * width), lambda i, m, lo, hi: (slot(i, m), 0))
    start_spec = pl.BlockSpec((1, 1, TILE), lambda i, m, lo, hi: (slot(i, m), 0, 0))
    lse_spec = pl.BlockSpec((3, 1, 1, TILE), lambda i, m, lo, hi: (0, slot(i, m), 0, 0))
    return pl.pallas_call(
        partial(attend_back_kernel, per),
        out_shape=jax.ShapeDtypeStruct((total, 3 * width), BF16),
        grid_spec=pltpu.PrefetchScalarGridSpec(
            num_scalar_prefetch=3,
            grid=(tiles,),
            in_specs=[
                q_spec,
                whole(keys.shape),
                whole(values.shape),
                q_spec,
                q_spec,
                start_spec,
                lse_spec,
                whole(low.shape),
                whole(high.shape),
            ],
            out_specs=gj_spec,
            scratch_shapes=[
                pltpu.VMEM((width, total), BF16),
                pltpu.VMEM((total, width), F32),
                pltpu.VMEM((total, width), F32),
                pltpu.VMEM((width, TILE), F32),
            ],
        ),
        compiler_params=params(),
        cost_estimate=COST,
        name="attend_back",
    )(meta, lo, hi, query, keys, values, attn, grad_vec, starts, lse, low, high)


SMALL = 16


def pack_small(gain_sum, shift_sum, bias, mlp_sums):
    third = 3 * D // 4
    which = lax.broadcasted_iota(jnp.int32, (8, D), 0)
    table = jnp.concatenate([jnp.zeros((4, D), F32), mlp_sums[0:4]], axis=0)
    table = jnp.where(which == 0, gain_sum, jnp.where(which == 1, shift_sum, table))
    head = jnp.where(which[:, :third] == 2, bias, table[:, :third])
    tail = jnp.concatenate([table[:, third:], jnp.zeros((8, 2 * third - D), F32)], axis=1)
    return jnp.concatenate([head, tail], axis=0)


def high_low(value):
    high = value.astype(BF16)
    return high, (value - high.astype(F32)).astype(BF16)


def weight_kernel(rows, meta, *refs):
    gj_ref, n_ref, gain, shift, w_ref, mlp_sums, keep, send, small, grad, bias = refs
    step = pl.program_id(0)

    @pl.when(step == 0)
    def _():
        grad[...] = jnp.zeros_like(grad)
        bias[...] = jnp.zeros_like(bias)

    joined = gj_ref[...]
    bias[0:1, :] += jnp.sum(joined.astype(F32), axis=0, keepdims=True)
    grad[...] += dot_tn(n_ref[...], joined)

    @pl.when(step == pl.num_programs(0) - 1)
    def _():
        total = bias[0:1, :]
        width = total.shape[1]
        parts = jnp.concatenate(
            [*high_low(jnp.broadcast_to(total, (8, width)))], axis=0
        )
        shift_sum = dot_nt(parts, w_ref[...])
        shift_sum = shift_sum[0:1] + shift_sum[8:9]
        ones = jnp.ones((16, width), BF16)
        high, low = high_low(grad[...] * w_ref[...].astype(F32))
        gain_sum = (dot_nt(ones, high) + dot_nt(ones, low))[0:1]
        columns = jnp.concatenate(
            [jnp.broadcast_to(row(gain), (8, D)), jnp.broadcast_to(row(shift), (8, D))], axis=0
        ).T
        grad[...] = grad[...] * columns[:, 0:1] + columns[:, 8:9] * total
        rest = pack_small(gain_sum, shift_sum, total, mlp_sums[...])
        small[...] = rest
        if fits(rows):
            store_chunks(lambda at: grad[at, :], keep, send, meta, rows, 1)
            keep[D // 2 :, :] = rest.astype(BF16)
            send[D // 2 :, :] = rest.astype(BF16)
        else:
            keep[...] = grad[...].astype(BF16)


def row_tiles(cols, tile=TILE):
    return pl.BlockSpec((tile, cols), lambda i, m: (i, 0))


def joined_weight(meta, grad, normed, gain, shift, w, mlp_sums, rows):
    total, width = grad.shape
    tile = 2 * TILE
    chunks = chunk_shapes(width, rows, SMALL)
    args = [gain, shift, w, mlp_sums]
    return pl.pallas_call(
        partial(weight_kernel, rows),
        out_shape=[jax.ShapeDtypeStruct(shape, BF16) for shape in chunks]
        + [jax.ShapeDtypeStruct((SMALL, width), F32)],
        grid_spec=pltpu.PrefetchScalarGridSpec(
            num_scalar_prefetch=1,
            grid=(total // tile,),
            in_specs=[row_tiles(width, tile), row_tiles(D, tile), *(whole(a.shape) for a in args)],
            out_specs=[*(whole(shape) for shape in chunks), whole((SMALL, width))],
            scratch_shapes=[pltpu.VMEM((D, width), F32), pltpu.VMEM((8, width), F32)],
        ),
        compiler_params=params(),
        cost_estimate=COST,
        name="joined_weight",
    )(meta, grad, normed, *args)


def norm_kernel(meta, *refs):
    gjs, es, (gain, w_ref), outs = refs[0:4], refs[4:8], refs[8:10], refs[10:]
    for gj_ref, e_in, out in zip(gjs, es, outs):
        grad_norm = dot_nt(gj_ref[...], w_ref[...])
        out[...] = (grad_norm * row(gain) + e_in[...].astype(F32)).astype(BF16)


def norm_grad(meta, grad, e_mlp, gain, w, seq):
    tile = TILE
    per = seq // tile

    def slot_tiles(slot, cols):
        return pl.BlockSpec((tile, cols), lambda i, m: (slot * per + i, 0))

    return pl.pallas_call(
        norm_kernel,
        out_shape=[jax.ShapeDtypeStruct((seq, D), BF16)] * 4,
        grid_spec=pltpu.PrefetchScalarGridSpec(
            num_scalar_prefetch=1,
            grid=(per,),
            in_specs=[
                *(slot_tiles(slot, grad.shape[1]) for slot in range(4)),
                *(slot_tiles(slot, D) for slot in range(4)),
                whole(gain.shape),
                whole(w.shape),
            ],
            out_specs=[slot_tiles(0, D)] * 4,
        ),
        compiler_params=params(),
        cost_estimate=COST,
        name="norm_grad",
    )(meta, *[grad] * 4, *[e_mlp] * 4, gain, w)


def simple(body, name, shapes, *args, specs=None):
    return pl.pallas_call(
        body,
        out_shape=[jax.ShapeDtypeStruct(shape, kind) for shape, kind in shapes],
        grid_spec=pltpu.PrefetchScalarGridSpec(
            num_scalar_prefetch=1,
            grid=(1,),
            in_specs=specs or [whole(a.shape) for a in args[1:]],
            out_specs=[whole(shape) for shape, _ in shapes],
        ),
        compiler_params=params(),
        cost_estimate=COST,
        name=name,
    )(*args)


def add_up(refs):
    total = refs[0][...].astype(F32)
    for ref in refs[1:]:
        total += ref[...].astype(F32)
    return total


def sums_kernel(counts, meta, *refs):
    ins, outs = refs[: sum(counts)], refs[sum(counts) :]
    for count, out in zip(counts, outs):
        out[...] = add_up(ins[:count]).astype(BF16)
        ins = ins[count:]


def block_sums(name, meta, steps, *jobs):
    specs, args, outs, out_specs = [], [], [], []
    for rows, terms in jobs:
        size, cols = rows // steps, terms[0][0].shape[1]
        for array, at in terms:
            specs.append(pl.BlockSpec((size, cols), lambda i, m, at=at // size: (at + i, 0)))
            args.append(array)
        outs.append(jax.ShapeDtypeStruct((rows, cols), BF16))
        out_specs.append(pl.BlockSpec((size, cols), lambda i, m: (i, 0)))
    return pl.pallas_call(
        partial(sums_kernel, [len(terms) for _, terms in jobs]),
        out_shape=outs,
        grid_spec=pltpu.PrefetchScalarGridSpec(
            num_scalar_prefetch=1, grid=(steps,), in_specs=specs, out_specs=out_specs
        ),
        compiler_params=params(),
        cost_estimate=COST,
        name=name,
    )(meta, *args)


def lower_kernel(meta, piece, *refs):
    *terms, down_ref, out_ref, up_ref = refs
    up_ref[...] = add_up(terms)
    cut = down_ref.shape[1]
    down_ref[...] = piece[:, :cut].astype(F32)
    out_ref[...] = piece[:, cut:].astype(F32).T[: out_ref.shape[0]]


def last_qkv_kernel(meta, *refs):
    *terms, sums, got_sums, kept, near, far, small = refs
    size = kept.shape[0]
    width = kept.shape[1]
    total = add_up(terms)
    rows = sums[...].astype(F32) + got_sums[...].astype(F32)
    for part in range(3):
        small[part * 8 : part * 8 + 8, :] = rows[0:8, part * width : (part + 1) * width]
    small[24:32, :] = rows[8:16, 0:width]
    near[size:, :] = small[...]
    far[size:, :] = small[...]
    query = jnp.concatenate([total[:, 0:128], total[:, 256:320]], axis=1)
    keys = jnp.concatenate([total[:, 128:256], total[:, 320:384]], axis=1)
    values = total[:, 384:576]
    plans = (
        (query, keys, values),
        (keys, query, values),
        (keys, values, query),
        (values, keys, query),
    )
    for blk, plan in enumerate(plans):

        @pl.when(meta[0] == blk)
        def _(plan=plan):
            kept[...] = plan[0]
            near[0:size, :] = plan[1]
            far[0:size, :] = plan[2]


def assemble_kernel(
    meta, kept, small, near, far, diag,
    qkv, b_qkv, b_out, b_up, b_down, gain1, shift1, gain2, shift2, table,
):
    size, width = kept.shape

    @pl.when(meta[0] % 2 == 0)
    def _():
        qkv[:, 0:width] = kept[...]
        qkv[:, 2 * width :] = far[0:size, :]

    @pl.when(meta[0] % 2 == 1)
    def _():
        qkv[:, 0:width] = far[0:size, :]
        qkv[:, 2 * width :] = kept[...]

    qkv[:, width : 2 * width] = near[0:size, :]
    table[0] = small[...]
    table[1] = near[size:, :]
    table[2] = far[size:, :]
    table[3] = diag[...]
    blocks = [table[jnp.bitwise_xor(meta[0], blk)] for blk in range(4)]
    total = blocks[0] + blocks[1] + blocks[2] + blocks[3]

    def vector(rows, index):
        parts = [rows[part * 8 + index : part * 8 + index + 1, :] for part in range(4)]
        return jnp.concatenate(parts, axis=1)

    for ref, index in ((gain1, 0), (shift1, 1), (gain2, 5), (shift2, 6), (b_out, 7), (b_down, 7)):
        ref[...] = vector(total, index).reshape(D)
    ups, parts = [], ([], [], [])
    for rows in blocks:
        ups.append(vector(rows, 4))
        joined = vector(rows, 2)
        parts[0].append(jnp.concatenate([joined[:, 0:128], joined[:, 256:320]], axis=1))
        parts[1].append(jnp.concatenate([joined[:, 128:256], joined[:, 320:384]], axis=1))
        parts[2].append(joined[:, 384:576])
    b_up[...] = jnp.concatenate(ups, axis=1).reshape(4 * D)
    b_qkv[...] = jnp.concatenate(parts[0] + parts[1] + parts[2], axis=1).reshape(3 * D)


def assemble(meta, kept, small, near, far, diag):
    size, width = kept.shape
    shapes = [((size, 3 * width), F32), ((3 * D,), F32), ((D,), F32), ((4 * D,), F32)]
    shapes += [((D,), F32)] * 5
    args = (kept, small, near, far, diag)
    return pl.pallas_call(
        assemble_kernel,
        out_shape=[jax.ShapeDtypeStruct(shape, kind) for shape, kind in shapes],
        grid_spec=pltpu.PrefetchScalarGridSpec(
            num_scalar_prefetch=1,
            grid=(1,),
            in_specs=[whole(a.shape) for a in args],
            out_specs=[whole(shape) for shape, _ in shapes],
            scratch_shapes=[pltpu.VMEM((4, 32, width), F32)],
        ),
        compiler_params=params(),
        cost_estimate=COST,
        name="assemble",
    )(meta, *args)


def next_send(terms, size):
    return sum(term[size // 2 : size].astype(F32) for term in terms).astype(BF16)


def reduce_plain(keep, got, masks):
    terms, size = [keep, got], keep.shape[0]
    for mask in masks:
        terms.append(swap(next_send(terms, size), "rows", mask))
        size //= 2
    return sum(term[:size].astype(F32) for term in terms)


def after(value, *others):
    return lax.optimization_barrier((value, others))[0]


def swap(value, axis, mask):
    size = lax.axis_size(axis)
    return lax.ppermute(value, axis, [(i, i ^ mask) for i in range(size)])


def add_low(left, right):
    return (left.astype(F32) + right.astype(F32)).astype(BF16)


def spread_rows(chunk):
    rows = lax.axis_size("rows")
    moves = [
        (r * 4 + b, (rows // 4 * b + r // 4) * 4 + r % 4) for r in range(rows) for b in range(4)
    ]
    return lax.ppermute(chunk, ("rows", "blk"), moves)


def split_columns(chunk):
    b = lax.axis_index("blk")
    q = jnp.concatenate([chunk[:, 0:128], chunk[:, 256:320]], axis=1)
    k = jnp.concatenate([chunk[:, 128:256], chunk[:, 320:384]], axis=1)
    v = chunk[:, 384:576]

    def choose(zero, one, two, three):
        return jnp.where(b < 2, jnp.where(b == 0, zero, one), jnp.where(b == 2, two, three))

    return choose(q, k, k, v), choose(k, q, v, k), choose(v, v, q, q)


def result_kernel(x_ref, even, near, far, b_out, b_down, out_ref):
    bias = row(b_out) + row(b_down)
    total = even[0].astype(F32) + near[0].astype(F32) + far[...].astype(F32)
    out_ref[...] = (x_ref[...].astype(F32) + bias + total).astype(BF16)


def token_kernel(x_ref, even, near, far, c_ref, out_ref):
    wide = x_ref[...].astype(F32)
    center = wide - jnp.mean(wide, axis=-1, keepdims=True)
    rate = lax.rsqrt(jnp.mean(center * center, axis=-1, keepdims=True) + EPS)
    normed = center * rate
    grad = even[...].astype(F32) + near[...].astype(F32) + far[...].astype(F32)
    mean = jnp.mean(grad, axis=-1, keepdims=True)
    along = jnp.mean(grad * normed, axis=-1, keepdims=True)
    back = rate * (grad - mean - normed * along)
    out_ref[...] = (c_ref[...].astype(F32) + back).astype(BF16)


def finish(body, name, seq, x, even, near, far, *more):
    flat = pl.BlockSpec((TILE, D), lambda i: (i, 0))
    own = pl.BlockSpec((1, TILE, D), lambda i: (0, i, 0))
    return pl.pallas_call(
        body,
        out_shape=jax.ShapeDtypeStruct((seq, D), BF16),
        grid=(seq // TILE,),
        in_specs=[
            *(own if a.ndim == 3 else flat for a in (x, even, near, far)),
            *(flat if a.ndim == 2 else whole(a.shape) for a in more),
        ],
        out_specs=flat,
        compiler_params=params(),
        cost_estimate=COST,
        name=name,
    )(x, even, near, far, *more)


def local(
    tokens, seg_ids, valid_len, ln1_gain, ln1_bias, w_qkv, b_qkv, w_out, b_out,
    ln2_gain, ln2_bias, w_up, b_up, w_down, b_down, cotangent,
):
    rows = lax.axis_size("rows")
    blk = lax.axis_index("blk")
    seq = tokens.shape[1]
    per = seq // TILE
    width = D // 4
    hid = FF // 4
    low, high = angle_parts(4 * seq)
    seg_row = jnp.pad(seg_ids.astype(BF16), ((0, EXTRA - 1), (0, D - seq)))
    tok_own = jnp.concatenate([tokens[0], seg_row], axis=0)
    cot_own = cotangent[0]

    cot_near = swap(cot_own, "blk", 1)
    tok_far = swap(tok_own, "blk", 2)
    tok_near = swap(tok_own, "blk", 1)
    cot_long = jnp.pad(cot_own, ((0, 2 * EXTRA), (0, 0)))
    cot_far = swap(cot_long, "blk", 2)

    meta = jnp.stack([blk, lax.axis_index("rows")]).astype(jnp.int32)
    mlp_args = (ln2_gain, ln2_bias, b_up, w_up, w_down, w_out, rows, seq)
    joined = (ln1_gain, ln1_bias, w_qkv, b_qkv, low, high)
    *first, query, keys, values, w_own, b_own = feed_forward(
        meta, (tok_own, tok_near), (cot_own, cot_near), *mlp_args, joined
    )
    meta = after(meta, b_own)

    def more(slot, m, tok, filled, slots=()):
        args = (ln1_gain, ln1_bias, low, high, w_own, b_own, filled, seq, slots)
        return project(slot, m, valid_len, tok, *args)

    tok_last = swap(after(tok_far, b_own), "blk", 1)
    joined = more(2, meta, tok_far, (query, keys, values))
    toks = (tok_own, tok_near, tok_far, tok_last)
    query, keys, values, starts, lo, hi = more(
        3, after(meta, joined[0]), tok_last, joined, toks
    )
    cot_last = swap(after(cot_far, lo), "blk", 1)
    cots = (cot_own, cot_near, cot_far, cot_last)
    attn, lse = attend(meta, lo, hi, query, keys, values, starts, per)

    meta = after(meta, lse)
    e_mlp, normed, grad_vec, mlp_sums, out_even, out_odd, *packets = feed_forward(
        meta, toks[2:], cots[2:], *mlp_args, before=first, near=cots[:2], attn=attn
    )
    up_keep, up_send = chunks_of(*packets[:2], rows, 1)
    low_keep, low_send = low_chunks(*packets[2:], rows)
    up_masks, low_masks = mask_order(rows, 1), mask_order(rows, 2)
    out_got = swap(out_odd, "blk", 1)
    up_got = swap(up_send, "rows", up_masks[0])
    low_got = swap(low_send, "rows", low_masks[0])

    meta = after(meta, mlp_sums)
    grad_joined = attend_back(
        meta, lo, hi, query, keys, values, attn, grad_vec, starts, lse, low, high, per
    )
    meta = after(meta, grad_joined)
    qkv_keep, qkv_send, small = joined_weight(
        meta, grad_joined, normed, ln1_gain, ln1_bias, w_own, mlp_sums, rows
    )
    qkv_keep, qkv_send = chunks_of(qkv_keep, qkv_send, rows, 1)
    qkv_got = swap(qkv_send, "rows", 1)

    half = D // 2
    if fits(rows):
        chunk = D // rows
        meta = after(meta, qkv_keep)
        up, lower = [up_keep, up_got], [low_keep, low_got]
        flat = [v.reshape(2 * seq, D) for v in (out_even, out_got)]
        up_send, low_send, out_send = block_sums(
            "first_sums",
            meta,
            2,
            (half // 2, [(term, half // 2) for term in up]),
            (half, [(term, half) for term in lower]),
            (seq, [(term, seq) for term in flat]),
        )
        up.append(swap(up_send, "rows", up_masks[1]))
        lower.append(swap(low_send, "rows", low_masks[1]))
    else:
        out_send = add_low(out_even[1], out_got[1])
    out_far = swap(out_send, "blk", 2)
    meta = after(meta, out_send)
    e_own, e_near, e_send, e_last = norm_grad(meta, grad_joined, e_mlp, ln1_gain, w_own, seq)
    e_last = swap(e_last, "blk", 1)
    e_near = swap(e_near, "blk", 1)
    if fits(rows):
        joined = [after(qkv_keep, e_own), qkv_got]
        tail = add_low(joined[0][half:], qkv_got[half:])
        qkv_send = jnp.concatenate([next_send(joined, half), tail])
        joined.append(swap(qkv_send, "rows", 2))
        meta = after(meta, qkv_send)
        low_send, up_send = block_sums(
            "second_sums",
            meta,
            1,
            (width, [(term, width) for term in lower]),
            (chunk, [(term, chunk) for term in up]),
        )
        lower.append(swap(low_send, "rows", low_masks[2]))
        up.append(swap(up_send, "rows", up_masks[2]))
        e_send = after(e_send, low_send, out_far)
    e_send = add_low(e_send, e_last)
    e_far = swap(e_send, "blk", 2)
    if fits(rows):
        joined[0] = after(joined[0], up_send, e_send)
        tail = add_low(after(qkv_send, up_send, e_send)[half // 2 :], joined[2][half // 2 :])
        qkv_send = jnp.concatenate([next_send(joined, half // 2), tail])
        joined.append(swap(qkv_send, "rows", 4))
        out_args = (after(tok_own, qkv_send), out_even, out_got, out_far, b_out, b_down)
        result = finish(result_kernel, "result", seq, *out_args)
        meta = after(meta, result)
        lower[0] = after(lower[0], result)
        piece = sum(term[:width].astype(F32) for term in lower).astype(BF16)
        meta = after(meta, piece)
        piece = spread_rows(piece)
        packet = ((chunk + 32, width), F32)
        last = pl.BlockSpec((SMALL, 3 * width), lambda i, m: (chunk // SMALL, 0))
        kept, near, far, small = simple(
            last_qkv_kernel,
            "last_qkv",
            [((chunk, width), F32), packet, packet, ((32, width), F32)],
            meta,
            *joined,
            qkv_send,
            joined[3],
            specs=[pl.BlockSpec((chunk, 3 * width), lambda i, m: (0, 0))] * 4 + [last] * 2,
        )
        near, far, diag = swap(near, "blk", 1), swap(far, "blk", 2), swap(small, "blk", 3)
        tok_args = (after(tok_own, small), e_own, e_near, e_far, cot_own)
        grad_tokens = finish(token_kernel, "token_grad", seq, *tok_args)
        meta = after(meta, grad_tokens)
        ends = [((width, hid // 2), F32), ((width // 2, width), F32), ((chunk, hid), F32)]
        specs = [whole(piece.shape)] + [pl.BlockSpec((chunk, hid), lambda i, m: (0, 0))] * 4
        down, out_w, up = simple(lower_kernel, "lower", ends, meta, piece, *up, specs=specs)
        meta = after(meta, down)
        down = down.T
        qkv, gb_qkv, gb_out, gb_up, gb_down, *norms = assemble(
            meta, kept, small, near, far, diag
        )
    else:
        up = reduce_plain(up_keep, up_got, up_masks[1:])
        weights = reduce_plain(low_keep, low_got, low_masks[1:])
        qkv = reduce_plain(qkv_keep, qkv_got, up_masks[1:])
        piece = spread_rows(weights).T
        cut = 4 * hid // rows
        down, out_w = piece[:cut], piece[cut:]
        kept, near, far = split_columns(qkv)
        near, far = swap(near, "blk", 1), swap(far, "blk", 2)
        ends = [jnp.where(blk % 2 == 0, a, b) for a, b in ((kept, far), (far, kept))]
        qkv = jnp.concatenate([ends[0], near, ends[1]], axis=1)
        out_args = (tok_own, out_even, out_got, out_far, b_out, b_down)
        result = finish(result_kernel, "result", seq, *out_args)
        tok_args = (tok_own, e_own, e_near, e_far, cot_own)
        grad_tokens = finish(token_kernel, "token_grad", seq, *tok_args)
        third = 3 * width
        table = jnp.concatenate([small[0:8], small[8:16, : D - third]], axis=1)
        mine = (jnp.arange(4) == blk)[:, None]
        joined = lax.psum(jnp.where(mine, small[2:3], 0.0), ("rows", "blk"))
        gb_up = lax.psum(jnp.where(mine, table[4:5], 0.0), ("rows", "blk")).reshape(FF)
        gb_qkv = jnp.concatenate(
            [
                jnp.concatenate([joined[:, 0:128], joined[:, 256:320]], axis=1).reshape(D),
                jnp.concatenate([joined[:, 128:256], joined[:, 320:384]], axis=1).reshape(D),
                joined[:, 384:576].reshape(D),
            ]
        )
        gain_1, shift_1, _, _, _, gain_2, shift_2, gb_out = lax.psum(table, ("rows", "blk"))
        norms, gb_down = (gain_1, shift_1, gain_2, shift_2), gb_out
    return (
        result[None],
        grad_tokens[None],
        qkv,
        out_w,
        up,
        down,
        gb_qkv,
        gb_out,
        gb_up,
        gb_down,
        *norms,
    )


def solution(mesh):
    split = P("rows", "blk")
    in_specs = (
        P("rows", "blk", None),
        split,
        P("rows"),
        *(P(),) * 12,
        P("rows", "blk", None),
    )
    out_specs = (
        P("rows", "blk", None),
        P("rows", "blk", None),
        *(split,) * 4,
        *(P(),) * 8,
    )
    return jax.shard_map(local, mesh=mesh, in_specs=in_specs, out_specs=out_specs, check_vma=False)
```

```python
import math
from functools import partial

import jax
import jax.numpy as jnp
import numpy as np
from jax import lax
from jax.experimental import pallas as pl
from jax.experimental.pallas import tpu as pltpu
from jax.sharding import PartitionSpec as P

D = 768
HEADS = 12
HDIM = 64
ROT = 16
FF = 3072
EPS = 1e-05
MASKED = -1e30
TILE = 256
VROWS = 80
LN2 = math.log(2.0)
EXTRA = 16
LANES = 128
F32 = jnp.float32
BF16 = jnp.bfloat16
COST = pl.CostEstimate(flops=0, bytes_accessed=0, transcendentals=0)
NT_DIMS = (((1,), (1,)), ((), ()))
TN_DIMS = (((0,), (0,)), ((), ()))


def dot(left, right):
    return jnp.dot(left, right, preferred_element_type=F32)


def dot_nt(left, right):
    return lax.dot_general(left, right, NT_DIMS, preferred_element_type=F32)


def dot_tn(left, right):
    return lax.dot_general(left, right, TN_DIMS, preferred_element_type=F32)


def normalize(value):
    center = value - jnp.mean(value, axis=-1, keepdims=True)
    spread = jnp.mean(center * center, axis=-1, keepdims=True)
    return center * lax.rsqrt(spread + EPS)


def angle_parts(length):
    dim = np.arange(LANES) % HDIM
    inverse = np.where(dim < ROT, 10000.0 ** (-2.0 * (dim % (ROT // 2)) / ROT), 0.0)
    high = (np.arange(length // LANES) * LANES)[:, None] * inverse
    low = np.arange(LANES)[:, None] * inverse
    parts = np.stack([np.cos(low), np.sin(low)]), np.stack([np.cos(high), np.sin(high)])
    return tuple(jnp.asarray(part, F32) for part in parts)


def rotation(low_ref, high_ref, tile):
    lane = lax.broadcasted_iota(jnp.int32, (1, LANES), 1) % HDIM
    sign = jnp.where(lane < ROT // 2, -1.0, 1.0)
    cos_rows, sin_rows = [], []
    for part in range(TILE // LANES):
        row = tile * (TILE // LANES) + part
        cos_high = high_ref[0, pl.ds(row, 1), :]
        sin_high = high_ref[1, pl.ds(row, 1), :]
        cos_rows.append(low_ref[0] * cos_high - low_ref[1] * sin_high)
        sin_rows.append((low_ref[1] * cos_high + low_ref[0] * sin_high) * sign)
    return jnp.concatenate(cos_rows, axis=0), jnp.concatenate(sin_rows, axis=0)


def swap_halves(value):
    lane = lax.broadcasted_iota(jnp.int32, value.shape, 1) % HDIM
    half = ROT // 2
    return jnp.where(
        lane < half, pltpu.roll(value, LANES - half, 1), pltpu.roll(value, half, 1)
    )


def true_block(meta_ref, slot):
    return jnp.bitwise_xor(meta_ref[0], slot)


def params(*semantics, vmem=None):
    return pltpu.CompilerParams(
        dimension_semantics=semantics or ("arbitrary",), vmem_limit_bytes=vmem or 67_043_328
    )


def whole(shape):
    return pl.BlockSpec(shape, lambda *_: (0,) * len(shape))


def own_blocks(refs, odd, into):
    places = ((0, 256), (128, 320), (384, 512))
    for part, (pair_at, third_at) in enumerate(places):
        left, right = refs[2 * part], refs[2 * part + 1]

        @pl.when(odd == 0)
        def _(left=left, right=right, pair_at=pair_at, third_at=third_at):
            into[:, pair_at : pair_at + 128] = left[...]
            into[:, third_at : third_at + 64] = right[:, 0:64]

        @pl.when(odd == 1)
        def _(left=left, right=right, pair_at=pair_at, third_at=third_at):
            into[:, pair_at : pair_at + 128] = jnp.concatenate(
                [left[:, 64:128], right[:, 0:64]], axis=1
            )
            into[:, third_at : third_at + 64] = right[:, 64:128]


def row(ref):
    return ref[...].reshape(1, ref.shape[0])


def own_bias(b_ref, odd, blk, into):
    blocks = []
    for part in range(3):
        for side in range(2):
            at = pl.multiple_of((part * (D // LANES) + side + 3 * blk // 2) * LANES, LANES)
            blocks.append(b_ref[pl.ds(at, LANES)].reshape(1, LANES))
    own_blocks(blocks, odd, into)


def project_tile(normed, gain, shift, w_ref, b_ref, low, high, tile, q_ref, k_ref, v_ref):
    attn_in = (normed * row(gain) + row(shift)).astype(BF16)
    joined = dot(attn_in, w_ref[...]) + b_ref[...]
    cos, sin = rotation(low, high, tile)
    scale = HDIM**-0.5 / LN2

    def turn(block):
        return block * cos + swap_halves(block) * sin

    query = turn(joined[:, 0:128]) * scale
    keys = turn(joined[:, 128:256])
    mixed = turn(joined[:, 256:384])
    q_ref[:, 0:128] = query.astype(BF16)
    k_ref[:, 0:128] = keys.astype(BF16)
    q_ref[:, 128:192] = (mixed[:, 0:64] * scale).astype(BF16)
    k_ref[:, 128:192] = mixed[:, 64:128].astype(BF16)
    v_ref[...] = joined[:, 384:576].astype(BF16)


def find_starts(seq, meta, valid, rows, start_ref, lo_ref, hi_ref):
    segs = [ref[0:1, 0:seq].astype(F32) for ref in rows]
    below = [
        sum(jnp.sum((seg < number).astype(F32), axis=1, keepdims=True) for seg in segs)
        for number in (1, 2, 3)
    ]
    per = seq // TILE
    iota = lax.broadcasted_iota(jnp.int32, (1, seq), 1)
    for slot, seg in enumerate(segs):
        block = true_block(meta, slot)
        begin = jnp.zeros((1, seq), F32)
        for number in (1, 2, 3):
            begin = jnp.where(seg == number, below[number - 1], begin)
        pos = iota + block * seq
        begin = jnp.where(pos < valid[0], begin.astype(jnp.int32), pos)
        for part in range(per):
            tile = begin[:, part * TILE : (part + 1) * TILE]
            start_ref[slot * per + part] = tile
            lo_ref[block * per + part] = jnp.min(tile) // TILE
            hi_ref[block * per + part] = (jnp.max(tile) + (TILE - 1)) // TILE


def qkv_kernel(slot, meta, valid, x_ref, gain, shift, low, high, w_ref, b_ref, *refs):
    per = pl.num_programs(0)
    tile = true_block(meta, slot) * per + pl.program_id(0)
    normed = normalize(x_ref[...].astype(F32))
    if slot == 3:
        segs, (*outs, start_ref, lo_ref, hi_ref) = refs[3:7], refs[7:]

        @pl.when(pl.program_id(0) == 0)
        def _():
            find_starts(per * TILE, meta, valid, segs, start_ref, lo_ref, hi_ref)
    else:
        outs = refs[3:]
    project_tile(normed, gain, shift, w_ref, b_ref, low, high, tile, *outs)


def project(slot, meta, valid, x, gain, shift, low, high, w, b, filled, seq, toks=()):
    width = D // 4
    per = seq // TILE
    tiles = 4 * per
    outs = [jax.ShapeDtypeStruct((4 * seq, width), BF16)] * 3
    out_specs = [pl.BlockSpec((TILE, width), lambda i, m, v: (slot * per + i, 0))] * 3
    args = [x, gain, shift, low, high, w, b, *filled, *toks]
    specs = [pl.BlockSpec((TILE, D), lambda i, m, v: (i, 0))]
    specs += [whole(a.shape) for a in args[1:7]]
    specs += [pl.BlockSpec(memory_space=pl.ANY)] * 3
    specs += [pl.BlockSpec((EXTRA, D), lambda i, m, v: (seq // EXTRA, 0)) for _ in toks]
    if toks:
        smem = pl.BlockSpec(memory_space=pltpu.SMEM)
        outs.append(jax.ShapeDtypeStruct((tiles, 1, TILE), jnp.int32))
        outs += [jax.ShapeDtypeStruct((tiles,), jnp.int32)] * 2
        out_specs += [whole((tiles, 1, TILE)), smem, smem]
    return pl.pallas_call(
        partial(qkv_kernel, slot),
        out_shape=outs,
        grid_spec=pltpu.PrefetchScalarGridSpec(
            num_scalar_prefetch=2, grid=(per,), in_specs=specs, out_specs=out_specs
        ),
        input_output_aliases={9 + i: i for i in range(3)},
        compiler_params=params(),
        cost_estimate=COST,
        name=f"qkv_{slot}",
    )(meta, valid, *args)


def mask_order(rows, first):
    masks = [1 << bit for bit in range(rows.bit_length() - 1)]
    return masks if first == 1 else masks[1::-1] + masks[2:]


def places(masks):
    order = [0]
    for mask in reversed(masks):
        order = order + [mask + i for i in order]
    return order


def fits(rows):
    return rows == 8 and D // rows % 32 == 0


def store_chunks(load, keep, send, meta, rows, first):
    size = D // rows
    for index, place in enumerate(places(mask_order(rows, first))):
        at = pl.multiple_of(jnp.bitwise_xor(meta[1], place) * size, 32)
        into = keep if index < rows // 2 else send
        row_at = index % (rows // 2) * size
        into[row_at : row_at + size, :] = load(pl.ds(at, size)).astype(into.dtype)


def store_low(grad, keep, send, meta, rows):
    size, hid = D // 4, FF // 4
    for index, place in enumerate(places(mask_order(rows, 2))):
        chunk = jnp.bitwise_xor(meta[1], place)
        at = pl.ds(pl.multiple_of(chunk % 4 * size, 64), size)
        down = pl.multiple_of(hid + chunk // 4 * (hid // 2), LANES)
        out = pl.multiple_of(2 * hid + chunk // 4 * LANES, LANES)
        into = keep if index < rows // 2 else send
        row_at = slice(index % (rows // 2) * size, (index % (rows // 2) + 1) * size)
        into[row_at, : hid // 2] = grad[at, pl.ds(down, hid // 2)].astype(BF16)
        into[row_at, hid // 2 :] = grad[at, pl.ds(out, LANES)].astype(BF16)


def low_shapes(rows):
    if fits(rows):
        return [(D, FF // 8 + LANES)] * 2
    return [(D, FF // 4 + 2 * LANES), (8, LANES)]


def low_chunks(keep, send, rows):
    if fits(rows):
        return keep, send
    hid, width, count = FF // 4, D // 4, rows // 4
    parts = [
        part.reshape(4, width, count, part.shape[1] // count).transpose(2, 0, 1, 3)
        for part in (keep[:, :hid], keep[:, hid : hid + width])
    ]
    chunks = jnp.concatenate(parts, axis=3).reshape(rows, width, -1)
    order = jnp.array(places(mask_order(rows, 2))) ^ lax.axis_index("rows")
    chunks = jnp.take(chunks, order, axis=0).reshape(rows * width, -1)
    return chunks[: rows * width // 2], chunks[rows * width // 2 :]


def chunk_shapes(cols, rows, extra=0):
    if fits(rows):
        return [(D // 2 + extra, cols)] * 2
    return [(D, cols), (8, LANES)]


def chunks_of(keep, send, rows, first):
    if fits(rows):
        return keep, send
    order = jnp.array(places(mask_order(rows, first))) ^ lax.axis_index("rows")
    parts = keep.reshape(rows, D // rows, keep.shape[1])
    parts = jnp.take(parts, order, axis=0).reshape(keep.shape)
    return parts[: D // 2], parts[D // 2 :]


def feed(normed, upstream, gain, shift, w_up, b_up, w_down):
    mlp_in = (normed * row(gain) + row(shift)).astype(BF16)
    hidden = dot(mlp_in, w_up[...]) + b_up
    cdf = 0.5 * (1.0 + lax.erf(hidden * (0.5**0.5)))
    act = (hidden * cdf).astype(BF16)
    slope = cdf + hidden * jnp.exp(-0.5 * hidden * hidden) * ((2.0 * math.pi) ** -0.5)
    grad_low = (slope * dot_nt(upstream, w_down[...])).astype(BF16)
    grad_norm = dot_nt(grad_low, w_up[...])
    return mlp_in, act, grad_low, grad_norm


def add_sums(sums, grad_low, grad_norm, normed):
    sums[0:1, :] += jnp.sum(grad_low.astype(F32), axis=0, keepdims=True)
    sums[1:2, :] += jnp.sum(grad_norm * normed, axis=0, keepdims=True)
    sums[2:3, :] += jnp.sum(grad_norm, axis=0, keepdims=True)


def own_row(ref, blk, size):
    return ref[pl.ds(pl.multiple_of(blk * size, LANES), size)].reshape(1, size)


def mlp_first_kernel(
    half, meta, xa, xb, ca, cb, gain, shift, b_up, w_up, w_down, w_out,
    gain1, shift1, b_qkv, low, high, w0, w1, w2, w3, w4, w5,
    mo_ref, e_ref, n_ref, gv_ref, sums, gup, gdown, q_ref, k_ref, v_ref, w_own, b_own, x_s, c_s,
):
    step = pl.program_id(0)

    @pl.when(step < half)
    def _():
        x_s[...] = xa[...]
        c_s[...] = ca[...]

    @pl.when(step >= half)
    def _():
        x_s[...] = xb[...]
        c_s[...] = cb[...]

    @pl.when(step == 0)
    def _():
        sums[...] = jnp.zeros_like(sums)
        gup[...] = jnp.zeros_like(gup)
        gdown[...] = jnp.zeros_like(gdown)
        odd = meta[0] % 2
        own_blocks((w0, w1, w2, w3, w4, w5), odd, w_own)
        own_bias(b_qkv, odd, meta[0], b_own)

    upstream = c_s[...]

    @pl.when(step < half)
    def _():
        sums[3:4, :] += jnp.sum(upstream.astype(F32), axis=0, keepdims=True)

    normed = normalize(x_s[...].astype(F32))
    n_ref[...] = normed.astype(BF16)
    tile = true_block(meta, step // half) * half + step % half
    project_tile(normed, gain1, shift1, w_own, b_own, low, high, tile, q_ref, k_ref, v_ref)
    bias = own_row(b_up, meta[0], gup.shape[1])
    mlp_in, act, grad_low, grad_norm = feed(normed, upstream, gain, shift, w_up, bias, w_down)
    mo_ref[...] = dot(act, w_down[...]).astype(BF16)
    add_sums(sums, grad_low, grad_norm, normed)
    e_ref[...] = (grad_norm * row(gain)).astype(BF16)
    gv_ref[...] = dot_nt(upstream, w_out[...]).astype(BF16)
    gup[...] += dot_tn(mlp_in, grad_low)
    gdown[...] += dot_tn(upstream, act)


def mlp_second_kernel(
    half, rows, meta, xa, xb, ca, cb, gain, shift, b_up, w_up, w_down, w_out,
    c0, c1, mo_in, o_near, o_far, sums_in, gup, gdown, *refs
):
    e_ref, n_ref, gv_ref, sums, even, odd, up_keep, up_send, low_keep, low_send = refs[3:13]
    x_s, c_s, n_s, grad = refs[13:]
    step = pl.program_id(0)
    hid = gup.shape[1]

    @pl.when(step < half)
    def _():
        x_s[...] = xa[...]
        c_s[...] = ca[...]
        n_s[...] = c0[...]

    @pl.when(step >= half)
    def _():
        x_s[...] = xb[...]
        c_s[...] = cb[...]
        n_s[...] = c1[...]

    @pl.when(step == 0)
    def _():
        sums[...] = sums_in[...]
        grad[:, 0:hid] = gup[...]
        grad[:, hid : 2 * hid] = gdown[...]
        grad[:, 2 * hid :] = jnp.zeros_like(grad[:, 2 * hid :])

    upstream = c_s[...]
    normed = normalize(x_s[...].astype(F32))
    n_ref[...] = normed.astype(BF16)
    bias = own_row(b_up, meta[0], hid)
    mlp_in, act, grad_low, grad_norm = feed(normed, upstream, gain, shift, w_up, bias, w_down)
    add_sums(sums, grad_low, grad_norm, normed)
    e_ref[...] = (grad_norm * row(gain)).astype(BF16)
    gv_ref[...] = dot_nt(upstream, w_out[...]).astype(BF16)
    grad[:, 0:hid] += dot_tn(mlp_in, grad_low)
    grad[:, hid : 2 * hid] += dot_tn(upstream, act)
    out_grad = dot_tn(upstream, o_far[...]) + dot_tn(n_s[...], o_near[...])
    side = out_grad.shape[1] // 2
    if fits(rows):
        grad[:, 2 * hid : 2 * hid + side] += out_grad[:, :side]
        grad[:, 2 * hid + LANES : 2 * hid + LANES + side] += out_grad[:, side:]
    else:
        grad[:, 2 * hid : 2 * hid + 2 * side] += out_grad
    far = (dot(act, w_down[...]) + dot(o_far[...], w_out[...])).astype(BF16)
    near = (mo_in[...].astype(F32) + dot(o_near[...], w_out[...])).astype(BF16)

    @pl.when(step < half)
    def _():
        even[0] = near
        even[1] = far

    @pl.when(step >= half)
    def _():
        odd[0] = near
        odd[1] = far

    @pl.when(step == pl.num_programs(0) - 1)
    def _():
        if fits(rows):
            store_chunks(lambda at: grad[at, 0:hid], up_keep, up_send, meta, rows, 1)
            store_low(grad, low_keep, low_send, meta, rows)
        else:
            up_keep[...] = grad[:, 0:hid].astype(BF16)
            low_keep[...] = grad[:, hid:].astype(BF16)


def feed_forward(
    meta, xs, cs, gain, shift, b_up, w_up, w_down, w_out, rows, seq,
    joined=None, before=None, near=None, attn=None,
):
    per = seq // TILE
    steps = 2 * per
    hid = FF // 4
    width = D // 4
    total = 4 * seq
    first = pl.BlockSpec((TILE, D), lambda i, m: (jnp.minimum(i, per - 1), 0))
    second = pl.BlockSpec((TILE, D), lambda i, m: (jnp.maximum(i - per, 0), 0))
    specs = [
        first,
        second,
        first,
        second,
        whole((D,)),
        whole((D,)),
        whole((FF,)),
        pl.BlockSpec((D, hid), lambda i, m: (0, m[0])),
        pl.BlockSpec((hid, D), lambda i, m: (m[0], 0)),
        pl.BlockSpec((width, D), lambda i, m: (m[0], 0)),
    ]
    args = [*xs, *cs, gain, shift, b_up, w_up, w_down, w_out]
    tile = pl.BlockSpec((TILE, D), lambda i, m: (i, 0))
    narrow = pl.BlockSpec((TILE, width), lambda i, m: (i, 0))
    sums = (8, D)
    scratch = [pltpu.VMEM((TILE, D), BF16), pltpu.VMEM((TILE, D), BF16)]
    pair = jax.ShapeDtypeStruct((steps * TILE, D), BF16)
    full = jax.ShapeDtypeStruct((total, D), BF16)
    vec = jax.ShapeDtypeStruct((total, width), BF16)
    if before is None:
        body = partial(mlp_first_kernel, per)
        gain1, shift1, w_qkv, b_qkv, low, high = joined
        args += [gain1, shift1, b_qkv, low, high]
        specs += [whole(a.shape) for a in args[-5:]]
        for part in range(3):
            for side in range(2):
                specs.append(
                    pl.BlockSpec(
                        (D, LANES),
                        lambda i, m, at=part * D // LANES + side: (0, at + 3 * m[0] // 2),
                    )
                )
                args.append(w_qkv)
        outs = [pair, full, full, vec, jax.ShapeDtypeStruct(sums, F32)]
        outs += [jax.ShapeDtypeStruct((D, hid), F32)] * 2 + [vec] * 3
        outs += [
            jax.ShapeDtypeStruct((D, 3 * width), BF16),
            jax.ShapeDtypeStruct((1, 3 * width), F32),
        ]
        out_specs = [tile, tile, tile, narrow, whole(sums)]
        out_specs += [whole((D, hid))] * 2 + [narrow] * 3
        out_specs += [whole((D, 3 * width)), whole((1, 3 * width))]
        aliases = {}
    else:
        body = partial(mlp_second_kernel, per, rows)
        mlp_out, norm_part, normed, grad_vec, sums_in, gup, gdown = before
        chunks = chunk_shapes(hid, rows) + low_shapes(rows)
        args += [*near, mlp_out, attn, attn, sums_in, gup, gdown, norm_part, normed, grad_vec]
        specs += [
            first,
            second,
            tile,
            narrow,
            pl.BlockSpec((TILE, width), lambda i, m: (i + steps, 0)),
            whole(sums),
            whole((D, hid)),
            whole((D, hid)),
            *(pl.BlockSpec(memory_space=pl.ANY),) * 3,
        ]
        aliases = {len(args) - 2 + i: i for i in range(3)}
        both = jax.ShapeDtypeStruct((2, seq, D), BF16)
        outs = [full, full, vec, jax.ShapeDtypeStruct(sums, F32), both, both]
        late = pl.BlockSpec((TILE, D), lambda i, m: (i + steps, 0))
        outs += [jax.ShapeDtypeStruct(shape, BF16) for shape in chunks]
        out_specs = [
            late,
            late,
            pl.BlockSpec((TILE, width), lambda i, m: (i + steps, 0)),
            whole(sums),
            pl.BlockSpec((2, TILE, D), lambda i, m: (0, jnp.minimum(i, per - 1), 0)),
            pl.BlockSpec((2, TILE, D), lambda i, m: (0, jnp.maximum(i - per, 0), 0)),
            *(whole(shape) for shape in chunks),
        ]
        scratch += [pltpu.VMEM((TILE, D), BF16), pltpu.VMEM((D, 2 * hid + 2 * LANES), F32)]
    return pl.pallas_call(
        body,
        out_shape=outs,
        grid_spec=pltpu.PrefetchScalarGridSpec(
            num_scalar_prefetch=1,
            grid=(steps,),
            in_specs=specs,
            out_specs=out_specs,
            scratch_shapes=scratch,
        ),
        input_output_aliases=aliases,
        compiler_params=params(),
        cost_estimate=COST,
        name="mlp_first" if before is None else "mlp_second",
    )(meta, *args)


def head_masks():
    lane = lax.broadcasted_iota(jnp.int32, (1, LANES), 1)
    first = jnp.where(lane < HDIM, 1.0, 0.0).astype(BF16)
    second = jnp.where(lane < HDIM, 0.0, 1.0).astype(BF16)
    return first, second


def slot_rows(meta, per, tile):
    slot = jnp.bitwise_xor(tile // per, meta[0])
    return pl.multiple_of((slot * per + tile % per) * TILE, TILE)


def by_head(first, second, block, third):
    return (block * first, block * second, third)


def transpose_all(from_ref, to_ref):
    @pl.loop(0, from_ref.shape[0] // TILE)
    def _(tile):
        rows = pl.ds(pl.multiple_of(tile * TILE, TILE), TILE)
        to_ref[:, rows] = from_ref[rows, :].astype(F32).T.astype(BF16)


def attend_kernel(per, meta, lo, hi, q_ref, k_ref, v_ref, start_ref, o_ref, lse_ref, vt_ref, acc, s_ref):
    mask0, mask1 = head_masks()
    tiles = k_ref.shape[0] // TILE
    qi = pl.program_id(0)

    @pl.when(qi == 0)
    def _():
        ones = jnp.where(lax.broadcasted_iota(jnp.int32, (VROWS - HDIM, TILE), 0) == 0, 1.0, 0.0)

        @pl.loop(0, tiles)
        def _(tile):
            rows = pl.ds(pl.multiple_of(tile * TILE, TILE), TILE)
            block = v_ref[rows, :].astype(F32).T
            for head in range(3):
                at = head * VROWS
                vt_ref[at : at + HDIM, rows] = block[head * HDIM : (head + 1) * HDIM].astype(BF16)
                vt_ref[at + HDIM : at + VROWS, rows] = ones.astype(BF16)

    key_iota = lax.broadcasted_iota(jnp.int32, (TILE, TILE), 0)
    query_iota = lax.broadcasted_iota(jnp.int32, (TILE, TILE), 1)
    queries = by_head(mask0, mask1, q_ref[:, 0:128], q_ref[:, 128:192])
    starts = start_ref[0]
    acc[...] = jnp.zeros_like(acc)

    def key_tile(turn):
        return jnp.where(turn == 0, qi, first + turn - 1)

    def score(masked, ki):
        k_rows = pl.ds(slot_rows(meta, per, ki), TILE)
        pair, third = k_ref[k_rows, 0:128], k_ref[k_rows, 128:192]
        scores = [dot_nt(third if head == 2 else pair, queries[head]) for head in range(3)]
        if masked:
            allowed = (key_iota >= starts - ki * TILE) & (key_iota <= query_iota + (qi - ki) * TILE)
            scores = [jnp.where(allowed, x, MASKED) for x in scores]
        return scores, [jnp.max(x, axis=0, keepdims=True) for x in scores]

    def value(ki, tops, peaks):
        k_rows = pl.ds(slot_rows(meta, per, ki), TILE)
        news = [jnp.maximum(top, peak) for top, peak in zip(tops, peaks)]
        fades = [jnp.exp2(top - new) for top, new in zip(tops, news)]
        weights = [jnp.exp2(s_ref[head] - news[head]).astype(BF16) for head in range(3)]
        terms = [
            dot(vt_ref[head * VROWS : (head + 1) * VROWS, k_rows], weights[head]) for head in range(3)
        ]
        return news, fades, terms

    def put(fades, terms):
        for head in range(3):
            cols = slice(head * VROWS, (head + 1) * VROWS)
            acc[cols, :] = acc[cols, :] * fades[head] + terms[head]

    def visit(masked, turn, carry):
        tops, peaks = carry
        scores, next_peaks = score(masked, key_tile(turn + 1))
        news, fades, terms = value(key_tile(turn), tops, peaks)
        peaks = next_peaks
        for head in range(3):
            s_ref[head] = scores[head]
        put(fades, terms)
        return tuple(news), tuple(peaks)

    first = lo[qi]
    full = jnp.minimum(hi[qi], qi)
    scores, peaks = score(True, qi)
    for head in range(3):
        s_ref[head] = scores[head]
    carry = ((jnp.full((1, TILE), MASKED, F32),) * 3, tuple(peaks))
    carry = lax.fori_loop(0, full - first, partial(visit, True), carry)
    carry = lax.fori_loop(full - first, qi - first, partial(visit, False), carry)
    tops, fades, terms = value(key_tile(qi - first), *carry)
    put(fades, terms)
    heads = []
    for head, top in enumerate(tops):
        at = head * VROWS
        total = acc[at + HDIM : at + HDIM + 1, :]
        heads.append(acc[at : at + HDIM, :] / total)
        lse_ref[head, 0] = top + jnp.log2(total)
    o_ref[...] = jnp.concatenate(heads, axis=0).T.astype(BF16)

def attend(meta, lo, hi, query, keys, values, starts, per):
    total, width = query.shape
    tiles = total // TILE
    def slot(i, m):
        return jnp.bitwise_xor(i // per, m[0]) * per + i % per
    q_spec = pl.BlockSpec((TILE, width), lambda i, m, lo, hi: (slot(i, m), 0))
    start_spec = pl.BlockSpec((1, 1, TILE), lambda i, m, lo, hi: (slot(i, m), 0, 0))
    lse_spec = pl.BlockSpec((3, 1, 1, TILE), lambda i, m, lo, hi: (0, slot(i, m), 0, 0))
    return pl.pallas_call(
        partial(attend_kernel, per),
        out_shape=[
            jax.ShapeDtypeStruct((total, width), BF16),
            jax.ShapeDtypeStruct((3, tiles, 1, TILE), F32),
        ],
        grid_spec=pltpu.PrefetchScalarGridSpec(
            num_scalar_prefetch=3,
            grid=(tiles,),
            in_specs=[q_spec, whole(keys.shape), whole(values.shape), start_spec],
            out_specs=[q_spec, lse_spec],
            scratch_shapes=[pltpu.VMEM((3 * VROWS, total), BF16), pltpu.VMEM((3 * VROWS, TILE), F32), pltpu.VMEM((3, TILE, TILE), F32)],
        ),
        compiler_params=params(),
        cost_estimate=COST,
        name="attend",
    )(meta, lo, hi, query, keys, values, starts)


def attend_back_kernel(
    per, meta, lo, hi, q_ref, k_ref, v_ref, o_ref, gv_ref, start_ref, lse_ref, low, high,
    gj_ref, kt_ref, dk_ref, dv_ref, dqt_ref
):
    mask0, mask1 = head_masks()
    tiles = k_ref.shape[0] // TILE
    qi = tiles - 1 - pl.program_id(0)

    @pl.when(pl.program_id(0) == 0)
    def _():
        transpose_all(k_ref, kt_ref)

    own_rows = pl.ds(slot_rows(meta, per, qi), TILE)
    key_iota = lax.broadcasted_iota(jnp.int32, (TILE, TILE), 0)
    query_iota = lax.broadcasted_iota(jnp.int32, (TILE, TILE), 1)
    queries = by_head(mask0, mask1, q_ref[:, 0:128], q_ref[:, 128:192])
    grads = by_head(mask0, mask1, gv_ref[:, 0:128], gv_ref[:, 128:192])
    starts = start_ref[0]
    lses = [lse_ref[head, 0] for head in range(3)]
    product = (gv_ref[...].astype(F32) * o_ref[...].astype(F32)).T
    deltas = [
        jnp.sum(product[head * HDIM : (head + 1) * HDIM], axis=0, keepdims=True)
        for head in range(3)
    ]
    dqt_ref[...] = jnp.zeros_like(dqt_ref)

    @pl.when(pl.program_id(0) == 0)
    def _():
        dk_ref[...] = jnp.zeros_like(dk_ref)
        dv_ref[...] = jnp.zeros_like(dv_ref)

    def load(ki):
        k_rows = pl.ds(slot_rows(meta, per, ki), TILE)
        return k_rows

    def score(masked, ki):
        k_rows = load(ki)
        pair, third = k_ref[k_rows, 0:128], k_ref[k_rows, 128:192]
        v_pair, v_third = v_ref[k_rows, 0:128], v_ref[k_rows, 128:192]
        scores = [dot_nt(third if head == 2 else pair, queries[head]) for head in range(3)]
        grad_probs = [dot_nt(v_third if head == 2 else v_pair, grads[head]) for head in range(3)]
        if masked:
            allowed = (key_iota >= starts - ki * TILE) & (key_iota <= query_iota + (qi - ki) * TILE)
            scores = [jnp.where(allowed, x, MASKED) for x in scores]
        return scores, grad_probs

    def terms(ki, scores, grad_probs):
        k_rows = load(ki)
        probs = [jnp.exp2(x - lse) for x, lse in zip(scores, lses)]
        grad_scores = [
            (p * (g - delta)).astype(BF16) for p, g, delta in zip(probs, grad_probs, deltas)
        ]
        dv = [dot(p.astype(BF16), g) for p, g in zip(probs, grads)]
        dk = [dot(g, q) for g, q in zip(grad_scores, queries)]
        dq = [
            dot(kt_ref[head * HDIM : (head + 1) * HDIM, k_rows], grad_scores[head])
            for head in range(3)
        ]
        return dk, dv, dq

    def add(ki, dk, dv, dq):
        k_rows = load(ki)
        for into, parts in ((dk_ref, dk), (dv_ref, dv)):
            into[k_rows, 0:128] += parts[0] + parts[1]
            into[k_rows, 128:192] += parts[2]
        for head in range(3):
            dqt_ref[head * HDIM : (head + 1) * HDIM, :] += dq[head]

    first = lo[qi]
    full = jnp.minimum(hi[qi], qi)

    def visit(masked, ki):
        add(ki, *terms(ki, *score(masked, ki)))

    @pl.loop(first, full)
    def _(ki):
        visit(True, ki)

    @pl.loop(full, qi)
    def _(ki):
        visit(False, ki)

    visit(True, qi)

    cos, sin = rotation(low, high, qi)

    def turn_back(block):
        return block * cos - swap_halves(block) * sin

    dq = dqt_ref[...].T * (HDIM**-0.5)
    dk = dk_ref[own_rows, :] * LN2
    gj_ref[:, 0:128] = turn_back(dq[:, 0:128]).astype(BF16)
    gj_ref[:, 128:256] = turn_back(dk[:, 0:128]).astype(BF16)
    mixed = jnp.concatenate([dq[:, 128:192], dk[:, 128:192]], axis=1)
    gj_ref[:, 256:384] = turn_back(mixed).astype(BF16)
    gj_ref[:, 384:576] = dv_ref[own_rows, :].astype(BF16)


def attend_back(
    meta, lo, hi, query, keys, values, attn, grad_vec, starts, lse, low, high, per
):
    total, width = query.shape
    tiles = total // TILE

    def slot(i, m):
        tile = tiles - 1 - i
        return jnp.bitwise_xor(tile // per, m[0]) * per + tile % per

    q_spec = pl.BlockSpec((TILE, width), lambda i, m, lo, hi: (slot(i, m), 0))
    gj_spec = pl.BlockSpec((TILE, 3 * width), lambda i, m, lo, hi: (slot(i, m), 0))
    start_spec = pl.BlockSpec((1, 1, TILE), lambda i, m, lo, hi: (slot(i, m), 0, 0))
    lse_spec = pl.BlockSpec((3, 1, 1, TILE), lambda i, m, lo, hi: (0, slot(i, m), 0, 0))
    return pl.pallas_call(
        partial(attend_back_kernel, per),
        out_shape=jax.ShapeDtypeStruct((total, 3 * width), BF16),
        grid_spec=pltpu.PrefetchScalarGridSpec(
            num_scalar_prefetch=3,
            grid=(tiles,),
            in_specs=[
                q_spec,
                whole(keys.shape),
                whole(values.shape),
                q_spec,
                q_spec,
                start_spec,
                lse_spec,
                whole(low.shape),
                whole(high.shape),
            ],
            out_specs=gj_spec,
            scratch_shapes=[
                pltpu.VMEM((width, total), BF16),
                pltpu.VMEM((total, width), F32),
                pltpu.VMEM((total, width), F32),
                pltpu.VMEM((width, TILE), F32),
            ],
        ),
        compiler_params=params(),
        cost_estimate=COST,
        name="attend_back",
    )(meta, lo, hi, query, keys, values, attn, grad_vec, starts, lse, low, high)


SMALL = 16


def pack_small(gain_sum, shift_sum, bias, mlp_sums):
    third = 3 * D // 4
    which = lax.broadcasted_iota(jnp.int32, (8, D), 0)
    table = jnp.concatenate([jnp.zeros((4, D), F32), mlp_sums[0:4]], axis=0)
    table = jnp.where(which == 0, gain_sum, jnp.where(which == 1, shift_sum, table))
    head = jnp.where(which[:, :third] == 2, bias, table[:, :third])
    tail = jnp.concatenate([table[:, third:], jnp.zeros((8, 2 * third - D), F32)], axis=1)
    return jnp.concatenate([head, tail], axis=0)


def high_low(value):
    high = value.astype(BF16)
    return high, (value - high.astype(F32)).astype(BF16)


def weight_kernel(rows, meta, *refs):
    gj_ref, n_ref, gain, shift, w_ref, mlp_sums, keep, send, small, grad, bias = refs
    step = pl.program_id(0)

    @pl.when(step == 0)
    def _():
        grad[...] = jnp.zeros_like(grad)
        bias[...] = jnp.zeros_like(bias)

    joined = gj_ref[...]
    bias[0:1, :] += jnp.sum(joined.astype(F32), axis=0, keepdims=True)
    grad[...] += dot_tn(n_ref[...], joined)

    @pl.when(step == pl.num_programs(0) - 1)
    def _():
        total = bias[0:1, :]
        width = total.shape[1]
        parts = jnp.concatenate(
            [*high_low(jnp.broadcast_to(total, (8, width)))], axis=0
        )
        shift_sum = dot_nt(parts, w_ref[...])
        shift_sum = shift_sum[0:1] + shift_sum[8:9]
        ones = jnp.ones((16, width), BF16)
        high, low = high_low(grad[...] * w_ref[...].astype(F32))
        gain_sum = (dot_nt(ones, high) + dot_nt(ones, low))[0:1]
        columns = jnp.concatenate(
            [jnp.broadcast_to(row(gain), (8, D)), jnp.broadcast_to(row(shift), (8, D))], axis=0
        ).T
        grad[...] = grad[...] * columns[:, 0:1] + columns[:, 8:9] * total
        rest = pack_small(gain_sum, shift_sum, total, mlp_sums[...])
        small[...] = rest
        if fits(rows):
            store_chunks(lambda at: grad[at, :], keep, send, meta, rows, 1)
            keep[D // 2 :, :] = rest.astype(BF16)
            send[D // 2 :, :] = rest.astype(BF16)
        else:
            keep[...] = grad[...].astype(BF16)


def row_tiles(cols, tile=TILE):
    return pl.BlockSpec((tile, cols), lambda i, m: (i, 0))


def joined_weight(meta, grad, normed, gain, shift, w, mlp_sums, rows):
    total, width = grad.shape
    tile = 2 * TILE
    chunks = chunk_shapes(width, rows, SMALL)
    args = [gain, shift, w, mlp_sums]
    return pl.pallas_call(
        partial(weight_kernel, rows),
        out_shape=[jax.ShapeDtypeStruct(shape, BF16) for shape in chunks]
        + [jax.ShapeDtypeStruct((SMALL, width), F32)],
        grid_spec=pltpu.PrefetchScalarGridSpec(
            num_scalar_prefetch=1,
            grid=(total // tile,),
            in_specs=[row_tiles(width, tile), row_tiles(D, tile), *(whole(a.shape) for a in args)],
            out_specs=[*(whole(shape) for shape in chunks), whole((SMALL, width))],
            scratch_shapes=[pltpu.VMEM((D, width), F32), pltpu.VMEM((8, width), F32)],
        ),
        compiler_params=params(),
        cost_estimate=COST,
        name="joined_weight",
    )(meta, grad, normed, *args)


def norm_kernel(meta, *refs):
    gjs, es, (gain, w_ref), outs = refs[0:4], refs[4:8], refs[8:10], refs[10:]
    for gj_ref, e_in, out in zip(gjs, es, outs):
        grad_norm = dot_nt(gj_ref[...], w_ref[...])
        out[...] = (grad_norm * row(gain) + e_in[...].astype(F32)).astype(BF16)


def norm_grad(meta, grad, e_mlp, gain, w, seq):
    tile = TILE
    per = seq // tile

    def slot_tiles(slot, cols):
        return pl.BlockSpec((tile, cols), lambda i, m: (slot * per + i, 0))

    return pl.pallas_call(
        norm_kernel,
        out_shape=[jax.ShapeDtypeStruct((seq, D), BF16)] * 4,
        grid_spec=pltpu.PrefetchScalarGridSpec(
            num_scalar_prefetch=1,
            grid=(per,),
            in_specs=[
                *(slot_tiles(slot, grad.shape[1]) for slot in range(4)),
                *(slot_tiles(slot, D) for slot in range(4)),
                whole(gain.shape),
                whole(w.shape),
            ],
            out_specs=[slot_tiles(0, D)] * 4,
        ),
        compiler_params=params(),
        cost_estimate=COST,
        name="norm_grad",
    )(meta, *[grad] * 4, *[e_mlp] * 4, gain, w)


def simple(body, name, shapes, *args, specs=None):
    return pl.pallas_call(
        body,
        out_shape=[jax.ShapeDtypeStruct(shape, kind) for shape, kind in shapes],
        grid_spec=pltpu.PrefetchScalarGridSpec(
            num_scalar_prefetch=1,
            grid=(1,),
            in_specs=specs or [whole(a.shape) for a in args[1:]],
            out_specs=[whole(shape) for shape, _ in shapes],
        ),
        compiler_params=params(),
        cost_estimate=COST,
        name=name,
    )(*args)


def add_up(refs):
    total = refs[0][...].astype(F32)
    for ref in refs[1:]:
        total += ref[...].astype(F32)
    return total


def sums_kernel(counts, meta, *refs):
    ins, outs = refs[: sum(counts)], refs[sum(counts) :]
    for count, out in zip(counts, outs):
        out[...] = add_up(ins[:count]).astype(BF16)
        ins = ins[count:]


def block_sums(name, meta, steps, *jobs):
    specs, args, outs, out_specs = [], [], [], []
    for rows, terms in jobs:
        size, cols = rows // steps, terms[0][0].shape[1]
        for array, at in terms:
            specs.append(pl.BlockSpec((size, cols), lambda i, m, at=at // size: (at + i, 0)))
            args.append(array)
        outs.append(jax.ShapeDtypeStruct((rows, cols), BF16))
        out_specs.append(pl.BlockSpec((size, cols), lambda i, m: (i, 0)))
    return pl.pallas_call(
        partial(sums_kernel, [len(terms) for _, terms in jobs]),
        out_shape=outs,
        grid_spec=pltpu.PrefetchScalarGridSpec(
            num_scalar_prefetch=1, grid=(steps,), in_specs=specs, out_specs=out_specs
        ),
        compiler_params=params(),
        cost_estimate=COST,
        name=name,
    )(meta, *args)


def lower_kernel(meta, piece, down_ref, out_ref):
    cut = down_ref.shape[1]
    down_ref[...] = piece[:, :cut].astype(F32)
    out_ref[...] = piece[:, cut:].astype(F32).T[: out_ref.shape[0]]


def last_qkv_kernel(meta, *refs):
    *terms, sums, got_sums, kept, near, far, small = refs
    size = kept.shape[0]
    width = kept.shape[1]
    total = add_up(terms)
    rows = sums[...].astype(F32) + got_sums[...].astype(F32)
    for part in range(3):
        small[part * 8 : part * 8 + 8, :] = rows[0:8, part * width : (part + 1) * width]
    small[24:32, :] = rows[8:16, 0:width]
    near[size:, :] = small[...]
    far[size:, :] = small[...]
    query = jnp.concatenate([total[:, 0:128], total[:, 256:320]], axis=1)
    keys = jnp.concatenate([total[:, 128:256], total[:, 320:384]], axis=1)
    values = total[:, 384:576]
    plans = (
        (query, keys, values),
        (keys, query, values),
        (keys, values, query),
        (values, keys, query),
    )
    for blk, plan in enumerate(plans):

        @pl.when(meta[0] == blk)
        def _(plan=plan):
            kept[...] = plan[0]
            near[0:size, :] = plan[1]
            far[0:size, :] = plan[2]


def assemble_kernel(
    meta, kept, small, near, far, diag,
    qkv, b_qkv, b_out, b_up, b_down, gain1, shift1, gain2, shift2, table,
):
    size, width = kept.shape

    @pl.when(meta[0] % 2 == 0)
    def _():
        qkv[:, 0:width] = kept[...]
        qkv[:, 2 * width :] = far[0:size, :]

    @pl.when(meta[0] % 2 == 1)
    def _():
        qkv[:, 0:width] = far[0:size, :]
        qkv[:, 2 * width :] = kept[...]

    qkv[:, width : 2 * width] = near[0:size, :]
    table[0] = small[...]
    table[1] = near[size:, :]
    table[2] = far[size:, :]
    table[3] = diag[...]
    blocks = [table[jnp.bitwise_xor(meta[0], blk)] for blk in range(4)]
    total = blocks[0] + blocks[1] + blocks[2] + blocks[3]

    def vector(rows, index):
        parts = [rows[part * 8 + index : part * 8 + index + 1, :] for part in range(4)]
        return jnp.concatenate(parts, axis=1)

    for ref, index in ((gain1, 0), (shift1, 1), (gain2, 5), (shift2, 6), (b_out, 7), (b_down, 7)):
        ref[...] = vector(total, index).reshape(D)
    ups, parts = [], ([], [], [])
    for rows in blocks:
        ups.append(vector(rows, 4))
        joined = vector(rows, 2)
        parts[0].append(jnp.concatenate([joined[:, 0:128], joined[:, 256:320]], axis=1))
        parts[1].append(jnp.concatenate([joined[:, 128:256], joined[:, 320:384]], axis=1))
        parts[2].append(joined[:, 384:576])
    b_up[...] = jnp.concatenate(ups, axis=1).reshape(4 * D)
    b_qkv[...] = jnp.concatenate(parts[0] + parts[1] + parts[2], axis=1).reshape(3 * D)


def assemble(meta, kept, small, near, far, diag):
    size, width = kept.shape
    shapes = [((size, 3 * width), F32), ((3 * D,), F32), ((D,), F32), ((4 * D,), F32)]
    shapes += [((D,), F32)] * 5
    args = (kept, small, near, far, diag)
    return pl.pallas_call(
        assemble_kernel,
        out_shape=[jax.ShapeDtypeStruct(shape, kind) for shape, kind in shapes],
        grid_spec=pltpu.PrefetchScalarGridSpec(
            num_scalar_prefetch=1,
            grid=(1,),
            in_specs=[whole(a.shape) for a in args],
            out_specs=[whole(shape) for shape, _ in shapes],
            scratch_shapes=[pltpu.VMEM((4, 32, width), F32)],
        ),
        compiler_params=params(),
        cost_estimate=COST,
        name="assemble",
    )(meta, *args)


def next_send(terms, size):
    return sum(term[size // 2 : size].astype(F32) for term in terms).astype(BF16)


def reduce_plain(keep, got, masks):
    terms, size = [keep, got], keep.shape[0]
    for mask in masks:
        terms.append(swap(next_send(terms, size), "rows", mask))
        size //= 2
    return sum(term[:size].astype(F32) for term in terms)


def after(value, *others):
    return lax.optimization_barrier((value, others))[0]


def swap(value, axis, mask):
    size = lax.axis_size(axis)
    return lax.ppermute(value, axis, [(i, i ^ mask) for i in range(size)])


def add_low(left, right):
    return (left.astype(F32) + right.astype(F32)).astype(BF16)


def spread_rows(chunk):
    rows = lax.axis_size("rows")
    moves = [
        (r * 4 + b, (rows // 4 * b + r // 4) * 4 + r % 4) for r in range(rows) for b in range(4)
    ]
    return lax.ppermute(chunk, ("rows", "blk"), moves)


def split_columns(chunk):
    b = lax.axis_index("blk")
    q = jnp.concatenate([chunk[:, 0:128], chunk[:, 256:320]], axis=1)
    k = jnp.concatenate([chunk[:, 128:256], chunk[:, 320:384]], axis=1)
    v = chunk[:, 384:576]

    def choose(zero, one, two, three):
        return jnp.where(b < 2, jnp.where(b == 0, zero, one), jnp.where(b == 2, two, three))

    return choose(q, k, k, v), choose(k, q, v, k), choose(v, v, q, q)


def result_kernel(x_ref, even, near, far, b_out, b_down, out_ref):
    bias = row(b_out) + row(b_down)
    total = even[0].astype(F32) + near[0].astype(F32) + far[...].astype(F32)
    out_ref[...] = (x_ref[...].astype(F32) + bias + total).astype(BF16)


def token_kernel(x_ref, even, near, far, c_ref, out_ref):
    wide = x_ref[...].astype(F32)
    center = wide - jnp.mean(wide, axis=-1, keepdims=True)
    rate = lax.rsqrt(jnp.mean(center * center, axis=-1, keepdims=True) + EPS)
    normed = center * rate
    grad = even[...].astype(F32) + near[...].astype(F32) + far[...].astype(F32)
    mean = jnp.mean(grad, axis=-1, keepdims=True)
    along = jnp.mean(grad * normed, axis=-1, keepdims=True)
    back = rate * (grad - mean - normed * along)
    out_ref[...] = (c_ref[...].astype(F32) + back).astype(BF16)


def finish(body, name, seq, x, even, near, far, *more):
    flat = pl.BlockSpec((TILE, D), lambda i: (i, 0))
    own = pl.BlockSpec((1, TILE, D), lambda i: (0, i, 0))
    return pl.pallas_call(
        body,
        out_shape=jax.ShapeDtypeStruct((seq, D), BF16),
        grid=(seq // TILE,),
        in_specs=[
            *(own if a.ndim == 3 else flat for a in (x, even, near, far)),
            *(flat if a.ndim == 2 else whole(a.shape) for a in more),
        ],
        out_specs=flat,
        compiler_params=params(),
        cost_estimate=COST,
        name=name,
    )(x, even, near, far, *more)


def local(
    tokens, seg_ids, valid_len, ln1_gain, ln1_bias, w_qkv, b_qkv, w_out, b_out,
    ln2_gain, ln2_bias, w_up, b_up, w_down, b_down, cotangent,
):
    rows = lax.axis_size("rows")
    blk = lax.axis_index("blk")
    seq = tokens.shape[1]
    per = seq // TILE
    width = D // 4
    hid = FF // 4
    low, high = angle_parts(4 * seq)
    seg_row = jnp.pad(seg_ids.astype(BF16), ((0, EXTRA - 1), (0, D - seq)))
    tok_own = jnp.concatenate([tokens[0], seg_row], axis=0)
    cot_own = cotangent[0]

    cot_near = swap(cot_own, "blk", 1)
    tok_far = swap(tok_own, "blk", 2)
    tok_near = swap(tok_own, "blk", 1)
    cot_long = jnp.pad(cot_own, ((0, 2 * EXTRA), (0, 0)))
    cot_far = swap(cot_long, "blk", 2)

    meta = jnp.stack([blk, lax.axis_index("rows")]).astype(jnp.int32)
    mlp_args = (ln2_gain, ln2_bias, b_up, w_up, w_down, w_out, rows, seq)
    joined = (ln1_gain, ln1_bias, w_qkv, b_qkv, low, high)
    *first, query, keys, values, w_own, b_own = feed_forward(
        meta, (tok_own, tok_near), (cot_own, cot_near), *mlp_args, joined
    )
    meta = after(meta, b_own)

    def more(slot, m, tok, filled, slots=()):
        args = (ln1_gain, ln1_bias, low, high, w_own, b_own, filled, seq, slots)
        return project(slot, m, valid_len, tok, *args)

    tok_last = swap(after(tok_far, b_own), "blk", 1)
    joined = more(2, meta, tok_far, (query, keys, values))
    toks = (tok_own, tok_near, tok_far, tok_last)
    query, keys, values, starts, lo, hi = more(
        3, after(meta, joined[0]), tok_last, joined, toks
    )
    cot_last = swap(after(cot_far, lo), "blk", 1)
    cots = (cot_own, cot_near, cot_far, cot_last)
    attn, lse = attend(meta, lo, hi, query, keys, values, starts, per)

    meta = after(meta, lse)
    e_mlp, normed, grad_vec, mlp_sums, out_even, out_odd, *packets = feed_forward(
        meta, toks[2:], cots[2:], *mlp_args, before=first, near=cots[:2], attn=attn
    )
    up_keep, up_send = chunks_of(*packets[:2], rows, 1)
    low_keep, low_send = low_chunks(*packets[2:], rows)
    up_masks, low_masks = mask_order(rows, 1), mask_order(rows, 2)
    out_got = swap(out_odd, "blk", 1)
    up_got = swap(up_send, "rows", up_masks[0])
    low_got = swap(low_send, "rows", low_masks[0])

    meta = after(meta, mlp_sums)
    grad_joined = attend_back(
        meta, lo, hi, query, keys, values, attn, grad_vec, starts, lse, low, high, per
    )
    meta = after(meta, grad_joined)
    qkv_keep, qkv_send, small = joined_weight(
        meta, grad_joined, normed, ln1_gain, ln1_bias, w_own, mlp_sums, rows
    )
    qkv_keep, qkv_send = chunks_of(qkv_keep, qkv_send, rows, 1)
    qkv_got = swap(qkv_send, "rows", 1)

    half = D // 2
    if fits(rows):
        chunk = D // rows
        meta = after(meta, qkv_keep)
        up, lower = [up_keep, up_got], [low_keep, low_got]
        flat = [v.reshape(2 * seq, D) for v in (out_even, out_got)]
        up_send, low_send, out_send = block_sums(
            "first_sums",
            meta,
            2,
            (half // 2, [(term, half // 2) for term in up]),
            (half, [(term, half) for term in lower]),
            (seq, [(term, seq) for term in flat]),
        )
        up.append(swap(up_send, "rows", up_masks[1]))
        lower.append(swap(low_send, "rows", low_masks[1]))
    else:
        out_send = add_low(out_even[1], out_got[1])
    out_far = swap(out_send, "blk", 2)
    meta = after(meta, out_send)
    e_own, e_near, e_send, e_last = norm_grad(meta, grad_joined, e_mlp, ln1_gain, w_own, seq)
    e_last = swap(e_last, "blk", 1)
    e_near = swap(e_near, "blk", 1)
    if fits(rows):
        joined = [after(qkv_keep, e_own), qkv_got]
        tail = add_low(joined[0][half:], qkv_got[half:])
        qkv_send = jnp.concatenate([next_send(joined, half), tail])
        joined.append(swap(qkv_send, "rows", 2))
        meta = after(meta, qkv_send)
        low_send = next_send(lower, half)
        lower.append(swap(low_send, "rows", low_masks[2]))
        e_send = after(e_send, low_send, out_far)
    e_send = add_low(e_send, e_last)
    e_far = swap(e_send, "blk", 2)
    if fits(rows):
        joined[0] = after(joined[0], e_send)
        tail = add_low(after(qkv_send, e_send)[half // 2 :], joined[2][half // 2 :])
        qkv_send = jnp.concatenate([next_send(joined, half // 2), tail])
        joined.append(swap(qkv_send, "rows", 4))
        up[0] = after(up[0], qkv_send)
        up_send = next_send(up, half // 2)
        up.append(swap(up_send, "rows", up_masks[2]))
        out_args = (after(tok_own, qkv_send), out_even, out_got, out_far, b_out, b_down)
        result = finish(result_kernel, "result", seq, *out_args)
        meta = after(meta, result)
        lower[0] = after(lower[0], result)
        piece = sum(term[:width].astype(F32) for term in lower).astype(BF16)
        meta = after(meta, piece)
        piece = spread_rows(piece)
        packet = ((chunk + 32, width), F32)
        last = pl.BlockSpec((SMALL, 3 * width), lambda i, m: (chunk // SMALL, 0))
        kept, near, far, small = simple(
            last_qkv_kernel,
            "last_qkv",
            [((chunk, width), F32), packet, packet, ((32, width), F32)],
            meta,
            *joined,
            qkv_send,
            joined[3],
            specs=[pl.BlockSpec((chunk, 3 * width), lambda i, m: (0, 0))] * 4 + [last] * 2,
        )
        near, far, diag = swap(near, "blk", 1), swap(far, "blk", 2), swap(small, "blk", 3)
        tok_args = (after(tok_own, small), e_own, e_near, e_far, cot_own)
        grad_tokens = finish(token_kernel, "token_grad", seq, *tok_args)
        meta = after(meta, grad_tokens)
        ends = [((width, hid // 2), F32), ((width // 2, width), F32)]
        down, out_w = simple(lower_kernel, "lower", ends, meta, piece)
        meta = after(meta, down)
        down = down.T
        qkv, gb_qkv, gb_out, gb_up, gb_down, *norms = assemble(
            meta, kept, small, near, far, diag
        )
        up[0] = after(up[0], qkv)
        up = sum(term[:chunk].astype(F32) for term in up)
    else:
        up = reduce_plain(up_keep, up_got, up_masks[1:])
        weights = reduce_plain(low_keep, low_got, low_masks[1:])
        qkv = reduce_plain(qkv_keep, qkv_got, up_masks[1:])
        piece = spread_rows(weights).T
        cut = 4 * hid // rows
        down, out_w = piece[:cut], piece[cut:]
        kept, near, far = split_columns(qkv)
        near, far = swap(near, "blk", 1), swap(far, "blk", 2)
        ends = [jnp.where(blk % 2 == 0, a, b) for a, b in ((kept, far), (far, kept))]
        qkv = jnp.concatenate([ends[0], near, ends[1]], axis=1)
        out_args = (tok_own, out_even, out_got, out_far, b_out, b_down)
        result = finish(result_kernel, "result", seq, *out_args)
        tok_args = (tok_own, e_own, e_near, e_far, cot_own)
        grad_tokens = finish(token_kernel, "token_grad", seq, *tok_args)
        third = 3 * width
        table = jnp.concatenate([small[0:8], small[8:16, : D - third]], axis=1)
        mine = (jnp.arange(4) == blk)[:, None]
        joined = lax.psum(jnp.where(mine, small[2:3], 0.0), ("rows", "blk"))
        gb_up = lax.psum(jnp.where(mine, table[4:5], 0.0), ("rows", "blk")).reshape(FF)
        gb_qkv = jnp.concatenate(
            [
                jnp.concatenate([joined[:, 0:128], joined[:, 256:320]], axis=1).reshape(D),
                jnp.concatenate([joined[:, 128:256], joined[:, 320:384]], axis=1).reshape(D),
                joined[:, 384:576].reshape(D),
            ]
        )
        gain_1, shift_1, _, _, _, gain_2, shift_2, gb_out = lax.psum(table, ("rows", "blk"))
        norms, gb_down = (gain_1, shift_1, gain_2, shift_2), gb_out
    return (
        result[None],
        grad_tokens[None],
        qkv,
        out_w,
        up,
        down,
        gb_qkv,
        gb_out,
        gb_up,
        gb_down,
        *norms,
    )


def solution(mesh):
    split = P("rows", "blk")
    in_specs = (
        P("rows", "blk", None),
        split,
        P("rows"),
        *(P(),) * 12,
        P("rows", "blk", None),
    )
    out_specs = (
        P("rows", "blk", None),
        P("rows", "blk", None),
        *(split,) * 4,
        *(P(),) * 8,
    )
    return jax.shard_map(local, mesh=mesh, in_specs=in_specs, out_specs=out_specs, check_vma=False)
```

```python
import math
from functools import partial

import jax
import jax.numpy as jnp
import numpy as np
from jax import lax
from jax.experimental import pallas as pl
from jax.experimental.pallas import tpu as pltpu
from jax.sharding import PartitionSpec as P

D = 768
HEADS = 12
HDIM = 64
ROT = 16
FF = 3072
EPS = 1e-05
MASKED = -1e30
TILE = 256
VROWS = 80
LN2 = math.log(2.0)
EXTRA = 16
LANES = 128
F32 = jnp.float32
BF16 = jnp.bfloat16
COST = pl.CostEstimate(flops=0, bytes_accessed=0, transcendentals=0)
NT_DIMS = (((1,), (1,)), ((), ()))
TN_DIMS = (((0,), (0,)), ((), ()))


def dot(left, right):
    return jnp.dot(left, right, preferred_element_type=F32)


def dot_nt(left, right):
    return lax.dot_general(left, right, NT_DIMS, preferred_element_type=F32)


def dot_tn(left, right):
    return lax.dot_general(left, right, TN_DIMS, preferred_element_type=F32)


def normalize(value):
    center = value - jnp.mean(value, axis=-1, keepdims=True)
    spread = jnp.mean(center * center, axis=-1, keepdims=True)
    return center * lax.rsqrt(spread + EPS)


def angle_parts(length):
    dim = np.arange(LANES) % HDIM
    inverse = np.where(dim < ROT, 10000.0 ** (-2.0 * (dim % (ROT // 2)) / ROT), 0.0)
    high = (np.arange(length // LANES) * LANES)[:, None] * inverse
    low = np.arange(LANES)[:, None] * inverse
    parts = np.stack([np.cos(low), np.sin(low)]), np.stack([np.cos(high), np.sin(high)])
    return tuple(jnp.asarray(part, F32) for part in parts)


def rotation(low_ref, high_ref, tile):
    lane = lax.broadcasted_iota(jnp.int32, (1, LANES), 1) % HDIM
    sign = jnp.where(lane < ROT // 2, -1.0, 1.0)
    cos_rows, sin_rows = [], []
    for part in range(TILE // LANES):
        row = tile * (TILE // LANES) + part
        cos_high = high_ref[0, pl.ds(row, 1), :]
        sin_high = high_ref[1, pl.ds(row, 1), :]
        cos_rows.append(low_ref[0] * cos_high - low_ref[1] * sin_high)
        sin_rows.append((low_ref[1] * cos_high + low_ref[0] * sin_high) * sign)
    return jnp.concatenate(cos_rows, axis=0), jnp.concatenate(sin_rows, axis=0)


def swap_halves(value):
    lane = lax.broadcasted_iota(jnp.int32, value.shape, 1) % HDIM
    half = ROT // 2
    return jnp.where(
        lane < half, pltpu.roll(value, LANES - half, 1), pltpu.roll(value, half, 1)
    )


def true_block(meta_ref, slot):
    return jnp.bitwise_xor(meta_ref[0], slot)


def params(*semantics, vmem=None):
    return pltpu.CompilerParams(
        dimension_semantics=semantics or ("arbitrary",), vmem_limit_bytes=vmem or 67_043_328
    )


def whole(shape):
    return pl.BlockSpec(shape, lambda *_: (0,) * len(shape))


def own_blocks(refs, odd, into):
    places = ((0, 256), (128, 320), (384, 512))
    for part, (pair_at, third_at) in enumerate(places):
        left, right = refs[2 * part], refs[2 * part + 1]

        @pl.when(odd == 0)
        def _(left=left, right=right, pair_at=pair_at, third_at=third_at):
            into[:, pair_at : pair_at + 128] = left[...]
            into[:, third_at : third_at + 64] = right[:, 0:64]

        @pl.when(odd == 1)
        def _(left=left, right=right, pair_at=pair_at, third_at=third_at):
            into[:, pair_at : pair_at + 128] = jnp.concatenate(
                [left[:, 64:128], right[:, 0:64]], axis=1
            )
            into[:, third_at : third_at + 64] = right[:, 64:128]


def row(ref):
    return ref[...].reshape(1, ref.shape[0])


def own_bias(b_ref, odd, blk, into):
    blocks = []
    for part in range(3):
        for side in range(2):
            at = pl.multiple_of((part * (D // LANES) + side + 3 * blk // 2) * LANES, LANES)
            blocks.append(b_ref[pl.ds(at, LANES)].reshape(1, LANES))
    own_blocks(blocks, odd, into)


def project_tile(normed, gain, shift, w_ref, b_ref, low, high, tile, q_ref, k_ref, v_ref):
    attn_in = (normed * row(gain) + row(shift)).astype(BF16)
    joined = dot(attn_in, w_ref[...]) + b_ref[...]
    cos, sin = rotation(low, high, tile)
    scale = HDIM**-0.5 / LN2

    def turn(block):
        return block * cos + swap_halves(block) * sin

    query = turn(joined[:, 0:128]) * scale
    keys = turn(joined[:, 128:256])
    mixed = turn(joined[:, 256:384])
    q_ref[:, 0:128] = query.astype(BF16)
    k_ref[:, 0:128] = keys.astype(BF16)
    q_ref[:, 128:192] = (mixed[:, 0:64] * scale).astype(BF16)
    k_ref[:, 128:192] = mixed[:, 64:128].astype(BF16)
    v_ref[...] = joined[:, 384:576].astype(BF16)


def find_starts(seq, meta, valid, pairs, start_ref, lo_ref, hi_ref):
    segs = [ref[at : at + 1, 0:seq].astype(F32) for ref in pairs for at in range(2)]
    below = [
        sum(jnp.sum((seg < number).astype(F32), axis=1, keepdims=True) for seg in segs)
        for number in (1, 2, 3)
    ]
    per = seq // TILE
    iota = lax.broadcasted_iota(jnp.int32, (1, seq), 1)
    for slot, seg in enumerate(segs):
        block = true_block(meta, slot)
        begin = jnp.zeros((1, seq), F32)
        for number in (1, 2, 3):
            begin = jnp.where(seg == number, below[number - 1], begin)
        pos = iota + block * seq
        begin = jnp.where(pos < valid[0], begin.astype(jnp.int32), pos)
        for part in range(per):
            tile = begin[:, part * TILE : (part + 1) * TILE]
            start_ref[slot * per + part] = tile
            lo_ref[block * per + part] = jnp.min(tile) // TILE
            hi_ref[block * per + part] = (jnp.max(tile) + (TILE - 1)) // TILE


def qkv_kernel(slot, meta, x_ref, gain, shift, low, high, w_ref, b_ref, *refs):
    per = pl.num_programs(0)
    tile = true_block(meta, slot) * per + pl.program_id(0)
    normed = normalize(x_ref[...].astype(F32))
    project_tile(normed, gain, shift, w_ref, b_ref, low, high, tile, *refs[3:])


def project(slot, meta, x, gain, shift, low, high, w, b, filled, seq):
    width = D // 4
    per = seq // TILE
    out = jax.ShapeDtypeStruct((4 * seq, width), BF16)
    out_spec = pl.BlockSpec((TILE, width), lambda i, m: (slot * per + i, 0))
    args = [x, gain, shift, low, high, w, b, *filled]
    specs = [pl.BlockSpec((TILE, D), lambda i, m: (i, 0))]
    specs += [whole(a.shape) for a in args[1:7]]
    specs += [pl.BlockSpec(memory_space=pl.ANY)] * 3
    return pl.pallas_call(
        partial(qkv_kernel, slot),
        out_shape=[out] * 3,
        grid_spec=pltpu.PrefetchScalarGridSpec(
            num_scalar_prefetch=1, grid=(per,), in_specs=specs, out_specs=[out_spec] * 3
        ),
        input_output_aliases={8 + i: i for i in range(3)},
        compiler_params=params(),
        cost_estimate=COST,
        name=f"qkv_{slot}",
    )(meta, *args)


def mask_order(rows, first):
    masks = [1 << bit for bit in range(rows.bit_length() - 1)]
    return masks if first == 1 else masks[1::-1] + masks[2:]


def places(masks):
    order = [0]
    for mask in reversed(masks):
        order = order + [mask + i for i in order]
    return order


def fits(rows):
    return rows == 8 and D // rows % 32 == 0


def store_chunks(load, keep, send, meta, rows, first):
    size = D // rows
    for index, place in enumerate(places(mask_order(rows, first))):
        at = pl.multiple_of(jnp.bitwise_xor(meta[1], place) * size, 32)
        into = keep if index < rows // 2 else send
        row_at = index % (rows // 2) * size
        into[row_at : row_at + size, :] = load(pl.ds(at, size)).astype(into.dtype)


def store_low(grad, keep, send, meta, rows):
    size, hid = D // 4, FF // 4
    for index, place in enumerate(places(mask_order(rows, 2))):
        chunk = jnp.bitwise_xor(meta[1], place)
        at = pl.ds(pl.multiple_of(chunk % 4 * size, 64), size)
        down = pl.multiple_of(hid + chunk // 4 * (hid // 2), LANES)
        out = pl.multiple_of(2 * hid + chunk // 4 * LANES, LANES)
        into = keep if index < rows // 2 else send
        row_at = slice(index % (rows // 2) * size, (index % (rows // 2) + 1) * size)
        into[row_at, : hid // 2] = grad[at, pl.ds(down, hid // 2)].astype(BF16)
        into[row_at, hid // 2 :] = grad[at, pl.ds(out, LANES)].astype(BF16)


def low_shapes(rows):
    if fits(rows):
        return [(D, FF // 8 + LANES)] * 2
    return [(D, FF // 4 + 2 * LANES), (8, LANES)]


def low_chunks(keep, send, rows):
    if fits(rows):
        return keep, send
    hid, width, count = FF // 4, D // 4, rows // 4
    parts = [
        part.reshape(4, width, count, part.shape[1] // count).transpose(2, 0, 1, 3)
        for part in (keep[:, :hid], keep[:, hid : hid + width])
    ]
    chunks = jnp.concatenate(parts, axis=3).reshape(rows, width, -1)
    order = jnp.array(places(mask_order(rows, 2))) ^ lax.axis_index("rows")
    chunks = jnp.take(chunks, order, axis=0).reshape(rows * width, -1)
    return chunks[: rows * width // 2], chunks[rows * width // 2 :]


def chunk_shapes(cols, rows, extra=0):
    if fits(rows):
        return [(D // 2 + extra, cols)] * 2
    return [(D, cols), (8, LANES)]


def chunks_of(keep, send, rows, first):
    if fits(rows):
        return keep, send
    order = jnp.array(places(mask_order(rows, first))) ^ lax.axis_index("rows")
    parts = keep.reshape(rows, D // rows, keep.shape[1])
    parts = jnp.take(parts, order, axis=0).reshape(keep.shape)
    return parts[: D // 2], parts[D // 2 :]


def feed(normed, upstream, gain, shift, w_up, b_up, w_down):
    mlp_in = (normed * row(gain) + row(shift)).astype(BF16)
    hidden = dot(mlp_in, w_up[...]) + b_up
    cdf = 0.5 * (1.0 + lax.erf(hidden * (0.5**0.5)))
    act = (hidden * cdf).astype(BF16)
    slope = cdf + hidden * jnp.exp(-0.5 * hidden * hidden) * ((2.0 * math.pi) ** -0.5)
    grad_low = (slope * dot_nt(upstream, w_down[...])).astype(BF16)
    grad_norm = dot_nt(grad_low, w_up[...])
    return mlp_in, act, grad_low, grad_norm


def add_sums(sums, grad_low, grad_norm, normed):
    sums[0:1, :] += jnp.sum(grad_low.astype(F32), axis=0, keepdims=True)
    sums[1:2, :] += jnp.sum(grad_norm * normed, axis=0, keepdims=True)
    sums[2:3, :] += jnp.sum(grad_norm, axis=0, keepdims=True)


def own_row(ref, blk, size):
    return ref[pl.ds(pl.multiple_of(blk * size, LANES), size)].reshape(1, size)


def mlp_first_kernel(
    half, meta, xa, xb, ca, cb, gain, shift, b_up, w_up, w_down, w_out,
    gain1, shift1, b_qkv, low, high, w0, w1, w2, w3, w4, w5,
    mo_ref, e_ref, n_ref, gv_ref, sums, gup, gdown, q_ref, k_ref, v_ref, w_own, b_own, x_s, c_s,
):
    step = pl.program_id(0)

    @pl.when(step < half)
    def _():
        x_s[...] = xa[...]
        c_s[...] = ca[...]

    @pl.when(step >= half)
    def _():
        x_s[...] = xb[...]
        c_s[...] = cb[...]

    @pl.when(step == 0)
    def _():
        sums[...] = jnp.zeros_like(sums)
        gup[...] = jnp.zeros_like(gup)
        gdown[...] = jnp.zeros_like(gdown)
        odd = meta[0] % 2
        own_blocks((w0, w1, w2, w3, w4, w5), odd, w_own)
        own_bias(b_qkv, odd, meta[0], b_own)

    upstream = c_s[...]

    @pl.when(step < half)
    def _():
        sums[3:4, :] += jnp.sum(upstream.astype(F32), axis=0, keepdims=True)

    normed = normalize(x_s[...].astype(F32))
    n_ref[...] = normed.astype(BF16)
    tile = true_block(meta, step // half) * half + step % half
    project_tile(normed, gain1, shift1, w_own, b_own, low, high, tile, q_ref, k_ref, v_ref)
    bias = own_row(b_up, meta[0], gup.shape[1])
    mlp_in, act, grad_low, grad_norm = feed(normed, upstream, gain, shift, w_up, bias, w_down)
    mo_ref[...] = dot(act, w_down[...]).astype(BF16)
    add_sums(sums, grad_low, grad_norm, normed)
    e_ref[...] = (grad_norm * row(gain)).astype(BF16)
    gv_ref[...] = dot_nt(upstream, w_out[...]).astype(BF16)
    gup[...] += dot_tn(mlp_in, grad_low)
    gdown[...] += dot_tn(upstream, act)


def mlp_second_kernel(
    half, rows, meta, xa, xb, ca, cb, gain, shift, b_up, w_up, w_down, w_out,
    c0, c1, mo_in, o_near, o_far, sums_in, gup, gdown, *refs
):
    e_ref, n_ref, gv_ref, sums, even, odd, up_keep, up_send, low_keep, low_send = refs[3:13]
    x_s, c_s, n_s, grad = refs[13:]
    step = pl.program_id(0)
    hid = gup.shape[1]

    @pl.when(step < half)
    def _():
        x_s[...] = xa[...]
        c_s[...] = ca[...]
        n_s[...] = c0[...]

    @pl.when(step >= half)
    def _():
        x_s[...] = xb[...]
        c_s[...] = cb[...]
        n_s[...] = c1[...]

    @pl.when(step == 0)
    def _():
        sums[...] = sums_in[...]
        grad[:, 0:hid] = gup[...]
        grad[:, hid : 2 * hid] = gdown[...]
        grad[:, 2 * hid :] = jnp.zeros_like(grad[:, 2 * hid :])

    upstream = c_s[...]
    normed = normalize(x_s[...].astype(F32))
    n_ref[...] = normed.astype(BF16)
    bias = own_row(b_up, meta[0], hid)
    mlp_in, act, grad_low, grad_norm = feed(normed, upstream, gain, shift, w_up, bias, w_down)
    add_sums(sums, grad_low, grad_norm, normed)
    e_ref[...] = (grad_norm * row(gain)).astype(BF16)
    gv_ref[...] = dot_nt(upstream, w_out[...]).astype(BF16)
    grad[:, 0:hid] += dot_tn(mlp_in, grad_low)
    grad[:, hid : 2 * hid] += dot_tn(upstream, act)
    out_grad = dot_tn(upstream, o_far[...]) + dot_tn(n_s[...], o_near[...])
    side = out_grad.shape[1] // 2
    if fits(rows):
        grad[:, 2 * hid : 2 * hid + side] += out_grad[:, :side]
        grad[:, 2 * hid + LANES : 2 * hid + LANES + side] += out_grad[:, side:]
    else:
        grad[:, 2 * hid : 2 * hid + 2 * side] += out_grad
    far = (dot(act, w_down[...]) + dot(o_far[...], w_out[...])).astype(BF16)
    near = (mo_in[...].astype(F32) + dot(o_near[...], w_out[...])).astype(BF16)

    @pl.when(step < half)
    def _():
        even[0] = near
        even[1] = far

    @pl.when(step >= half)
    def _():
        odd[0] = near
        odd[1] = far

    @pl.when(step == pl.num_programs(0) - 1)
    def _():
        if fits(rows):
            store_chunks(lambda at: grad[at, 0:hid], up_keep, up_send, meta, rows, 1)
            store_low(grad, low_keep, low_send, meta, rows)
        else:
            up_keep[...] = grad[:, 0:hid].astype(BF16)
            low_keep[...] = grad[:, hid:].astype(BF16)


def feed_forward(
    meta, xs, cs, gain, shift, b_up, w_up, w_down, w_out, rows, seq,
    joined=None, before=None, near=None, attn=None,
):
    per = seq // TILE
    steps = 2 * per
    hid = FF // 4
    width = D // 4
    total = 4 * seq
    first = pl.BlockSpec((TILE, D), lambda i, m: (jnp.minimum(i, per - 1), 0))
    second = pl.BlockSpec((TILE, D), lambda i, m: (jnp.maximum(i - per, 0), 0))
    specs = [
        first,
        second,
        first,
        second,
        whole((D,)),
        whole((D,)),
        whole((FF,)),
        pl.BlockSpec((D, hid), lambda i, m: (0, m[0])),
        pl.BlockSpec((hid, D), lambda i, m: (m[0], 0)),
        pl.BlockSpec((width, D), lambda i, m: (m[0], 0)),
    ]
    args = [*xs, *cs, gain, shift, b_up, w_up, w_down, w_out]
    tile = pl.BlockSpec((TILE, D), lambda i, m: (i, 0))
    narrow = pl.BlockSpec((TILE, width), lambda i, m: (i, 0))
    sums = (8, D)
    scratch = [pltpu.VMEM((TILE, D), BF16), pltpu.VMEM((TILE, D), BF16)]
    pair = jax.ShapeDtypeStruct((steps * TILE, D), BF16)
    full = jax.ShapeDtypeStruct((total, D), BF16)
    vec = jax.ShapeDtypeStruct((total, width), BF16)
    if before is None:
        body = partial(mlp_first_kernel, per)
        gain1, shift1, w_qkv, b_qkv, low, high = joined
        args += [gain1, shift1, b_qkv, low, high]
        specs += [whole(a.shape) for a in args[-5:]]
        for part in range(3):
            for side in range(2):
                specs.append(
                    pl.BlockSpec(
                        (D, LANES),
                        lambda i, m, at=part * D // LANES + side: (0, at + 3 * m[0] // 2),
                    )
                )
                args.append(w_qkv)
        outs = [pair, full, full, vec, jax.ShapeDtypeStruct(sums, F32)]
        outs += [jax.ShapeDtypeStruct((D, hid), F32)] * 2 + [vec] * 3
        outs += [
            jax.ShapeDtypeStruct((D, 3 * width), BF16),
            jax.ShapeDtypeStruct((1, 3 * width), F32),
        ]
        out_specs = [tile, tile, tile, narrow, whole(sums)]
        out_specs += [whole((D, hid))] * 2 + [narrow] * 3
        out_specs += [whole((D, 3 * width)), whole((1, 3 * width))]
        aliases = {}
    else:
        body = partial(mlp_second_kernel, per, rows)
        mlp_out, norm_part, normed, grad_vec, sums_in, gup, gdown = before
        chunks = chunk_shapes(hid, rows) + low_shapes(rows)
        args += [*near, mlp_out, attn, attn, sums_in, gup, gdown, norm_part, normed, grad_vec]
        specs += [
            first,
            second,
            tile,
            narrow,
            pl.BlockSpec((TILE, width), lambda i, m: (i + steps, 0)),
            whole(sums),
            whole((D, hid)),
            whole((D, hid)),
            *(pl.BlockSpec(memory_space=pl.ANY),) * 3,
        ]
        aliases = {len(args) - 2 + i: i for i in range(3)}
        both = jax.ShapeDtypeStruct((2, seq, D), BF16)
        outs = [full, full, vec, jax.ShapeDtypeStruct(sums, F32), both, both]
        late = pl.BlockSpec((TILE, D), lambda i, m: (i + steps, 0))
        outs += [jax.ShapeDtypeStruct(shape, BF16) for shape in chunks]
        out_specs = [
            late,
            late,
            pl.BlockSpec((TILE, width), lambda i, m: (i + steps, 0)),
            whole(sums),
            pl.BlockSpec((2, TILE, D), lambda i, m: (0, jnp.minimum(i, per - 1), 0)),
            pl.BlockSpec((2, TILE, D), lambda i, m: (0, jnp.maximum(i - per, 0), 0)),
            *(whole(shape) for shape in chunks),
        ]
        scratch += [pltpu.VMEM((TILE, D), BF16), pltpu.VMEM((D, 2 * hid + 2 * LANES), F32)]
    return pl.pallas_call(
        body,
        out_shape=outs,
        grid_spec=pltpu.PrefetchScalarGridSpec(
            num_scalar_prefetch=1,
            grid=(steps,),
            in_specs=specs,
            out_specs=out_specs,
            scratch_shapes=scratch,
        ),
        input_output_aliases=aliases,
        compiler_params=params(),
        cost_estimate=COST,
        name="mlp_first" if before is None else "mlp_second",
    )(meta, *args)


def head_masks():
    lane = lax.broadcasted_iota(jnp.int32, (1, LANES), 1)
    first = jnp.where(lane < HDIM, 1.0, 0.0).astype(BF16)
    second = jnp.where(lane < HDIM, 0.0, 1.0).astype(BF16)
    return first, second


def slot_rows(meta, per, tile):
    slot = jnp.bitwise_xor(tile // per, meta[0])
    return pl.multiple_of((slot * per + tile % per) * TILE, TILE)


def by_head(first, second, block, third):
    return (block * first, block * second, third)


def transpose_all(from_ref, to_ref):
    @pl.loop(0, from_ref.shape[0] // TILE)
    def _(tile):
        rows = pl.ds(pl.multiple_of(tile * TILE, TILE), TILE)
        to_ref[:, rows] = from_ref[rows, :].astype(F32).T.astype(BF16)


def attend_kernel(
    per, meta, valid, q_ref, k_ref, v_ref, pair_own, pair_far,
    o_ref, lse_ref, starts_ref, lo, hi, vt_ref, acc, s_ref,
):
    mask0, mask1 = head_masks()
    tiles = k_ref.shape[0] // TILE
    qi = pl.program_id(0)

    @pl.when(qi == 0)
    def _():
        find_starts(per * TILE, meta, valid, (pair_own, pair_far), starts_ref, lo, hi)
        ones = jnp.where(lax.broadcasted_iota(jnp.int32, (VROWS - HDIM, TILE), 0) == 0, 1.0, 0.0)

        @pl.loop(0, tiles)
        def _(tile):
            rows = pl.ds(pl.multiple_of(tile * TILE, TILE), TILE)
            block = v_ref[rows, :].astype(F32).T
            for head in range(3):
                at = head * VROWS
                vt_ref[at : at + HDIM, rows] = block[head * HDIM : (head + 1) * HDIM].astype(BF16)
                vt_ref[at + HDIM : at + VROWS, rows] = ones.astype(BF16)

    key_iota = lax.broadcasted_iota(jnp.int32, (TILE, TILE), 0)
    query_iota = lax.broadcasted_iota(jnp.int32, (TILE, TILE), 1)
    queries = by_head(mask0, mask1, q_ref[:, 0:128], q_ref[:, 128:192])
    starts = starts_ref[jnp.bitwise_xor(qi // per, meta[0]) * per + qi % per]
    acc[...] = jnp.zeros_like(acc)

    def key_tile(turn):
        return jnp.where(turn == 0, qi, first + turn - 1)

    def score(masked, ki):
        k_rows = pl.ds(slot_rows(meta, per, ki), TILE)
        pair, third = k_ref[k_rows, 0:128], k_ref[k_rows, 128:192]
        scores = [dot_nt(third if head == 2 else pair, queries[head]) for head in range(3)]
        if masked:
            allowed = (key_iota >= starts - ki * TILE) & (key_iota <= query_iota + (qi - ki) * TILE)
            scores = [jnp.where(allowed, x, MASKED) for x in scores]
        return scores, [jnp.max(x, axis=0, keepdims=True) for x in scores]

    def value(ki, tops, peaks):
        k_rows = pl.ds(slot_rows(meta, per, ki), TILE)
        news = [jnp.maximum(top, peak) for top, peak in zip(tops, peaks)]
        fades = [jnp.exp2(top - new) for top, new in zip(tops, news)]
        weights = [jnp.exp2(s_ref[head] - news[head]).astype(BF16) for head in range(3)]
        terms = [
            dot(vt_ref[head * VROWS : (head + 1) * VROWS, k_rows], weights[head]) for head in range(3)
        ]
        return news, fades, terms

    def put(fades, terms):
        for head in range(3):
            cols = slice(head * VROWS, (head + 1) * VROWS)
            acc[cols, :] = acc[cols, :] * fades[head] + terms[head]

    def visit(masked, turn, carry):
        tops, peaks = carry
        scores, next_peaks = score(masked, key_tile(turn + 1))
        news, fades, terms = value(key_tile(turn), tops, peaks)
        peaks = next_peaks
        for head in range(3):
            s_ref[head] = scores[head]
        put(fades, terms)
        return tuple(news), tuple(peaks)

    first = lo[qi]
    full = jnp.minimum(hi[qi], qi)
    scores, peaks = score(True, qi)
    for head in range(3):
        s_ref[head] = scores[head]
    carry = ((jnp.full((1, TILE), MASKED, F32),) * 3, tuple(peaks))
    carry = lax.fori_loop(0, full - first, partial(visit, True), carry)
    carry = lax.fori_loop(full - first, qi - first, partial(visit, False), carry)
    tops, fades, terms = value(key_tile(qi - first), *carry)
    put(fades, terms)
    heads = []
    for head, top in enumerate(tops):
        at = head * VROWS
        total = acc[at + HDIM : at + HDIM + 1, :]
        heads.append(acc[at : at + HDIM, :] / total)
        lse_ref[head, 0] = top + jnp.log2(total)
    o_ref[...] = jnp.concatenate(heads, axis=0).T.astype(BF16)

def attend(meta, valid_len, query, keys, values, seg_pair, cot_far, per):
    total, width = query.shape
    tiles = total // TILE

    def slot(i, m):
        return jnp.bitwise_xor(i // per, m[0]) * per + i % per

    q_spec = pl.BlockSpec((TILE, width), lambda i, m, v: (slot(i, m), 0))
    lse_spec = pl.BlockSpec((3, 1, 1, TILE), lambda i, m, v: (0, slot(i, m), 0, 0))
    far_spec = pl.BlockSpec((EXTRA, D), lambda i, m, v: (per * TILE // EXTRA, 0))
    smem = pl.BlockSpec(memory_space=pltpu.SMEM)
    return pl.pallas_call(
        partial(attend_kernel, per),
        out_shape=[
            jax.ShapeDtypeStruct((total, width), BF16),
            jax.ShapeDtypeStruct((3, tiles, 1, TILE), F32),
            jax.ShapeDtypeStruct((tiles, 1, TILE), jnp.int32),
            jax.ShapeDtypeStruct((tiles,), jnp.int32),
            jax.ShapeDtypeStruct((tiles,), jnp.int32),
        ],
        grid_spec=pltpu.PrefetchScalarGridSpec(
            num_scalar_prefetch=2,
            grid=(tiles,),
            in_specs=[
                q_spec,
                whole(keys.shape),
                whole(values.shape),
                whole(seg_pair.shape),
                far_spec,
            ],
            out_specs=[q_spec, lse_spec, whole((tiles, 1, TILE)), smem, smem],
            scratch_shapes=[
                pltpu.VMEM((3 * VROWS, total), BF16),
                pltpu.VMEM((3 * VROWS, TILE), F32),
                pltpu.VMEM((3, TILE, TILE), F32),
            ],
        ),
        compiler_params=params(),
        cost_estimate=COST,
        name="attend",
    )(meta, valid_len, query, keys, values, seg_pair, cot_far)


def attend_back_kernel(
    per, meta, lo, hi, q_ref, k_ref, v_ref, o_ref, gv_ref, start_ref, lse_ref, low, high,
    gj_ref, kt_ref, dk_ref, dv_ref, dqt_ref
):
    mask0, mask1 = head_masks()
    tiles = k_ref.shape[0] // TILE
    qi = tiles - 1 - pl.program_id(0)

    @pl.when(pl.program_id(0) == 0)
    def _():
        transpose_all(k_ref, kt_ref)

    own_rows = pl.ds(slot_rows(meta, per, qi), TILE)
    key_iota = lax.broadcasted_iota(jnp.int32, (TILE, TILE), 0)
    query_iota = lax.broadcasted_iota(jnp.int32, (TILE, TILE), 1)
    queries = by_head(mask0, mask1, q_ref[:, 0:128], q_ref[:, 128:192])
    grads = by_head(mask0, mask1, gv_ref[:, 0:128], gv_ref[:, 128:192])
    starts = start_ref[0]
    lses = [lse_ref[head, 0] for head in range(3)]
    product = (gv_ref[...].astype(F32) * o_ref[...].astype(F32)).T
    deltas = [
        jnp.sum(product[head * HDIM : (head + 1) * HDIM], axis=0, keepdims=True)
        for head in range(3)
    ]
    dqt_ref[...] = jnp.zeros_like(dqt_ref)

    @pl.when(pl.program_id(0) == 0)
    def _():
        dk_ref[...] = jnp.zeros_like(dk_ref)
        dv_ref[...] = jnp.zeros_like(dv_ref)

    def load(ki):
        k_rows = pl.ds(slot_rows(meta, per, ki), TILE)
        return k_rows

    def score(masked, ki):
        k_rows = load(ki)
        pair, third = k_ref[k_rows, 0:128], k_ref[k_rows, 128:192]
        v_pair, v_third = v_ref[k_rows, 0:128], v_ref[k_rows, 128:192]
        scores = [dot_nt(third if head == 2 else pair, queries[head]) for head in range(3)]
        grad_probs = [dot_nt(v_third if head == 2 else v_pair, grads[head]) for head in range(3)]
        if masked:
            allowed = (key_iota >= starts - ki * TILE) & (key_iota <= query_iota + (qi - ki) * TILE)
            scores = [jnp.where(allowed, x, MASKED) for x in scores]
        return scores, grad_probs

    def terms(ki, scores, grad_probs):
        k_rows = load(ki)
        probs = [jnp.exp2(x - lse) for x, lse in zip(scores, lses)]
        grad_scores = [
            (p * (g - delta)).astype(BF16) for p, g, delta in zip(probs, grad_probs, deltas)
        ]
        dv = [dot(p.astype(BF16), g) for p, g in zip(probs, grads)]
        dk = [dot(g, q) for g, q in zip(grad_scores, queries)]
        dq = [
            dot(kt_ref[head * HDIM : (head + 1) * HDIM, k_rows], grad_scores[head])
            for head in range(3)
        ]
        return dk, dv, dq

    def add(ki, dk, dv, dq):
        k_rows = load(ki)
        for into, parts in ((dk_ref, dk), (dv_ref, dv)):
            into[k_rows, 0:128] += parts[0] + parts[1]
            into[k_rows, 128:192] += parts[2]
        for head in range(3):
            dqt_ref[head * HDIM : (head + 1) * HDIM, :] += dq[head]

    first = lo[qi]
    full = jnp.minimum(hi[qi], qi)

    def visit(masked, ki):
        add(ki, *terms(ki, *score(masked, ki)))

    @pl.loop(first, full)
    def _(ki):
        visit(True, ki)

    @pl.loop(full, qi)
    def _(ki):
        visit(False, ki)

    visit(True, qi)

    cos, sin = rotation(low, high, qi)

    def turn_back(block):
        return block * cos - swap_halves(block) * sin

    dq = dqt_ref[...].T * (HDIM**-0.5)
    dk = dk_ref[own_rows, :] * LN2
    gj_ref[:, 0:128] = turn_back(dq[:, 0:128]).astype(BF16)
    gj_ref[:, 128:256] = turn_back(dk[:, 0:128]).astype(BF16)
    mixed = jnp.concatenate([dq[:, 128:192], dk[:, 128:192]], axis=1)
    gj_ref[:, 256:384] = turn_back(mixed).astype(BF16)
    gj_ref[:, 384:576] = dv_ref[own_rows, :].astype(BF16)


def attend_back(
    meta, lo, hi, query, keys, values, attn, grad_vec, starts, lse, low, high, per
):
    total, width = query.shape
    tiles = total // TILE

    def slot(i, m):
        tile = tiles - 1 - i
        return jnp.bitwise_xor(tile // per, m[0]) * per + tile % per

    q_spec = pl.BlockSpec((TILE, width), lambda i, m, lo, hi: (slot(i, m), 0))
    gj_spec = pl.BlockSpec((TILE, 3 * width), lambda i, m, lo, hi: (slot(i, m), 0))
    start_spec = pl.BlockSpec((1, 1, TILE), lambda i, m, lo, hi: (slot(i, m), 0, 0))
    lse_spec = pl.BlockSpec((3, 1, 1, TILE), lambda i, m, lo, hi: (0, slot(i, m), 0, 0))
    return pl.pallas_call(
        partial(attend_back_kernel, per),
        out_shape=jax.ShapeDtypeStruct((total, 3 * width), BF16),
        grid_spec=pltpu.PrefetchScalarGridSpec(
            num_scalar_prefetch=3,
            grid=(tiles,),
            in_specs=[
                q_spec,
                whole(keys.shape),
                whole(values.shape),
                q_spec,
                q_spec,
                start_spec,
                lse_spec,
                whole(low.shape),
                whole(high.shape),
            ],
            out_specs=gj_spec,
            scratch_shapes=[
                pltpu.VMEM((width, total), BF16),
                pltpu.VMEM((total, width), F32),
                pltpu.VMEM((total, width), F32),
                pltpu.VMEM((width, TILE), F32),
            ],
        ),
        compiler_params=params(),
        cost_estimate=COST,
        name="attend_back",
    )(meta, lo, hi, query, keys, values, attn, grad_vec, starts, lse, low, high)


SMALL = 16


def pack_small(gain_sum, shift_sum, bias, mlp_sums):
    third = 3 * D // 4
    which = lax.broadcasted_iota(jnp.int32, (8, D), 0)
    table = jnp.concatenate([jnp.zeros((4, D), F32), mlp_sums[0:4]], axis=0)
    table = jnp.where(which == 0, gain_sum, jnp.where(which == 1, shift_sum, table))
    head = jnp.where(which[:, :third] == 2, bias, table[:, :third])
    tail = jnp.concatenate([table[:, third:], jnp.zeros((8, 2 * third - D), F32)], axis=1)
    return jnp.concatenate([head, tail], axis=0)


def high_low(value):
    high = value.astype(BF16)
    return high, (value - high.astype(F32)).astype(BF16)


def weight_kernel(rows, meta, *refs):
    gj_ref, n_ref, gain, shift, w_ref, mlp_sums, keep, send, small, grad, bias = refs
    step = pl.program_id(0)

    @pl.when(step == 0)
    def _():
        grad[...] = jnp.zeros_like(grad)
        bias[...] = jnp.zeros_like(bias)

    joined = gj_ref[...]
    bias[0:1, :] += jnp.sum(joined.astype(F32), axis=0, keepdims=True)
    grad[...] += dot_tn(n_ref[...], joined)

    @pl.when(step == pl.num_programs(0) - 1)
    def _():
        total = bias[0:1, :]
        width = total.shape[1]
        parts = jnp.concatenate(
            [*high_low(jnp.broadcast_to(total, (8, width)))], axis=0
        )
        shift_sum = dot_nt(parts, w_ref[...])
        shift_sum = shift_sum[0:1] + shift_sum[8:9]
        ones = jnp.ones((16, width), BF16)
        high, low = high_low(grad[...] * w_ref[...].astype(F32))
        gain_sum = (dot_nt(ones, high) + dot_nt(ones, low))[0:1]
        columns = jnp.concatenate(
            [jnp.broadcast_to(row(gain), (8, D)), jnp.broadcast_to(row(shift), (8, D))], axis=0
        ).T
        grad[...] = grad[...] * columns[:, 0:1] + columns[:, 8:9] * total
        rest = pack_small(gain_sum, shift_sum, total, mlp_sums[...])
        small[...] = rest
        if fits(rows):
            store_chunks(lambda at: grad[at, :], keep, send, meta, rows, 1)
            keep[D // 2 :, :] = rest.astype(BF16)
            send[D // 2 :, :] = rest.astype(BF16)
        else:
            keep[...] = grad[...].astype(BF16)


def row_tiles(cols, tile=TILE):
    return pl.BlockSpec((tile, cols), lambda i, m: (i, 0))


def joined_weight(meta, grad, normed, gain, shift, w, mlp_sums, rows):
    total, width = grad.shape
    tile = 2 * TILE
    chunks = chunk_shapes(width, rows, SMALL)
    args = [gain, shift, w, mlp_sums]
    return pl.pallas_call(
        partial(weight_kernel, rows),
        out_shape=[jax.ShapeDtypeStruct(shape, BF16) for shape in chunks]
        + [jax.ShapeDtypeStruct((SMALL, width), F32)],
        grid_spec=pltpu.PrefetchScalarGridSpec(
            num_scalar_prefetch=1,
            grid=(total // tile,),
            in_specs=[row_tiles(width, tile), row_tiles(D, tile), *(whole(a.shape) for a in args)],
            out_specs=[*(whole(shape) for shape in chunks), whole((SMALL, width))],
            scratch_shapes=[pltpu.VMEM((D, width), F32), pltpu.VMEM((8, width), F32)],
        ),
        compiler_params=params(),
        cost_estimate=COST,
        name="joined_weight",
    )(meta, grad, normed, *args)


def norm_kernel(meta, *refs):
    gjs, es, (gain, w_ref), outs = refs[0:4], refs[4:8], refs[8:10], refs[10:]
    for gj_ref, e_in, out in zip(gjs, es, outs):
        grad_norm = dot_nt(gj_ref[...], w_ref[...])
        out[...] = (grad_norm * row(gain) + e_in[...].astype(F32)).astype(BF16)


def norm_grad(meta, grad, e_mlp, gain, w, seq):
    tile = TILE
    per = seq // tile

    def slot_tiles(slot, cols):
        return pl.BlockSpec((tile, cols), lambda i, m: (slot * per + i, 0))

    return pl.pallas_call(
        norm_kernel,
        out_shape=[jax.ShapeDtypeStruct((seq, D), BF16)] * 4,
        grid_spec=pltpu.PrefetchScalarGridSpec(
            num_scalar_prefetch=1,
            grid=(per,),
            in_specs=[
                *(slot_tiles(slot, grad.shape[1]) for slot in range(4)),
                *(slot_tiles(slot, D) for slot in range(4)),
                whole(gain.shape),
                whole(w.shape),
            ],
            out_specs=[slot_tiles(0, D)] * 4,
        ),
        compiler_params=params(),
        cost_estimate=COST,
        name="norm_grad",
    )(meta, *[grad] * 4, *[e_mlp] * 4, gain, w)


def simple(body, name, shapes, *args, specs=None):
    return pl.pallas_call(
        body,
        out_shape=[jax.ShapeDtypeStruct(shape, kind) for shape, kind in shapes],
        grid_spec=pltpu.PrefetchScalarGridSpec(
            num_scalar_prefetch=1,
            grid=(1,),
            in_specs=specs or [whole(a.shape) for a in args[1:]],
            out_specs=[whole(shape) for shape, _ in shapes],
        ),
        compiler_params=params(),
        cost_estimate=COST,
        name=name,
    )(*args)


def add_up(refs):
    total = refs[0][...].astype(F32)
    for ref in refs[1:]:
        total += ref[...].astype(F32)
    return total


def sums_kernel(counts, meta, *refs):
    ins, outs = refs[: sum(counts)], refs[sum(counts) :]
    for count, out in zip(counts, outs):
        out[...] = add_up(ins[:count]).astype(BF16)
        ins = ins[count:]


def block_sums(name, meta, steps, *jobs):
    specs, args, outs, out_specs = [], [], [], []
    for rows, terms in jobs:
        size, cols = rows // steps, terms[0][0].shape[1]
        for array, at in terms:
            specs.append(pl.BlockSpec((size, cols), lambda i, m, at=at // size: (at + i, 0)))
            args.append(array)
        outs.append(jax.ShapeDtypeStruct((rows, cols), BF16))
        out_specs.append(pl.BlockSpec((size, cols), lambda i, m: (i, 0)))
    return pl.pallas_call(
        partial(sums_kernel, [len(terms) for _, terms in jobs]),
        out_shape=outs,
        grid_spec=pltpu.PrefetchScalarGridSpec(
            num_scalar_prefetch=1, grid=(steps,), in_specs=specs, out_specs=out_specs
        ),
        compiler_params=params(),
        cost_estimate=COST,
        name=name,
    )(meta, *args)


def lower_kernel(meta, piece, down_ref, out_ref):
    cut = down_ref.shape[1]
    down_ref[...] = piece[:, :cut].astype(F32)
    out_ref[...] = piece[:, cut:].astype(F32).T[: out_ref.shape[0]]


def last_qkv_kernel(meta, *refs):
    *terms, sums, got_sums, kept, near, far, small = refs
    size = kept.shape[0]
    width = kept.shape[1]
    total = add_up(terms)
    rows = sums[...].astype(F32) + got_sums[...].astype(F32)
    for part in range(3):
        small[part * 8 : part * 8 + 8, :] = rows[0:8, part * width : (part + 1) * width]
    small[24:32, :] = rows[8:16, 0:width]
    near[size:, :] = small[...]
    far[size:, :] = small[...]
    query = jnp.concatenate([total[:, 0:128], total[:, 256:320]], axis=1)
    keys = jnp.concatenate([total[:, 128:256], total[:, 320:384]], axis=1)
    values = total[:, 384:576]
    plans = (
        (query, keys, values),
        (keys, query, values),
        (keys, values, query),
        (values, keys, query),
    )
    for blk, plan in enumerate(plans):

        @pl.when(meta[0] == blk)
        def _(plan=plan):
            kept[...] = plan[0]
            near[0:size, :] = plan[1]
            far[0:size, :] = plan[2]


def assemble_kernel(
    meta, kept, small, near, far, diag,
    qkv, b_qkv, b_out, b_up, b_down, gain1, shift1, gain2, shift2, table,
):
    size, width = kept.shape

    @pl.when(meta[0] % 2 == 0)
    def _():
        qkv[:, 0:width] = kept[...]
        qkv[:, 2 * width :] = far[0:size, :]

    @pl.when(meta[0] % 2 == 1)
    def _():
        qkv[:, 0:width] = far[0:size, :]
        qkv[:, 2 * width :] = kept[...]

    qkv[:, width : 2 * width] = near[0:size, :]
    table[0] = small[...]
    table[1] = near[size:, :]
    table[2] = far[size:, :]
    table[3] = diag[...]
    blocks = [table[jnp.bitwise_xor(meta[0], blk)] for blk in range(4)]
    total = blocks[0] + blocks[1] + blocks[2] + blocks[3]

    def vector(rows, index):
        parts = [rows[part * 8 + index : part * 8 + index + 1, :] for part in range(4)]
        return jnp.concatenate(parts, axis=1)

    for ref, index in ((gain1, 0), (shift1, 1), (gain2, 5), (shift2, 6), (b_out, 7), (b_down, 7)):
        ref[...] = vector(total, index).reshape(D)
    ups, parts = [], ([], [], [])
    for rows in blocks:
        ups.append(vector(rows, 4))
        joined = vector(rows, 2)
        parts[0].append(jnp.concatenate([joined[:, 0:128], joined[:, 256:320]], axis=1))
        parts[1].append(jnp.concatenate([joined[:, 128:256], joined[:, 320:384]], axis=1))
        parts[2].append(joined[:, 384:576])
    b_up[...] = jnp.concatenate(ups, axis=1).reshape(4 * D)
    b_qkv[...] = jnp.concatenate(parts[0] + parts[1] + parts[2], axis=1).reshape(3 * D)


def assemble(meta, kept, small, near, far, diag):
    size, width = kept.shape
    shapes = [((size, 3 * width), F32), ((3 * D,), F32), ((D,), F32), ((4 * D,), F32)]
    shapes += [((D,), F32)] * 5
    args = (kept, small, near, far, diag)
    return pl.pallas_call(
        assemble_kernel,
        out_shape=[jax.ShapeDtypeStruct(shape, kind) for shape, kind in shapes],
        grid_spec=pltpu.PrefetchScalarGridSpec(
            num_scalar_prefetch=1,
            grid=(1,),
            in_specs=[whole(a.shape) for a in args],
            out_specs=[whole(shape) for shape, _ in shapes],
            scratch_shapes=[pltpu.VMEM((4, 32, width), F32)],
        ),
        compiler_params=params(),
        cost_estimate=COST,
        name="assemble",
    )(meta, *args)


def next_send(terms, size):
    return sum(term[size // 2 : size].astype(F32) for term in terms).astype(BF16)


def reduce_plain(keep, got, masks):
    terms, size = [keep, got], keep.shape[0]
    for mask in masks:
        terms.append(swap(next_send(terms, size), "rows", mask))
        size //= 2
    return sum(term[:size].astype(F32) for term in terms)


def after(value, *others):
    return lax.optimization_barrier((value, others))[0]


def swap(value, axis, mask):
    size = lax.axis_size(axis)
    return lax.ppermute(value, axis, [(i, i ^ mask) for i in range(size)])


def add_low(left, right):
    return (left.astype(F32) + right.astype(F32)).astype(BF16)


def spread_rows(chunk):
    rows = lax.axis_size("rows")
    moves = [
        (r * 4 + b, (rows // 4 * b + r // 4) * 4 + r % 4) for r in range(rows) for b in range(4)
    ]
    return lax.ppermute(chunk, ("rows", "blk"), moves)


def split_columns(chunk):
    b = lax.axis_index("blk")
    q = jnp.concatenate([chunk[:, 0:128], chunk[:, 256:320]], axis=1)
    k = jnp.concatenate([chunk[:, 128:256], chunk[:, 320:384]], axis=1)
    v = chunk[:, 384:576]

    def choose(zero, one, two, three):
        return jnp.where(b < 2, jnp.where(b == 0, zero, one), jnp.where(b == 2, two, three))

    return choose(q, k, k, v), choose(k, q, v, k), choose(v, v, q, q)


def result_kernel(x_ref, even, near, far, b_out, b_down, out_ref):
    bias = row(b_out) + row(b_down)
    total = even[0].astype(F32) + near[0].astype(F32) + far[...].astype(F32)
    out_ref[...] = (x_ref[...].astype(F32) + bias + total).astype(BF16)


def token_kernel(x_ref, even, near, far, c_ref, out_ref):
    wide = x_ref[...].astype(F32)
    center = wide - jnp.mean(wide, axis=-1, keepdims=True)
    rate = lax.rsqrt(jnp.mean(center * center, axis=-1, keepdims=True) + EPS)
    normed = center * rate
    grad = even[...].astype(F32) + near[...].astype(F32) + far[...].astype(F32)
    mean = jnp.mean(grad, axis=-1, keepdims=True)
    along = jnp.mean(grad * normed, axis=-1, keepdims=True)
    back = rate * (grad - mean - normed * along)
    out_ref[...] = (c_ref[...].astype(F32) + back).astype(BF16)


def finish(body, name, seq, x, even, near, far, *more):
    flat = pl.BlockSpec((TILE, D), lambda i: (i, 0))
    own = pl.BlockSpec((1, TILE, D), lambda i: (0, i, 0))
    return pl.pallas_call(
        body,
        out_shape=jax.ShapeDtypeStruct((seq, D), BF16),
        grid=(seq // TILE,),
        in_specs=[
            *(own if a.ndim == 3 else flat for a in (x, even, near, far)),
            *(flat if a.ndim == 2 else whole(a.shape) for a in more),
        ],
        out_specs=flat,
        compiler_params=params(),
        cost_estimate=COST,
        name=name,
    )(x, even, near, far, *more)


def local(
    tokens, seg_ids, valid_len, ln1_gain, ln1_bias, w_qkv, b_qkv, w_out, b_out,
    ln2_gain, ln2_bias, w_up, b_up, w_down, b_down, cotangent,
):
    rows = lax.axis_size("rows")
    blk = lax.axis_index("blk")
    seq = tokens.shape[1]
    per = seq // TILE
    width = D // 4
    hid = FF // 4
    low, high = angle_parts(4 * seq)
    tok_own, cot_own = tokens[0], cotangent[0]

    cot_near = swap(cot_own, "blk", 1)
    tok_far = swap(tok_own, "blk", 2)
    tok_near = swap(tok_own, "blk", 1)
    seg_own = seg_ids.astype(BF16)
    seg_pair = jnp.concatenate([seg_own, swap(seg_own, "blk", 1)])
    seg_pair = jnp.pad(seg_pair, ((0, EXTRA - 2), (0, D - seq)))
    cot_long = jnp.concatenate([cot_own, seg_pair])
    cot_far = swap(cot_long, "blk", 2)

    meta = jnp.stack([blk, lax.axis_index("rows")]).astype(jnp.int32)
    mlp_args = (ln2_gain, ln2_bias, b_up, w_up, w_down, w_out, rows, seq)
    joined = (ln1_gain, ln1_bias, w_qkv, b_qkv, low, high)
    *first, query, keys, values, w_own, b_own = feed_forward(
        meta, (tok_own, tok_near), (cot_own, cot_near), *mlp_args, joined
    )
    meta = after(meta, b_own)

    def more(slot, m, tok, filled):
        args = (ln1_gain, ln1_bias, low, high, w_own, b_own, filled, seq)
        return project(slot, m, tok, *args)

    tok_last = swap(after(tok_far, b_own), "blk", 1)
    joined = more(2, meta, tok_far, (query, keys, values))
    query, keys, values = more(3, after(meta, joined[0]), tok_last, joined)
    cot_last = swap(after(cot_far, query), "blk", 1)
    cots = (cot_own, cot_near, cot_far, cot_last)
    attn, lse, starts, lo, hi = attend(
        meta, valid_len, query, keys, values, seg_pair, cot_far, per
    )

    meta = after(meta, lse)
    e_mlp, normed, grad_vec, mlp_sums, out_even, out_odd, *packets = feed_forward(
        meta, (tok_far, tok_last), cots[2:], *mlp_args, before=first, near=cots[:2], attn=attn
    )
    up_keep, up_send = chunks_of(*packets[:2], rows, 1)
    low_keep, low_send = low_chunks(*packets[2:], rows)
    up_masks, low_masks = mask_order(rows, 1), mask_order(rows, 2)
    out_got = swap(out_odd, "blk", 1)
    up_got = swap(up_send, "rows", up_masks[0])
    low_got = swap(low_send, "rows", low_masks[0])

    meta = after(meta, mlp_sums)
    grad_joined = attend_back(
        meta, lo, hi, query, keys, values, attn, grad_vec, starts, lse, low, high, per
    )
    meta = after(meta, grad_joined)
    qkv_keep, qkv_send, small = joined_weight(
        meta, grad_joined, normed, ln1_gain, ln1_bias, w_own, mlp_sums, rows
    )
    qkv_keep, qkv_send = chunks_of(qkv_keep, qkv_send, rows, 1)
    qkv_got = swap(qkv_send, "rows", 1)

    half = D // 2
    if fits(rows):
        chunk = D // rows
        meta = after(meta, qkv_keep)
        up, lower = [up_keep, up_got], [low_keep, low_got]
        flat = [v.reshape(2 * seq, D) for v in (out_even, out_got)]
        up_send, low_send, out_send = block_sums(
            "first_sums",
            meta,
            2,
            (half // 2, [(term, half // 2) for term in up]),
            (half, [(term, half) for term in lower]),
            (seq, [(term, seq) for term in flat]),
        )
        up.append(swap(up_send, "rows", up_masks[1]))
        lower.append(swap(low_send, "rows", low_masks[1]))
    else:
        out_send = add_low(out_even[1], out_got[1])
    out_far = swap(out_send, "blk", 2)
    meta = after(meta, out_send)
    e_own, e_near, e_send, e_last = norm_grad(meta, grad_joined, e_mlp, ln1_gain, w_own, seq)
    e_last = swap(e_last, "blk", 1)
    e_near = swap(e_near, "blk", 1)
    if fits(rows):
        joined = [after(qkv_keep, e_own), qkv_got]
        tail = add_low(joined[0][half:], qkv_got[half:])
        qkv_send = jnp.concatenate([next_send(joined, half), tail])
        joined.append(swap(qkv_send, "rows", 2))
        meta = after(meta, qkv_send)
        low_send = next_send(lower, half)
        lower.append(swap(low_send, "rows", low_masks[2]))
        e_send = after(e_send, low_send, out_far)
    e_send = add_low(e_send, e_last)
    e_far = swap(e_send, "blk", 2)
    if fits(rows):
        joined[0] = after(joined[0], e_send)
        tail = add_low(after(qkv_send, e_send)[half // 2 :], joined[2][half // 2 :])
        qkv_send = jnp.concatenate([next_send(joined, half // 2), tail])
        joined.append(swap(qkv_send, "rows", 4))
        up[0] = after(up[0], qkv_send)
        up_send = next_send(up, half // 2)
        up.append(swap(up_send, "rows", up_masks[2]))
        out_args = (after(tok_own, qkv_send), out_even, out_got, out_far, b_out, b_down)
        result = finish(result_kernel, "result", seq, *out_args)
        meta = after(meta, result)
        lower[0] = after(lower[0], result)
        piece = sum(term[:width].astype(F32) for term in lower).astype(BF16)
        meta = after(meta, piece)
        piece = spread_rows(piece)
        packet = ((chunk + 32, width), F32)
        last = pl.BlockSpec((SMALL, 3 * width), lambda i, m: (chunk // SMALL, 0))
        kept, near, far, small = simple(
            last_qkv_kernel,
            "last_qkv",
            [((chunk, width), F32), packet, packet, ((32, width), F32)],
            meta,
            *joined,
            qkv_send,
            joined[3],
            specs=[pl.BlockSpec((chunk, 3 * width), lambda i, m: (0, 0))] * 4 + [last] * 2,
        )
        near, far, diag = swap(near, "blk", 1), swap(far, "blk", 2), swap(small, "blk", 3)
        tok_args = (after(tok_own, small), e_own, e_near, e_far, cot_own)
        grad_tokens = finish(token_kernel, "token_grad", seq, *tok_args)
        meta = after(meta, grad_tokens)
        ends = [((width, hid // 2), F32), ((width // 2, width), F32)]
        down, out_w = simple(lower_kernel, "lower", ends, meta, piece)
        meta = after(meta, down)
        down = down.T
        qkv, gb_qkv, gb_out, gb_up, gb_down, *norms = assemble(
            meta, kept, small, near, far, diag
        )
        up[0] = after(up[0], qkv)
        up = sum(term[:chunk].astype(F32) for term in up)
    else:
        up = reduce_plain(up_keep, up_got, up_masks[1:])
        weights = reduce_plain(low_keep, low_got, low_masks[1:])
        qkv = reduce_plain(qkv_keep, qkv_got, up_masks[1:])
        piece = spread_rows(weights).T
        cut = 4 * hid // rows
        down, out_w = piece[:cut], piece[cut:]
        kept, near, far = split_columns(qkv)
        near, far = swap(near, "blk", 1), swap(far, "blk", 2)
        ends = [jnp.where(blk % 2 == 0, a, b) for a, b in ((kept, far), (far, kept))]
        qkv = jnp.concatenate([ends[0], near, ends[1]], axis=1)
        out_args = (tok_own, out_even, out_got, out_far, b_out, b_down)
        result = finish(result_kernel, "result", seq, *out_args)
        tok_args = (tok_own, e_own, e_near, e_far, cot_own)
        grad_tokens = finish(token_kernel, "token_grad", seq, *tok_args)
        third = 3 * width
        table = jnp.concatenate([small[0:8], small[8:16, : D - third]], axis=1)
        mine = (jnp.arange(4) == blk)[:, None]
        joined = lax.psum(jnp.where(mine, small[2:3], 0.0), ("rows", "blk"))
        gb_up = lax.psum(jnp.where(mine, table[4:5], 0.0), ("rows", "blk")).reshape(FF)
        gb_qkv = jnp.concatenate(
            [
                jnp.concatenate([joined[:, 0:128], joined[:, 256:320]], axis=1).reshape(D),
                jnp.concatenate([joined[:, 128:256], joined[:, 320:384]], axis=1).reshape(D),
                joined[:, 384:576].reshape(D),
            ]
        )
        gain_1, shift_1, _, _, _, gain_2, shift_2, gb_out = lax.psum(table, ("rows", "blk"))
        norms, gb_down = (gain_1, shift_1, gain_2, shift_2), gb_out
    return (
        result[None],
        grad_tokens[None],
        qkv,
        out_w,
        up,
        down,
        gb_qkv,
        gb_out,
        gb_up,
        gb_down,
        *norms,
    )


def solution(mesh):
    split = P("rows", "blk")
    in_specs = (
        P("rows", "blk", None),
        split,
        P("rows"),
        *(P(),) * 12,
        P("rows", "blk", None),
    )
    out_specs = (
        P("rows", "blk", None),
        P("rows", "blk", None),
        *(split,) * 4,
        *(P(),) * 8,
    )
    return jax.shard_map(local, mesh=mesh, in_specs=in_specs, out_specs=out_specs, check_vma=False)
```

```python
import math
from functools import partial

import jax
import jax.numpy as jnp
import numpy as np
from jax import lax
from jax.experimental import pallas as pl
from jax.experimental.pallas import tpu as pltpu
from jax.sharding import PartitionSpec as P

D = 768
HEADS = 12
HDIM = 64
ROT = 16
FF = 3072
EPS = 1e-05
MASKED = -1e30
TILE = 256
VROWS = 80
LN2 = math.log(2.0)
EXTRA = 16
LANES = 128
F32 = jnp.float32
BF16 = jnp.bfloat16
COST = pl.CostEstimate(flops=0, bytes_accessed=0, transcendentals=0)
NT_DIMS = (((1,), (1,)), ((), ()))
TN_DIMS = (((0,), (0,)), ((), ()))


def dot(left, right):
    return jnp.dot(left, right, preferred_element_type=F32)


def dot_nt(left, right):
    return lax.dot_general(left, right, NT_DIMS, preferred_element_type=F32)


def dot_tn(left, right):
    return lax.dot_general(left, right, TN_DIMS, preferred_element_type=F32)


def normalize(value):
    center = value - jnp.mean(value, axis=-1, keepdims=True)
    spread = jnp.mean(center * center, axis=-1, keepdims=True)
    return center * lax.rsqrt(spread + EPS)


def angle_parts(length):
    dim = np.arange(LANES) % HDIM
    inverse = np.where(dim < ROT, 10000.0 ** (-2.0 * (dim % (ROT // 2)) / ROT), 0.0)
    high = (np.arange(length // LANES) * LANES)[:, None] * inverse
    low = np.arange(LANES)[:, None] * inverse
    parts = np.stack([np.cos(low), np.sin(low)]), np.stack([np.cos(high), np.sin(high)])
    return tuple(jnp.asarray(part, F32) for part in parts)


def rotation(low_ref, high_ref, tile):
    lane = lax.broadcasted_iota(jnp.int32, (1, LANES), 1) % HDIM
    sign = jnp.where(lane < ROT // 2, -1.0, 1.0)
    cos_rows, sin_rows = [], []
    for part in range(TILE // LANES):
        row = tile * (TILE // LANES) + part
        cos_high = high_ref[0, pl.ds(row, 1), :]
        sin_high = high_ref[1, pl.ds(row, 1), :]
        cos_rows.append(low_ref[0] * cos_high - low_ref[1] * sin_high)
        sin_rows.append((low_ref[1] * cos_high + low_ref[0] * sin_high) * sign)
    return jnp.concatenate(cos_rows, axis=0), jnp.concatenate(sin_rows, axis=0)


def swap_halves(value):
    lane = lax.broadcasted_iota(jnp.int32, value.shape, 1) % HDIM
    half = ROT // 2
    return jnp.where(
        lane < half, pltpu.roll(value, LANES - half, 1), pltpu.roll(value, half, 1)
    )


def true_block(meta_ref, slot):
    return jnp.bitwise_xor(meta_ref[0], slot)


def params(*semantics, vmem=None):
    return pltpu.CompilerParams(
        dimension_semantics=semantics or ("arbitrary",), vmem_limit_bytes=vmem or 67_043_328
    )


def whole(shape):
    return pl.BlockSpec(shape, lambda *_: (0,) * len(shape))


def own_blocks(refs, odd, into):
    places = ((0, 256), (128, 320), (384, 512))
    for part, (pair_at, third_at) in enumerate(places):
        left, right = refs[2 * part], refs[2 * part + 1]

        @pl.when(odd == 0)
        def _(left=left, right=right, pair_at=pair_at, third_at=third_at):
            into[:, pair_at : pair_at + 128] = left[...]
            into[:, third_at : third_at + 64] = right[:, 0:64]

        @pl.when(odd == 1)
        def _(left=left, right=right, pair_at=pair_at, third_at=third_at):
            into[:, pair_at : pair_at + 128] = jnp.concatenate(
                [left[:, 64:128], right[:, 0:64]], axis=1
            )
            into[:, third_at : third_at + 64] = right[:, 64:128]


def row(ref):
    return ref[...].reshape(1, ref.shape[0])


def own_bias(b_ref, odd, blk, into):
    blocks = []
    for part in range(3):
        for side in range(2):
            at = pl.multiple_of((part * (D // LANES) + side + 3 * blk // 2) * LANES, LANES)
            blocks.append(b_ref[pl.ds(at, LANES)].reshape(1, LANES))
    own_blocks(blocks, odd, into)


def project_tile(normed, gain, shift, w_ref, b_ref, low, high, tile, q_ref, k_ref, v_ref):
    attn_in = (normed * row(gain) + row(shift)).astype(BF16)
    joined = dot(attn_in, w_ref[...]) + b_ref[...]
    cos, sin = rotation(low, high, tile)
    scale = HDIM**-0.5 / LN2

    def turn(block):
        return block * cos + swap_halves(block) * sin

    query = turn(joined[:, 0:128]) * scale
    keys = turn(joined[:, 128:256])
    mixed = turn(joined[:, 256:384])
    q_ref[:, 0:128] = query.astype(BF16)
    k_ref[:, 0:128] = keys.astype(BF16)
    q_ref[:, 128:192] = (mixed[:, 0:64] * scale).astype(BF16)
    k_ref[:, 128:192] = mixed[:, 64:128].astype(BF16)
    v_ref[...] = joined[:, 384:576].astype(BF16)


def find_starts(seq, meta, valid, pairs, start_ref, lo_ref, hi_ref):
    segs = [ref[at : at + 1, 0:seq].astype(F32) for ref in pairs for at in range(2)]
    below = [
        sum(jnp.sum((seg < number).astype(F32), axis=1, keepdims=True) for seg in segs)
        for number in (1, 2, 3)
    ]
    per = seq // TILE
    iota = lax.broadcasted_iota(jnp.int32, (1, seq), 1)
    for slot, seg in enumerate(segs):
        block = true_block(meta, slot)
        begin = jnp.zeros((1, seq), F32)
        for number in (1, 2, 3):
            begin = jnp.where(seg == number, below[number - 1], begin)
        pos = iota + block * seq
        begin = jnp.where(pos < valid[0], begin.astype(jnp.int32), pos)
        for part in range(per):
            tile = begin[:, part * TILE : (part + 1) * TILE]
            start_ref[slot * per + part] = tile
            lo_ref[block * per + part] = jnp.min(tile) // TILE
            hi_ref[block * per + part] = (jnp.max(tile) + (TILE - 1)) // TILE


def qkv_kernel(slot, meta, x_ref, gain, shift, low, high, w_ref, b_ref, *refs):
    per = pl.num_programs(0)
    tile = true_block(meta, slot) * per + pl.program_id(0)
    normed = normalize(x_ref[...].astype(F32))
    project_tile(normed, gain, shift, w_ref, b_ref, low, high, tile, *refs[3:])


def project(slot, meta, x, gain, shift, low, high, w, b, filled, seq):
    width = D // 4
    per = seq // TILE
    out = jax.ShapeDtypeStruct((4 * seq, width), BF16)
    out_spec = pl.BlockSpec((TILE, width), lambda i, m: (slot * per + i, 0))
    args = [x, gain, shift, low, high, w, b, *filled]
    specs = [pl.BlockSpec((TILE, D), lambda i, m: (i, 0))]
    specs += [whole(a.shape) for a in args[1:7]]
    specs += [pl.BlockSpec(memory_space=pl.ANY)] * 3
    return pl.pallas_call(
        partial(qkv_kernel, slot),
        out_shape=[out] * 3,
        grid_spec=pltpu.PrefetchScalarGridSpec(
            num_scalar_prefetch=1, grid=(per,), in_specs=specs, out_specs=[out_spec] * 3
        ),
        input_output_aliases={8 + i: i for i in range(3)},
        compiler_params=params(),
        cost_estimate=COST,
        name=f"qkv_{slot}",
    )(meta, *args)


def mask_order(rows, first):
    masks = [1 << bit for bit in range(rows.bit_length() - 1)]
    return masks if first == 1 else masks[1::-1] + masks[2:]


def places(masks):
    order = [0]
    for mask in reversed(masks):
        order = order + [mask + i for i in order]
    return order


def fits(rows):
    return rows == 8 and D // rows % 32 == 0


def store_chunks(load, keep, send, meta, rows, first):
    size = D // rows
    for index, place in enumerate(places(mask_order(rows, first))):
        at = pl.multiple_of(jnp.bitwise_xor(meta[1], place) * size, 32)
        into = keep if index < rows // 2 else send
        row_at = index % (rows // 2) * size
        into[row_at : row_at + size, :] = load(pl.ds(at, size)).astype(into.dtype)


def store_low(grad, keep, send, meta, rows):
    size, hid = D // 4, FF // 4
    for index, place in enumerate(places(mask_order(rows, 2))):
        chunk = jnp.bitwise_xor(meta[1], place)
        at = pl.ds(pl.multiple_of(chunk % 4 * size, 64), size)
        down = pl.multiple_of(hid + chunk // 4 * (hid // 2), LANES)
        out = pl.multiple_of(2 * hid + chunk // 4 * LANES, LANES)
        into = keep if index < rows // 2 else send
        row_at = slice(index % (rows // 2) * size, (index % (rows // 2) + 1) * size)
        into[row_at, : hid // 2] = grad[at, pl.ds(down, hid // 2)].astype(BF16)
        into[row_at, hid // 2 :] = grad[at, pl.ds(out, LANES)].astype(BF16)


def low_shapes(rows):
    if fits(rows):
        return [(D, FF // 8 + LANES)] * 2
    return [(D, FF // 4 + 2 * LANES), (8, LANES)]


def low_chunks(keep, send, rows):
    if fits(rows):
        return keep, send
    hid, width, count = FF // 4, D // 4, rows // 4
    parts = [
        part.reshape(4, width, count, part.shape[1] // count).transpose(2, 0, 1, 3)
        for part in (keep[:, :hid], keep[:, hid : hid + width])
    ]
    chunks = jnp.concatenate(parts, axis=3).reshape(rows, width, -1)
    order = jnp.array(places(mask_order(rows, 2))) ^ lax.axis_index("rows")
    chunks = jnp.take(chunks, order, axis=0).reshape(rows * width, -1)
    return chunks[: rows * width // 2], chunks[rows * width // 2 :]


def chunk_shapes(cols, rows, extra=0):
    if fits(rows):
        return [(D // 2 + extra, cols)] * 2
    return [(D, cols), (8, LANES)]


def chunks_of(keep, send, rows, first):
    if fits(rows):
        return keep, send
    order = jnp.array(places(mask_order(rows, first))) ^ lax.axis_index("rows")
    parts = keep.reshape(rows, D // rows, keep.shape[1])
    parts = jnp.take(parts, order, axis=0).reshape(keep.shape)
    return parts[: D // 2], parts[D // 2 :]


def feed(normed, upstream, gain, shift, w_up, b_up, w_down):
    mlp_in = (normed * row(gain) + row(shift)).astype(BF16)
    hidden = dot(mlp_in, w_up[...]) + b_up
    cdf = 0.5 * (1.0 + lax.erf(hidden * (0.5**0.5)))
    act = (hidden * cdf).astype(BF16)
    slope = cdf + hidden * jnp.exp(-0.5 * hidden * hidden) * ((2.0 * math.pi) ** -0.5)
    grad_low = (slope * dot_nt(upstream, w_down[...])).astype(BF16)
    grad_norm = dot_nt(grad_low, w_up[...])
    return mlp_in, act, grad_low, grad_norm


def add_sums(sums, grad_low, grad_norm, normed):
    sums[0:1, :] += jnp.sum(grad_low.astype(F32), axis=0, keepdims=True)
    sums[1:2, :] += jnp.sum(grad_norm * normed, axis=0, keepdims=True)
    sums[2:3, :] += jnp.sum(grad_norm, axis=0, keepdims=True)


def own_row(ref, blk, size):
    return ref[pl.ds(pl.multiple_of(blk * size, LANES), size)].reshape(1, size)


def mlp_first_kernel(
    half, meta, xa, xb, ca, cb, gain, shift, b_up, w_up, w_down, w_out,
    gain1, shift1, b_qkv, low, high, w0, w1, w2, w3, w4, w5,
    mo_ref, e_ref, n_ref, gv_ref, sums, gup, gdown, q_ref, k_ref, v_ref, w_own, b_own, x_s, c_s,
):
    step = pl.program_id(0)

    @pl.when(step < half)
    def _():
        x_s[...] = xa[...]
        c_s[...] = ca[...]

    @pl.when(step >= half)
    def _():
        x_s[...] = xb[...]
        c_s[...] = cb[...]

    @pl.when(step == 0)
    def _():
        sums[...] = jnp.zeros_like(sums)
        gup[...] = jnp.zeros_like(gup)
        gdown[...] = jnp.zeros_like(gdown)
        odd = meta[0] % 2
        own_blocks((w0, w1, w2, w3, w4, w5), odd, w_own)
        own_bias(b_qkv, odd, meta[0], b_own)

    upstream = c_s[...]

    @pl.when(step < half)
    def _():
        sums[3:4, :] += jnp.sum(upstream.astype(F32), axis=0, keepdims=True)

    normed = normalize(x_s[...].astype(F32))
    n_ref[...] = normed.astype(BF16)
    tile = true_block(meta, step // half) * half + step % half
    project_tile(normed, gain1, shift1, w_own, b_own, low, high, tile, q_ref, k_ref, v_ref)
    bias = own_row(b_up, meta[0], gup.shape[1])
    mlp_in, act, grad_low, grad_norm = feed(normed, upstream, gain, shift, w_up, bias, w_down)
    mo_ref[...] = dot(act, w_down[...]).astype(BF16)
    add_sums(sums, grad_low, grad_norm, normed)
    e_ref[...] = (grad_norm * row(gain)).astype(BF16)
    gv_ref[...] = dot_nt(upstream, w_out[...]).astype(BF16)
    gup[...] += dot_tn(mlp_in, grad_low)
    gdown[...] += dot_tn(upstream, act)


def mlp_second_kernel(
    half, rows, meta, xa, xb, ca, cb, gain, shift, b_up, w_up, w_down, w_out,
    c0, c1, mo_in, o_near, o_far, sums_in, gup, gdown, *refs
):
    e_ref, n_ref, gv_ref, sums, even, odd, up_keep, up_send, low_keep, low_send = refs[3:13]
    x_s, c_s, n_s, grad = refs[13:]
    step = pl.program_id(0)
    hid = gup.shape[1]

    @pl.when(step < half)
    def _():
        x_s[...] = xa[...]
        c_s[...] = ca[...]
        n_s[...] = c0[...]

    @pl.when(step >= half)
    def _():
        x_s[...] = xb[...]
        c_s[...] = cb[...]
        n_s[...] = c1[...]

    @pl.when(step == 0)
    def _():
        sums[...] = sums_in[...]
        grad[:, 0:hid] = gup[...]
        grad[:, hid : 2 * hid] = gdown[...]
        grad[:, 2 * hid :] = jnp.zeros_like(grad[:, 2 * hid :])

    upstream = c_s[...]
    normed = normalize(x_s[...].astype(F32))
    n_ref[...] = normed.astype(BF16)
    bias = own_row(b_up, meta[0], hid)
    mlp_in, act, grad_low, grad_norm = feed(normed, upstream, gain, shift, w_up, bias, w_down)
    add_sums(sums, grad_low, grad_norm, normed)
    e_ref[...] = (grad_norm * row(gain)).astype(BF16)
    gv_ref[...] = dot_nt(upstream, w_out[...]).astype(BF16)
    grad[:, 0:hid] += dot_tn(mlp_in, grad_low)
    grad[:, hid : 2 * hid] += dot_tn(upstream, act)
    out_grad = dot_tn(upstream, o_far[...]) + dot_tn(n_s[...], o_near[...])
    side = out_grad.shape[1] // 2
    if fits(rows):
        grad[:, 2 * hid : 2 * hid + side] += out_grad[:, :side]
        grad[:, 2 * hid + LANES : 2 * hid + LANES + side] += out_grad[:, side:]
    else:
        grad[:, 2 * hid : 2 * hid + 2 * side] += out_grad
    far = (dot(act, w_down[...]) + dot(o_far[...], w_out[...])).astype(BF16)
    near = (mo_in[...].astype(F32) + dot(o_near[...], w_out[...])).astype(BF16)

    @pl.when(step < half)
    def _():
        even[0] = near
        even[1] = far

    @pl.when(step >= half)
    def _():
        odd[0] = near
        odd[1] = far

    @pl.when(step == pl.num_programs(0) - 1)
    def _():
        if fits(rows):
            store_chunks(lambda at: grad[at, 0:hid], up_keep, up_send, meta, rows, 1)
            store_low(grad, low_keep, low_send, meta, rows)
        else:
            up_keep[...] = grad[:, 0:hid].astype(BF16)
            low_keep[...] = grad[:, hid:].astype(BF16)


def feed_forward(
    meta, xs, cs, gain, shift, b_up, w_up, w_down, w_out, rows, seq,
    joined=None, before=None, near=None, attn=None,
):
    per = seq // TILE
    steps = 2 * per
    hid = FF // 4
    width = D // 4
    total = 4 * seq
    first = pl.BlockSpec((TILE, D), lambda i, m: (jnp.minimum(i, per - 1), 0))
    second = pl.BlockSpec((TILE, D), lambda i, m: (jnp.maximum(i - per, 0), 0))
    specs = [
        first,
        second,
        first,
        second,
        whole((D,)),
        whole((D,)),
        whole((FF,)),
        pl.BlockSpec((D, hid), lambda i, m: (0, m[0])),
        pl.BlockSpec((hid, D), lambda i, m: (m[0], 0)),
        pl.BlockSpec((width, D), lambda i, m: (m[0], 0)),
    ]
    args = [*xs, *cs, gain, shift, b_up, w_up, w_down, w_out]
    tile = pl.BlockSpec((TILE, D), lambda i, m: (i, 0))
    narrow = pl.BlockSpec((TILE, width), lambda i, m: (i, 0))
    sums = (8, D)
    scratch = [pltpu.VMEM((TILE, D), BF16), pltpu.VMEM((TILE, D), BF16)]
    pair = jax.ShapeDtypeStruct((steps * TILE, D), BF16)
    full = jax.ShapeDtypeStruct((total, D), BF16)
    vec = jax.ShapeDtypeStruct((total, width), BF16)
    if before is None:
        body = partial(mlp_first_kernel, per)
        gain1, shift1, w_qkv, b_qkv, low, high = joined
        args += [gain1, shift1, b_qkv, low, high]
        specs += [whole(a.shape) for a in args[-5:]]
        for part in range(3):
            for side in range(2):
                specs.append(
                    pl.BlockSpec(
                        (D, LANES),
                        lambda i, m, at=part * D // LANES + side: (0, at + 3 * m[0] // 2),
                    )
                )
                args.append(w_qkv)
        outs = [pair, full, full, vec, jax.ShapeDtypeStruct(sums, F32)]
        outs += [jax.ShapeDtypeStruct((D, hid), F32)] * 2 + [vec] * 3
        outs += [
            jax.ShapeDtypeStruct((D, 3 * width), BF16),
            jax.ShapeDtypeStruct((1, 3 * width), F32),
        ]
        out_specs = [tile, tile, tile, narrow, whole(sums)]
        out_specs += [whole((D, hid))] * 2 + [narrow] * 3
        out_specs += [whole((D, 3 * width)), whole((1, 3 * width))]
        aliases = {}
    else:
        body = partial(mlp_second_kernel, per, rows)
        mlp_out, norm_part, normed, grad_vec, sums_in, gup, gdown = before
        chunks = chunk_shapes(hid, rows) + low_shapes(rows)
        args += [*near, mlp_out, attn, attn, sums_in, gup, gdown, norm_part, normed, grad_vec]
        specs += [
            first,
            second,
            tile,
            narrow,
            pl.BlockSpec((TILE, width), lambda i, m: (i + steps, 0)),
            whole(sums),
            whole((D, hid)),
            whole((D, hid)),
            *(pl.BlockSpec(memory_space=pl.ANY),) * 3,
        ]
        aliases = {len(args) - 2 + i: i for i in range(3)}
        both = jax.ShapeDtypeStruct((2, seq, D), BF16)
        outs = [full, full, vec, jax.ShapeDtypeStruct(sums, F32), both, both]
        late = pl.BlockSpec((TILE, D), lambda i, m: (i + steps, 0))
        outs += [jax.ShapeDtypeStruct(shape, BF16) for shape in chunks]
        out_specs = [
            late,
            late,
            pl.BlockSpec((TILE, width), lambda i, m: (i + steps, 0)),
            whole(sums),
            pl.BlockSpec((2, TILE, D), lambda i, m: (0, jnp.minimum(i, per - 1), 0)),
            pl.BlockSpec((2, TILE, D), lambda i, m: (0, jnp.maximum(i - per, 0), 0)),
            *(whole(shape) for shape in chunks),
        ]
        scratch += [pltpu.VMEM((TILE, D), BF16), pltpu.VMEM((D, 2 * hid + 2 * LANES), F32)]
    return pl.pallas_call(
        body,
        out_shape=outs,
        grid_spec=pltpu.PrefetchScalarGridSpec(
            num_scalar_prefetch=1,
            grid=(steps,),
            in_specs=specs,
            out_specs=out_specs,
            scratch_shapes=scratch,
        ),
        input_output_aliases=aliases,
        compiler_params=params(),
        cost_estimate=COST,
        name="mlp_first" if before is None else "mlp_second",
    )(meta, *args)


def head_masks():
    lane = lax.broadcasted_iota(jnp.int32, (1, LANES), 1)
    first = jnp.where(lane < HDIM, 1.0, 0.0).astype(BF16)
    second = jnp.where(lane < HDIM, 0.0, 1.0).astype(BF16)
    return first, second


def slot_rows(meta, per, tile):
    slot = jnp.bitwise_xor(tile // per, meta[0])
    return pl.multiple_of((slot * per + tile % per) * TILE, TILE)


def by_head(first, second, block, third):
    return (block * first, block * second, third)


def transpose_all(from_ref, to_ref):
    @pl.loop(0, from_ref.shape[0] // TILE)
    def _(tile):
        rows = pl.ds(pl.multiple_of(tile * TILE, TILE), TILE)
        to_ref[:, rows] = from_ref[rows, :].astype(F32).T.astype(BF16)


def attend_kernel(
    per, meta, valid, q_ref, k_ref, v_ref, pair_own, pair_far,
    o_ref, lse_ref, starts_ref, lo, hi, vt_ref, acc, s_ref,
):
    mask0, mask1 = head_masks()
    tiles = k_ref.shape[0] // TILE
    qi = pl.program_id(0)

    @pl.when(qi == 0)
    def _():
        find_starts(per * TILE, meta, valid, (pair_own, pair_far), starts_ref, lo, hi)
        ones = jnp.where(lax.broadcasted_iota(jnp.int32, (VROWS - HDIM, TILE), 0) == 0, 1.0, 0.0)

        @pl.loop(0, tiles)
        def _(tile):
            rows = pl.ds(pl.multiple_of(tile * TILE, TILE), TILE)
            block = v_ref[rows, :].astype(F32).T
            for head in range(3):
                at = head * VROWS
                vt_ref[at : at + HDIM, rows] = block[head * HDIM : (head + 1) * HDIM].astype(BF16)
                vt_ref[at + HDIM : at + VROWS, rows] = ones.astype(BF16)

    key_iota = lax.broadcasted_iota(jnp.int32, (TILE, TILE), 0)
    query_iota = lax.broadcasted_iota(jnp.int32, (TILE, TILE), 1)
    queries = by_head(mask0, mask1, q_ref[:, 0:128], q_ref[:, 128:192])
    starts = starts_ref[jnp.bitwise_xor(qi // per, meta[0]) * per + qi % per]
    acc[...] = jnp.zeros_like(acc)

    def key_tile(turn):
        return jnp.where(turn == 0, qi, first + turn - 1)

    def score(masked, ki):
        k_rows = pl.ds(slot_rows(meta, per, ki), TILE)
        pair, third = k_ref[k_rows, 0:128], k_ref[k_rows, 128:192]
        scores = [dot_nt(third if head == 2 else pair, queries[head]) for head in range(3)]
        if masked:
            allowed = (key_iota >= starts - ki * TILE) & (key_iota <= query_iota + (qi - ki) * TILE)
            scores = [jnp.where(allowed, x, MASKED) for x in scores]
        return scores, [jnp.max(x, axis=0, keepdims=True) for x in scores]

    def value(ki, tops, peaks):
        k_rows = pl.ds(slot_rows(meta, per, ki), TILE)
        news = [jnp.maximum(top, peak) for top, peak in zip(tops, peaks)]
        fades = [jnp.exp2(top - new) for top, new in zip(tops, news)]
        weights = [jnp.exp2(s_ref[head] - news[head]).astype(BF16) for head in range(3)]
        terms = [
            dot(vt_ref[head * VROWS : (head + 1) * VROWS, k_rows], weights[head]) for head in range(3)
        ]
        return news, fades, terms

    def put(fades, terms):
        for head in range(3):
            cols = slice(head * VROWS, (head + 1) * VROWS)
            acc[cols, :] = acc[cols, :] * fades[head] + terms[head]

    def visit(masked, turn, carry):
        tops, peaks = carry
        scores, next_peaks = score(masked, key_tile(turn + 1))
        news, fades, terms = value(key_tile(turn), tops, peaks)
        peaks = next_peaks
        for head in range(3):
            s_ref[head] = scores[head]
        put(fades, terms)
        return tuple(news), tuple(peaks)

    first = lo[qi]
    full = jnp.minimum(hi[qi], qi)
    scores, peaks = score(True, qi)
    for head in range(3):
        s_ref[head] = scores[head]
    carry = ((jnp.full((1, TILE), MASKED, F32),) * 3, tuple(peaks))
    carry = lax.fori_loop(0, full - first, partial(visit, True), carry)
    carry = lax.fori_loop(full - first, qi - first, partial(visit, False), carry)
    tops, fades, terms = value(key_tile(qi - first), *carry)
    put(fades, terms)
    heads = []
    for head, top in enumerate(tops):
        at = head * VROWS
        total = acc[at + HDIM : at + HDIM + 1, :]
        heads.append(acc[at : at + HDIM, :] / total)
        lse_ref[head, 0] = top + jnp.log2(total)
    o_ref[...] = jnp.concatenate(heads, axis=0).T.astype(BF16)

def attend(meta, valid_len, query, keys, values, seg_pair, cot_far, per):
    total, width = query.shape
    tiles = total // TILE

    def slot(i, m):
        return jnp.bitwise_xor(i // per, m[0]) * per + i % per

    q_spec = pl.BlockSpec((TILE, width), lambda i, m, v: (slot(i, m), 0))
    lse_spec = pl.BlockSpec((3, 1, 1, TILE), lambda i, m, v: (0, slot(i, m), 0, 0))
    far_spec = pl.BlockSpec((EXTRA, D), lambda i, m, v: (per * TILE // EXTRA, 0))
    smem = pl.BlockSpec(memory_space=pltpu.SMEM)
    return pl.pallas_call(
        partial(attend_kernel, per),
        out_shape=[
            jax.ShapeDtypeStruct((total, width), BF16),
            jax.ShapeDtypeStruct((3, tiles, 1, TILE), F32),
            jax.ShapeDtypeStruct((tiles, 1, TILE), jnp.int32),
            jax.ShapeDtypeStruct((tiles,), jnp.int32),
            jax.ShapeDtypeStruct((tiles,), jnp.int32),
        ],
        grid_spec=pltpu.PrefetchScalarGridSpec(
            num_scalar_prefetch=2,
            grid=(tiles,),
            in_specs=[
                q_spec,
                whole(keys.shape),
                whole(values.shape),
                whole(seg_pair.shape),
                far_spec,
            ],
            out_specs=[q_spec, lse_spec, whole((tiles, 1, TILE)), smem, smem],
            scratch_shapes=[
                pltpu.VMEM((3 * VROWS, total), BF16),
                pltpu.VMEM((3 * VROWS, TILE), F32),
                pltpu.VMEM((3, TILE, TILE), F32),
            ],
        ),
        compiler_params=params(),
        cost_estimate=COST,
        name="attend",
    )(meta, valid_len, query, keys, values, seg_pair, cot_far)


def attend_back_kernel(
    per, meta, lo, hi, q_ref, k_ref, v_ref, o_ref, gv_ref, start_ref, lse_ref, low, high,
    gj_ref, kt_ref, dk_ref, dv_ref, dqt_ref
):
    mask0, mask1 = head_masks()
    tiles = k_ref.shape[0] // TILE
    qi = tiles - 1 - pl.program_id(0)

    @pl.when(pl.program_id(0) == 0)
    def _():
        transpose_all(k_ref, kt_ref)

    own_rows = pl.ds(slot_rows(meta, per, qi), TILE)
    key_iota = lax.broadcasted_iota(jnp.int32, (TILE, TILE), 0)
    query_iota = lax.broadcasted_iota(jnp.int32, (TILE, TILE), 1)
    queries = by_head(mask0, mask1, q_ref[:, 0:128], q_ref[:, 128:192])
    grads = by_head(mask0, mask1, gv_ref[:, 0:128], gv_ref[:, 128:192])
    starts = start_ref[0]
    lses = [lse_ref[head, 0] for head in range(3)]
    product = (gv_ref[...].astype(F32) * o_ref[...].astype(F32)).T
    deltas = [
        jnp.sum(product[head * HDIM : (head + 1) * HDIM], axis=0, keepdims=True)
        for head in range(3)
    ]
    dqt_ref[...] = jnp.zeros_like(dqt_ref)

    @pl.when(pl.program_id(0) == 0)
    def _():
        dk_ref[...] = jnp.zeros_like(dk_ref)
        dv_ref[...] = jnp.zeros_like(dv_ref)

    def load(ki):
        k_rows = pl.ds(slot_rows(meta, per, ki), TILE)
        return k_rows

    def score(masked, ki):
        k_rows = load(ki)
        pair, third = k_ref[k_rows, 0:128], k_ref[k_rows, 128:192]
        v_pair, v_third = v_ref[k_rows, 0:128], v_ref[k_rows, 128:192]
        scores = [dot_nt(third if head == 2 else pair, queries[head]) for head in range(3)]
        grad_probs = [dot_nt(v_third if head == 2 else v_pair, grads[head]) for head in range(3)]
        if masked:
            allowed = (key_iota >= starts - ki * TILE) & (key_iota <= query_iota + (qi - ki) * TILE)
            scores = [jnp.where(allowed, x, MASKED) for x in scores]
        return scores, grad_probs

    def terms(ki, scores, grad_probs):
        k_rows = load(ki)
        probs = [jnp.exp2(x - lse) for x, lse in zip(scores, lses)]
        grad_scores = [
            (p * (g - delta)).astype(BF16) for p, g, delta in zip(probs, grad_probs, deltas)
        ]
        dv = [dot(p.astype(BF16), g) for p, g in zip(probs, grads)]
        dk = [dot(g, q) for g, q in zip(grad_scores, queries)]
        dq = [
            dot(kt_ref[head * HDIM : (head + 1) * HDIM, k_rows], grad_scores[head])
            for head in range(3)
        ]
        return dk, dv, dq

    def add(ki, dk, dv, dq):
        k_rows = load(ki)
        for into, parts in ((dk_ref, dk), (dv_ref, dv)):
            into[k_rows, 0:128] += parts[0] + parts[1]
            into[k_rows, 128:192] += parts[2]
        for head in range(3):
            dqt_ref[head * HDIM : (head + 1) * HDIM, :] += dq[head]

    first = lo[qi]
    full = jnp.minimum(hi[qi], qi)

    def visit(masked, ki):
        add(ki, *terms(ki, *score(masked, ki)))

    @pl.loop(first, full)
    def _(ki):
        visit(True, ki)

    @pl.loop(full, qi)
    def _(ki):
        visit(False, ki)

    visit(True, qi)

    cos, sin = rotation(low, high, qi)

    def turn_back(block):
        return block * cos - swap_halves(block) * sin

    dq = dqt_ref[...].T * (HDIM**-0.5)
    dk = dk_ref[own_rows, :] * LN2
    gj_ref[:, 0:128] = turn_back(dq[:, 0:128]).astype(BF16)
    gj_ref[:, 128:256] = turn_back(dk[:, 0:128]).astype(BF16)
    mixed = jnp.concatenate([dq[:, 128:192], dk[:, 128:192]], axis=1)
    gj_ref[:, 256:384] = turn_back(mixed).astype(BF16)
    gj_ref[:, 384:576] = dv_ref[own_rows, :].astype(BF16)


def attend_back(
    meta, lo, hi, query, keys, values, attn, grad_vec, starts, lse, low, high, per
):
    total, width = query.shape
    tiles = total // TILE

    def slot(i, m):
        tile = tiles - 1 - i
        return jnp.bitwise_xor(tile // per, m[0]) * per + tile % per

    q_spec = pl.BlockSpec((TILE, width), lambda i, m, lo, hi: (slot(i, m), 0))
    gj_spec = pl.BlockSpec((TILE, 3 * width), lambda i, m, lo, hi: (slot(i, m), 0))
    start_spec = pl.BlockSpec((1, 1, TILE), lambda i, m, lo, hi: (slot(i, m), 0, 0))
    lse_spec = pl.BlockSpec((3, 1, 1, TILE), lambda i, m, lo, hi: (0, slot(i, m), 0, 0))
    return pl.pallas_call(
        partial(attend_back_kernel, per),
        out_shape=jax.ShapeDtypeStruct((total, 3 * width), BF16),
        grid_spec=pltpu.PrefetchScalarGridSpec(
            num_scalar_prefetch=3,
            grid=(tiles,),
            in_specs=[
                q_spec,
                whole(keys.shape),
                whole(values.shape),
                q_spec,
                q_spec,
                start_spec,
                lse_spec,
                whole(low.shape),
                whole(high.shape),
            ],
            out_specs=gj_spec,
            scratch_shapes=[
                pltpu.VMEM((width, total), BF16),
                pltpu.VMEM((total, width), F32),
                pltpu.VMEM((total, width), F32),
                pltpu.VMEM((width, TILE), F32),
            ],
        ),
        compiler_params=params(),
        cost_estimate=COST,
        name="attend_back",
    )(meta, lo, hi, query, keys, values, attn, grad_vec, starts, lse, low, high)


SMALL = 16


def pack_small(gain_sum, shift_sum, bias, mlp_sums):
    third = 3 * D // 4
    which = lax.broadcasted_iota(jnp.int32, (8, D), 0)
    table = jnp.concatenate([jnp.zeros((4, D), F32), mlp_sums[0:4]], axis=0)
    table = jnp.where(which == 0, gain_sum, jnp.where(which == 1, shift_sum, table))
    head = jnp.where(which[:, :third] == 2, bias, table[:, :third])
    tail = jnp.concatenate([table[:, third:], jnp.zeros((8, 2 * third - D), F32)], axis=1)
    return jnp.concatenate([head, tail], axis=0)


def high_low(value):
    high = value.astype(BF16)
    return high, (value - high.astype(F32)).astype(BF16)


def weight_kernel(rows, meta, *refs):
    gj_ref, n_ref, gain, shift, w_ref, mlp_sums, keep, send, small, grad, bias = refs
    step = pl.program_id(0)

    @pl.when(step == 0)
    def _():
        grad[...] = jnp.zeros_like(grad)
        bias[...] = jnp.zeros_like(bias)

    joined = gj_ref[...]
    bias[0:1, :] += jnp.sum(joined.astype(F32), axis=0, keepdims=True)
    grad[...] += dot_tn(n_ref[...], joined)

    @pl.when(step == pl.num_programs(0) - 1)
    def _():
        total = bias[0:1, :]
        width = total.shape[1]
        parts = jnp.concatenate(
            [*high_low(jnp.broadcast_to(total, (8, width)))], axis=0
        )
        shift_sum = dot_nt(parts, w_ref[...])
        shift_sum = shift_sum[0:1] + shift_sum[8:9]
        ones = jnp.ones((16, width), BF16)
        high, low = high_low(grad[...] * w_ref[...].astype(F32))
        gain_sum = (dot_nt(ones, high) + dot_nt(ones, low))[0:1]
        columns = jnp.concatenate(
            [jnp.broadcast_to(row(gain), (8, D)), jnp.broadcast_to(row(shift), (8, D))], axis=0
        ).T
        grad[...] = grad[...] * columns[:, 0:1] + columns[:, 8:9] * total
        rest = pack_small(gain_sum, shift_sum, total, mlp_sums[...])
        small[...] = rest
        if fits(rows):
            store_chunks(lambda at: grad[at, :], keep, send, meta, rows, 1)
            keep[D // 2 :, :] = rest.astype(BF16)
            send[D // 2 :, :] = rest.astype(BF16)
        else:
            keep[...] = grad[...].astype(BF16)


def row_tiles(cols, tile=TILE):
    return pl.BlockSpec((tile, cols), lambda i, m: (i, 0))


def joined_weight(meta, grad, normed, gain, shift, w, mlp_sums, rows):
    total, width = grad.shape
    tile = 2 * TILE
    chunks = chunk_shapes(width, rows, SMALL)
    args = [gain, shift, w, mlp_sums]
    return pl.pallas_call(
        partial(weight_kernel, rows),
        out_shape=[jax.ShapeDtypeStruct(shape, BF16) for shape in chunks]
        + [jax.ShapeDtypeStruct((SMALL, width), F32)],
        grid_spec=pltpu.PrefetchScalarGridSpec(
            num_scalar_prefetch=1,
            grid=(total // tile,),
            in_specs=[row_tiles(width, tile), row_tiles(D, tile), *(whole(a.shape) for a in args)],
            out_specs=[*(whole(shape) for shape in chunks), whole((SMALL, width))],
            scratch_shapes=[pltpu.VMEM((D, width), F32), pltpu.VMEM((8, width), F32)],
        ),
        compiler_params=params(),
        cost_estimate=COST,
        name="joined_weight",
    )(meta, grad, normed, *args)


def norm_kernel(meta, *refs):
    gjs, es, (gain, w_ref), outs = refs[0:4], refs[4:8], refs[8:10], refs[10:]
    for gj_ref, e_in, out in zip(gjs, es, outs):
        grad_norm = dot_nt(gj_ref[...], w_ref[...])
        out[...] = (grad_norm * row(gain) + e_in[...].astype(F32)).astype(BF16)


def norm_grad(meta, grad, e_mlp, gain, w, seq):
    tile = TILE
    per = seq // tile

    def slot_tiles(slot, cols):
        return pl.BlockSpec((tile, cols), lambda i, m: (slot * per + i, 0))

    return pl.pallas_call(
        norm_kernel,
        out_shape=[jax.ShapeDtypeStruct((seq, D), BF16)] * 4,
        grid_spec=pltpu.PrefetchScalarGridSpec(
            num_scalar_prefetch=1,
            grid=(per,),
            in_specs=[
                *(slot_tiles(slot, grad.shape[1]) for slot in range(4)),
                *(slot_tiles(slot, D) for slot in range(4)),
                whole(gain.shape),
                whole(w.shape),
            ],
            out_specs=[slot_tiles(0, D)] * 4,
        ),
        compiler_params=params(),
        cost_estimate=COST,
        name="norm_grad",
    )(meta, *[grad] * 4, *[e_mlp] * 4, gain, w)


def simple(body, name, shapes, *args, specs=None):
    return pl.pallas_call(
        body,
        out_shape=[jax.ShapeDtypeStruct(shape, kind) for shape, kind in shapes],
        grid_spec=pltpu.PrefetchScalarGridSpec(
            num_scalar_prefetch=1,
            grid=(1,),
            in_specs=specs or [whole(a.shape) for a in args[1:]],
            out_specs=[whole(shape) for shape, _ in shapes],
        ),
        compiler_params=params(),
        cost_estimate=COST,
        name=name,
    )(*args)


def add_up(refs):
    total = refs[0][...].astype(F32)
    for ref in refs[1:]:
        total += ref[...].astype(F32)
    return total


def sums_kernel(counts, meta, *refs):
    ins, outs = refs[: sum(counts)], refs[sum(counts) :]
    for count, out in zip(counts, outs):
        out[...] = add_up(ins[:count]).astype(BF16)
        ins = ins[count:]


def block_sums(name, meta, steps, *jobs):
    specs, args, outs, out_specs = [], [], [], []
    for rows, terms in jobs:
        size, cols = rows // steps, terms[0][0].shape[1]
        for array, at in terms:
            specs.append(pl.BlockSpec((size, cols), lambda i, m, at=at // size: (at + i, 0)))
            args.append(array)
        outs.append(jax.ShapeDtypeStruct((rows, cols), BF16))
        out_specs.append(pl.BlockSpec((size, cols), lambda i, m: (i, 0)))
    return pl.pallas_call(
        partial(sums_kernel, [len(terms) for _, terms in jobs]),
        out_shape=outs,
        grid_spec=pltpu.PrefetchScalarGridSpec(
            num_scalar_prefetch=1, grid=(steps,), in_specs=specs, out_specs=out_specs
        ),
        compiler_params=params(),
        cost_estimate=COST,
        name=name,
    )(meta, *args)


def lower_kernel(meta, piece, down_ref, out_ref):
    cut = down_ref.shape[1]
    down_ref[...] = piece[:, :cut].astype(F32)
    out_ref[...] = piece[:, cut:].astype(F32).T[: out_ref.shape[0]]


def last_qkv_kernel(meta, *refs):
    *terms, sums, got_sums, kept, near, far, small = refs
    size = kept.shape[0]
    width = kept.shape[1]
    total = add_up(terms)
    rows = sums[...].astype(F32) + got_sums[...].astype(F32)
    for part in range(3):
        small[part * 8 : part * 8 + 8, :] = rows[0:8, part * width : (part + 1) * width]
    small[24:32, :] = rows[8:16, 0:width]
    near[size:, :] = small[...]
    far[size:, :] = small[...]
    query = jnp.concatenate([total[:, 0:128], total[:, 256:320]], axis=1)
    keys = jnp.concatenate([total[:, 128:256], total[:, 320:384]], axis=1)
    values = total[:, 384:576]
    plans = (
        (query, keys, values),
        (keys, query, values),
        (keys, values, query),
        (values, keys, query),
    )
    for blk, plan in enumerate(plans):

        @pl.when(meta[0] == blk)
        def _(plan=plan):
            kept[...] = plan[0]
            near[0:size, :] = plan[1]
            far[0:size, :] = plan[2]


def assemble_kernel(
    meta, kept, small, near, far, diag,
    qkv, b_qkv, b_out, b_up, b_down, gain1, shift1, gain2, shift2, table,
):
    size, width = kept.shape

    @pl.when(meta[0] % 2 == 0)
    def _():
        qkv[:, 0:width] = kept[...]
        qkv[:, 2 * width :] = far[0:size, :]

    @pl.when(meta[0] % 2 == 1)
    def _():
        qkv[:, 0:width] = far[0:size, :]
        qkv[:, 2 * width :] = kept[...]

    qkv[:, width : 2 * width] = near[0:size, :]
    table[0] = small[...]
    table[1] = near[size:, :]
    table[2] = far[size:, :]
    table[3] = diag[...]
    blocks = [table[jnp.bitwise_xor(meta[0], blk)] for blk in range(4)]
    total = blocks[0] + blocks[1] + blocks[2] + blocks[3]

    def vector(rows, index):
        parts = [rows[part * 8 + index : part * 8 + index + 1, :] for part in range(4)]
        return jnp.concatenate(parts, axis=1)

    for ref, index in ((gain1, 0), (shift1, 1), (gain2, 5), (shift2, 6), (b_out, 7), (b_down, 7)):
        ref[...] = vector(total, index).reshape(D)
    ups, parts = [], ([], [], [])
    for rows in blocks:
        ups.append(vector(rows, 4))
        joined = vector(rows, 2)
        parts[0].append(jnp.concatenate([joined[:, 0:128], joined[:, 256:320]], axis=1))
        parts[1].append(jnp.concatenate([joined[:, 128:256], joined[:, 320:384]], axis=1))
        parts[2].append(joined[:, 384:576])
    b_up[...] = jnp.concatenate(ups, axis=1).reshape(4 * D)
    b_qkv[...] = jnp.concatenate(parts[0] + parts[1] + parts[2], axis=1).reshape(3 * D)


def assemble(meta, kept, small, near, far, diag):
    size, width = kept.shape
    shapes = [((size, 3 * width), F32), ((3 * D,), F32), ((D,), F32), ((4 * D,), F32)]
    shapes += [((D,), F32)] * 5
    args = (kept, small, near, far, diag)
    return pl.pallas_call(
        assemble_kernel,
        out_shape=[jax.ShapeDtypeStruct(shape, kind) for shape, kind in shapes],
        grid_spec=pltpu.PrefetchScalarGridSpec(
            num_scalar_prefetch=1,
            grid=(1,),
            in_specs=[whole(a.shape) for a in args],
            out_specs=[whole(shape) for shape, _ in shapes],
            scratch_shapes=[pltpu.VMEM((4, 32, width), F32)],
        ),
        compiler_params=params(),
        cost_estimate=COST,
        name="assemble",
    )(meta, *args)


def next_send(terms, size):
    return sum(term[size // 2 : size].astype(F32) for term in terms).astype(BF16)


def reduce_plain(keep, got, masks):
    terms, size = [keep, got], keep.shape[0]
    for mask in masks:
        terms.append(swap(next_send(terms, size), "rows", mask))
        size //= 2
    return sum(term[:size].astype(F32) for term in terms)


def after(value, *others):
    return lax.optimization_barrier((value, others))[0]


def swap(value, axis, mask):
    size = lax.axis_size(axis)
    return lax.ppermute(value, axis, [(i, i ^ mask) for i in range(size)])


def add_low(left, right):
    return (left.astype(F32) + right.astype(F32)).astype(BF16)


def spread_rows(chunk):
    rows = lax.axis_size("rows")
    moves = [
        (r * 4 + b, (rows // 4 * b + r // 4) * 4 + r % 4) for r in range(rows) for b in range(4)
    ]
    return lax.ppermute(chunk, ("rows", "blk"), moves)


def split_columns(chunk):
    b = lax.axis_index("blk")
    q = jnp.concatenate([chunk[:, 0:128], chunk[:, 256:320]], axis=1)
    k = jnp.concatenate([chunk[:, 128:256], chunk[:, 320:384]], axis=1)
    v = chunk[:, 384:576]

    def choose(zero, one, two, three):
        return jnp.where(b < 2, jnp.where(b == 0, zero, one), jnp.where(b == 2, two, three))

    return choose(q, k, k, v), choose(k, q, v, k), choose(v, v, q, q)


def result_kernel(x_ref, even, near, far, b_out, b_down, out_ref):
    bias = row(b_out) + row(b_down)
    total = even[0].astype(F32) + near[0].astype(F32) + far[...].astype(F32)
    out_ref[...] = (x_ref[...].astype(F32) + bias + total).astype(BF16)


def token_kernel(x_ref, even, near, far, c_ref, out_ref):
    wide = x_ref[...].astype(F32)
    center = wide - jnp.mean(wide, axis=-1, keepdims=True)
    rate = lax.rsqrt(jnp.mean(center * center, axis=-1, keepdims=True) + EPS)
    normed = center * rate
    grad = even[...].astype(F32) + near[...].astype(F32) + far[...].astype(F32)
    mean = jnp.mean(grad, axis=-1, keepdims=True)
    along = jnp.mean(grad * normed, axis=-1, keepdims=True)
    back = rate * (grad - mean - normed * along)
    out_ref[...] = (c_ref[...].astype(F32) + back).astype(BF16)


def finish(body, name, seq, x, even, near, far, *more):
    flat = pl.BlockSpec((TILE, D), lambda i: (i, 0))
    own = pl.BlockSpec((1, TILE, D), lambda i: (0, i, 0))
    return pl.pallas_call(
        body,
        out_shape=jax.ShapeDtypeStruct((seq, D), BF16),
        grid=(seq // TILE,),
        in_specs=[
            *(own if a.ndim == 3 else flat for a in (x, even, near, far)),
            *(flat if a.ndim == 2 else whole(a.shape) for a in more),
        ],
        out_specs=flat,
        compiler_params=params(),
        cost_estimate=COST,
        name=name,
    )(x, even, near, far, *more)


def local(
    tokens, seg_ids, valid_len, ln1_gain, ln1_bias, w_qkv, b_qkv, w_out, b_out,
    ln2_gain, ln2_bias, w_up, b_up, w_down, b_down, cotangent,
):
    rows = lax.axis_size("rows")
    blk = lax.axis_index("blk")
    seq = tokens.shape[1]
    per = seq // TILE
    width = D // 4
    hid = FF // 4
    low, high = angle_parts(4 * seq)
    tok_own, cot_own = tokens[0], cotangent[0]

    cot_near = swap(cot_own, "blk", 1)
    tok_far = swap(tok_own, "blk", 2)
    tok_near = swap(tok_own, "blk", 1)
    seg_own = seg_ids.astype(BF16)
    seg_pair = jnp.concatenate([seg_own, swap(seg_own, "blk", 1)])
    seg_pair = jnp.pad(seg_pair, ((0, EXTRA - 2), (0, D - seq)))
    cot_long = jnp.concatenate([cot_own, seg_pair])
    cot_far = swap(cot_long, "blk", 2)

    meta = jnp.stack([blk, lax.axis_index("rows")]).astype(jnp.int32)
    mlp_args = (ln2_gain, ln2_bias, b_up, w_up, w_down, w_out, rows, seq)
    joined = (ln1_gain, ln1_bias, w_qkv, b_qkv, low, high)
    *first, query, keys, values, w_own, b_own = feed_forward(
        meta, (tok_own, tok_near), (cot_own, cot_near), *mlp_args, joined
    )
    meta = after(meta, b_own)

    def more(slot, m, tok, filled):
        args = (ln1_gain, ln1_bias, low, high, w_own, b_own, filled, seq)
        return project(slot, m, tok, *args)

    tok_last = swap(after(tok_far, b_own), "blk", 1)
    joined = more(2, meta, tok_far, (query, keys, values))
    query, keys, values = more(3, after(meta, joined[0]), tok_last, joined)
    cot_last = swap(after(cot_far, query), "blk", 1)
    cots = (cot_own, cot_near, cot_far, cot_last)
    attn, lse, starts, lo, hi = attend(
        meta, valid_len, query, keys, values, seg_pair, cot_far, per
    )

    meta = after(meta, lse)
    e_mlp, normed, grad_vec, mlp_sums, out_even, out_odd, *packets = feed_forward(
        meta, (tok_far, tok_last), cots[2:], *mlp_args, before=first, near=cots[:2], attn=attn
    )
    up_keep, up_send = chunks_of(*packets[:2], rows, 1)
    low_keep, low_send = low_chunks(*packets[2:], rows)
    up_masks, low_masks = mask_order(rows, 1), mask_order(rows, 2)
    out_got = swap(out_odd, "blk", 1)
    up_got = swap(up_send, "rows", up_masks[0])
    low_got = swap(low_send, "rows", low_masks[0])

    meta = after(meta, mlp_sums)
    grad_joined = attend_back(
        meta, lo, hi, query, keys, values, attn, grad_vec, starts, lse, low, high, per
    )
    meta = after(meta, grad_joined)
    qkv_keep, qkv_send, small = joined_weight(
        meta, grad_joined, normed, ln1_gain, ln1_bias, w_own, mlp_sums, rows
    )
    qkv_keep, qkv_send = chunks_of(qkv_keep, qkv_send, rows, 1)
    qkv_got = swap(qkv_send, "rows", 1)

    half = D // 2
    if fits(rows):
        chunk = D // rows
        meta = after(meta, qkv_keep)
        up, lower = [up_keep, up_got], [low_keep, low_got]
        flat = [v.reshape(2 * seq, D) for v in (out_even, out_got)]
        up_send, low_send, out_send = block_sums(
            "first_sums",
            meta,
            2,
            (half // 2, [(term, half // 2) for term in up]),
            (half, [(term, half) for term in lower]),
            (seq, [(term, seq) for term in flat]),
        )
        up.append(swap(up_send, "rows", up_masks[1]))
        lower.append(swap(low_send, "rows", low_masks[1]))
    else:
        out_send = add_low(out_even[1], out_got[1])
    out_far = swap(out_send, "blk", 2)
    meta = after(meta, out_send)
    e_own, e_near, e_send, e_last = norm_grad(meta, grad_joined, e_mlp, ln1_gain, w_own, seq)
    e_last = swap(e_last, "blk", 1)
    e_near = swap(e_near, "blk", 1)
    if fits(rows):
        joined = [after(qkv_keep, e_own), qkv_got]
        tail = add_low(joined[0][half:], qkv_got[half:])
        qkv_send = jnp.concatenate([next_send(joined, half), tail])
        joined.append(swap(qkv_send, "rows", 2))
        meta = after(meta, qkv_send)
        low_send = next_send(lower, half)
        lower.append(swap(low_send, "rows", low_masks[2]))
        e_send = after(e_send, low_send, out_far)
    e_send = add_low(e_send, e_last)
    e_far = swap(e_send, "blk", 2)
    if fits(rows):
        joined[0] = after(joined[0], e_send)
        tail = add_low(after(qkv_send, e_send)[half // 2 :], joined[2][half // 2 :])
        qkv_send = jnp.concatenate([next_send(joined, half // 2), tail])
        joined.append(swap(qkv_send, "rows", 4))
        up[0] = after(up[0], qkv_send)
        up_send = next_send(up, half // 2)
        up.append(swap(up_send, "rows", up_masks[2]))
        out_args = (after(tok_own, qkv_send), out_even, out_got, out_far, b_out, b_down)
        result = finish(result_kernel, "result", seq, *out_args)
        meta = after(meta, result)
        lower[0] = after(lower[0], result, up_send)
        piece = sum(term[:width].astype(F32) for term in lower).astype(BF16)
        meta = after(meta, piece)
        piece = spread_rows(piece)
        packet = ((chunk + 32, width), F32)
        last = pl.BlockSpec((SMALL, 3 * width), lambda i, m: (chunk // SMALL, 0))
        kept, near, far, small = simple(
            last_qkv_kernel,
            "last_qkv",
            [((chunk, width), F32), packet, packet, ((32, width), F32)],
            meta,
            *joined,
            qkv_send,
            joined[3],
            specs=[pl.BlockSpec((chunk, 3 * width), lambda i, m: (0, 0))] * 4 + [last] * 2,
        )
        near, far, diag = swap(near, "blk", 1), swap(far, "blk", 2), swap(small, "blk", 3)
        tok_args = (after(tok_own, small), e_own, e_near, e_far, cot_own)
        grad_tokens = finish(token_kernel, "token_grad", seq, *tok_args)
        meta = after(meta, grad_tokens)
        ends = [((width, hid // 2), F32), ((width // 2, width), F32)]
        down, out_w = simple(lower_kernel, "lower", ends, meta, piece)
        meta = after(meta, down)
        down = down.T
        qkv, gb_qkv, gb_out, gb_up, gb_down, *norms = assemble(
            meta, kept, small, near, far, diag
        )
        up[0] = after(up[0], qkv)
        up = sum(term[:chunk].astype(F32) for term in up)
    else:
        up = reduce_plain(up_keep, up_got, up_masks[1:])
        weights = reduce_plain(low_keep, low_got, low_masks[1:])
        qkv = reduce_plain(qkv_keep, qkv_got, up_masks[1:])
        piece = spread_rows(weights).T
        cut = 4 * hid // rows
        down, out_w = piece[:cut], piece[cut:]
        kept, near, far = split_columns(qkv)
        near, far = swap(near, "blk", 1), swap(far, "blk", 2)
        ends = [jnp.where(blk % 2 == 0, a, b) for a, b in ((kept, far), (far, kept))]
        qkv = jnp.concatenate([ends[0], near, ends[1]], axis=1)
        out_args = (tok_own, out_even, out_got, out_far, b_out, b_down)
        result = finish(result_kernel, "result", seq, *out_args)
        tok_args = (tok_own, e_own, e_near, e_far, cot_own)
        grad_tokens = finish(token_kernel, "token_grad", seq, *tok_args)
        third = 3 * width
        table = jnp.concatenate([small[0:8], small[8:16, : D - third]], axis=1)
        mine = (jnp.arange(4) == blk)[:, None]
        joined = lax.psum(jnp.where(mine, small[2:3], 0.0), ("rows", "blk"))
        gb_up = lax.psum(jnp.where(mine, table[4:5], 0.0), ("rows", "blk")).reshape(FF)
        gb_qkv = jnp.concatenate(
            [
                jnp.concatenate([joined[:, 0:128], joined[:, 256:320]], axis=1).reshape(D),
                jnp.concatenate([joined[:, 128:256], joined[:, 320:384]], axis=1).reshape(D),
                joined[:, 384:576].reshape(D),
            ]
        )
        gain_1, shift_1, _, _, _, gain_2, shift_2, gb_out = lax.psum(table, ("rows", "blk"))
        norms, gb_down = (gain_1, shift_1, gain_2, shift_2), gb_out
    return (
        result[None],
        grad_tokens[None],
        qkv,
        out_w,
        up,
        down,
        gb_qkv,
        gb_out,
        gb_up,
        gb_down,
        *norms,
    )


def solution(mesh):
    split = P("rows", "blk")
    in_specs = (
        P("rows", "blk", None),
        split,
        P("rows"),
        *(P(),) * 12,
        P("rows", "blk", None),
    )
    out_specs = (
        P("rows", "blk", None),
        P("rows", "blk", None),
        *(split,) * 4,
        *(P(),) * 8,
    )
    return jax.shard_map(local, mesh=mesh, in_specs=in_specs, out_specs=out_specs, check_vma=False)
```

```python
import math
from functools import partial

import jax
import jax.numpy as jnp
import numpy as np
from jax import lax
from jax.experimental import pallas as pl
from jax.experimental.pallas import tpu as pltpu
from jax.sharding import PartitionSpec as P

D = 768
HEADS = 12
HDIM = 64
ROT = 16
FF = 3072
EPS = 1e-05
MASKED = -1e30
TILE = 256
VROWS = 80
LN2 = math.log(2.0)
EXTRA = 16
LANES = 128
F32 = jnp.float32
BF16 = jnp.bfloat16
COST = pl.CostEstimate(flops=0, bytes_accessed=0, transcendentals=0)
NT_DIMS = (((1,), (1,)), ((), ()))
TN_DIMS = (((0,), (0,)), ((), ()))


def dot(left, right):
    return jnp.dot(left, right, preferred_element_type=F32)


def dot_nt(left, right):
    return lax.dot_general(left, right, NT_DIMS, preferred_element_type=F32)


def dot_tn(left, right):
    return lax.dot_general(left, right, TN_DIMS, preferred_element_type=F32)


def normalize(value):
    center = value - jnp.mean(value, axis=-1, keepdims=True)
    spread = jnp.mean(center * center, axis=-1, keepdims=True)
    return center * lax.rsqrt(spread + EPS)


def angle_parts(length):
    dim = np.arange(LANES) % HDIM
    inverse = np.where(dim < ROT, 10000.0 ** (-2.0 * (dim % (ROT // 2)) / ROT), 0.0)
    high = (np.arange(length // LANES) * LANES)[:, None] * inverse
    low = np.arange(LANES)[:, None] * inverse
    parts = np.stack([np.cos(low), np.sin(low)]), np.stack([np.cos(high), np.sin(high)])
    return tuple(jnp.asarray(part, F32) for part in parts)


def rotation(low_ref, high_ref, tile):
    lane = lax.broadcasted_iota(jnp.int32, (1, LANES), 1) % HDIM
    sign = jnp.where(lane < ROT // 2, -1.0, 1.0)
    cos_rows, sin_rows = [], []
    for part in range(TILE // LANES):
        row = tile * (TILE // LANES) + part
        cos_high = high_ref[0, pl.ds(row, 1), :]
        sin_high = high_ref[1, pl.ds(row, 1), :]
        cos_rows.append(low_ref[0] * cos_high - low_ref[1] * sin_high)
        sin_rows.append((low_ref[1] * cos_high + low_ref[0] * sin_high) * sign)
    return jnp.concatenate(cos_rows, axis=0), jnp.concatenate(sin_rows, axis=0)


def swap_halves(value):
    lane = lax.broadcasted_iota(jnp.int32, value.shape, 1) % HDIM
    half = ROT // 2
    return jnp.where(
        lane < half, pltpu.roll(value, LANES - half, 1), pltpu.roll(value, half, 1)
    )


def true_block(meta_ref, slot):
    return jnp.bitwise_xor(meta_ref[0], slot)


def params(*semantics, vmem=None):
    return pltpu.CompilerParams(
        dimension_semantics=semantics or ("arbitrary",), vmem_limit_bytes=vmem or 67_043_328
    )


def whole(shape):
    return pl.BlockSpec(shape, lambda *_: (0,) * len(shape))


def own_blocks(refs, odd, into):
    places = ((0, 256), (128, 320), (384, 512))
    for part, (pair_at, third_at) in enumerate(places):
        left, right = refs[2 * part], refs[2 * part + 1]

        @pl.when(odd == 0)
        def _(left=left, right=right, pair_at=pair_at, third_at=third_at):
            into[:, pair_at : pair_at + 128] = left[...]
            into[:, third_at : third_at + 64] = right[:, 0:64]

        @pl.when(odd == 1)
        def _(left=left, right=right, pair_at=pair_at, third_at=third_at):
            into[:, pair_at : pair_at + 128] = jnp.concatenate(
                [left[:, 64:128], right[:, 0:64]], axis=1
            )
            into[:, third_at : third_at + 64] = right[:, 64:128]


def row(ref):
    return ref[...].reshape(1, ref.shape[0])


def own_bias(b_ref, odd, blk, into):
    blocks = []
    for part in range(3):
        for side in range(2):
            at = pl.multiple_of((part * (D // LANES) + side + 3 * blk // 2) * LANES, LANES)
            blocks.append(b_ref[pl.ds(at, LANES)].reshape(1, LANES))
    own_blocks(blocks, odd, into)


def project_tile(normed, gain, shift, w_ref, b_ref, low, high, tile, q_ref, k_ref, v_ref):
    attn_in = (normed * row(gain) + row(shift)).astype(BF16)
    joined = dot(attn_in, w_ref[...]) + b_ref[...]
    cos, sin = rotation(low, high, tile)
    scale = HDIM**-0.5 / LN2

    def turn(block):
        return block * cos + swap_halves(block) * sin

    query = turn(joined[:, 0:128]) * scale
    keys = turn(joined[:, 128:256])
    mixed = turn(joined[:, 256:384])
    q_ref[:, 0:128] = query.astype(BF16)
    k_ref[:, 0:128] = keys.astype(BF16)
    q_ref[:, 128:192] = (mixed[:, 0:64] * scale).astype(BF16)
    k_ref[:, 128:192] = mixed[:, 64:128].astype(BF16)
    v_ref[...] = joined[:, 384:576].astype(BF16)


def find_starts(seq, meta, valid, pairs, start_ref, lo_ref, hi_ref):
    segs = [ref[at : at + 1, 0:seq].astype(F32) for ref in pairs for at in range(2)]
    below = [
        sum(jnp.sum((seg < number).astype(F32), axis=1, keepdims=True) for seg in segs)
        for number in (1, 2, 3)
    ]
    per = seq // TILE
    iota = lax.broadcasted_iota(jnp.int32, (1, seq), 1)
    for slot, seg in enumerate(segs):
        block = true_block(meta, slot)
        begin = jnp.zeros((1, seq), F32)
        for number in (1, 2, 3):
            begin = jnp.where(seg == number, below[number - 1], begin)
        pos = iota + block * seq
        begin = jnp.where(pos < valid[0], begin.astype(jnp.int32), pos)
        for part in range(per):
            tile = begin[:, part * TILE : (part + 1) * TILE]
            start_ref[slot * per + part] = tile
            lo_ref[block * per + part] = jnp.min(tile) // TILE
            hi_ref[block * per + part] = (jnp.max(tile) + (TILE - 1)) // TILE


def qkv_kernel(slot, meta, x_ref, gain, shift, low, high, w_ref, b_ref, *refs):
    per = pl.num_programs(0)
    tile = true_block(meta, slot) * per + pl.program_id(0)
    normed = normalize(x_ref[...].astype(F32))
    project_tile(normed, gain, shift, w_ref, b_ref, low, high, tile, *refs[3:])


def project(slot, meta, x, gain, shift, low, high, w, b, filled, seq):
    width = D // 4
    per = seq // TILE
    out = jax.ShapeDtypeStruct((4 * seq, width), BF16)
    out_spec = pl.BlockSpec((TILE, width), lambda i, m: (slot * per + i, 0))
    args = [x, gain, shift, low, high, w, b, *filled]
    specs = [pl.BlockSpec((TILE, D), lambda i, m: (i, 0))]
    specs += [whole(a.shape) for a in args[1:7]]
    specs += [pl.BlockSpec(memory_space=pl.ANY)] * 3
    return pl.pallas_call(
        partial(qkv_kernel, slot),
        out_shape=[out] * 3,
        grid_spec=pltpu.PrefetchScalarGridSpec(
            num_scalar_prefetch=1, grid=(per,), in_specs=specs, out_specs=[out_spec] * 3
        ),
        input_output_aliases={8 + i: i for i in range(3)},
        compiler_params=params(),
        cost_estimate=COST,
        name=f"qkv_{slot}",
    )(meta, *args)


def mask_order(rows, first):
    masks = [1 << bit for bit in range(rows.bit_length() - 1)]
    return masks if first == 1 else masks[1::-1] + masks[2:]


def places(masks):
    order = [0]
    for mask in reversed(masks):
        order = order + [mask + i for i in order]
    return order


def fits(rows):
    return rows == 8 and D // rows % 32 == 0


def store_chunks(load, keep, send, meta, rows, first):
    size = D // rows
    for index, place in enumerate(places(mask_order(rows, first))):
        at = pl.multiple_of(jnp.bitwise_xor(meta[1], place) * size, 32)
        into = keep if index < rows // 2 else send
        row_at = index % (rows // 2) * size
        into[row_at : row_at + size, :] = load(pl.ds(at, size)).astype(into.dtype)


def store_low(grad, keep, send, meta, rows):
    size, hid = D // 4, FF // 4
    for index, place in enumerate(places(mask_order(rows, 2))):
        chunk = jnp.bitwise_xor(meta[1], place)
        at = pl.ds(pl.multiple_of(chunk % 4 * size, 64), size)
        down = pl.multiple_of(hid + chunk // 4 * (hid // 2), LANES)
        out = pl.multiple_of(2 * hid + chunk // 4 * LANES, LANES)
        into = keep if index < rows // 2 else send
        row_at = slice(index % (rows // 2) * size, (index % (rows // 2) + 1) * size)
        into[row_at, : hid // 2] = grad[at, pl.ds(down, hid // 2)].astype(BF16)
        into[row_at, hid // 2 :] = grad[at, pl.ds(out, LANES)].astype(BF16)


def low_shapes(rows):
    if fits(rows):
        return [(D, FF // 8 + LANES)] * 2
    return [(D, FF // 4 + 2 * LANES), (8, LANES)]


def low_chunks(keep, send, rows):
    if fits(rows):
        return keep, send
    hid, width, count = FF // 4, D // 4, rows // 4
    parts = [
        part.reshape(4, width, count, part.shape[1] // count).transpose(2, 0, 1, 3)
        for part in (keep[:, :hid], keep[:, hid : hid + width])
    ]
    chunks = jnp.concatenate(parts, axis=3).reshape(rows, width, -1)
    order = jnp.array(places(mask_order(rows, 2))) ^ lax.axis_index("rows")
    chunks = jnp.take(chunks, order, axis=0).reshape(rows * width, -1)
    return chunks[: rows * width // 2], chunks[rows * width // 2 :]


def chunk_shapes(cols, rows, extra=0):
    if fits(rows):
        return [(D // 2 + extra, cols)] * 2
    return [(D, cols), (8, LANES)]


def chunks_of(keep, send, rows, first):
    if fits(rows):
        return keep, send
    order = jnp.array(places(mask_order(rows, first))) ^ lax.axis_index("rows")
    parts = keep.reshape(rows, D // rows, keep.shape[1])
    parts = jnp.take(parts, order, axis=0).reshape(keep.shape)
    return parts[: D // 2], parts[D // 2 :]


def feed(normed, upstream, gain, shift, w_up, b_up, w_down):
    mlp_in = (normed * row(gain) + row(shift)).astype(BF16)
    hidden = dot(mlp_in, w_up[...]) + b_up
    cdf = 0.5 * (1.0 + lax.erf(hidden * (0.5**0.5)))
    act = (hidden * cdf).astype(BF16)
    slope = cdf + hidden * jnp.exp(-0.5 * hidden * hidden) * ((2.0 * math.pi) ** -0.5)
    grad_low = (slope * dot_nt(upstream, w_down[...])).astype(BF16)
    grad_norm = dot_nt(grad_low, w_up[...])
    return mlp_in, act, grad_low, grad_norm


def add_sums(sums, grad_low, grad_norm, normed):
    sums[0:1, :] += jnp.sum(grad_low.astype(F32), axis=0, keepdims=True)
    sums[1:2, :] += jnp.sum(grad_norm * normed, axis=0, keepdims=True)
    sums[2:3, :] += jnp.sum(grad_norm, axis=0, keepdims=True)


def own_row(ref, blk, size):
    return ref[pl.ds(pl.multiple_of(blk * size, LANES), size)].reshape(1, size)


def mlp_first_kernel(
    half, meta, xa, xb, ca, cb, gain, shift, b_up, w_up, w_down, w_out,
    gain1, shift1, b_qkv, low, high, w0, w1, w2, w3, w4, w5,
    mo_ref, e_ref, n_ref, gv_ref, sums, gup, gdown, q_ref, k_ref, v_ref, w_own, b_own, x_s, c_s,
):
    step = pl.program_id(0)

    @pl.when(step < half)
    def _():
        x_s[...] = xa[...]
        c_s[...] = ca[...]

    @pl.when(step >= half)
    def _():
        x_s[...] = xb[...]
        c_s[...] = cb[...]

    @pl.when(step == 0)
    def _():
        sums[...] = jnp.zeros_like(sums)
        gup[...] = jnp.zeros_like(gup)
        gdown[...] = jnp.zeros_like(gdown)
        odd = meta[0] % 2
        own_blocks((w0, w1, w2, w3, w4, w5), odd, w_own)
        own_bias(b_qkv, odd, meta[0], b_own)

    upstream = c_s[...]

    @pl.when(step < half)
    def _():
        sums[3:4, :] += jnp.sum(upstream.astype(F32), axis=0, keepdims=True)

    normed = normalize(x_s[...].astype(F32))
    n_ref[...] = normed.astype(BF16)
    tile = true_block(meta, step // half) * half + step % half
    project_tile(normed, gain1, shift1, w_own, b_own, low, high, tile, q_ref, k_ref, v_ref)
    bias = own_row(b_up, meta[0], gup.shape[1])
    mlp_in, act, grad_low, grad_norm = feed(normed, upstream, gain, shift, w_up, bias, w_down)
    mo_ref[...] = dot(act, w_down[...]).astype(BF16)
    add_sums(sums, grad_low, grad_norm, normed)
    e_ref[...] = (grad_norm * row(gain)).astype(BF16)
    gv_ref[...] = dot_nt(upstream, w_out[...]).astype(BF16)
    gup[...] += dot_tn(mlp_in, grad_low)
    gdown[...] += dot_tn(upstream, act)


def mlp_second_kernel(
    half, rows, meta, xa, xb, ca, cb, gain, shift, b_up, w_up, w_down, w_out,
    c0, c1, mo_in, o_near, o_far, sums_in, gup, gdown, *refs
):
    e_ref, n_ref, gv_ref, sums, even, odd, up_keep, up_send, low_keep, low_send = refs[3:13]
    x_s, c_s, n_s, grad = refs[13:]
    step = pl.program_id(0)
    hid = gup.shape[1]

    @pl.when(step < half)
    def _():
        x_s[...] = xa[...]
        c_s[...] = ca[...]
        n_s[...] = c0[...]

    @pl.when(step >= half)
    def _():
        x_s[...] = xb[...]
        c_s[...] = cb[...]
        n_s[...] = c1[...]

    @pl.when(step == 0)
    def _():
        sums[...] = sums_in[...]
        grad[:, 0:hid] = gup[...]
        grad[:, hid : 2 * hid] = gdown[...]
        grad[:, 2 * hid :] = jnp.zeros_like(grad[:, 2 * hid :])

    upstream = c_s[...]
    normed = normalize(x_s[...].astype(F32))
    n_ref[...] = normed.astype(BF16)
    bias = own_row(b_up, meta[0], hid)
    mlp_in, act, grad_low, grad_norm = feed(normed, upstream, gain, shift, w_up, bias, w_down)
    add_sums(sums, grad_low, grad_norm, normed)
    e_ref[...] = (grad_norm * row(gain)).astype(BF16)
    gv_ref[...] = dot_nt(upstream, w_out[...]).astype(BF16)
    grad[:, 0:hid] += dot_tn(mlp_in, grad_low)
    grad[:, hid : 2 * hid] += dot_tn(upstream, act)
    out_grad = dot_tn(upstream, o_far[...]) + dot_tn(n_s[...], o_near[...])
    side = out_grad.shape[1] // 2
    if fits(rows):
        grad[:, 2 * hid : 2 * hid + side] += out_grad[:, :side]
        grad[:, 2 * hid + LANES : 2 * hid + LANES + side] += out_grad[:, side:]
    else:
        grad[:, 2 * hid : 2 * hid + 2 * side] += out_grad
    far = (dot(act, w_down[...]) + dot(o_far[...], w_out[...])).astype(BF16)
    near = (mo_in[...].astype(F32) + dot(o_near[...], w_out[...])).astype(BF16)

    @pl.when(step < half)
    def _():
        even[0] = near
        even[1] = far

    @pl.when(step >= half)
    def _():
        odd[0] = near
        odd[1] = far

    @pl.when(step == pl.num_programs(0) - 1)
    def _():
        if fits(rows):
            store_chunks(lambda at: grad[at, 0:hid], up_keep, up_send, meta, rows, 1)
            store_low(grad, low_keep, low_send, meta, rows)
        else:
            up_keep[...] = grad[:, 0:hid].astype(BF16)
            low_keep[...] = grad[:, hid:].astype(BF16)


def feed_forward(
    meta, xs, cs, gain, shift, b_up, w_up, w_down, w_out, rows, seq,
    joined=None, before=None, near=None, attn=None,
):
    per = seq // TILE
    steps = 2 * per
    hid = FF // 4
    width = D // 4
    total = 4 * seq
    first = pl.BlockSpec((TILE, D), lambda i, m: (jnp.minimum(i, per - 1), 0))
    second = pl.BlockSpec((TILE, D), lambda i, m: (jnp.maximum(i - per, 0), 0))
    specs = [
        first,
        second,
        first,
        second,
        whole((D,)),
        whole((D,)),
        whole((FF,)),
        pl.BlockSpec((D, hid), lambda i, m: (0, m[0])),
        pl.BlockSpec((hid, D), lambda i, m: (m[0], 0)),
        pl.BlockSpec((width, D), lambda i, m: (m[0], 0)),
    ]
    args = [*xs, *cs, gain, shift, b_up, w_up, w_down, w_out]
    tile = pl.BlockSpec((TILE, D), lambda i, m: (i, 0))
    narrow = pl.BlockSpec((TILE, width), lambda i, m: (i, 0))
    sums = (8, D)
    scratch = [pltpu.VMEM((TILE, D), BF16), pltpu.VMEM((TILE, D), BF16)]
    pair = jax.ShapeDtypeStruct((steps * TILE, D), BF16)
    full = jax.ShapeDtypeStruct((total, D), BF16)
    vec = jax.ShapeDtypeStruct((total, width), BF16)
    if before is None:
        body = partial(mlp_first_kernel, per)
        gain1, shift1, w_qkv, b_qkv, low, high = joined
        args += [gain1, shift1, b_qkv, low, high]
        specs += [whole(a.shape) for a in args[-5:]]
        for part in range(3):
            for side in range(2):
                specs.append(
                    pl.BlockSpec(
                        (D, LANES),
                        lambda i, m, at=part * D // LANES + side: (0, at + 3 * m[0] // 2),
                    )
                )
                args.append(w_qkv)
        outs = [pair, full, full, vec, jax.ShapeDtypeStruct(sums, F32)]
        outs += [jax.ShapeDtypeStruct((D, hid), F32)] * 2 + [vec] * 3
        outs += [
            jax.ShapeDtypeStruct((D, 3 * width), BF16),
            jax.ShapeDtypeStruct((1, 3 * width), F32),
        ]
        out_specs = [tile, tile, tile, narrow, whole(sums)]
        out_specs += [whole((D, hid))] * 2 + [narrow] * 3
        out_specs += [whole((D, 3 * width)), whole((1, 3 * width))]
        aliases = {}
    else:
        body = partial(mlp_second_kernel, per, rows)
        mlp_out, norm_part, normed, grad_vec, sums_in, gup, gdown = before
        chunks = chunk_shapes(hid, rows) + low_shapes(rows)
        args += [*near, mlp_out, attn, attn, sums_in, gup, gdown, norm_part, normed, grad_vec]
        specs += [
            first,
            second,
            tile,
            narrow,
            pl.BlockSpec((TILE, width), lambda i, m: (i + steps, 0)),
            whole(sums),
            whole((D, hid)),
            whole((D, hid)),
            *(pl.BlockSpec(memory_space=pl.ANY),) * 3,
        ]
        aliases = {len(args) - 2 + i: i for i in range(3)}
        both = jax.ShapeDtypeStruct((2, seq, D), BF16)
        outs = [full, full, vec, jax.ShapeDtypeStruct(sums, F32), both, both]
        late = pl.BlockSpec((TILE, D), lambda i, m: (i + steps, 0))
        outs += [jax.ShapeDtypeStruct(shape, BF16) for shape in chunks]
        out_specs = [
            late,
            late,
            pl.BlockSpec((TILE, width), lambda i, m: (i + steps, 0)),
            whole(sums),
            pl.BlockSpec((2, TILE, D), lambda i, m: (0, jnp.minimum(i, per - 1), 0)),
            pl.BlockSpec((2, TILE, D), lambda i, m: (0, jnp.maximum(i - per, 0), 0)),
            *(whole(shape) for shape in chunks),
        ]
        scratch += [pltpu.VMEM((TILE, D), BF16), pltpu.VMEM((D, 2 * hid + 2 * LANES), F32)]
    return pl.pallas_call(
        body,
        out_shape=outs,
        grid_spec=pltpu.PrefetchScalarGridSpec(
            num_scalar_prefetch=1,
            grid=(steps,),
            in_specs=specs,
            out_specs=out_specs,
            scratch_shapes=scratch,
        ),
        input_output_aliases=aliases,
        compiler_params=params(),
        cost_estimate=COST,
        name="mlp_first" if before is None else "mlp_second",
    )(meta, *args)


def head_masks():
    lane = lax.broadcasted_iota(jnp.int32, (1, LANES), 1)
    first = jnp.where(lane < HDIM, 1.0, 0.0).astype(BF16)
    second = jnp.where(lane < HDIM, 0.0, 1.0).astype(BF16)
    return first, second


def slot_rows(meta, per, tile):
    slot = jnp.bitwise_xor(tile // per, meta[0])
    return pl.multiple_of((slot * per + tile % per) * TILE, TILE)


def by_head(first, second, block, third):
    return (block * first, block * second, third)


def transpose_all(from_ref, to_ref):
    @pl.loop(0, from_ref.shape[0] // TILE)
    def _(tile):
        rows = pl.ds(pl.multiple_of(tile * TILE, TILE), TILE)
        to_ref[:, rows] = from_ref[rows, :].astype(F32).T.astype(BF16)


def attend_kernel(
    per, meta, valid, q_ref, k_ref, v_ref, pair_own, pair_far,
    o_ref, lse_ref, starts_ref, lo, hi, vt_ref, acc, s_ref,
):
    mask0, mask1 = head_masks()
    tiles = k_ref.shape[0] // TILE
    qi = pl.program_id(0)

    @pl.when(qi == 0)
    def _():
        find_starts(per * TILE, meta, valid, (pair_own, pair_far), starts_ref, lo, hi)
        ones = jnp.where(lax.broadcasted_iota(jnp.int32, (VROWS - HDIM, TILE), 0) == 0, 1.0, 0.0)

        @pl.loop(0, tiles)
        def _(tile):
            rows = pl.ds(pl.multiple_of(tile * TILE, TILE), TILE)
            block = v_ref[rows, :].astype(F32).T
            for head in range(3):
                at = head * VROWS
                vt_ref[at : at + HDIM, rows] = block[head * HDIM : (head + 1) * HDIM].astype(BF16)
                vt_ref[at + HDIM : at + VROWS, rows] = ones.astype(BF16)

    key_iota = lax.broadcasted_iota(jnp.int32, (TILE, TILE), 0)
    query_iota = lax.broadcasted_iota(jnp.int32, (TILE, TILE), 1)
    queries = by_head(mask0, mask1, q_ref[:, 0:128], q_ref[:, 128:192])
    starts = starts_ref[jnp.bitwise_xor(qi // per, meta[0]) * per + qi % per]
    acc[...] = jnp.zeros_like(acc)

    def key_tile(turn):
        return jnp.where(turn == 0, qi, first + turn - 1)

    def score(masked, ki):
        k_rows = pl.ds(slot_rows(meta, per, ki), TILE)
        pair, third = k_ref[k_rows, 0:128], k_ref[k_rows, 128:192]
        scores = [dot_nt(third if head == 2 else pair, queries[head]) for head in range(3)]
        if masked:
            allowed = (key_iota >= starts - ki * TILE) & (key_iota <= query_iota + (qi - ki) * TILE)
            scores = [jnp.where(allowed, x, MASKED) for x in scores]
        return scores, [jnp.max(x, axis=0, keepdims=True) for x in scores]

    def value(ki, tops, peaks):
        k_rows = pl.ds(slot_rows(meta, per, ki), TILE)
        news = [jnp.maximum(top, peak) for top, peak in zip(tops, peaks)]
        fades = [jnp.exp2(top - new) for top, new in zip(tops, news)]
        weights = [jnp.exp2(s_ref[head] - news[head]).astype(BF16) for head in range(3)]
        terms = [
            dot(vt_ref[head * VROWS : (head + 1) * VROWS, k_rows], weights[head]) for head in range(3)
        ]
        return news, fades, terms

    def put(fades, terms):
        for head in range(3):
            cols = slice(head * VROWS, (head + 1) * VROWS)
            acc[cols, :] = acc[cols, :] * fades[head] + terms[head]

    def visit(masked, turn, carry):
        tops, peaks = carry
        scores, next_peaks = score(masked, key_tile(turn + 1))
        news, fades, terms = value(key_tile(turn), tops, peaks)
        peaks = next_peaks
        for head in range(3):
            s_ref[head] = scores[head]
        put(fades, terms)
        return tuple(news), tuple(peaks)

    first = lo[qi]
    full = jnp.minimum(hi[qi], qi)
    scores, peaks = score(True, qi)
    for head in range(3):
        s_ref[head] = scores[head]
    carry = ((jnp.full((1, TILE), MASKED, F32),) * 3, tuple(peaks))
    carry = lax.fori_loop(0, full - first, partial(visit, True), carry)
    carry = lax.fori_loop(full - first, qi - first, partial(visit, False), carry)
    tops, fades, terms = value(key_tile(qi - first), *carry)
    put(fades, terms)
    heads = []
    for head, top in enumerate(tops):
        at = head * VROWS
        total = acc[at + HDIM : at + HDIM + 1, :]
        heads.append(acc[at : at + HDIM, :] / total)
        lse_ref[head, 0] = top + jnp.log2(total)
    o_ref[...] = jnp.concatenate(heads, axis=0).T.astype(BF16)

def attend(meta, valid_len, query, keys, values, seg_pair, cot_far, per):
    total, width = query.shape
    tiles = total // TILE

    def slot(i, m):
        return jnp.bitwise_xor(i // per, m[0]) * per + i % per

    q_spec = pl.BlockSpec((TILE, width), lambda i, m, v: (slot(i, m), 0))
    lse_spec = pl.BlockSpec((3, 1, 1, TILE), lambda i, m, v: (0, slot(i, m), 0, 0))
    far_spec = pl.BlockSpec((EXTRA, D), lambda i, m, v: (per * TILE // EXTRA, 0))
    smem = pl.BlockSpec(memory_space=pltpu.SMEM)
    return pl.pallas_call(
        partial(attend_kernel, per),
        out_shape=[
            jax.ShapeDtypeStruct((total, width), BF16),
            jax.ShapeDtypeStruct((3, tiles, 1, TILE), F32),
            jax.ShapeDtypeStruct((tiles, 1, TILE), jnp.int32),
            jax.ShapeDtypeStruct((tiles,), jnp.int32),
            jax.ShapeDtypeStruct((tiles,), jnp.int32),
        ],
        grid_spec=pltpu.PrefetchScalarGridSpec(
            num_scalar_prefetch=2,
            grid=(tiles,),
            in_specs=[
                q_spec,
                whole(keys.shape),
                whole(values.shape),
                whole(seg_pair.shape),
                far_spec,
            ],
            out_specs=[q_spec, lse_spec, whole((tiles, 1, TILE)), smem, smem],
            scratch_shapes=[
                pltpu.VMEM((3 * VROWS, total), BF16),
                pltpu.VMEM((3 * VROWS, TILE), F32),
                pltpu.VMEM((3, TILE, TILE), F32),
            ],
        ),
        compiler_params=params(),
        cost_estimate=COST,
        name="attend",
    )(meta, valid_len, query, keys, values, seg_pair, cot_far)


def attend_back_kernel(
    per, meta, lo, hi, q_ref, k_ref, v_ref, o_ref, gv_ref, start_ref, lse_ref, low, high,
    gj_ref, kt_ref, dk_ref, dv_ref, dqt_ref
):
    mask0, mask1 = head_masks()
    tiles = k_ref.shape[0] // TILE
    qi = tiles - 1 - pl.program_id(0)

    @pl.when(pl.program_id(0) == 0)
    def _():
        transpose_all(k_ref, kt_ref)

    own_rows = pl.ds(slot_rows(meta, per, qi), TILE)
    key_iota = lax.broadcasted_iota(jnp.int32, (TILE, TILE), 0)
    query_iota = lax.broadcasted_iota(jnp.int32, (TILE, TILE), 1)
    queries = by_head(mask0, mask1, q_ref[:, 0:128], q_ref[:, 128:192])
    grads = by_head(mask0, mask1, gv_ref[:, 0:128], gv_ref[:, 128:192])
    starts = start_ref[0]
    lses = [lse_ref[head, 0] for head in range(3)]
    product = (gv_ref[...].astype(F32) * o_ref[...].astype(F32)).T
    deltas = [
        jnp.sum(product[head * HDIM : (head + 1) * HDIM], axis=0, keepdims=True)
        for head in range(3)
    ]
    dqt_ref[...] = jnp.zeros_like(dqt_ref)

    @pl.when(pl.program_id(0) == 0)
    def _():
        dk_ref[...] = jnp.zeros_like(dk_ref)
        dv_ref[...] = jnp.zeros_like(dv_ref)

    def load(ki):
        k_rows = pl.ds(slot_rows(meta, per, ki), TILE)
        return k_rows

    def score(masked, ki):
        k_rows = load(ki)
        pair, third = k_ref[k_rows, 0:128], k_ref[k_rows, 128:192]
        v_pair, v_third = v_ref[k_rows, 0:128], v_ref[k_rows, 128:192]
        scores = [dot_nt(third if head == 2 else pair, queries[head]) for head in range(3)]
        grad_probs = [dot_nt(v_third if head == 2 else v_pair, grads[head]) for head in range(3)]
        if masked:
            allowed = (key_iota >= starts - ki * TILE) & (key_iota <= query_iota + (qi - ki) * TILE)
            scores = [jnp.where(allowed, x, MASKED) for x in scores]
        return scores, grad_probs

    def terms(ki, scores, grad_probs):
        k_rows = load(ki)
        probs = [jnp.exp2(x - lse) for x, lse in zip(scores, lses)]
        grad_scores = [
            (p * (g - delta)).astype(BF16) for p, g, delta in zip(probs, grad_probs, deltas)
        ]
        dv = [dot(p.astype(BF16), g) for p, g in zip(probs, grads)]
        dk = [dot(g, q) for g, q in zip(grad_scores, queries)]
        dq = [
            dot(kt_ref[head * HDIM : (head + 1) * HDIM, k_rows], grad_scores[head])
            for head in range(3)
        ]
        return dk, dv, dq

    def add(ki, dk, dv, dq):
        k_rows = load(ki)
        for into, parts in ((dk_ref, dk), (dv_ref, dv)):
            into[k_rows, 0:128] += parts[0] + parts[1]
            into[k_rows, 128:192] += parts[2]
        for head in range(3):
            dqt_ref[head * HDIM : (head + 1) * HDIM, :] += dq[head]

    first = lo[qi]
    full = jnp.minimum(hi[qi], qi)

    def visit(masked, ki):
        add(ki, *terms(ki, *score(masked, ki)))

    @pl.loop(first, full)
    def _(ki):
        visit(True, ki)

    @pl.loop(full, qi)
    def _(ki):
        visit(False, ki)

    visit(True, qi)

    cos, sin = rotation(low, high, qi)

    def turn_back(block):
        return block * cos - swap_halves(block) * sin

    dq = dqt_ref[...].T * (HDIM**-0.5)
    dk = dk_ref[own_rows, :] * LN2
    gj_ref[:, 0:128] = turn_back(dq[:, 0:128]).astype(BF16)
    gj_ref[:, 128:256] = turn_back(dk[:, 0:128]).astype(BF16)
    mixed = jnp.concatenate([dq[:, 128:192], dk[:, 128:192]], axis=1)
    gj_ref[:, 256:384] = turn_back(mixed).astype(BF16)
    gj_ref[:, 384:576] = dv_ref[own_rows, :].astype(BF16)


def attend_back(
    meta, lo, hi, query, keys, values, attn, grad_vec, starts, lse, low, high, per
):
    total, width = query.shape
    tiles = total // TILE

    def slot(i, m):
        tile = tiles - 1 - i
        return jnp.bitwise_xor(tile // per, m[0]) * per + tile % per

    q_spec = pl.BlockSpec((TILE, width), lambda i, m, lo, hi: (slot(i, m), 0))
    gj_spec = pl.BlockSpec((TILE, 3 * width), lambda i, m, lo, hi: (slot(i, m), 0))
    start_spec = pl.BlockSpec((1, 1, TILE), lambda i, m, lo, hi: (slot(i, m), 0, 0))
    lse_spec = pl.BlockSpec((3, 1, 1, TILE), lambda i, m, lo, hi: (0, slot(i, m), 0, 0))
    return pl.pallas_call(
        partial(attend_back_kernel, per),
        out_shape=jax.ShapeDtypeStruct((total, 3 * width), BF16),
        grid_spec=pltpu.PrefetchScalarGridSpec(
            num_scalar_prefetch=3,
            grid=(tiles,),
            in_specs=[
                q_spec,
                whole(keys.shape),
                whole(values.shape),
                q_spec,
                q_spec,
                start_spec,
                lse_spec,
                whole(low.shape),
                whole(high.shape),
            ],
            out_specs=gj_spec,
            scratch_shapes=[
                pltpu.VMEM((width, total), BF16),
                pltpu.VMEM((total, width), F32),
                pltpu.VMEM((total, width), F32),
                pltpu.VMEM((width, TILE), F32),
            ],
        ),
        compiler_params=params(),
        cost_estimate=COST,
        name="attend_back",
    )(meta, lo, hi, query, keys, values, attn, grad_vec, starts, lse, low, high)


SMALL = 16


def pack_small(gain_sum, shift_sum, bias, mlp_sums):
    third = 3 * D // 4
    which = lax.broadcasted_iota(jnp.int32, (8, D), 0)
    table = jnp.concatenate([jnp.zeros((4, D), F32), mlp_sums[0:4]], axis=0)
    table = jnp.where(which == 0, gain_sum, jnp.where(which == 1, shift_sum, table))
    head = jnp.where(which[:, :third] == 2, bias, table[:, :third])
    tail = jnp.concatenate([table[:, third:], jnp.zeros((8, 2 * third - D), F32)], axis=1)
    return jnp.concatenate([head, tail], axis=0)


def high_low(value):
    high = value.astype(BF16)
    return high, (value - high.astype(F32)).astype(BF16)


def weight_kernel(rows, meta, *refs):
    gj_ref, n_ref, gain, shift, w_ref, mlp_sums, keep, send, small, grad, bias = refs
    step = pl.program_id(0)

    @pl.when(step == 0)
    def _():
        grad[...] = jnp.zeros_like(grad)
        bias[...] = jnp.zeros_like(bias)

    joined = gj_ref[...]
    bias[0:1, :] += jnp.sum(joined.astype(F32), axis=0, keepdims=True)
    grad[...] += dot_tn(n_ref[...], joined)

    @pl.when(step == pl.num_programs(0) - 1)
    def _():
        total = bias[0:1, :]
        width = total.shape[1]
        parts = jnp.concatenate(
            [*high_low(jnp.broadcast_to(total, (8, width)))], axis=0
        )
        shift_sum = dot_nt(parts, w_ref[...])
        shift_sum = shift_sum[0:1] + shift_sum[8:9]
        ones = jnp.ones((16, width), BF16)
        high, low = high_low(grad[...] * w_ref[...].astype(F32))
        gain_sum = (dot_nt(ones, high) + dot_nt(ones, low))[0:1]
        columns = jnp.concatenate(
            [jnp.broadcast_to(row(gain), (8, D)), jnp.broadcast_to(row(shift), (8, D))], axis=0
        ).T
        grad[...] = grad[...] * columns[:, 0:1] + columns[:, 8:9] * total
        rest = pack_small(gain_sum, shift_sum, total, mlp_sums[...])
        small[...] = rest
        if fits(rows):
            store_chunks(lambda at: grad[at, :], keep, send, meta, rows, 1)
            keep[D // 2 :, :] = rest.astype(BF16)
            send[D // 2 :, :] = rest.astype(BF16)
        else:
            keep[...] = grad[...].astype(BF16)


def row_tiles(cols, tile=TILE):
    return pl.BlockSpec((tile, cols), lambda i, m: (i, 0))


def joined_weight(meta, grad, normed, gain, shift, w, mlp_sums, rows):
    total, width = grad.shape
    tile = 2 * TILE
    chunks = chunk_shapes(width, rows, SMALL)
    args = [gain, shift, w, mlp_sums]
    return pl.pallas_call(
        partial(weight_kernel, rows),
        out_shape=[jax.ShapeDtypeStruct(shape, BF16) for shape in chunks]
        + [jax.ShapeDtypeStruct((SMALL, width), F32)],
        grid_spec=pltpu.PrefetchScalarGridSpec(
            num_scalar_prefetch=1,
            grid=(total // tile,),
            in_specs=[row_tiles(width, tile), row_tiles(D, tile), *(whole(a.shape) for a in args)],
            out_specs=[*(whole(shape) for shape in chunks), whole((SMALL, width))],
            scratch_shapes=[pltpu.VMEM((D, width), F32), pltpu.VMEM((8, width), F32)],
        ),
        compiler_params=params(),
        cost_estimate=COST,
        name="joined_weight",
    )(meta, grad, normed, *args)


def norm_kernel(meta, *refs):
    gjs, es, (gain, w_ref), outs = refs[0:4], refs[4:8], refs[8:10], refs[10:]
    for gj_ref, e_in, out in zip(gjs, es, outs):
        grad_norm = dot_nt(gj_ref[...], w_ref[...])
        out[...] = (grad_norm * row(gain) + e_in[...].astype(F32)).astype(BF16)


def norm_grad(meta, grad, e_mlp, gain, w, seq):
    tile = TILE
    per = seq // tile

    def slot_tiles(slot, cols):
        return pl.BlockSpec((tile, cols), lambda i, m: (slot * per + i, 0))

    return pl.pallas_call(
        norm_kernel,
        out_shape=[jax.ShapeDtypeStruct((seq, D), BF16)] * 4,
        grid_spec=pltpu.PrefetchScalarGridSpec(
            num_scalar_prefetch=1,
            grid=(per,),
            in_specs=[
                *(slot_tiles(slot, grad.shape[1]) for slot in range(4)),
                *(slot_tiles(slot, D) for slot in range(4)),
                whole(gain.shape),
                whole(w.shape),
            ],
            out_specs=[slot_tiles(0, D)] * 4,
        ),
        compiler_params=params(),
        cost_estimate=COST,
        name="norm_grad",
    )(meta, *[grad] * 4, *[e_mlp] * 4, gain, w)


def simple(body, name, shapes, *args, specs=None):
    return pl.pallas_call(
        body,
        out_shape=[jax.ShapeDtypeStruct(shape, kind) for shape, kind in shapes],
        grid_spec=pltpu.PrefetchScalarGridSpec(
            num_scalar_prefetch=1,
            grid=(1,),
            in_specs=specs or [whole(a.shape) for a in args[1:]],
            out_specs=[whole(shape) for shape, _ in shapes],
        ),
        compiler_params=params(),
        cost_estimate=COST,
        name=name,
    )(*args)


def add_up(refs):
    total = refs[0][...].astype(F32)
    for ref in refs[1:]:
        total += ref[...].astype(F32)
    return total


def sums_kernel(counts, meta, *refs):
    ins, outs = refs[: sum(counts)], refs[sum(counts) :]
    for count, out in zip(counts, outs):
        out[...] = add_up(ins[:count]).astype(BF16)
        ins = ins[count:]


def block_sums(name, meta, steps, *jobs):
    specs, args, outs, out_specs = [], [], [], []
    for rows, terms in jobs:
        size, cols = rows // steps, terms[0][0].shape[1]
        for array, at in terms:
            specs.append(pl.BlockSpec((size, cols), lambda i, m, at=at // size: (at + i, 0)))
            args.append(array)
        outs.append(jax.ShapeDtypeStruct((rows, cols), BF16))
        out_specs.append(pl.BlockSpec((size, cols), lambda i, m: (i, 0)))
    return pl.pallas_call(
        partial(sums_kernel, [len(terms) for _, terms in jobs]),
        out_shape=outs,
        grid_spec=pltpu.PrefetchScalarGridSpec(
            num_scalar_prefetch=1, grid=(steps,), in_specs=specs, out_specs=out_specs
        ),
        compiler_params=params(),
        cost_estimate=COST,
        name=name,
    )(meta, *args)


def lower_kernel(meta, piece, down_ref, out_ref):
    cut = down_ref.shape[1]
    down_ref[...] = piece[:, :cut].astype(F32)
    out_ref[...] = piece[:, cut:].astype(F32).T[: out_ref.shape[0]]


def last_qkv_kernel(meta, *refs):
    *terms, sums, got_sums, kept, near, far, small = refs
    size = kept.shape[0]
    width = kept.shape[1]
    total = add_up(terms)
    rows = sums[...].astype(F32) + got_sums[...].astype(F32)
    for part in range(3):
        small[part * 8 : part * 8 + 8, :] = rows[0:8, part * width : (part + 1) * width]
    small[24:32, :] = rows[8:16, 0:width]
    near[size:, :] = small[...]
    far[size:, :] = small[...]
    query = jnp.concatenate([total[:, 0:128], total[:, 256:320]], axis=1)
    keys = jnp.concatenate([total[:, 128:256], total[:, 320:384]], axis=1)
    values = total[:, 384:576]
    plans = (
        (query, keys, values),
        (keys, query, values),
        (keys, values, query),
        (values, keys, query),
    )
    for blk, plan in enumerate(plans):

        @pl.when(meta[0] == blk)
        def _(plan=plan):
            kept[...] = plan[0]
            near[0:size, :] = plan[1]
            far[0:size, :] = plan[2]


def assemble_kernel(
    meta, kept, small, near, far, diag,
    qkv, b_qkv, b_out, b_up, b_down, gain1, shift1, gain2, shift2, table,
):
    size, width = kept.shape

    @pl.when(meta[0] % 2 == 0)
    def _():
        qkv[:, 0:width] = kept[...]
        qkv[:, 2 * width :] = far[0:size, :]

    @pl.when(meta[0] % 2 == 1)
    def _():
        qkv[:, 0:width] = far[0:size, :]
        qkv[:, 2 * width :] = kept[...]

    qkv[:, width : 2 * width] = near[0:size, :]
    table[0] = small[...]
    table[1] = near[size:, :]
    table[2] = far[size:, :]
    table[3] = diag[...]
    blocks = [table[jnp.bitwise_xor(meta[0], blk)] for blk in range(4)]
    total = blocks[0] + blocks[1] + blocks[2] + blocks[3]

    def vector(rows, index):
        parts = [rows[part * 8 + index : part * 8 + index + 1, :] for part in range(4)]
        return jnp.concatenate(parts, axis=1)

    for ref, index in ((gain1, 0), (shift1, 1), (gain2, 5), (shift2, 6), (b_out, 7), (b_down, 7)):
        ref[...] = vector(total, index).reshape(D)
    ups, parts = [], ([], [], [])
    for rows in blocks:
        ups.append(vector(rows, 4))
        joined = vector(rows, 2)
        parts[0].append(jnp.concatenate([joined[:, 0:128], joined[:, 256:320]], axis=1))
        parts[1].append(jnp.concatenate([joined[:, 128:256], joined[:, 320:384]], axis=1))
        parts[2].append(joined[:, 384:576])
    b_up[...] = jnp.concatenate(ups, axis=1).reshape(4 * D)
    b_qkv[...] = jnp.concatenate(parts[0] + parts[1] + parts[2], axis=1).reshape(3 * D)


def assemble(meta, kept, small, near, far, diag):
    size, width = kept.shape
    shapes = [((size, 3 * width), F32), ((3 * D,), F32), ((D,), F32), ((4 * D,), F32)]
    shapes += [((D,), F32)] * 5
    args = (kept, small, near, far, diag)
    return pl.pallas_call(
        assemble_kernel,
        out_shape=[jax.ShapeDtypeStruct(shape, kind) for shape, kind in shapes],
        grid_spec=pltpu.PrefetchScalarGridSpec(
            num_scalar_prefetch=1,
            grid=(1,),
            in_specs=[whole(a.shape) for a in args],
            out_specs=[whole(shape) for shape, _ in shapes],
            scratch_shapes=[pltpu.VMEM((4, 32, width), F32)],
        ),
        compiler_params=params(),
        cost_estimate=COST,
        name="assemble",
    )(meta, *args)


def next_send(terms, size):
    return sum(term[size // 2 : size].astype(F32) for term in terms).astype(BF16)


def reduce_plain(keep, got, masks):
    terms, size = [keep, got], keep.shape[0]
    for mask in masks:
        terms.append(swap(next_send(terms, size), "rows", mask))
        size //= 2
    return sum(term[:size].astype(F32) for term in terms)


def after(value, *others):
    return lax.optimization_barrier((value, others))[0]


def swap(value, axis, mask):
    size = lax.axis_size(axis)
    return lax.ppermute(value, axis, [(i, i ^ mask) for i in range(size)])


def add_low(left, right):
    return (left.astype(F32) + right.astype(F32)).astype(BF16)


def spread_rows(chunk):
    rows = lax.axis_size("rows")
    moves = [
        (r * 4 + b, (rows // 4 * b + r // 4) * 4 + r % 4) for r in range(rows) for b in range(4)
    ]
    return lax.ppermute(chunk, ("rows", "blk"), moves)


def split_columns(chunk):
    b = lax.axis_index("blk")
    q = jnp.concatenate([chunk[:, 0:128], chunk[:, 256:320]], axis=1)
    k = jnp.concatenate([chunk[:, 128:256], chunk[:, 320:384]], axis=1)
    v = chunk[:, 384:576]

    def choose(zero, one, two, three):
        return jnp.where(b < 2, jnp.where(b == 0, zero, one), jnp.where(b == 2, two, three))

    return choose(q, k, k, v), choose(k, q, v, k), choose(v, v, q, q)


def result_kernel(x_ref, even, near, far, b_out, b_down, out_ref):
    bias = row(b_out) + row(b_down)
    total = even[0].astype(F32) + near[0].astype(F32) + far[...].astype(F32)
    out_ref[...] = (x_ref[...].astype(F32) + bias + total).astype(BF16)


def token_kernel(x_ref, even, near, far, c_ref, out_ref):
    wide = x_ref[...].astype(F32)
    center = wide - jnp.mean(wide, axis=-1, keepdims=True)
    rate = lax.rsqrt(jnp.mean(center * center, axis=-1, keepdims=True) + EPS)
    normed = center * rate
    grad = even[...].astype(F32) + near[...].astype(F32) + far[...].astype(F32)
    mean = jnp.mean(grad, axis=-1, keepdims=True)
    along = jnp.mean(grad * normed, axis=-1, keepdims=True)
    back = rate * (grad - mean - normed * along)
    out_ref[...] = (c_ref[...].astype(F32) + back).astype(BF16)


def finish(body, name, seq, x, even, near, far, *more):
    flat = pl.BlockSpec((TILE, D), lambda i: (i, 0))
    own = pl.BlockSpec((1, TILE, D), lambda i: (0, i, 0))
    return pl.pallas_call(
        body,
        out_shape=jax.ShapeDtypeStruct((seq, D), BF16),
        grid=(seq // TILE,),
        in_specs=[
            *(own if a.ndim == 3 else flat for a in (x, even, near, far)),
            *(flat if a.ndim == 2 else whole(a.shape) for a in more),
        ],
        out_specs=flat,
        compiler_params=params(),
        cost_estimate=COST,
        name=name,
    )(x, even, near, far, *more)


def local(
    tokens, seg_ids, valid_len, ln1_gain, ln1_bias, w_qkv, b_qkv, w_out, b_out,
    ln2_gain, ln2_bias, w_up, b_up, w_down, b_down, cotangent,
):
    rows = lax.axis_size("rows")
    blk = lax.axis_index("blk")
    seq = tokens.shape[1]
    per = seq // TILE
    width = D // 4
    hid = FF // 4
    low, high = angle_parts(4 * seq)
    tok_own, cot_own = tokens[0], cotangent[0]

    cot_near = swap(cot_own, "blk", 1)
    tok_far = swap(tok_own, "blk", 2)
    tok_near = swap(tok_own, "blk", 1)
    seg_own = seg_ids.astype(BF16)
    seg_pair = jnp.concatenate([seg_own, swap(seg_own, "blk", 1)])
    seg_pair = jnp.pad(seg_pair, ((0, EXTRA - 2), (0, D - seq)))
    cot_long = jnp.concatenate([cot_own, seg_pair])
    cot_far = swap(cot_long, "blk", 2)

    meta = jnp.stack([blk, lax.axis_index("rows")]).astype(jnp.int32)
    mlp_args = (ln2_gain, ln2_bias, b_up, w_up, w_down, w_out, rows, seq)
    joined = (ln1_gain, ln1_bias, w_qkv, b_qkv, low, high)
    *first, query, keys, values, w_own, b_own = feed_forward(
        meta, (tok_own, tok_near), (cot_own, cot_near), *mlp_args, joined
    )
    meta = after(meta, b_own)

    def more(slot, m, tok, filled):
        args = (ln1_gain, ln1_bias, low, high, w_own, b_own, filled, seq)
        return project(slot, m, tok, *args)

    tok_last = swap(after(tok_far, b_own), "blk", 1)
    joined = more(2, meta, tok_far, (query, keys, values))
    query, keys, values = more(3, after(meta, joined[0]), tok_last, joined)
    cot_last = swap(after(cot_far, query), "blk", 1)
    cots = (cot_own, cot_near, cot_far, cot_last)
    attn, lse, starts, lo, hi = attend(
        meta, valid_len, query, keys, values, seg_pair, cot_far, per
    )

    meta = after(meta, lse)
    e_mlp, normed, grad_vec, mlp_sums, out_even, out_odd, *packets = feed_forward(
        meta, (tok_far, tok_last), cots[2:], *mlp_args, before=first, near=cots[:2], attn=attn
    )
    up_keep, up_send = chunks_of(*packets[:2], rows, 1)
    low_keep, low_send = low_chunks(*packets[2:], rows)
    up_masks, low_masks = mask_order(rows, 1), mask_order(rows, 2)
    out_got = swap(out_odd, "blk", 1)
    up_got = swap(up_send, "rows", up_masks[0])
    low_got = swap(low_send, "rows", low_masks[0])

    meta = after(meta, mlp_sums)
    grad_joined = attend_back(
        meta, lo, hi, query, keys, values, attn, grad_vec, starts, lse, low, high, per
    )
    meta = after(meta, grad_joined)
    qkv_keep, qkv_send, small = joined_weight(
        meta, grad_joined, normed, ln1_gain, ln1_bias, w_own, mlp_sums, rows
    )
    qkv_keep, qkv_send = chunks_of(qkv_keep, qkv_send, rows, 1)
    qkv_got = swap(qkv_send, "rows", 1)

    half = D // 2
    if fits(rows):
        chunk = D // rows
        meta = after(meta, qkv_keep)
        up, lower = [up_keep, up_got], [low_keep, low_got]
        flat = [v.reshape(2 * seq, D) for v in (out_even, out_got)]
        up_send, low_send, out_send = block_sums(
            "first_sums",
            meta,
            1,
            (half // 2, [(term, half // 2) for term in up]),
            (half, [(term, half) for term in lower]),
            (seq, [(term, seq) for term in flat]),
        )
        up.append(swap(up_send, "rows", up_masks[1]))
        lower.append(swap(low_send, "rows", low_masks[1]))
    else:
        out_send = add_low(out_even[1], out_got[1])
    out_far = swap(out_send, "blk", 2)
    meta = after(meta, out_send)
    e_own, e_near, e_send, e_last = norm_grad(meta, grad_joined, e_mlp, ln1_gain, w_own, seq)
    e_last = swap(e_last, "blk", 1)
    e_near = swap(e_near, "blk", 1)
    if fits(rows):
        joined = [after(qkv_keep, e_own), qkv_got]
        tail = add_low(joined[0][half:], qkv_got[half:])
        qkv_send = jnp.concatenate([next_send(joined, half), tail])
        joined.append(swap(qkv_send, "rows", 2))
        meta = after(meta, qkv_send)
        low_send = next_send(lower, half)
        lower.append(swap(low_send, "rows", low_masks[2]))
        e_send = after(e_send, low_send, out_far)
    e_send = add_low(e_send, e_last)
    e_far = swap(e_send, "blk", 2)
    if fits(rows):
        joined[0] = after(joined[0], e_send)
        tail = add_low(after(qkv_send, e_send)[half // 2 :], joined[2][half // 2 :])
        qkv_send = jnp.concatenate([next_send(joined, half // 2), tail])
        joined.append(swap(qkv_send, "rows", 4))
        up[0] = after(up[0], qkv_send)
        up_send = next_send(up, half // 2)
        up.append(swap(up_send, "rows", up_masks[2]))
        out_args = (after(tok_own, qkv_send), out_even, out_got, out_far, b_out, b_down)
        result = finish(result_kernel, "result", seq, *out_args)
        meta = after(meta, result)
        lower[0] = after(lower[0], result, up_send)
        piece = sum(term[:width].astype(F32) for term in lower).astype(BF16)
        meta = after(meta, piece)
        piece = spread_rows(piece)
        packet = ((chunk + 32, width), F32)
        last = pl.BlockSpec((SMALL, 3 * width), lambda i, m: (chunk // SMALL, 0))
        kept, near, far, small = simple(
            last_qkv_kernel,
            "last_qkv",
            [((chunk, width), F32), packet, packet, ((32, width), F32)],
            meta,
            *joined,
            qkv_send,
            joined[3],
            specs=[pl.BlockSpec((chunk, 3 * width), lambda i, m: (0, 0))] * 4 + [last] * 2,
        )
        near, far, diag = swap(near, "blk", 1), swap(far, "blk", 2), swap(small, "blk", 3)
        tok_args = (after(tok_own, small), e_own, e_near, e_far, cot_own)
        grad_tokens = finish(token_kernel, "token_grad", seq, *tok_args)
        meta = after(meta, grad_tokens)
        ends = [((width, hid // 2), F32), ((width // 2, width), F32)]
        down, out_w = simple(lower_kernel, "lower", ends, meta, piece)
        meta = after(meta, down)
        down = down.T
        qkv, gb_qkv, gb_out, gb_up, gb_down, *norms = assemble(
            meta, kept, small, near, far, diag
        )
        up[0] = after(up[0], qkv)
        up = sum(term[:chunk].astype(F32) for term in up)
    else:
        up = reduce_plain(up_keep, up_got, up_masks[1:])
        weights = reduce_plain(low_keep, low_got, low_masks[1:])
        qkv = reduce_plain(qkv_keep, qkv_got, up_masks[1:])
        piece = spread_rows(weights).T
        cut = 4 * hid // rows
        down, out_w = piece[:cut], piece[cut:]
        kept, near, far = split_columns(qkv)
        near, far = swap(near, "blk", 1), swap(far, "blk", 2)
        ends = [jnp.where(blk % 2 == 0, a, b) for a, b in ((kept, far), (far, kept))]
        qkv = jnp.concatenate([ends[0], near, ends[1]], axis=1)
        out_args = (tok_own, out_even, out_got, out_far, b_out, b_down)
        result = finish(result_kernel, "result", seq, *out_args)
        tok_args = (tok_own, e_own, e_near, e_far, cot_own)
        grad_tokens = finish(token_kernel, "token_grad", seq, *tok_args)
        third = 3 * width
        table = jnp.concatenate([small[0:8], small[8:16, : D - third]], axis=1)
        mine = (jnp.arange(4) == blk)[:, None]
        joined = lax.psum(jnp.where(mine, small[2:3], 0.0), ("rows", "blk"))
        gb_up = lax.psum(jnp.where(mine, table[4:5], 0.0), ("rows", "blk")).reshape(FF)
        gb_qkv = jnp.concatenate(
            [
                jnp.concatenate([joined[:, 0:128], joined[:, 256:320]], axis=1).reshape(D),
                jnp.concatenate([joined[:, 128:256], joined[:, 320:384]], axis=1).reshape(D),
                joined[:, 384:576].reshape(D),
            ]
        )
        gain_1, shift_1, _, _, _, gain_2, shift_2, gb_out = lax.psum(table, ("rows", "blk"))
        norms, gb_down = (gain_1, shift_1, gain_2, shift_2), gb_out
    return (
        result[None],
        grad_tokens[None],
        qkv,
        out_w,
        up,
        down,
        gb_qkv,
        gb_out,
        gb_up,
        gb_down,
        *norms,
    )


def solution(mesh):
    split = P("rows", "blk")
    in_specs = (
        P("rows", "blk", None),
        split,
        P("rows"),
        *(P(),) * 12,
        P("rows", "blk", None),
    )
    out_specs = (
        P("rows", "blk", None),
        P("rows", "blk", None),
        *(split,) * 4,
        *(P(),) * 8,
    )
    return jax.shard_map(local, mesh=mesh, in_specs=in_specs, out_specs=out_specs, check_vma=False)
```

```python
import math
from functools import partial

import jax
import jax.numpy as jnp
import numpy as np
from jax import lax
from jax.experimental import pallas as pl
from jax.experimental.pallas import tpu as pltpu
from jax.sharding import PartitionSpec as P

D = 768
HEADS = 12
HDIM = 64
ROT = 16
FF = 3072
EPS = 1e-05
MASKED = -1e30
TILE = 256
VROWS = 80
LN2 = math.log(2.0)
EXTRA = 16
LANES = 128
F32 = jnp.float32
BF16 = jnp.bfloat16
COST = pl.CostEstimate(flops=0, bytes_accessed=0, transcendentals=0)
NT_DIMS = (((1,), (1,)), ((), ()))
TN_DIMS = (((0,), (0,)), ((), ()))


def dot(left, right):
    return jnp.dot(left, right, preferred_element_type=F32)


def dot_nt(left, right):
    return lax.dot_general(left, right, NT_DIMS, preferred_element_type=F32)


def dot_tn(left, right):
    return lax.dot_general(left, right, TN_DIMS, preferred_element_type=F32)


def normalize(value):
    center = value - jnp.mean(value, axis=-1, keepdims=True)
    spread = jnp.mean(center * center, axis=-1, keepdims=True)
    return center * lax.rsqrt(spread + EPS)


def angle_parts(length):
    dim = np.arange(LANES) % HDIM
    inverse = np.where(dim < ROT, 10000.0 ** (-2.0 * (dim % (ROT // 2)) / ROT), 0.0)
    high = (np.arange(length // LANES) * LANES)[:, None] * inverse
    low = np.arange(LANES)[:, None] * inverse
    parts = np.stack([np.cos(low), np.sin(low)]), np.stack([np.cos(high), np.sin(high)])
    return tuple(jnp.asarray(part, F32) for part in parts)


def rotation(low_ref, high_ref, tile):
    lane = lax.broadcasted_iota(jnp.int32, (1, LANES), 1) % HDIM
    sign = jnp.where(lane < ROT // 2, -1.0, 1.0)
    cos_rows, sin_rows = [], []
    for part in range(TILE // LANES):
        row = tile * (TILE // LANES) + part
        cos_high = high_ref[0, pl.ds(row, 1), :]
        sin_high = high_ref[1, pl.ds(row, 1), :]
        cos_rows.append(low_ref[0] * cos_high - low_ref[1] * sin_high)
        sin_rows.append((low_ref[1] * cos_high + low_ref[0] * sin_high) * sign)
    return jnp.concatenate(cos_rows, axis=0), jnp.concatenate(sin_rows, axis=0)


def swap_halves(value):
    lane = lax.broadcasted_iota(jnp.int32, value.shape, 1) % HDIM
    half = ROT // 2
    return jnp.where(
        lane < half, pltpu.roll(value, LANES - half, 1), pltpu.roll(value, half, 1)
    )


def true_block(meta_ref, slot):
    return jnp.bitwise_xor(meta_ref[0], slot)


def params(*semantics, vmem=None):
    return pltpu.CompilerParams(
        dimension_semantics=semantics or ("arbitrary",), vmem_limit_bytes=vmem or 67_043_328
    )


def whole(shape):
    return pl.BlockSpec(shape, lambda *_: (0,) * len(shape))


def own_blocks(refs, odd, into):
    places = ((0, 256), (128, 320), (384, 512))
    for part, (pair_at, third_at) in enumerate(places):
        left, right = refs[2 * part], refs[2 * part + 1]

        @pl.when(odd == 0)
        def _(left=left, right=right, pair_at=pair_at, third_at=third_at):
            into[:, pair_at : pair_at + 128] = left[...]
            into[:, third_at : third_at + 64] = right[:, 0:64]

        @pl.when(odd == 1)
        def _(left=left, right=right, pair_at=pair_at, third_at=third_at):
            into[:, pair_at : pair_at + 128] = jnp.concatenate(
                [left[:, 64:128], right[:, 0:64]], axis=1
            )
            into[:, third_at : third_at + 64] = right[:, 64:128]


def row(ref):
    return ref[...].reshape(1, ref.shape[0])


def own_bias(b_ref, odd, blk, into):
    blocks = []
    for part in range(3):
        for side in range(2):
            at = pl.multiple_of((part * (D // LANES) + side + 3 * blk // 2) * LANES, LANES)
            blocks.append(b_ref[pl.ds(at, LANES)].reshape(1, LANES))
    own_blocks(blocks, odd, into)


def project_tile(normed, gain, shift, w_ref, b_ref, low, high, tile, q_ref, k_ref, v_ref):
    attn_in = (normed * row(gain) + row(shift)).astype(BF16)
    joined = dot(attn_in, w_ref[...]) + b_ref[...]
    cos, sin = rotation(low, high, tile)
    scale = HDIM**-0.5 / LN2

    def turn(block):
        return block * cos + swap_halves(block) * sin

    query = turn(joined[:, 0:128]) * scale
    keys = turn(joined[:, 128:256])
    mixed = turn(joined[:, 256:384])
    q_ref[:, 0:128] = query.astype(BF16)
    k_ref[:, 0:128] = keys.astype(BF16)
    q_ref[:, 128:192] = (mixed[:, 0:64] * scale).astype(BF16)
    k_ref[:, 128:192] = mixed[:, 64:128].astype(BF16)
    v_ref[...] = joined[:, 384:576].astype(BF16)


def find_starts(seq, meta, valid, pairs, start_ref, lo_ref, hi_ref):
    segs = [ref[at : at + 1, 0:seq].astype(F32) for ref in pairs for at in range(2)]
    below = [
        sum(jnp.sum((seg < number).astype(F32), axis=1, keepdims=True) for seg in segs)
        for number in (1, 2, 3)
    ]
    per = seq // TILE
    iota = lax.broadcasted_iota(jnp.int32, (1, seq), 1)
    for slot, seg in enumerate(segs):
        block = true_block(meta, slot)
        begin = jnp.zeros((1, seq), F32)
        for number in (1, 2, 3):
            begin = jnp.where(seg == number, below[number - 1], begin)
        pos = iota + block * seq
        begin = jnp.where(pos < valid[0], begin.astype(jnp.int32), pos)
        for part in range(per):
            tile = begin[:, part * TILE : (part + 1) * TILE]
            start_ref[slot * per + part] = tile
            lo_ref[block * per + part] = jnp.min(tile) // TILE
            hi_ref[block * per + part] = (jnp.max(tile) + (TILE - 1)) // TILE


def qkv_kernel(slot, meta, x_ref, gain, shift, low, high, w_ref, b_ref, *refs):
    per = pl.num_programs(0)
    tile = true_block(meta, slot) * per + pl.program_id(0)
    normed = normalize(x_ref[...].astype(F32))
    project_tile(normed, gain, shift, w_ref, b_ref, low, high, tile, *refs[3:])


def project(slot, meta, x, gain, shift, low, high, w, b, filled, seq):
    width = D // 4
    per = seq // TILE
    out = jax.ShapeDtypeStruct((4 * seq, width), BF16)
    out_spec = pl.BlockSpec((TILE, width), lambda i, m: (slot * per + i, 0))
    args = [x, gain, shift, low, high, w, b, *filled]
    specs = [pl.BlockSpec((TILE, D), lambda i, m: (i, 0))]
    specs += [whole(a.shape) for a in args[1:7]]
    specs += [pl.BlockSpec(memory_space=pl.ANY)] * 3
    return pl.pallas_call(
        partial(qkv_kernel, slot),
        out_shape=[out] * 3,
        grid_spec=pltpu.PrefetchScalarGridSpec(
            num_scalar_prefetch=1, grid=(per,), in_specs=specs, out_specs=[out_spec] * 3
        ),
        input_output_aliases={8 + i: i for i in range(3)},
        compiler_params=params(),
        cost_estimate=COST,
        name=f"qkv_{slot}",
    )(meta, *args)


def mask_order(rows, first):
    masks = [1 << bit for bit in range(rows.bit_length() - 1)]
    return masks if first == 1 else masks[1::-1] + masks[2:]


def places(masks):
    order = [0]
    for mask in reversed(masks):
        order = order + [mask + i for i in order]
    return order


def fits(rows):
    return rows == 8 and D // rows % 32 == 0


def store_chunks(load, keep, send, meta, rows, first):
    size = D // rows
    for index, place in enumerate(places(mask_order(rows, first))):
        at = pl.multiple_of(jnp.bitwise_xor(meta[1], place) * size, 32)
        into = keep if index < rows // 2 else send
        row_at = index % (rows // 2) * size
        into[row_at : row_at + size, :] = load(pl.ds(at, size)).astype(into.dtype)


def store_low(grad, keep, send, meta, rows):
    size, hid = D // 4, FF // 4
    for index, place in enumerate(places(mask_order(rows, 2))):
        chunk = jnp.bitwise_xor(meta[1], place)
        at = pl.ds(pl.multiple_of(chunk % 4 * size, 64), size)
        down = pl.multiple_of(hid + chunk // 4 * (hid // 2), LANES)
        out = pl.multiple_of(2 * hid + chunk // 4 * LANES, LANES)
        into = keep if index < rows // 2 else send
        row_at = slice(index % (rows // 2) * size, (index % (rows // 2) + 1) * size)
        into[row_at, : hid // 2] = grad[at, pl.ds(down, hid // 2)].astype(BF16)
        into[row_at, hid // 2 :] = grad[at, pl.ds(out, LANES)].astype(BF16)


def low_shapes(rows):
    if fits(rows):
        return [(D, FF // 8 + LANES)] * 2
    return [(D, FF // 4 + 2 * LANES), (8, LANES)]


def low_chunks(keep, send, rows):
    if fits(rows):
        return keep, send
    hid, width, count = FF // 4, D // 4, rows // 4
    parts = [
        part.reshape(4, width, count, part.shape[1] // count).transpose(2, 0, 1, 3)
        for part in (keep[:, :hid], keep[:, hid : hid + width])
    ]
    chunks = jnp.concatenate(parts, axis=3).reshape(rows, width, -1)
    order = jnp.array(places(mask_order(rows, 2))) ^ lax.axis_index("rows")
    chunks = jnp.take(chunks, order, axis=0).reshape(rows * width, -1)
    return chunks[: rows * width // 2], chunks[rows * width // 2 :]


def chunk_shapes(cols, rows, extra=0):
    if fits(rows):
        return [(D // 2 + extra, cols)] * 2
    return [(D, cols), (8, LANES)]


def chunks_of(keep, send, rows, first):
    if fits(rows):
        return keep, send
    order = jnp.array(places(mask_order(rows, first))) ^ lax.axis_index("rows")
    parts = keep.reshape(rows, D // rows, keep.shape[1])
    parts = jnp.take(parts, order, axis=0).reshape(keep.shape)
    return parts[: D // 2], parts[D // 2 :]


def feed(normed, upstream, gain, shift, w_up, b_up, w_down):
    mlp_in = (normed * row(gain) + row(shift)).astype(BF16)
    hidden = dot(mlp_in, w_up[...]) + b_up
    cdf = 0.5 * (1.0 + lax.erf(hidden * (0.5**0.5)))
    act = (hidden * cdf).astype(BF16)
    slope = cdf + hidden * jnp.exp(-0.5 * hidden * hidden) * ((2.0 * math.pi) ** -0.5)
    grad_low = (slope * dot_nt(upstream, w_down[...])).astype(BF16)
    grad_norm = dot_nt(grad_low, w_up[...])
    return mlp_in, act, grad_low, grad_norm


def add_sums(sums, grad_low, grad_norm, normed):
    sums[0:1, :] += jnp.sum(grad_low.astype(F32), axis=0, keepdims=True)
    sums[1:2, :] += jnp.sum(grad_norm * normed, axis=0, keepdims=True)
    sums[2:3, :] += jnp.sum(grad_norm, axis=0, keepdims=True)


def own_row(ref, blk, size):
    return ref[pl.ds(pl.multiple_of(blk * size, LANES), size)].reshape(1, size)


def mlp_first_kernel(
    half, meta, xa, xb, ca, cb, gain, shift, b_up, w_up, w_down, w_out,
    gain1, shift1, b_qkv, low, high, w0, w1, w2, w3, w4, w5,
    mo_ref, e_ref, n_ref, gv_ref, sums, gup, gdown, q_ref, k_ref, v_ref, w_own, b_own, x_s, c_s,
):
    step = pl.program_id(0)

    @pl.when(step < half)
    def _():
        x_s[...] = xa[...]
        c_s[...] = ca[...]

    @pl.when(step >= half)
    def _():
        x_s[...] = xb[...]
        c_s[...] = cb[...]

    @pl.when(step == 0)
    def _():
        sums[...] = jnp.zeros_like(sums)
        gup[...] = jnp.zeros_like(gup)
        gdown[...] = jnp.zeros_like(gdown)
        odd = meta[0] % 2
        own_blocks((w0, w1, w2, w3, w4, w5), odd, w_own)
        own_bias(b_qkv, odd, meta[0], b_own)

    upstream = c_s[...]

    @pl.when(step < half)
    def _():
        sums[3:4, :] += jnp.sum(upstream.astype(F32), axis=0, keepdims=True)

    normed = normalize(x_s[...].astype(F32))
    n_ref[...] = normed.astype(BF16)
    tile = true_block(meta, step // half) * half + step % half
    project_tile(normed, gain1, shift1, w_own, b_own, low, high, tile, q_ref, k_ref, v_ref)
    bias = own_row(b_up, meta[0], gup.shape[1])
    mlp_in, act, grad_low, grad_norm = feed(normed, upstream, gain, shift, w_up, bias, w_down)
    mo_ref[...] = dot(act, w_down[...]).astype(BF16)
    add_sums(sums, grad_low, grad_norm, normed)
    e_ref[...] = (grad_norm * row(gain)).astype(BF16)
    gv_ref[...] = dot_nt(upstream, w_out[...]).astype(BF16)
    gup[...] += dot_tn(mlp_in, grad_low)
    gdown[...] += dot_tn(upstream, act)


def mlp_second_kernel(
    half, rows, meta, xa, xb, ca, cb, gain, shift, b_up, w_up, w_down, w_out,
    c0, c1, mo_in, o_near, o_far, sums_in, gup, gdown, *refs
):
    e_ref, n_ref, gv_ref, sums, even, odd, up_keep, up_send, low_keep, low_send = refs[3:13]
    x_s, c_s, n_s, grad = refs[13:]
    step = pl.program_id(0)
    hid = gup.shape[1]

    @pl.when(step < half)
    def _():
        x_s[...] = xa[...]
        c_s[...] = ca[...]
        n_s[...] = c0[...]

    @pl.when(step >= half)
    def _():
        x_s[...] = xb[...]
        c_s[...] = cb[...]
        n_s[...] = c1[...]

    @pl.when(step == 0)
    def _():
        sums[...] = sums_in[...]
        grad[:, 0:hid] = gup[...]
        grad[:, hid : 2 * hid] = gdown[...]
        grad[:, 2 * hid :] = jnp.zeros_like(grad[:, 2 * hid :])

    upstream = c_s[...]
    normed = normalize(x_s[...].astype(F32))
    n_ref[...] = normed.astype(BF16)
    bias = own_row(b_up, meta[0], hid)
    mlp_in, act, grad_low, grad_norm = feed(normed, upstream, gain, shift, w_up, bias, w_down)
    add_sums(sums, grad_low, grad_norm, normed)
    e_ref[...] = (grad_norm * row(gain)).astype(BF16)
    gv_ref[...] = dot_nt(upstream, w_out[...]).astype(BF16)
    grad[:, 0:hid] += dot_tn(mlp_in, grad_low)
    grad[:, hid : 2 * hid] += dot_tn(upstream, act)
    out_grad = dot_tn(upstream, o_far[...]) + dot_tn(n_s[...], o_near[...])
    side = out_grad.shape[1] // 2
    if fits(rows):
        grad[:, 2 * hid : 2 * hid + side] += out_grad[:, :side]
        grad[:, 2 * hid + LANES : 2 * hid + LANES + side] += out_grad[:, side:]
    else:
        grad[:, 2 * hid : 2 * hid + 2 * side] += out_grad
    far = (dot(act, w_down[...]) + dot(o_far[...], w_out[...])).astype(BF16)
    near = (mo_in[...].astype(F32) + dot(o_near[...], w_out[...])).astype(BF16)

    @pl.when(step < half)
    def _():
        even[0] = near
        even[1] = far

    @pl.when(step >= half)
    def _():
        odd[0] = near
        odd[1] = far

    @pl.when(step == pl.num_programs(0) - 1)
    def _():
        if fits(rows):
            store_chunks(lambda at: grad[at, 0:hid], up_keep, up_send, meta, rows, 1)
            store_low(grad, low_keep, low_send, meta, rows)
        else:
            up_keep[...] = grad[:, 0:hid].astype(BF16)
            low_keep[...] = grad[:, hid:].astype(BF16)


def feed_forward(
    meta, xs, cs, gain, shift, b_up, w_up, w_down, w_out, rows, seq,
    joined=None, before=None, near=None, attn=None,
):
    per = seq // TILE
    steps = 2 * per
    hid = FF // 4
    width = D // 4
    total = 4 * seq
    first = pl.BlockSpec((TILE, D), lambda i, m: (jnp.minimum(i, per - 1), 0))
    second = pl.BlockSpec((TILE, D), lambda i, m: (jnp.maximum(i - per, 0), 0))
    specs = [
        first,
        second,
        first,
        second,
        whole((D,)),
        whole((D,)),
        whole((FF,)),
        pl.BlockSpec((D, hid), lambda i, m: (0, m[0])),
        pl.BlockSpec((hid, D), lambda i, m: (m[0], 0)),
        pl.BlockSpec((width, D), lambda i, m: (m[0], 0)),
    ]
    args = [*xs, *cs, gain, shift, b_up, w_up, w_down, w_out]
    tile = pl.BlockSpec((TILE, D), lambda i, m: (i, 0))
    narrow = pl.BlockSpec((TILE, width), lambda i, m: (i, 0))
    sums = (8, D)
    scratch = [pltpu.VMEM((TILE, D), BF16), pltpu.VMEM((TILE, D), BF16)]
    pair = jax.ShapeDtypeStruct((steps * TILE, D), BF16)
    full = jax.ShapeDtypeStruct((total, D), BF16)
    vec = jax.ShapeDtypeStruct((total, width), BF16)
    if before is None:
        body = partial(mlp_first_kernel, per)
        gain1, shift1, w_qkv, b_qkv, low, high = joined
        args += [gain1, shift1, b_qkv, low, high]
        specs += [whole(a.shape) for a in args[-5:]]
        for part in range(3):
            for side in range(2):
                specs.append(
                    pl.BlockSpec(
                        (D, LANES),
                        lambda i, m, at=part * D // LANES + side: (0, at + 3 * m[0] // 2),
                    )
                )
                args.append(w_qkv)
        outs = [pair, full, full, vec, jax.ShapeDtypeStruct(sums, F32)]
        outs += [jax.ShapeDtypeStruct((D, hid), F32)] * 2 + [vec] * 3
        outs += [
            jax.ShapeDtypeStruct((D, 3 * width), BF16),
            jax.ShapeDtypeStruct((1, 3 * width), F32),
        ]
        out_specs = [tile, tile, tile, narrow, whole(sums)]
        out_specs += [whole((D, hid))] * 2 + [narrow] * 3
        out_specs += [whole((D, 3 * width)), whole((1, 3 * width))]
        aliases = {}
    else:
        body = partial(mlp_second_kernel, per, rows)
        mlp_out, norm_part, normed, grad_vec, sums_in, gup, gdown = before
        chunks = chunk_shapes(hid, rows) + low_shapes(rows)
        args += [*near, mlp_out, attn, attn, sums_in, gup, gdown, norm_part, normed, grad_vec]
        specs += [
            first,
            second,
            tile,
            narrow,
            pl.BlockSpec((TILE, width), lambda i, m: (i + steps, 0)),
            whole(sums),
            whole((D, hid)),
            whole((D, hid)),
            *(pl.BlockSpec(memory_space=pl.ANY),) * 3,
        ]
        aliases = {len(args) - 2 + i: i for i in range(3)}
        both = jax.ShapeDtypeStruct((2, seq, D), BF16)
        outs = [full, full, vec, jax.ShapeDtypeStruct(sums, F32), both, both]
        late = pl.BlockSpec((TILE, D), lambda i, m: (i + steps, 0))
        outs += [jax.ShapeDtypeStruct(shape, BF16) for shape in chunks]
        out_specs = [
            late,
            late,
            pl.BlockSpec((TILE, width), lambda i, m: (i + steps, 0)),
            whole(sums),
            pl.BlockSpec((2, TILE, D), lambda i, m: (0, jnp.minimum(i, per - 1), 0)),
            pl.BlockSpec((2, TILE, D), lambda i, m: (0, jnp.maximum(i - per, 0), 0)),
            *(whole(shape) for shape in chunks),
        ]
        scratch += [pltpu.VMEM((TILE, D), BF16), pltpu.VMEM((D, 2 * hid + 2 * LANES), F32)]
    return pl.pallas_call(
        body,
        out_shape=outs,
        grid_spec=pltpu.PrefetchScalarGridSpec(
            num_scalar_prefetch=1,
            grid=(steps,),
            in_specs=specs,
            out_specs=out_specs,
            scratch_shapes=scratch,
        ),
        input_output_aliases=aliases,
        compiler_params=params(),
        cost_estimate=COST,
        name="mlp_first" if before is None else "mlp_second",
    )(meta, *args)


def head_masks():
    lane = lax.broadcasted_iota(jnp.int32, (1, LANES), 1)
    first = jnp.where(lane < HDIM, 1.0, 0.0).astype(BF16)
    second = jnp.where(lane < HDIM, 0.0, 1.0).astype(BF16)
    return first, second


def slot_rows(meta, per, tile):
    slot = jnp.bitwise_xor(tile // per, meta[0])
    return pl.multiple_of((slot * per + tile % per) * TILE, TILE)


def by_head(first, second, block, third):
    return (block * first, block * second, third)


def transpose_all(from_ref, to_ref):
    @pl.loop(0, from_ref.shape[0] // TILE)
    def _(tile):
        rows = pl.ds(pl.multiple_of(tile * TILE, TILE), TILE)
        to_ref[:, rows] = from_ref[rows, :].astype(F32).T.astype(BF16)


def attend_kernel(
    per, meta, valid, q_ref, k_ref, v_ref, pair_own, pair_far,
    o_ref, lse_ref, starts_ref, lo, hi, vt_ref, acc, s_ref,
):
    mask0, mask1 = head_masks()
    tiles = k_ref.shape[0] // TILE
    qi = pl.program_id(0)

    @pl.when(qi == 0)
    def _():
        find_starts(per * TILE, meta, valid, (pair_own, pair_far), starts_ref, lo, hi)
        ones = jnp.where(lax.broadcasted_iota(jnp.int32, (VROWS - HDIM, TILE), 0) == 0, 1.0, 0.0)

        @pl.loop(0, tiles)
        def _(tile):
            rows = pl.ds(pl.multiple_of(tile * TILE, TILE), TILE)
            block = v_ref[rows, :].astype(F32).T
            for head in range(3):
                at = head * VROWS
                vt_ref[at : at + HDIM, rows] = block[head * HDIM : (head + 1) * HDIM].astype(BF16)
                vt_ref[at + HDIM : at + VROWS, rows] = ones.astype(BF16)

    key_iota = lax.broadcasted_iota(jnp.int32, (TILE, TILE), 0)
    query_iota = lax.broadcasted_iota(jnp.int32, (TILE, TILE), 1)
    queries = by_head(mask0, mask1, q_ref[:, 0:128], q_ref[:, 128:192])
    starts = starts_ref[jnp.bitwise_xor(qi // per, meta[0]) * per + qi % per]
    acc[...] = jnp.zeros_like(acc)

    def key_tile(turn):
        return jnp.where(turn == 0, qi, first + turn - 1)

    def score(masked, ki):
        k_rows = pl.ds(slot_rows(meta, per, ki), TILE)
        pair, third = k_ref[k_rows, 0:128], k_ref[k_rows, 128:192]
        scores = [dot_nt(third if head == 2 else pair, queries[head]) for head in range(3)]
        if masked:
            allowed = (key_iota >= starts - ki * TILE) & (key_iota <= query_iota + (qi - ki) * TILE)
            scores = [jnp.where(allowed, x, MASKED) for x in scores]
        return scores, [jnp.max(x, axis=0, keepdims=True) for x in scores]

    def value(ki, tops, peaks):
        k_rows = pl.ds(slot_rows(meta, per, ki), TILE)
        news = [jnp.maximum(top, peak) for top, peak in zip(tops, peaks)]
        fades = [jnp.exp2(top - new) for top, new in zip(tops, news)]
        weights = [jnp.exp2(s_ref[head] - news[head]).astype(BF16) for head in range(3)]
        terms = [
            dot(vt_ref[head * VROWS : (head + 1) * VROWS, k_rows], weights[head]) for head in range(3)
        ]
        return news, fades, terms

    def put(fades, terms):
        for head in range(3):
            cols = slice(head * VROWS, (head + 1) * VROWS)
            acc[cols, :] = acc[cols, :] * fades[head] + terms[head]

    def visit(masked, turn, carry):
        tops, peaks = carry
        scores, next_peaks = score(masked, key_tile(turn + 1))
        news, fades, terms = value(key_tile(turn), tops, peaks)
        peaks = next_peaks
        for head in range(3):
            s_ref[head] = scores[head]
        put(fades, terms)
        return tuple(news), tuple(peaks)

    first = lo[qi]
    full = jnp.minimum(hi[qi], qi)
    scores, peaks = score(True, qi)
    for head in range(3):
        s_ref[head] = scores[head]
    carry = ((jnp.full((1, TILE), MASKED, F32),) * 3, tuple(peaks))
    carry = lax.fori_loop(0, full - first, partial(visit, True), carry)
    carry = lax.fori_loop(full - first, qi - first, partial(visit, False), carry)
    tops, fades, terms = value(key_tile(qi - first), *carry)
    put(fades, terms)
    heads = []
    for head, top in enumerate(tops):
        at = head * VROWS
        total = acc[at + HDIM : at + HDIM + 1, :]
        heads.append(acc[at : at + HDIM, :] / total)
        lse_ref[head, 0] = top + jnp.log2(total)
    o_ref[...] = jnp.concatenate(heads, axis=0).T.astype(BF16)

def attend(meta, valid_len, query, keys, values, seg_pair, cot_far, per):
    total, width = query.shape
    tiles = total // TILE

    def slot(i, m):
        return jnp.bitwise_xor(i // per, m[0]) * per + i % per

    q_spec = pl.BlockSpec((TILE, width), lambda i, m, v: (slot(i, m), 0))
    lse_spec = pl.BlockSpec((3, 1, 1, TILE), lambda i, m, v: (0, slot(i, m), 0, 0))
    far_spec = pl.BlockSpec((EXTRA, D), lambda i, m, v: (per * TILE // EXTRA, 0))
    smem = pl.BlockSpec(memory_space=pltpu.SMEM)
    return pl.pallas_call(
        partial(attend_kernel, per),
        out_shape=[
            jax.ShapeDtypeStruct((total, width), BF16),
            jax.ShapeDtypeStruct((3, tiles, 1, TILE), F32),
            jax.ShapeDtypeStruct((tiles, 1, TILE), jnp.int32),
            jax.ShapeDtypeStruct((tiles,), jnp.int32),
            jax.ShapeDtypeStruct((tiles,), jnp.int32),
        ],
        grid_spec=pltpu.PrefetchScalarGridSpec(
            num_scalar_prefetch=2,
            grid=(tiles,),
            in_specs=[
                q_spec,
                whole(keys.shape),
                whole(values.shape),
                whole(seg_pair.shape),
                far_spec,
            ],
            out_specs=[q_spec, lse_spec, whole((tiles, 1, TILE)), smem, smem],
            scratch_shapes=[
                pltpu.VMEM((3 * VROWS, total), BF16),
                pltpu.VMEM((3 * VROWS, TILE), F32),
                pltpu.VMEM((3, TILE, TILE), F32),
            ],
        ),
        compiler_params=params(),
        cost_estimate=COST,
        name="attend",
    )(meta, valid_len, query, keys, values, seg_pair, cot_far)


def attend_back_kernel(
    per, meta, lo, hi, q_ref, k_ref, v_ref, o_ref, gv_ref, start_ref, lse_ref, low, high,
    gj_ref, kt_ref, dk_ref, dv_ref, dqt_ref
):
    mask0, mask1 = head_masks()
    tiles = k_ref.shape[0] // TILE
    qi = tiles - 1 - pl.program_id(0)

    @pl.when(pl.program_id(0) == 0)
    def _():
        transpose_all(k_ref, kt_ref)

    own_rows = pl.ds(slot_rows(meta, per, qi), TILE)
    key_iota = lax.broadcasted_iota(jnp.int32, (TILE, TILE), 0)
    query_iota = lax.broadcasted_iota(jnp.int32, (TILE, TILE), 1)
    queries = by_head(mask0, mask1, q_ref[:, 0:128], q_ref[:, 128:192])
    grads = by_head(mask0, mask1, gv_ref[:, 0:128], gv_ref[:, 128:192])
    starts = start_ref[0]
    lses = [lse_ref[head, 0] for head in range(3)]
    product = (gv_ref[...].astype(F32) * o_ref[...].astype(F32)).T
    deltas = [
        jnp.sum(product[head * HDIM : (head + 1) * HDIM], axis=0, keepdims=True)
        for head in range(3)
    ]
    dqt_ref[...] = jnp.zeros_like(dqt_ref)

    @pl.when(pl.program_id(0) == 0)
    def _():
        dk_ref[...] = jnp.zeros_like(dk_ref)
        dv_ref[...] = jnp.zeros_like(dv_ref)

    def load(ki):
        k_rows = pl.ds(slot_rows(meta, per, ki), TILE)
        return k_rows

    def score(masked, ki):
        k_rows = load(ki)
        pair, third = k_ref[k_rows, 0:128], k_ref[k_rows, 128:192]
        v_pair, v_third = v_ref[k_rows, 0:128], v_ref[k_rows, 128:192]
        scores = [dot_nt(third if head == 2 else pair, queries[head]) for head in range(3)]
        grad_probs = [dot_nt(v_third if head == 2 else v_pair, grads[head]) for head in range(3)]
        if masked:
            allowed = (key_iota >= starts - ki * TILE) & (key_iota <= query_iota + (qi - ki) * TILE)
            scores = [jnp.where(allowed, x, MASKED) for x in scores]
        return scores, grad_probs

    def terms(ki, scores, grad_probs):
        k_rows = load(ki)
        probs = [jnp.exp2(x - lse) for x, lse in zip(scores, lses)]
        grad_scores = [
            (p * (g - delta)).astype(BF16) for p, g, delta in zip(probs, grad_probs, deltas)
        ]
        dv = [dot(p.astype(BF16), g) for p, g in zip(probs, grads)]
        dk = [dot(g, q) for g, q in zip(grad_scores, queries)]
        dq = [
            dot(kt_ref[head * HDIM : (head + 1) * HDIM, k_rows], grad_scores[head])
            for head in range(3)
        ]
        return dk, dv, dq

    def add(ki, dk, dv, dq):
        k_rows = load(ki)
        for into, parts in ((dk_ref, dk), (dv_ref, dv)):
            into[k_rows, 0:128] += parts[0] + parts[1]
            into[k_rows, 128:192] += parts[2]
        for head in range(3):
            dqt_ref[head * HDIM : (head + 1) * HDIM, :] += dq[head]

    first = lo[qi]
    full = jnp.minimum(hi[qi], qi)

    def visit(masked, ki):
        add(ki, *terms(ki, *score(masked, ki)))

    @pl.loop(first, full)
    def _(ki):
        visit(True, ki)

    @pl.loop(full, qi)
    def _(ki):
        visit(False, ki)

    visit(True, qi)

    cos, sin = rotation(low, high, qi)

    def turn_back(block):
        return block * cos - swap_halves(block) * sin

    dq = dqt_ref[...].T * (HDIM**-0.5)
    dk = dk_ref[own_rows, :] * LN2
    gj_ref[:, 0:128] = turn_back(dq[:, 0:128]).astype(BF16)
    gj_ref[:, 128:256] = turn_back(dk[:, 0:128]).astype(BF16)
    mixed = jnp.concatenate([dq[:, 128:192], dk[:, 128:192]], axis=1)
    gj_ref[:, 256:384] = turn_back(mixed).astype(BF16)
    gj_ref[:, 384:576] = dv_ref[own_rows, :].astype(BF16)


def attend_back(
    meta, lo, hi, query, keys, values, attn, grad_vec, starts, lse, low, high, per
):
    total, width = query.shape
    tiles = total // TILE

    def slot(i, m):
        tile = tiles - 1 - i
        return jnp.bitwise_xor(tile // per, m[0]) * per + tile % per

    q_spec = pl.BlockSpec((TILE, width), lambda i, m, lo, hi: (slot(i, m), 0))
    gj_spec = pl.BlockSpec((TILE, 3 * width), lambda i, m, lo, hi: (slot(i, m), 0))
    start_spec = pl.BlockSpec((1, 1, TILE), lambda i, m, lo, hi: (slot(i, m), 0, 0))
    lse_spec = pl.BlockSpec((3, 1, 1, TILE), lambda i, m, lo, hi: (0, slot(i, m), 0, 0))
    return pl.pallas_call(
        partial(attend_back_kernel, per),
        out_shape=jax.ShapeDtypeStruct((total, 3 * width), BF16),
        grid_spec=pltpu.PrefetchScalarGridSpec(
            num_scalar_prefetch=3,
            grid=(tiles,),
            in_specs=[
                q_spec,
                whole(keys.shape),
                whole(values.shape),
                q_spec,
                q_spec,
                start_spec,
                lse_spec,
                whole(low.shape),
                whole(high.shape),
            ],
            out_specs=gj_spec,
            scratch_shapes=[
                pltpu.VMEM((width, total), BF16),
                pltpu.VMEM((total, width), F32),
                pltpu.VMEM((total, width), F32),
                pltpu.VMEM((width, TILE), F32),
            ],
        ),
        compiler_params=params(),
        cost_estimate=COST,
        name="attend_back",
    )(meta, lo, hi, query, keys, values, attn, grad_vec, starts, lse, low, high)


SMALL = 16


def pack_small(gain_sum, shift_sum, bias, mlp_sums):
    third = 3 * D // 4
    which = lax.broadcasted_iota(jnp.int32, (8, D), 0)
    table = jnp.concatenate([jnp.zeros((4, D), F32), mlp_sums[0:4]], axis=0)
    table = jnp.where(which == 0, gain_sum, jnp.where(which == 1, shift_sum, table))
    head = jnp.where(which[:, :third] == 2, bias, table[:, :third])
    tail = jnp.concatenate([table[:, third:], jnp.zeros((8, 2 * third - D), F32)], axis=1)
    return jnp.concatenate([head, tail], axis=0)


def high_low(value):
    high = value.astype(BF16)
    return high, (value - high.astype(F32)).astype(BF16)


def weight_kernel(rows, meta, *refs):
    gj_ref, n_ref, gain, shift, w_ref, mlp_sums, keep, send, small, grad, bias = refs
    step = pl.program_id(0)

    @pl.when(step == 0)
    def _():
        grad[...] = jnp.zeros_like(grad)
        bias[...] = jnp.zeros_like(bias)

    joined = gj_ref[...]
    bias[0:1, :] += jnp.sum(joined.astype(F32), axis=0, keepdims=True)
    grad[...] += dot_tn(n_ref[...], joined)

    @pl.when(step == pl.num_programs(0) - 1)
    def _():
        total = bias[0:1, :]
        width = total.shape[1]
        parts = jnp.concatenate(
            [*high_low(jnp.broadcast_to(total, (8, width)))], axis=0
        )
        shift_sum = dot_nt(parts, w_ref[...])
        shift_sum = shift_sum[0:1] + shift_sum[8:9]
        ones = jnp.ones((16, width), BF16)
        high, low = high_low(grad[...] * w_ref[...].astype(F32))
        gain_sum = (dot_nt(ones, high) + dot_nt(ones, low))[0:1]
        columns = jnp.concatenate(
            [jnp.broadcast_to(row(gain), (8, D)), jnp.broadcast_to(row(shift), (8, D))], axis=0
        ).T
        grad[...] = grad[...] * columns[:, 0:1] + columns[:, 8:9] * total
        rest = pack_small(gain_sum, shift_sum, total, mlp_sums[...])
        small[...] = rest
        if fits(rows):
            store_chunks(lambda at: grad[at, :], keep, send, meta, rows, 1)
            keep[D // 2 :, :] = rest.astype(BF16)
            send[D // 2 :, :] = rest.astype(BF16)
        else:
            keep[...] = grad[...].astype(BF16)


def row_tiles(cols, tile=TILE):
    return pl.BlockSpec((tile, cols), lambda i, m: (i, 0))


def joined_weight(meta, grad, normed, gain, shift, w, mlp_sums, rows):
    total, width = grad.shape
    tile = 4 * TILE
    chunks = chunk_shapes(width, rows, SMALL)
    args = [gain, shift, w, mlp_sums]
    return pl.pallas_call(
        partial(weight_kernel, rows),
        out_shape=[jax.ShapeDtypeStruct(shape, BF16) for shape in chunks]
        + [jax.ShapeDtypeStruct((SMALL, width), F32)],
        grid_spec=pltpu.PrefetchScalarGridSpec(
            num_scalar_prefetch=1,
            grid=(total // tile,),
            in_specs=[row_tiles(width, tile), row_tiles(D, tile), *(whole(a.shape) for a in args)],
            out_specs=[*(whole(shape) for shape in chunks), whole((SMALL, width))],
            scratch_shapes=[pltpu.VMEM((D, width), F32), pltpu.VMEM((8, width), F32)],
        ),
        compiler_params=params(),
        cost_estimate=COST,
        name="joined_weight",
    )(meta, grad, normed, *args)


def norm_kernel(meta, *refs):
    gjs, es, (gain, w_ref), outs = refs[0:4], refs[4:8], refs[8:10], refs[10:]
    for gj_ref, e_in, out in zip(gjs, es, outs):
        grad_norm = dot_nt(gj_ref[...], w_ref[...])
        out[...] = (grad_norm * row(gain) + e_in[...].astype(F32)).astype(BF16)


def norm_grad(meta, grad, e_mlp, gain, w, seq):
    tile = TILE
    per = seq // tile

    def slot_tiles(slot, cols):
        return pl.BlockSpec((tile, cols), lambda i, m: (slot * per + i, 0))

    return pl.pallas_call(
        norm_kernel,
        out_shape=[jax.ShapeDtypeStruct((seq, D), BF16)] * 4,
        grid_spec=pltpu.PrefetchScalarGridSpec(
            num_scalar_prefetch=1,
            grid=(per,),
            in_specs=[
                *(slot_tiles(slot, grad.shape[1]) for slot in range(4)),
                *(slot_tiles(slot, D) for slot in range(4)),
                whole(gain.shape),
                whole(w.shape),
            ],
            out_specs=[slot_tiles(0, D)] * 4,
        ),
        compiler_params=params(),
        cost_estimate=COST,
        name="norm_grad",
    )(meta, *[grad] * 4, *[e_mlp] * 4, gain, w)


def simple(body, name, shapes, *args, specs=None):
    return pl.pallas_call(
        body,
        out_shape=[jax.ShapeDtypeStruct(shape, kind) for shape, kind in shapes],
        grid_spec=pltpu.PrefetchScalarGridSpec(
            num_scalar_prefetch=1,
            grid=(1,),
            in_specs=specs or [whole(a.shape) for a in args[1:]],
            out_specs=[whole(shape) for shape, _ in shapes],
        ),
        compiler_params=params(),
        cost_estimate=COST,
        name=name,
    )(*args)


def add_up(refs):
    total = refs[0][...].astype(F32)
    for ref in refs[1:]:
        total += ref[...].astype(F32)
    return total


def sums_kernel(counts, meta, *refs):
    ins, outs = refs[: sum(counts)], refs[sum(counts) :]
    for count, out in zip(counts, outs):
        out[...] = add_up(ins[:count]).astype(BF16)
        ins = ins[count:]


def block_sums(name, meta, steps, *jobs):
    specs, args, outs, out_specs = [], [], [], []
    for rows, terms in jobs:
        size, cols = rows // steps, terms[0][0].shape[1]
        for array, at in terms:
            specs.append(pl.BlockSpec((size, cols), lambda i, m, at=at // size: (at + i, 0)))
            args.append(array)
        outs.append(jax.ShapeDtypeStruct((rows, cols), BF16))
        out_specs.append(pl.BlockSpec((size, cols), lambda i, m: (i, 0)))
    return pl.pallas_call(
        partial(sums_kernel, [len(terms) for _, terms in jobs]),
        out_shape=outs,
        grid_spec=pltpu.PrefetchScalarGridSpec(
            num_scalar_prefetch=1, grid=(steps,), in_specs=specs, out_specs=out_specs
        ),
        compiler_params=params(),
        cost_estimate=COST,
        name=name,
    )(meta, *args)


def lower_kernel(meta, piece, down_ref, out_ref):
    cut = down_ref.shape[1]
    down_ref[...] = piece[:, :cut].astype(F32)
    out_ref[...] = piece[:, cut:].astype(F32).T[: out_ref.shape[0]]


def last_qkv_kernel(meta, *refs):
    *terms, sums, got_sums, kept, near, far, small = refs
    size = kept.shape[0]
    width = kept.shape[1]
    total = add_up(terms)
    rows = sums[...].astype(F32) + got_sums[...].astype(F32)
    for part in range(3):
        small[part * 8 : part * 8 + 8, :] = rows[0:8, part * width : (part + 1) * width]
    small[24:32, :] = rows[8:16, 0:width]
    near[size:, :] = small[...]
    far[size:, :] = small[...]
    query = jnp.concatenate([total[:, 0:128], total[:, 256:320]], axis=1)
    keys = jnp.concatenate([total[:, 128:256], total[:, 320:384]], axis=1)
    values = total[:, 384:576]
    plans = (
        (query, keys, values),
        (keys, query, values),
        (keys, values, query),
        (values, keys, query),
    )
    for blk, plan in enumerate(plans):

        @pl.when(meta[0] == blk)
        def _(plan=plan):
            kept[...] = plan[0]
            near[0:size, :] = plan[1]
            far[0:size, :] = plan[2]


def assemble_kernel(
    meta, kept, small, near, far, diag,
    qkv, b_qkv, b_out, b_up, b_down, gain1, shift1, gain2, shift2, table,
):
    size, width = kept.shape

    @pl.when(meta[0] % 2 == 0)
    def _():
        qkv[:, 0:width] = kept[...]
        qkv[:, 2 * width :] = far[0:size, :]

    @pl.when(meta[0] % 2 == 1)
    def _():
        qkv[:, 0:width] = far[0:size, :]
        qkv[:, 2 * width :] = kept[...]

    qkv[:, width : 2 * width] = near[0:size, :]
    table[0] = small[...]
    table[1] = near[size:, :]
    table[2] = far[size:, :]
    table[3] = diag[...]
    blocks = [table[jnp.bitwise_xor(meta[0], blk)] for blk in range(4)]
    total = blocks[0] + blocks[1] + blocks[2] + blocks[3]

    def vector(rows, index):
        parts = [rows[part * 8 + index : part * 8 + index + 1, :] for part in range(4)]
        return jnp.concatenate(parts, axis=1)

    for ref, index in ((gain1, 0), (shift1, 1), (gain2, 5), (shift2, 6), (b_out, 7), (b_down, 7)):
        ref[...] = vector(total, index).reshape(D)
    ups, parts = [], ([], [], [])
    for rows in blocks:
        ups.append(vector(rows, 4))
        joined = vector(rows, 2)
        parts[0].append(jnp.concatenate([joined[:, 0:128], joined[:, 256:320]], axis=1))
        parts[1].append(jnp.concatenate([joined[:, 128:256], joined[:, 320:384]], axis=1))
        parts[2].append(joined[:, 384:576])
    b_up[...] = jnp.concatenate(ups, axis=1).reshape(4 * D)
    b_qkv[...] = jnp.concatenate(parts[0] + parts[1] + parts[2], axis=1).reshape(3 * D)


def assemble(meta, kept, small, near, far, diag):
    size, width = kept.shape
    shapes = [((size, 3 * width), F32), ((3 * D,), F32), ((D,), F32), ((4 * D,), F32)]
    shapes += [((D,), F32)] * 5
    args = (kept, small, near, far, diag)
    return pl.pallas_call(
        assemble_kernel,
        out_shape=[jax.ShapeDtypeStruct(shape, kind) for shape, kind in shapes],
        grid_spec=pltpu.PrefetchScalarGridSpec(
            num_scalar_prefetch=1,
            grid=(1,),
            in_specs=[whole(a.shape) for a in args],
            out_specs=[whole(shape) for shape, _ in shapes],
            scratch_shapes=[pltpu.VMEM((4, 32, width), F32)],
        ),
        compiler_params=params(),
        cost_estimate=COST,
        name="assemble",
    )(meta, *args)


def next_send(terms, size):
    return sum(term[size // 2 : size].astype(F32) for term in terms).astype(BF16)


def reduce_plain(keep, got, masks):
    terms, size = [keep, got], keep.shape[0]
    for mask in masks:
        terms.append(swap(next_send(terms, size), "rows", mask))
        size //= 2
    return sum(term[:size].astype(F32) for term in terms)


def after(value, *others):
    return lax.optimization_barrier((value, others))[0]


def swap(value, axis, mask):
    size = lax.axis_size(axis)
    return lax.ppermute(value, axis, [(i, i ^ mask) for i in range(size)])


def add_low(left, right):
    return (left.astype(F32) + right.astype(F32)).astype(BF16)


def spread_rows(chunk):
    rows = lax.axis_size("rows")
    moves = [
        (r * 4 + b, (rows // 4 * b + r // 4) * 4 + r % 4) for r in range(rows) for b in range(4)
    ]
    return lax.ppermute(chunk, ("rows", "blk"), moves)


def split_columns(chunk):
    b = lax.axis_index("blk")
    q = jnp.concatenate([chunk[:, 0:128], chunk[:, 256:320]], axis=1)
    k = jnp.concatenate([chunk[:, 128:256], chunk[:, 320:384]], axis=1)
    v = chunk[:, 384:576]

    def choose(zero, one, two, three):
        return jnp.where(b < 2, jnp.where(b == 0, zero, one), jnp.where(b == 2, two, three))

    return choose(q, k, k, v), choose(k, q, v, k), choose(v, v, q, q)


def result_kernel(x_ref, even, near, far, b_out, b_down, out_ref):
    bias = row(b_out) + row(b_down)
    total = even[0].astype(F32) + near[0].astype(F32) + far[...].astype(F32)
    out_ref[...] = (x_ref[...].astype(F32) + bias + total).astype(BF16)


def token_kernel(x_ref, even, near, far, c_ref, out_ref):
    wide = x_ref[...].astype(F32)
    center = wide - jnp.mean(wide, axis=-1, keepdims=True)
    rate = lax.rsqrt(jnp.mean(center * center, axis=-1, keepdims=True) + EPS)
    normed = center * rate
    grad = even[...].astype(F32) + near[...].astype(F32) + far[...].astype(F32)
    mean = jnp.mean(grad, axis=-1, keepdims=True)
    along = jnp.mean(grad * normed, axis=-1, keepdims=True)
    back = rate * (grad - mean - normed * along)
    out_ref[...] = (c_ref[...].astype(F32) + back).astype(BF16)


def finish(body, name, seq, x, even, near, far, *more):
    flat = pl.BlockSpec((TILE, D), lambda i: (i, 0))
    own = pl.BlockSpec((1, TILE, D), lambda i: (0, i, 0))
    return pl.pallas_call(
        body,
        out_shape=jax.ShapeDtypeStruct((seq, D), BF16),
        grid=(seq // TILE,),
        in_specs=[
            *(own if a.ndim == 3 else flat for a in (x, even, near, far)),
            *(flat if a.ndim == 2 else whole(a.shape) for a in more),
        ],
        out_specs=flat,
        compiler_params=params(),
        cost_estimate=COST,
        name=name,
    )(x, even, near, far, *more)


def local(
    tokens, seg_ids, valid_len, ln1_gain, ln1_bias, w_qkv, b_qkv, w_out, b_out,
    ln2_gain, ln2_bias, w_up, b_up, w_down, b_down, cotangent,
):
    rows = lax.axis_size("rows")
    blk = lax.axis_index("blk")
    seq = tokens.shape[1]
    per = seq // TILE
    width = D // 4
    hid = FF // 4
    low, high = angle_parts(4 * seq)
    tok_own, cot_own = tokens[0], cotangent[0]

    cot_near = swap(cot_own, "blk", 1)
    tok_far = swap(tok_own, "blk", 2)
    tok_near = swap(tok_own, "blk", 1)
    seg_own = seg_ids.astype(BF16)
    seg_pair = jnp.concatenate([seg_own, swap(seg_own, "blk", 1)])
    seg_pair = jnp.pad(seg_pair, ((0, EXTRA - 2), (0, D - seq)))
    cot_long = jnp.concatenate([cot_own, seg_pair])
    cot_far = swap(cot_long, "blk", 2)

    meta = jnp.stack([blk, lax.axis_index("rows")]).astype(jnp.int32)
    mlp_args = (ln2_gain, ln2_bias, b_up, w_up, w_down, w_out, rows, seq)
    joined = (ln1_gain, ln1_bias, w_qkv, b_qkv, low, high)
    *first, query, keys, values, w_own, b_own = feed_forward(
        meta, (tok_own, tok_near), (cot_own, cot_near), *mlp_args, joined
    )
    meta = after(meta, b_own)

    def more(slot, m, tok, filled):
        args = (ln1_gain, ln1_bias, low, high, w_own, b_own, filled, seq)
        return project(slot, m, tok, *args)

    tok_last = swap(after(tok_far, b_own), "blk", 1)
    joined = more(2, meta, tok_far, (query, keys, values))
    query, keys, values = more(3, after(meta, joined[0]), tok_last, joined)
    cot_last = swap(after(cot_far, query), "blk", 1)
    cots = (cot_own, cot_near, cot_far, cot_last)
    attn, lse, starts, lo, hi = attend(
        meta, valid_len, query, keys, values, seg_pair, cot_far, per
    )

    meta = after(meta, lse)
    e_mlp, normed, grad_vec, mlp_sums, out_even, out_odd, *packets = feed_forward(
        meta, (tok_far, tok_last), cots[2:], *mlp_args, before=first, near=cots[:2], attn=attn
    )
    up_keep, up_send = chunks_of(*packets[:2], rows, 1)
    low_keep, low_send = low_chunks(*packets[2:], rows)
    up_masks, low_masks = mask_order(rows, 1), mask_order(rows, 2)
    out_got = swap(out_odd, "blk", 1)
    up_got = swap(up_send, "rows", up_masks[0])
    low_got = swap(low_send, "rows", low_masks[0])

    meta = after(meta, mlp_sums)
    grad_joined = attend_back(
        meta, lo, hi, query, keys, values, attn, grad_vec, starts, lse, low, high, per
    )
    meta = after(meta, grad_joined)
    qkv_keep, qkv_send, small = joined_weight(
        meta, grad_joined, normed, ln1_gain, ln1_bias, w_own, mlp_sums, rows
    )
    qkv_keep, qkv_send = chunks_of(qkv_keep, qkv_send, rows, 1)
    qkv_got = swap(qkv_send, "rows", 1)

    half = D // 2
    if fits(rows):
        chunk = D // rows
        meta = after(meta, qkv_keep)
        up, lower = [up_keep, up_got], [low_keep, low_got]
        flat = [v.reshape(2 * seq, D) for v in (out_even, out_got)]
        up_send, low_send, out_send = block_sums(
            "first_sums",
            meta,
            1,
            (half // 2, [(term, half // 2) for term in up]),
            (half, [(term, half) for term in lower]),
            (seq, [(term, seq) for term in flat]),
        )
        up.append(swap(up_send, "rows", up_masks[1]))
        lower.append(swap(low_send, "rows", low_masks[1]))
    else:
        out_send = add_low(out_even[1], out_got[1])
    out_far = swap(out_send, "blk", 2)
    meta = after(meta, out_send)
    e_own, e_near, e_send, e_last = norm_grad(meta, grad_joined, e_mlp, ln1_gain, w_own, seq)
    e_last = swap(e_last, "blk", 1)
    e_near = swap(e_near, "blk", 1)
    if fits(rows):
        joined = [after(qkv_keep, e_own), qkv_got]
        tail = add_low(joined[0][half:], qkv_got[half:])
        qkv_send = jnp.concatenate([next_send(joined, half), tail])
        joined.append(swap(qkv_send, "rows", 2))
        meta = after(meta, qkv_send)
        low_send = next_send(lower, half)
        lower.append(swap(low_send, "rows", low_masks[2]))
        e_send = after(e_send, low_send, out_far)
    e_send = add_low(e_send, e_last)
    e_far = swap(e_send, "blk", 2)
    if fits(rows):
        joined[0] = after(joined[0], e_send)
        tail = add_low(after(qkv_send, e_send)[half // 2 :], joined[2][half // 2 :])
        qkv_send = jnp.concatenate([next_send(joined, half // 2), tail])
        joined.append(swap(qkv_send, "rows", 4))
        up[0] = after(up[0], qkv_send)
        up_send = next_send(up, half // 2)
        up.append(swap(up_send, "rows", up_masks[2]))
        out_args = (after(tok_own, qkv_send), out_even, out_got, out_far, b_out, b_down)
        result = finish(result_kernel, "result", seq, *out_args)
        meta = after(meta, result)
        lower[0] = after(lower[0], result, up_send)
        piece = sum(term[:width].astype(F32) for term in lower).astype(BF16)
        meta = after(meta, piece)
        piece = spread_rows(piece)
        packet = ((chunk + 32, width), F32)
        last = pl.BlockSpec((SMALL, 3 * width), lambda i, m: (chunk // SMALL, 0))
        kept, near, far, small = simple(
            last_qkv_kernel,
            "last_qkv",
            [((chunk, width), F32), packet, packet, ((32, width), F32)],
            meta,
            *joined,
            qkv_send,
            joined[3],
            specs=[pl.BlockSpec((chunk, 3 * width), lambda i, m: (0, 0))] * 4 + [last] * 2,
        )
        near, far, diag = swap(near, "blk", 1), swap(far, "blk", 2), swap(small, "blk", 3)
        tok_args = (after(tok_own, small), e_own, e_near, e_far, cot_own)
        grad_tokens = finish(token_kernel, "token_grad", seq, *tok_args)
        meta = after(meta, grad_tokens)
        ends = [((width, hid // 2), F32), ((width // 2, width), F32)]
        down, out_w = simple(lower_kernel, "lower", ends, meta, piece)
        meta = after(meta, down)
        down = down.T
        qkv, gb_qkv, gb_out, gb_up, gb_down, *norms = assemble(
            meta, kept, small, near, far, diag
        )
        up[0] = after(up[0], qkv)
        up = sum(term[:chunk].astype(F32) for term in up)
    else:
        up = reduce_plain(up_keep, up_got, up_masks[1:])
        weights = reduce_plain(low_keep, low_got, low_masks[1:])
        qkv = reduce_plain(qkv_keep, qkv_got, up_masks[1:])
        piece = spread_rows(weights).T
        cut = 4 * hid // rows
        down, out_w = piece[:cut], piece[cut:]
        kept, near, far = split_columns(qkv)
        near, far = swap(near, "blk", 1), swap(far, "blk", 2)
        ends = [jnp.where(blk % 2 == 0, a, b) for a, b in ((kept, far), (far, kept))]
        qkv = jnp.concatenate([ends[0], near, ends[1]], axis=1)
        out_args = (tok_own, out_even, out_got, out_far, b_out, b_down)
        result = finish(result_kernel, "result", seq, *out_args)
        tok_args = (tok_own, e_own, e_near, e_far, cot_own)
        grad_tokens = finish(token_kernel, "token_grad", seq, *tok_args)
        third = 3 * width
        table = jnp.concatenate([small[0:8], small[8:16, : D - third]], axis=1)
        mine = (jnp.arange(4) == blk)[:, None]
        joined = lax.psum(jnp.where(mine, small[2:3], 0.0), ("rows", "blk"))
        gb_up = lax.psum(jnp.where(mine, table[4:5], 0.0), ("rows", "blk")).reshape(FF)
        gb_qkv = jnp.concatenate(
            [
                jnp.concatenate([joined[:, 0:128], joined[:, 256:320]], axis=1).reshape(D),
                jnp.concatenate([joined[:, 128:256], joined[:, 320:384]], axis=1).reshape(D),
                joined[:, 384:576].reshape(D),
            ]
        )
        gain_1, shift_1, _, _, _, gain_2, shift_2, gb_out = lax.psum(table, ("rows", "blk"))
        norms, gb_down = (gain_1, shift_1, gain_2, shift_2), gb_out
    return (
        result[None],
        grad_tokens[None],
        qkv,
        out_w,
        up,
        down,
        gb_qkv,
        gb_out,
        gb_up,
        gb_down,
        *norms,
    )


def solution(mesh):
    split = P("rows", "blk")
    in_specs = (
        P("rows", "blk", None),
        split,
        P("rows"),
        *(P(),) * 12,
        P("rows", "blk", None),
    )
    out_specs = (
        P("rows", "blk", None),
        P("rows", "blk", None),
        *(split,) * 4,
        *(P(),) * 8,
    )
    return jax.shard_map(local, mesh=mesh, in_specs=in_specs, out_specs=out_specs, check_vma=False)
```
